32 devices in a mesh: fsdp: 4 (over y, x), ctx: 2 (over core), tp: 4 (over z).
Axes of the slice: x: 2, y: 2, z: 4, core: 2. Of those that a mesh axis runs over, the one named last changes fastest.
Arguments:
- layer_input: bfloat16 [4, 1024, 768], P('fsdp', 'ctx'), may hold values from -6 to 6
- doc_ids: int32 [4, 1024], P('fsdp'), may hold values from 0 to 2, never falling along the last dimension, each value on 1 to 800 neighbouring positions
- query_weight: bfloat16 [768, 768], P(('fsdp', 'ctx'), 'tp'), may hold values from -0.109375 to 0.109375
- key_weight: bfloat16 [768, 768], P(('fsdp', 'ctx'), 'tp'), may hold values from -0.109375 to 0.109375
- value_weight: bfloat16 [768, 768], P(('fsdp', 'ctx'), 'tp'), may hold values from -0.21875 to 0.21875
- output_weight: bfloat16 [768, 768], P(('fsdp', 'ctx'), 'tp'), may hold values from -0.875 to 0.875
- gate_weight: bfloat16 [768, 2048], P(('fsdp', 'ctx'), 'tp'), may hold values from -0.21875 to 0.21875
- up_weight: bfloat16 [768, 2048], P(('fsdp', 'ctx'), 'tp'), may hold values from -0.21875 to 0.21875
- down_weight: bfloat16 [768, 2048], P(('fsdp', 'ctx'), 'tp'), may hold values from -0.1875 to 0.1875
- first_gain: bfloat16 [768], P(('fsdp', 'ctx')), may hold values from 0.5 to 1.5
- second_gain: bfloat16 [768], P(('fsdp', 'ctx')), may hold values from 0.5 to 1.5
- position_bias: float32 [32, 12], P(None, 'tp'), may hold values from -4 to 4
- cotangent: bfloat16 [4, 1024, 768], P('fsdp', 'ctx'), may hold values from -6 to 6
Outputs:
- layer_output: bfloat16 [4, 1024, 768], P('fsdp', 'ctx')
- input_gradient: float32 [4, 1024, 768], P('fsdp', 'ctx')
- query_gradient: float32 [768, 768], P(('fsdp', 'ctx'), 'tp')
- key_gradient: float32 [768, 768], P(('fsdp', 'ctx'), 'tp')
- value_gradient: float32 [768, 768], P(('fsdp', 'ctx'), 'tp')
- output_gradient: float32 [768, 768], P(('fsdp', 'ctx'), 'tp')
- gate_gradient: float32 [768, 2048], P(('fsdp', 'ctx'), 'tp')
- up_gradient: float32 [768, 2048], P(('fsdp', 'ctx'), 'tp')
- down_gradient: float32 [768, 2048], P(('fsdp', 'ctx'), 'tp')
- first_gain_gradient: float32 [768], P(('fsdp', 'ctx'))
- second_gain_gradient: float32 [768], P(('fsdp', 'ctx'))
- bias_gradient: float32 [32, 12], P(None, 'tp')
The draws below stay inside these ranges and needn't reach their ends.
Inputs may be any that keep to these rules, and one draw needn't show every extreme that they name: `doc_ids`: along each sequence the numbers never fall; each of 0 to 2 covers 1 to 800 positions of every sequence, and one covers exactly 800.
All inputs are finite; a program needn't handle non-finite values.
Results may differ from the reference program's by a relative error of at most 0.02.
Values may be sent and summed in bfloat16 or wider, within the bound.
A program may use at most 128 MiB of HBM per device.

```python
import math
import jax
import jax.numpy as jnp
import numpy as np
from jax import lax

D = 768
H = 12
DH = 64
FF = 2048
BUCKETS = 32
L = 1024
SEGS = 3
DOC_MOST = 800
HD = 768
SEQS = 4


def steps_of(stream_key, shape, split, least, top_value):
    factor_of = 1.0
    for position, parts in split:
        steps = jax.random.uniform(jax.random.fold_in(jax.random.fold_in(stream_key, 6), position), (parts,), jnp.float32, least / len(split), top_value / len(split))
        factor_of = factor_of * jnp.repeat(jnp.exp(steps), shape[position] // parts).reshape((-1,) + (1,) * (len(shape) - 1 - position))
    return factor_of


def split_up(count, total, reach, skew):
    loads = [(1 << 20) // math.isqrt(standing ** skew) + 1 for standing in range(2, count + 1)]
    rest, given = total - reach - (count - 1), [1] * (count - 1)
    while rest > 0:
        free = [i for i in range(count - 1) if given[i] < reach]
        whole, left = sum([loads[i] for i in free]), rest
        for i in free:
            extra = min(reach - given[i], max(1, left * loads[i] // whole), rest)
            given[i] = given[i] + extra
            rest = rest - extra
    return np.array([reach] + given)


def ragged(stream_key, amount, total, most, slope):
    if amount == 2:
        one = jax.random.randint(stream_key, (), max(1, total - most), min(most, total - 1) + 1)
        return jnp.stack([one, total - one])
    sizes = jnp.asarray(split_up(amount, total, most, slope), jnp.int32)
    pairs = (amount - 1) // 2
    donor, receiver = sizes[1:1 + 2 * pairs:2], sizes[2:2 + 2 * pairs:2]
    slack = jnp.minimum(donor - 1, most - receiver)
    passed = jax.random.randint(jax.random.fold_in(stream_key, 1), (pairs,), 0, 1 << 20) % (slack + 1)
    sizes = sizes.at[1:1 + 2 * pairs:2].set(donor - passed).at[2:2 + 2 * pairs:2].set(receiver + passed)
    return sizes[jax.random.permutation(jax.random.fold_in(stream_key, 2), amount)]


def normal_values(own_key, dims, deviation, bound, pieces=(), held_as=jnp.bfloat16):
    array = jax.random.normal(own_key, dims, jnp.float32) * deviation
    if len(pieces) > 0:
        array = steps_of(own_key, dims, pieces, -0.22, 0.18) * array
    return jnp.clip(array, min=-bound, max=bound).astype(held_as)


def setup_inputs(seed: int = 0) -> dict:
    arg_keys = jax.random.split(jax.random.key(seed), 14)
    layer_input = normal_values(arg_keys[0], (SEQS, L, D), 1.0, 6.0, ((0, 4), (1, 2)))
    doc_ids = jax.vmap(lambda own: jnp.searchsorted(jnp.cumsum(ragged(own, SEGS, L, DOC_MOST, 1)), jnp.arange(L), side="right"))(jax.random.split(arg_keys[1], SEQS)).reshape((SEQS, L)).astype(jnp.int32)
    query_weight = normal_values(arg_keys[2], (D, HD), (4 * D) ** -0.5, 0.109375, ((0, 8), (1, 4)))
    key_weight = normal_values(arg_keys[3], (D, HD), (4 * D) ** -0.5, 0.109375, ((0, 8), (1, 4)))
    value_weight = normal_values(arg_keys[4], (D, HD), D ** -0.5, 0.21875, ((0, 8), (1, 4)))
    output_weight = normal_values(arg_keys[5], (D, HD), (HD // 16) ** -0.5, 0.875, ((0, 8), (1, 4)))
    gate_weight = normal_values(arg_keys[6], (D, FF), D ** -0.5, 0.21875, ((0, 8), (1, 4)))
    up_weight = normal_values(arg_keys[7], (D, FF), D ** -0.5, 0.21875, ((0, 8), (1, 4)))
    down_weight = normal_values(arg_keys[8], (D, FF), (FF // 2) ** -0.5, 0.1875, ((0, 8), (1, 4)))
    first_gain = jnp.clip(1.0 + 0.1 * jax.random.normal(arg_keys[9], (D,), jnp.float32), 0.5, 1.5).astype(jnp.bfloat16)
    second_gain = jnp.clip(1.0 + 0.1 * jax.random.normal(arg_keys[10], (D,), jnp.float32), 0.5, 1.5).astype(jnp.bfloat16)
    position_bias = normal_values(arg_keys[11], (BUCKETS, H), 1.0, 4.0, ((1, 4),), jnp.float32)
    cotangent = normal_values(arg_keys[12], (SEQS, L, D), 1.0, 6.0, ((0, 4), (1, 2)))
    return dict(layer_input=layer_input, doc_ids=doc_ids, query_weight=query_weight, key_weight=key_weight, value_weight=value_weight, output_weight=output_weight, gate_weight=gate_weight, up_weight=up_weight, down_weight=down_weight, first_gain=first_gain, second_gain=second_gain, position_bias=position_bias, cotangent=cotangent)


epsilon = 1e-06
masked_score = -1000000000.0
bucket_edges = (12, 16, 23, 32, 46, 64, 91)
highest = lax.Precision.HIGHEST

@jax.custom_vjp
def low(v):
    return lax.optimization_barrier(v.astype(jnp.bfloat16)).astype(jnp.float32)

@jax.custom_vjp
def low_back(v):
    return v

def low_keep(v):
    return (low(v), None)

def low_pass(kept, grad):
    return (grad,)

def back_keep(v):
    return (v, None)

def back_low(kept, grad):
    return (low(grad),)
low.defvjp(low_keep, low_pass)
low_back.defvjp(back_keep, back_low)

def bucket_of(relative):
    distance = jnp.abs(relative)
    beyond = jnp.zeros_like(distance) + 8
    for edge_value in bucket_edges:
        beyond = beyond + (distance >= edge_value).astype(jnp.int32)
    inside = jnp.where(distance < 8, distance, beyond)
    return (jnp.where(relative > 0, 16, 0) + inside).astype(jnp.int32)

def rms_norm(values, gain_vector):
    inverse = lax.rsqrt(lax.optimization_barrier(jnp.mean(values * values, axis=-1, keepdims=True)) + epsilon)
    return values * inverse * gain_vector

def layer_one(params, tokens, id_row):
    query_weight, key_weight, value_weight, output_weight, gate_weight, up_weight, down_weight, first_gain, second_gain, position_bias = params
    normed_one = low(rms_norm(tokens, first_gain))
    queries = low(low_back(jnp.dot(normed_one, query_weight, precision=highest)))
    keys = low(low_back(jnp.dot(normed_one, key_weight, precision=highest)))
    values = low(low_back(jnp.dot(normed_one, value_weight, precision=highest)))
    query_heads = queries.reshape(L, H, DH)
    key_heads = keys.reshape(L, H, DH)
    value_heads = values.reshape(L, H, DH)
    raw_scores = low_back(jnp.einsum('qhd,khd->hqk', query_heads, key_heads, precision=highest))
    positions = jnp.arange(L, dtype=jnp.int32)
    buckets = bucket_of(positions[None, :] - positions[:, None])
    bias_values = jnp.transpose(position_bias[buckets], (2, 0, 1))
    same_doc = id_row[:, None] == id_row[None, :]
    scores = jnp.where(same_doc[None], raw_scores + bias_values, masked_score)
    probabilities = low(jax.nn.softmax(scores, axis=-1))
    attended = jnp.einsum('hqk,khd->qhd', probabilities, value_heads, precision=highest).reshape(L, HD)
    attended = low(low_back(attended))
    attention = low_back(jnp.dot(attended, output_weight.T, precision=highest))
    residual = tokens + attention
    normed_two = low(rms_norm(residual, second_gain))
    gate_pre = low_back(jnp.dot(normed_two, gate_weight, precision=highest))
    up_pre = low_back(jnp.dot(normed_two, up_weight, precision=highest))
    activated = low(jax.nn.gelu(gate_pre, approximate=True) * up_pre)
    return residual + low_back(jnp.dot(activated, down_weight.T, precision=highest))

def reference(layer_input, doc_ids, query_weight, key_weight, value_weight, output_weight, gate_weight, up_weight, down_weight, first_gain, second_gain, position_bias, cotangent):
    params = tuple((weight_array.astype(jnp.float32) for weight_array in (query_weight, key_weight, value_weight, output_weight, gate_weight, up_weight, down_weight, first_gain, second_gain, position_bias)))

    def whole(inputs, weights_now):

        def one_sequence(packed):
            return layer_one(weights_now, packed[0], packed[1])
        return lax.map(jax.checkpoint(one_sequence), (inputs, doc_ids))
    outputs, pullback = jax.vjp(whole, layer_input.astype(jnp.float32), params)
    input_gradient, gradients = pullback(cotangent.astype(jnp.float32))
    return (outputs.astype(jnp.bfloat16), input_gradient, gradients[0], gradients[1], gradients[2], gradients[3], gradients[4], gradients[5], gradients[6], gradients[7], gradients[8], gradients[9])
```

```python
import functools

import jax
import jax.numpy as jnp
from jax import lax
from jax.experimental import pallas as pl
from jax.experimental.pallas import tpu as pltpu
from jax.sharding import PartitionSpec as P

DH = 64


epsilon = 1e-06
masked_score = -1000000000.0
bucket_edges = (12, 16, 23, 32, 46, 64, 91)
highest = lax.Precision.HIGHEST


def bucket_of(relative):
    distance = jnp.abs(relative)
    beyond = jnp.zeros_like(distance) + 8
    for edge_value in bucket_edges:
        beyond = beyond + (distance >= edge_value).astype(jnp.int32)
    inside = jnp.where(distance < 8, distance, beyond)
    return jnp.where(relative > 0, 16, 0) + inside


def rms_norm(values, gain_vector):
    inverse = lax.rsqrt(jnp.mean(values * values, axis=-1, keepdims=True) + epsilon)
    return values * inverse * gain_vector


def gated_unit(gate_in, up_in):
    return jax.nn.gelu(gate_in, approximate=True) * up_in


def relative_bias(bias_table, query_rows, key_rows, offset):
    span_width = key_rows + query_rows
    relative = lax.iota(jnp.int32, span_width) - (query_rows - 1) - offset
    one_hot = (
        bucket_of(relative)[:, None] == lax.iota(jnp.int32, bias_table.shape[0])[None, :]
    ).astype(jnp.float32)
    per_shift = jnp.dot(one_hot, bias_table, precision=highest).T
    heads_here = bias_table.shape[1]
    toeplitz = jnp.broadcast_to(per_shift[:, None, :], (heads_here, query_rows, span_width))
    toeplitz = toeplitz.reshape(heads_here, query_rows * span_width)[
        :, : query_rows * (span_width - 1)
    ]
    toeplitz = toeplitz.reshape(heads_here, query_rows, span_width - 1)
    return (toeplitz[:, :, query_rows - 1 : query_rows - 1 + key_rows], one_hot)


def diagonal_sums(grad_scores, query_rows, key_rows):
    heads_here = grad_scores.shape[0]
    span_width = key_rows + query_rows
    placed = jnp.pad(grad_scores, ((0, 0), (0, 0), (query_rows - 1, 0)))
    placed = placed.reshape(heads_here, query_rows * (span_width - 1))
    placed = jnp.pad(placed, ((0, 0), (0, query_rows)))
    return jnp.sum(placed.reshape(heads_here, query_rows, span_width), axis=1)


def on_device(
    layer_input,
    doc_ids,
    query_weight,
    key_weight,
    value_weight,
    output_weight,
    gate_weight,
    up_weight,
    down_weight,
    first_gain,
    second_gain,
    position_bias,
    cotangent,
):
    query_rows = layer_input.shape[1]
    key_rows = query_rows * lax.axis_size("ctx")
    heads_here = position_bias.shape[1]
    head_width = heads_here * DH
    offset = lax.axis_index("ctx") * query_rows
    everything = (
        query_weight,
        key_weight,
        value_weight,
        output_weight,
        gate_weight,
        up_weight,
        down_weight,
        first_gain,
        second_gain,
    )
    (
        full_query,
        full_key,
        full_value,
        full_output,
        full_gate,
        full_up,
        full_down,
        gain_one,
        gain_two,
    ) = (
        lax.all_gather(everything[0], ("fsdp", "ctx"), axis=0, tiled=True),
        lax.all_gather(everything[1], ("fsdp", "ctx"), axis=0, tiled=True),
        lax.all_gather(everything[2], ("fsdp", "ctx"), axis=0, tiled=True),
        lax.all_gather(everything[3], ("fsdp", "ctx"), axis=0, tiled=True),
        lax.all_gather(everything[4], ("fsdp", "ctx"), axis=0, tiled=True),
        lax.all_gather(everything[5], ("fsdp", "ctx"), axis=0, tiled=True),
        lax.all_gather(everything[6], ("fsdp", "ctx"), axis=0, tiled=True),
        lax.all_gather(everything[7], ("fsdp", "ctx"), axis=0, tiled=True),
        lax.all_gather(everything[8], ("fsdp", "ctx"), axis=0, tiled=True),
    )
    inputs = layer_input.astype(jnp.float32)
    gain_first = gain_one.astype(jnp.float32)
    gain_second = gain_two.astype(jnp.float32)
    normed_one = rms_norm(inputs, gain_first).astype(jnp.bfloat16)
    queries = jnp.dot(normed_one, full_query, preferred_element_type=jnp.float32).astype(
        jnp.bfloat16
    )
    keys_local = jnp.dot(normed_one, full_key, preferred_element_type=jnp.float32).astype(
        jnp.bfloat16
    )
    values_local = jnp.dot(normed_one, full_value, preferred_element_type=jnp.float32).astype(
        jnp.bfloat16
    )
    keys_all, values_all = (
        lax.all_gather(keys_local, "ctx", axis=1, tiled=True),
        lax.all_gather(values_local, "ctx", axis=1, tiled=True),
    )
    bias_block, one_hot = relative_bias(position_bias, query_rows, key_rows, offset)

    def scores_of(query_heads, key_heads, id_row):
        raw_scores = jnp.einsum(
            "qhd,khd->hqk", query_heads, key_heads, preferred_element_type=jnp.float32
        )
        own_ids = lax.dynamic_slice_in_dim(id_row, offset, query_rows)
        same_doc = own_ids[:, None] == id_row[None, :]
        return jnp.where(same_doc[None], raw_scores + bias_block, masked_score)

    def forward_one(packed):
        query_seq, key_seq, value_seq, id_row = packed
        scores = scores_of(
            query_seq.reshape(query_rows, heads_here, DH),
            key_seq.reshape(key_rows, heads_here, DH),
            id_row,
        )
        row_max = jnp.max(scores, axis=-1, keepdims=True)
        exponentials = jnp.exp(scores - row_max)
        row_total = jnp.sum(exponentials, axis=-1, keepdims=True)
        probabilities = (exponentials / row_total).astype(jnp.bfloat16)
        attended = jnp.einsum(
            "hqk,khd->qhd",
            probabilities,
            value_seq.reshape(key_rows, heads_here, DH),
            preferred_element_type=jnp.float32,
        )
        log_row = row_max[..., 0] + jnp.log(row_total[..., 0])
        return (attended.reshape(query_rows, head_width).astype(jnp.bfloat16), log_row)

    attended, log_sums = lax.map(forward_one, (queries, keys_all, values_all, doc_ids))
    attention_terms = jnp.einsum(
        "sqe,de->sqd", attended, full_output, preferred_element_type=jnp.float32
    )
    residual = inputs + lax.psum(attention_terms.astype(jnp.bfloat16), "tp").astype(jnp.float32)
    normed_two = rms_norm(residual, gain_second).astype(jnp.bfloat16)
    gate_pre = jnp.dot(normed_two, full_gate, preferred_element_type=jnp.float32)
    up_pre = jnp.dot(normed_two, full_up, preferred_element_type=jnp.float32)
    activated = gated_unit(gate_pre, up_pre).astype(jnp.bfloat16)
    ffn_terms = jnp.einsum("sqf,df->sqd", activated, full_down, preferred_element_type=jnp.float32)
    output_rows = (
        residual + lax.psum(ffn_terms.astype(jnp.bfloat16), "tp").astype(jnp.float32)
    ).astype(jnp.bfloat16)
    grad_activated = jnp.einsum(
        "sqd,df->sqf", cotangent, full_down, preferred_element_type=jnp.float32
    )
    down_grad = jnp.einsum("sqd,sqf->df", cotangent, activated, preferred_element_type=jnp.float32)
    gated_value, gated_back = jax.vjp(gated_unit, gate_pre, up_pre)
    grad_gate, grad_up = gated_back(grad_activated)
    grad_gate = grad_gate.astype(jnp.bfloat16)
    grad_up = grad_up.astype(jnp.bfloat16)
    gate_grad = jnp.einsum("sqd,sqf->df", normed_two, grad_gate, preferred_element_type=jnp.float32)
    up_grad = jnp.einsum("sqd,sqf->df", normed_two, grad_up, preferred_element_type=jnp.float32)
    normed_two_terms = jnp.einsum(
        "sqf,df->sqd", grad_gate, full_gate, preferred_element_type=jnp.float32
    ) + jnp.einsum("sqf,df->sqd", grad_up, full_up, preferred_element_type=jnp.float32)
    grad_normed_two = lax.psum(normed_two_terms.astype(jnp.bfloat16), "tp").astype(jnp.float32)
    second_value, second_back = jax.vjp(rms_norm, residual, gain_second)
    grad_residual, second_gain_grad = second_back(grad_normed_two)
    grad_residual = grad_residual + cotangent.astype(jnp.float32)
    grad_low = grad_residual.astype(jnp.bfloat16)
    grad_attended = jnp.einsum(
        "sqd,de->sqe", grad_low, full_output, preferred_element_type=jnp.float32
    ).astype(jnp.bfloat16)
    output_grad = jnp.einsum("sqd,sqe->de", grad_low, attended, preferred_element_type=jnp.float32)

    def backward_one(running, packed):
        query_seq, key_seq, value_seq, id_row, grad_seq, log_row = packed
        query_heads = query_seq.reshape(query_rows, heads_here, DH)
        key_heads = key_seq.reshape(key_rows, heads_here, DH)
        value_heads = value_seq.reshape(key_rows, heads_here, DH)
        grad_heads = grad_seq.reshape(query_rows, heads_here, DH)
        scores = scores_of(query_heads, key_heads, id_row)
        probabilities = jnp.exp(scores - log_row[..., None])
        grad_probs = jnp.einsum(
            "qhd,khd->hqk", grad_heads, value_heads, preferred_element_type=jnp.float32
        )
        grad_values = jnp.einsum(
            "hqk,qhd->khd",
            probabilities.astype(jnp.bfloat16),
            grad_heads,
            preferred_element_type=jnp.float32,
        )
        grad_scores = probabilities * (
            grad_probs - jnp.sum(probabilities * grad_probs, axis=-1, keepdims=True)
        )
        low_scores = grad_scores.astype(jnp.bfloat16)
        grad_queries = jnp.einsum(
            "hqk,khd->qhd", low_scores, key_heads, preferred_element_type=jnp.float32
        )
        grad_keys = jnp.einsum(
            "hqk,qhd->khd", low_scores, query_heads, preferred_element_type=jnp.float32
        )
        running = running + diagonal_sums(grad_scores, query_rows, key_rows)
        return (
            running,
            (
                grad_queries.reshape(query_rows, head_width).astype(jnp.bfloat16),
                grad_keys.reshape(key_rows, head_width),
                grad_values.reshape(key_rows, head_width),
            ),
        )

    shift_grads, (grad_queries, key_parts, value_parts) = lax.scan(
        backward_one,
        jnp.zeros((heads_here, query_rows + key_rows), jnp.float32),
        (queries, keys_all, values_all, doc_ids, grad_attended, log_sums),
    )
    grad_keys, grad_values = (
        lax.psum_scatter(
            key_parts.astype(jnp.bfloat16), "ctx", scatter_dimension=1, tiled=True
        ).astype(jnp.float32),
        lax.psum_scatter(
            value_parts.astype(jnp.bfloat16), "ctx", scatter_dimension=1, tiled=True
        ).astype(jnp.float32),
    )
    grad_keys = grad_keys.astype(jnp.bfloat16)
    grad_values = grad_values.astype(jnp.bfloat16)
    normed_one_terms = (
        jnp.einsum("sqe,de->sqd", grad_queries, full_query, preferred_element_type=jnp.float32)
        + jnp.einsum("sqe,de->sqd", grad_keys, full_key, preferred_element_type=jnp.float32)
        + jnp.einsum("sqe,de->sqd", grad_values, full_value, preferred_element_type=jnp.float32)
    )
    grad_normed_one = lax.psum(normed_one_terms.astype(jnp.bfloat16), "tp").astype(jnp.float32)
    query_grad = jnp.einsum(
        "sqd,sqe->de", normed_one, grad_queries, preferred_element_type=jnp.float32
    )
    key_grad = jnp.einsum("sqd,sqe->de", normed_one, grad_keys, preferred_element_type=jnp.float32)
    value_grad = jnp.einsum(
        "sqd,sqe->de", normed_one, grad_values, preferred_element_type=jnp.float32
    )
    first_value, first_back = jax.vjp(rms_norm, inputs, gain_first)
    grad_inputs, first_gain_grad = first_back(grad_normed_one)
    input_rows = grad_residual + grad_inputs
    bias_gradient = lax.psum(jnp.dot(one_hot.T, shift_grads.T, precision=highest), ("fsdp", "ctx"))
    (
        query_total,
        key_total,
        value_total,
        output_total,
        gate_total,
        up_total,
        down_total,
        first_total,
        second_total,
    ) = (
        lax.psum_scatter(query_grad, ("fsdp", "ctx"), scatter_dimension=0, tiled=True),
        lax.psum_scatter(key_grad, ("fsdp", "ctx"), scatter_dimension=0, tiled=True),
        lax.psum_scatter(value_grad, ("fsdp", "ctx"), scatter_dimension=0, tiled=True),
        lax.psum_scatter(output_grad, ("fsdp", "ctx"), scatter_dimension=0, tiled=True),
        lax.psum_scatter(gate_grad, ("fsdp", "ctx"), scatter_dimension=0, tiled=True),
        lax.psum_scatter(up_grad, ("fsdp", "ctx"), scatter_dimension=0, tiled=True),
        lax.psum_scatter(down_grad, ("fsdp", "ctx"), scatter_dimension=0, tiled=True),
        lax.psum_scatter(first_gain_grad, ("fsdp", "ctx"), scatter_dimension=0, tiled=True),
        lax.psum_scatter(second_gain_grad, ("fsdp", "ctx"), scatter_dimension=0, tiled=True),
    )
    return (
        output_rows,
        input_rows,
        query_total,
        key_total,
        value_total,
        output_total,
        gate_total,
        up_total,
        down_total,
        first_total,
        second_total,
        bias_gradient,
    )


MESH = pl.DeviceIdType.MESH
bf16, f32 = jnp.bfloat16, jnp.float32
BLOCK = 128
QUERY_BLOCK = 256
CHUNK = 64


def contract(left, right, left_dim, right_dim, precision=None):
    return lax.dot_general(
        left,
        right,
        (((left_dim,), (right_dim,)), ((), ())),
        preferred_element_type=f32,
        precision=precision,
    )


def iota(shape, dim):
    return lax.broadcasted_iota(jnp.int32, shape, dim)


def layer_kernel(
    shards,
    x_ref,
    cot_ref,
    ids_ref,
    gains_ref,
    wq_ref,
    wk_ref,
    wv_ref,
    wo_ref,
    wg_ref,
    wu_ref,
    wd_ref,
    table_ref,
    out_ref,
    gin_ref,
    gq_ref,
    gk_ref,
    gv_ref,
    go_ref,
    gg_ref,
    gu_ref,
    gd_ref,
    gains_out_ref,
    bias_out_ref,
    wa,
    wf,
    gains_all,
    gain_rows,
    tiles,
    masked_bias,
    score,
    expo,
    low_score,
    snd,
    part,
    tot,
    resid,
    grad_res,
    n1,
    n2,
    grl,
    n1t,
    act,
    ggate,
    gup,
    q_t,
    k_all,
    v_all,
    k_t,
    v_t,
    att_t,
    dos_t,
    dq_t,
    linv,
    delta,
    dk,
    dv,
    near,
    pick,
    dkv_send,
    dkv_recv,
    dkv,
    gsa,
    gsf,
    ra,
    rf,
    sa,
    sf,
    ra2,
    rf2,
    small,
    small_all,
    ag_send,
    ag_recv,
    kv_send,
    kv_recv,
    s1,
    r1,
    s2,
    r2,
    dkv_ssem,
    dkv_rsem,
    rs_send,
    rs_recv,
    rs2_send,
    rs2_recv,
    sm_send,
    sm_recv,
):
    groups = shards // 2
    f, c, t = lax.axis_index("fsdp"), lax.axis_index("ctx"), lax.axis_index("tp")
    me = f * 2 + c
    rows, width = x_ref.shape
    keys = k_all.shape[0]
    head_width = wq_ref.shape[1]
    heads = head_width // DH
    units = wg_ref.shape[1]
    shard = wq_ref.shape[0]
    chunks = rows // CHUNK
    partner = (f, 1 - c, t)
    outer = jnp.logical_or(t == 0, t == 3)
    inner = jnp.logical_or(t == 1, t == 2)
    near_end = jnp.where(t < 2, 1, 2)
    far_end = jnp.where(t < 2, 0, 3)
    middle = 3 - t

    def remote(source, target, send_sem, recv_sem, device):
        return pltpu.make_async_remote_copy(
            src_ref=source,
            dst_ref=target,
            send_sem=send_sem,
            recv_sem=recv_sem,
            device_id=device,
            device_id_type=MESH,
        )

    barrier = pltpu.get_barrier_semaphore()
    for k in range(groups):
        for kc in range(2):
            if k or kc:
                pl.semaphore_signal(
                    barrier, inc=1, device_id=(f ^ k, c ^ kc, t), device_id_type=MESH
                )

    @pl.when(outer)
    def _():
        pl.semaphore_signal(barrier, inc=1, device_id=(f, c, near_end), device_id_type=MESH)

    @pl.when(inner)
    def _():
        pl.semaphore_signal(barrier, inc=1, device_id=(f, c, far_end), device_id_type=MESH)
        pl.semaphore_signal(barrier, inc=1, device_id=(f, c, middle), device_id_type=MESH)

    wa[me, 0] = wq_ref[...]
    wa[me, 1] = wk_ref[...]
    wa[me, 2] = wv_ref[...]
    wa[me, 3] = wo_ref[...]
    wf[me, 0] = wg_ref[...]
    wf[me, 1] = wu_ref[...]
    wf[me, 2] = wd_ref[...]
    gains_all[me] = gains_ref[...]

    @pl.when(outer)
    def _():
        pl.semaphore_wait(barrier, shards)

    @pl.when(inner)
    def _():
        pl.semaphore_wait(barrier, shards + 1)

    def piece(g, index):
        if g == 0:
            return wa.at[index, 0:3]
        if g == 1:
            return wa.at[index, 3:4]
        if g == 2:
            return wf.at[index, 0:2]
        if g == 3:
            return wf.at[index, 2:3]
        return gains_all.at[index]

    def gather_out(g, k):
        view = piece(g, me)
        return remote(view, view, ag_send.at[g, k - 1], ag_recv.at[g, k - 1], (f ^ k, c, t))

    def gather_over(g, k):
        view = piece(g, (f ^ k) * 2 + c)
        slot = groups - 1 + k
        return remote(view, view, ag_send.at[g, slot], ag_recv.at[g, slot], partner)

    def gather_start(g):
        for k in range(1, groups):
            gather_out(g, k).start()
        gather_over(g, 0).start()

    def gather_relay(g):
        for k in range(1, groups):
            gather_out(g, k).wait_recv()
            gather_over(g, k).start()

    def gather_finish(g):
        for k in range(groups):
            gather_over(g, k).wait_recv()

    def gather_drain(g):
        for k in range(1, groups):
            gather_out(g, k).wait_send()
        for k in range(groups):
            gather_over(g, k).wait_send()

    def span(j):
        return pl.ds(pl.multiple_of(j * CHUNK, CHUNK), CHUNK)

    def end_copy(a, j):
        return remote(
            snd.at[a, span(j)], part.at[a, span(j)], s1.at[a, j], r1.at[a, j], (f, c, near_end)
        )

    def mid_copy(a, j):
        return remote(
            snd.at[a, span(j)], tot.at[a, span(j)], s1.at[a, j], r2.at[a, j], (f, c, middle)
        )

    def total_copy(a, j):
        return remote(
            tot.at[a, span(j)], tot.at[a, span(j)], s2.at[a, j], r2.at[a, j], (f, c, far_end)
        )

    def put(a, j):
        @pl.when(outer)
        def _():
            end_copy(a, j).start()

    def relay_a(a, j):
        @pl.when(inner)
        def _():
            end_copy(a, j).wait_recv()
            snd[a, span(j)] = (
                snd[a, span(j)].astype(f32) + part[a, span(j)].astype(f32)
            ).astype(bf16)
            mid_copy(a, j).start()

    def relay_b(a, j):
        @pl.when(inner)
        def _():
            mid_copy(a, j).wait_recv()
            tot[a, span(j)] = (
                snd[a, span(j)].astype(f32) + tot[a, span(j)].astype(f32)
            ).astype(bf16)
            total_copy(a, j).start()

    def finish(a, j):
        @pl.when(outer)
        def _():
            total_copy(a, j).wait_recv()

    def advance(a, s):
        @pl.when(s < chunks)
        def _():
            relay_a(a, jnp.minimum(s, chunks - 1))

        @pl.when(jnp.logical_and(s >= 2, s - 2 < chunks))
        def _():
            relay_b(a, jnp.clip(s - 2, 0, chunks - 1))

    def drain(a):
        def body(j, carry):
            @pl.when(outer)
            def _():
                end_copy(a, j).wait_send()

            @pl.when(inner)
            def _():
                mid_copy(a, j).wait_send()
                total_copy(a, j).wait_send()

            return carry

        lax.fori_loop(0, chunks, body, 0)

    gather_start(4)
    gather_start(0)

    half = table_ref.shape[0] // 2
    far = half - 1
    row_of, column_of = iota((BLOCK, BLOCK), 0), iota((BLOCK, BLOCK), 1)
    for h in range(heads):
        tiles[h, 0] = jnp.full((BLOCK, BLOCK), table_ref[far, h], f32)
        tiles[h, 4] = jnp.full((BLOCK, BLOCK), table_ref[half + far, h], f32)
    for d in (-1, 0, 1):
        bucket = bucket_of(d * BLOCK + row_of - column_of)
        members = range(half) if d < 0 else range(half, 2 * half) if d > 0 else range(2 * half)

        def per_head(h, carry, bucket=bucket, members=members, d=d):
            filled = jnp.zeros((BLOCK, BLOCK), f32)
            for b in members:
                filled = jnp.where(bucket == b, table_ref[b, h], filled)
            tiles[h, d + 2] = filled
            return carry

        lax.fori_loop(0, heads, per_head, 0)

    def bias_rows(kb, carry):
        key_rows = pl.ds(pl.multiple_of(kb * BLOCK, BLOCK), BLOCK)
        key_ids = jnp.broadcast_to(ids_ref[0:1, key_rows].astype(f32), (BLOCK, BLOCK)).T
        for qb in range(rows // BLOCK):
            start = pl.multiple_of(c * rows + qb * BLOCK, BLOCK)
            query_ids = ids_ref[0:1, pl.ds(start, BLOCK)].astype(f32)
            same = key_ids == query_ids
            d = jnp.clip(kb - c * (rows // BLOCK) - qb, -2, 2) + 2
            for h in range(heads):
                masked_bias[h, key_rows, qb * BLOCK : (qb + 1) * BLOCK] = jnp.where(
                    same, tiles[h, d], masked_score
                )
        return carry

    lax.fori_loop(0, keys // BLOCK, bias_rows, 0)
    near[...] = jnp.zeros_like(near)
    dk[...] = jnp.zeros_like(dk)
    dv[...] = jnp.zeros_like(dv)
    small[...] = jnp.zeros_like(small)

    gather_relay(4)
    gather_relay(0)
    for g in (1, 2, 3):
        gather_start(g)
    gather_finish(4)
    spread = jnp.zeros((8, width), f32)
    for i in range(shards):
        one_hot = (iota((BLOCK, width), 1) == iota((BLOCK, width), 0) + i * shard).astype(f32)
        spread = spread + contract(gains_all[i].astype(bf16), one_hot.astype(bf16), 1, 0)
    gain_rows[...] = spread

    def block_rows(b, size=BLOCK):
        return pl.ds(pl.multiple_of(b * size, size), size)

    def inverse_rms(values):
        return lax.rsqrt(jnp.mean(values * values, axis=-1, keepdims=True) + epsilon)

    def norm_one(b, carry):
        at = block_rows(b)
        xs = x_ref[at, :].astype(f32)
        n1[at, :] = (xs * inverse_rms(xs) * gain_rows[0:1, :]).astype(bf16)
        return carry

    lax.fori_loop(0, rows // BLOCK, norm_one, 0)
    gather_finish(0)

    def weight(buffer, a):
        return buffer[:, a].reshape(width, buffer.shape[-1])

    own_keys = pl.ds(pl.multiple_of(c * rows, rows), rows)
    normed = n1[...]
    k_all[own_keys, :] = contract(normed, weight(wa, 1), 1, 0).astype(bf16)
    v_all[own_keys, :] = contract(normed, weight(wa, 2), 1, 0).astype(bf16)
    kv_copies = [
        remote(ref.at[own_keys], ref.at[own_keys], kv_send.at[n], kv_recv.at[n], partner)
        for n, ref in enumerate((k_all, v_all))
    ]
    for copy in kv_copies:
        copy.start()
    q_t[...] = contract(normed, weight(wa, 0), 1, 0).astype(bf16).T
    n1t[...] = normed.T
    gather_relay(1)
    for copy in kv_copies:
        copy.wait_recv()
    k_t[...] = k_all[...].T
    v_t[...] = v_all[...].T
    gather_finish(1)

    head_of = iota((head_width, QUERY_BLOCK), 0)

    def head_only(values, h):
        inside = jnp.logical_and(head_of >= h * DH, head_of < (h + 1) * DH)
        return jnp.where(inside, values, jnp.zeros_like(values))

    def attend(qb, carry):
        at = block_rows(qb, QUERY_BLOCK)
        for h in range(heads):
            queries = head_only(q_t[:, at], h)
            top = jnp.full((8, QUERY_BLOCK), -jnp.inf, f32)
            for kb in range(keys // BLOCK):
                span_k = slice(kb * BLOCK, (kb + 1) * BLOCK)
                block = contract(k_all[span_k, :], queries, 1, 0) + masked_bias[h, span_k, at]
                score[span_k, :] = block
                top = jnp.maximum(top, jnp.max(block.reshape(BLOCK // 8, 8, QUERY_BLOCK), axis=0))
            top = jnp.max(top, axis=0, keepdims=True)
            total = jnp.zeros((8, QUERY_BLOCK), f32)
            for kb in range(keys // BLOCK):
                span_k = slice(kb * BLOCK, (kb + 1) * BLOCK)
                block = jnp.exp(score[span_k, :] - top)
                expo[h, span_k, at] = block.astype(bf16)
                total = total + jnp.sum(block.reshape(BLOCK // 8, 8, QUERY_BLOCK), axis=0)
            inverse = 1.0 / jnp.sum(total, axis=0, keepdims=True)
            linv[h : h + 1, at] = inverse
            mixed = contract(v_t[h * DH : (h + 1) * DH, :], expo[h, :, at], 1, 0)
            att_t[h * DH : (h + 1) * DH, at] = (mixed * inverse).astype(bf16)
        attended = att_t[:, at].T
        snd[0, at, :] = contract(attended, weight(wa, 3), 1, 1).astype(bf16)
        for j in range(QUERY_BLOCK // CHUNK):
            put(0, qb * (QUERY_BLOCK // CHUNK) + j)
        return carry

    lax.fori_loop(0, rows // QUERY_BLOCK, attend, 0)

    for g in (2, 3):
        gather_relay(g)
    for g in (2, 3):
        gather_finish(g)

    per_block = BLOCK // CHUNK
    scale = 0.7978845608028654
    advance(0, 0)
    advance(0, 1)

    def feed_forward(b, carry):
        for j in range(per_block):
            advance(0, b * per_block + 2 + j)
        for j in range(per_block):
            finish(0, b * per_block + j)
        at = block_rows(b)
        res = x_ref[at, :].astype(f32) + tot[0, at, :].astype(f32)
        resid[at, :] = res
        normed = (res * inverse_rms(res) * gain_rows[1:2, :]).astype(bf16)
        n2[at, :] = normed
        gate = contract(normed, weight(wf, 0), 1, 0)
        up = contract(normed, weight(wf, 1), 1, 0)
        down = weight(wf, 2)
        grad_act = contract(cot_ref[at, :], down, 1, 0)
        square = gate * gate
        curve = jnp.tanh(scale * (gate + 0.044715 * square * gate))
        left = 0.5 * (1.0 + curve)
        value = gate * left
        slope = left + 0.5 * gate * (1.0 - curve * curve) * scale * (1.0 + 0.134145 * square)
        low_act = (value * up).astype(bf16)
        low_gate = (grad_act * up * slope).astype(bf16)
        low_up = (grad_act * value).astype(bf16)
        act[at, :] = low_act
        ggate[at, :] = low_gate
        gup[at, :] = low_up
        snd[1, at, :] = (
            contract(low_gate, weight(wf, 0), 1, 1) + contract(low_up, weight(wf, 1), 1, 1)
        ).astype(bf16)
        for j in range(per_block):
            put(1, b * per_block + j)
        snd[2, at, :] = contract(low_act, down, 1, 1).astype(bf16)
        return carry

    lax.fori_loop(0, rows // BLOCK, feed_forward, 0)

    def put_all(a):
        def body(j, carry):
            put(a, j)
            return carry

        lax.fori_loop(0, chunks, body, 0)

    put_all(2)

    def sent(n, which):
        if n == 0:
            return gsf.at[:, which]
        return gsa.at[:, which, 3:4] if n == 1 else gsa.at[:, which, 0:3]

    def landed(n):
        return rf.at[...] if n == 0 else ra.at[:, 3:4] if n == 1 else ra.at[:, 0:3]

    def over_copy(n):
        return remote(sent(n, 1 - c), landed(n), rs_send.at[n], rs_recv.at[n], partner)

    def summed(n, index):
        return sf.at[index] if n == 0 else sa.at[index, 3:4] if n == 1 else sa.at[index, 0:3]

    def arrived(n, k):
        return rf2.at[k - 1] if n == 0 else ra2.at[k - 1, 3:4] if n == 1 else ra2.at[k - 1, 0:3]

    def out_copy(n, k):
        return remote(
            summed(n, f ^ k), arrived(n, k), rs2_send.at[n, k - 1], rs2_recv.at[n, k - 1],
            (f ^ k, c, t),
        )

    members_of = {0: (0, 1, 2), 1: (3,), 2: (0, 1, 2)}
    results = {
        0: (gg_ref, gu_ref, gd_ref),
        1: (go_ref,),
        2: (gq_ref, gk_ref, gv_ref),
    }

    def reduce_send(n):
        over_copy(n).wait_recv()
        own, got, total = (gsf, rf, sf) if n == 0 else (gsa, ra, sa)

        def body(k, carry):
            index = jnp.bitwise_xor(f, groups - 1 - k)
            for a in members_of[n]:
                total[index, a] = (
                    own[index, c, a].astype(f32) + got[index, a].astype(f32)
                ).astype(bf16)
            return carry

        lax.fori_loop(0, groups, body, 0)
        for k in range(1, groups):
            out_copy(n, k).start()

    def reduce_finish(n):
        total, got = (sf, rf2) if n == 0 else (sa, ra2)
        for k in range(1, groups):
            out_copy(n, k).wait_recv()
        for a, result in zip(members_of[n], results[n]):
            value = total[f, a].astype(f32)
            for k in range(1, groups):
                value = value + got[k - 1, a].astype(f32)
            result[...] = value

    def reduce_drain(n):
        over_copy(n).wait_send()
        for k in range(1, groups):
            out_copy(n, k).wait_send()

    both = 2 * shard

    def wide_columns(i):
        return pl.ds(pl.multiple_of(i * both, both), both)

    def store_grad(buffer, i, a, value):
        buffer[i, :, a] = value.astype(bf16).reshape(2, shard, value.shape[-1])

    n2_t = n2[...].T
    cot_t = cot_ref[...].T
    for i in range(groups):
        cut = slice(i * both, (i + 1) * both)
        store_grad(gsf, i, 0, contract(n2_t[cut], ggate[...], 1, 0))
        store_grad(gsf, i, 1, contract(n2_t[cut], gup[...], 1, 0))
        store_grad(gsf, i, 2, contract(cot_t[cut], act[...], 1, 0))
    over_copy(0).start()

    advance(1, 0)
    advance(1, 1)

    def residual_back(b, carry):
        for j in range(per_block):
            advance(1, b * per_block + 2 + j)
        for j in range(per_block):
            finish(1, b * per_block + j)
        at = block_rows(b)
        grad_in = tot[1, at, :].astype(f32)
        res = resid[at, :]
        inverse = inverse_rms(res)
        u = res * inverse
        small[1:2, :] += jnp.sum(grad_in * u, axis=0, keepdims=True)
        g = grad_in * gain_rows[1:2, :]
        grad = cot_ref[at, :].astype(f32) + inverse * (
            g - u * jnp.mean(g * u, axis=-1, keepdims=True)
        )
        grad_res[at, :] = grad
        low_grad = grad.astype(bf16)
        grl[at, :] = low_grad
        grad_att = contract(low_grad, weight(wa, 3), 1, 0).astype(bf16)
        scaled = grad_att.T.astype(f32) * jnp.concatenate(
            [jnp.broadcast_to(linv[h : h + 1, at], (DH, BLOCK)) for h in range(heads)], axis=0
        )
        scaled = scaled.astype(bf16)
        dos_t[:, at] = scaled
        delta[0:heads, at] = jnp.sum(
            (scaled.astype(f32) * att_t[:, at].astype(f32)).reshape(heads, DH, BLOCK), axis=1
        )
        return carry

    lax.fori_loop(0, rows // BLOCK, residual_back, 0)
    reduce_send(0)

    extra = dk.shape[1] - head_width
    query_blocks = rows // BLOCK

    def attend_back(qb, carry):
        at = block_rows(qb, QUERY_BLOCK)
        for h in range(heads):
            grads = head_only(dos_t[:, at], h)
            queries = head_only(q_t[:, at], h)
            flag = iota((extra, QUERY_BLOCK), 0)
            lane = iota((extra, QUERY_BLOCK), 1)
            flags = jnp.zeros((extra, QUERY_BLOCK), f32)
            for j in range(QUERY_BLOCK // BLOCK):
                hit = jnp.logical_and(
                    flag == h * query_blocks + qb * (QUERY_BLOCK // BLOCK) + j,
                    jnp.logical_and(lane >= j * BLOCK, lane < (j + 1) * BLOCK),
                )
                flags = jnp.where(hit, 1.0, flags)
            flagged = jnp.concatenate([queries, flags.astype(bf16)], axis=0)
            shift = delta[h : h + 1, at]
            for kb in range(keys // BLOCK):
                span_k = slice(kb * BLOCK, (kb + 1) * BLOCK)
                block = contract(v_all[span_k, :], grads, 1, 0)
                low_score[span_k, :] = (
                    expo[h, span_k, at].astype(f32) * (block - shift)
                ).astype(bf16)
            dv[...] += contract(expo[h, :, at], grads, 1, 1)
            dk[...] += contract(low_score[...], flagged, 1, 1)
            dq_t[h * DH : (h + 1) * DH, at] = contract(
                k_t[h * DH : (h + 1) * DH, :], low_score[...], 1, 0
            ).astype(bf16)
            for j in range(QUERY_BLOCK // BLOCK):
                home = c * query_blocks + qb * (QUERY_BLOCK // BLOCK) + j
                for d in (-1, 0, 1):
                    kb = home + d
                    valid = jnp.logical_and(kb >= 0, kb < keys // BLOCK)

                    @pl.when(valid)
                    def _():
                        where_k = jnp.clip(kb, 0, keys // BLOCK - 1)
                        near[h, d + 1] += low_score[
                            block_rows(where_k), j * BLOCK : (j + 1) * BLOCK
                        ].astype(f32)

        return carry

    lax.fori_loop(0, rows // QUERY_BLOCK, attend_back, 0)

    other_keys = pl.ds(pl.multiple_of((1 - c) * rows, rows), rows)
    dkv_send[0] = dk[other_keys, 0:head_width].astype(bf16)
    dkv_send[1] = dv[other_keys, :].astype(bf16)
    dkv_copy = remote(dkv_send.at[...], dkv_recv.at[...], dkv_ssem.at[0], dkv_rsem.at[0], partner)
    dkv_copy.start()
    grl_t = grl[...].T
    for i in range(groups):
        cut = slice(i * both, (i + 1) * both)
        store_grad(gsa, i, 3, contract(grl_t[cut], att_t[...], 1, 1))
    over_copy(1).start()
    dkv_copy.wait_recv()
    dkv[0] = (dk[own_keys, 0:head_width] + dkv_recv[0].astype(f32)).astype(bf16)
    dkv[1] = (dv[own_keys, :] + dkv_recv[1].astype(f32)).astype(bf16)

    def project_back(b, carry):
        at = block_rows(b)
        total = contract(dq_t[:, at].T, weight(wa, 0), 1, 1)
        total = total + contract(dkv[0, at, :], weight(wa, 1), 1, 1)
        total = total + contract(dkv[1, at, :], weight(wa, 2), 1, 1)
        snd[3, at, :] = total.astype(bf16)
        for j in range(per_block):
            put(3, b * per_block + j)
        return carry

    lax.fori_loop(0, rows // BLOCK, project_back, 0)

    def advance_all(a):
        def body(s, carry):
            advance(a, s)
            return carry

        lax.fori_loop(0, chunks + 2, body, 0)

    def weights_back(i, carry):
        cut = n1t[wide_columns(i), :]
        store_grad(gsa, i, 0, contract(cut, dq_t[...], 1, 1))
        store_grad(gsa, i, 1, contract(cut, dkv[0], 1, 0))
        store_grad(gsa, i, 2, contract(cut, dkv[1], 1, 0))
        return carry

    lax.fori_loop(0, groups, weights_back, 0)
    over_copy(2).start()
    reduce_send(1)
    reduce_send(2)

    advance_all(2)

    def bucket_sums(h, carry):
        for b in range(2 * half):
            summed_block = jnp.zeros((8, BLOCK), f32)
            for d in (-1, 0) if b < half else (0, 1):
                bucket = bucket_of(d * BLOCK + row_of - column_of)
                chosen = jnp.where(bucket == b, near[h, d + 1], 0.0)
                summed_block = summed_block + jnp.sum(
                    chosen.reshape(BLOCK // 8, 8, BLOCK), axis=0
                )
            pick[b : b + 1, :] = jnp.sum(summed_block, axis=0, keepdims=True)
        sums = contract(jnp.ones((8, BLOCK), f32), pick[...], 1, 1, highest)
        small[:, 0 : 2 * half] += jnp.where(iota((8, 2 * half), 0) == 2 + h, sums, 0.0)
        return carry

    lax.fori_loop(0, heads, bucket_sums, 0)
    tail = dk.shape[1] - BLOCK
    first_lane = head_width - tail
    column_sums = dk[:, tail:]
    block_row = iota((keys, BLOCK), 0)
    lane = iota((keys, BLOCK), 1)
    left_sum = jnp.zeros((1, BLOCK), f32)
    right_sum = jnp.zeros((1, BLOCK), f32)
    for j in range(query_blocks):
        mine = jnp.zeros((keys, BLOCK), jnp.bool_)
        for h in range(heads):
            mine = jnp.logical_or(mine, lane == first_lane + h * query_blocks + j)
        home = c * query_blocks + j
        is_left = jnp.logical_and(mine, block_row < (home - 1) * BLOCK)
        is_right = jnp.logical_and(mine, block_row >= (home + 2) * BLOCK)
        left_sum += jnp.sum(jnp.where(is_left, column_sums, 0.0), axis=0, keepdims=True)
        right_sum += jnp.sum(jnp.where(is_right, column_sums, 0.0), axis=0, keepdims=True)
    from_lane, to_lane = iota((BLOCK, BLOCK), 0), iota((BLOCK, BLOCK), 1)
    for h in range(heads):
        start = first_lane + h * query_blocks
        inside = jnp.logical_and(from_lane >= start, from_lane < start + query_blocks)
        left_pick = jnp.logical_and(inside, to_lane == far).astype(f32)
        right_pick = jnp.logical_and(inside, to_lane == half + far).astype(f32)
        small[2 + h : 3 + h, 0:BLOCK] += (
            contract(jnp.broadcast_to(left_sum, (8, BLOCK)), left_pick, 1, 0, highest)
            + contract(jnp.broadcast_to(right_sum, (8, BLOCK)), right_pick, 1, 0, highest)
        )[0:1]

    advance_all(3)

    def input_back(b, carry):
        for j in range(per_block):
            finish(3, b * per_block + j)
        at = block_rows(b)
        grad_in = tot[3, at, :].astype(f32)
        xs = x_ref[at, :].astype(f32)
        inverse = inverse_rms(xs)
        u = xs * inverse
        small[0:1, :] += jnp.sum(grad_in * u, axis=0, keepdims=True)
        g = grad_in * gain_rows[0:1, :]
        gin_ref[at, :] = grad_res[at, :] + inverse * (
            g - u * jnp.mean(g * u, axis=-1, keepdims=True)
        )
        return carry

    lax.fori_loop(0, rows // BLOCK, input_back, 0)

    small_copies = [
        remote(
            small.at[...], small_all.at[me], sm_send.at[k * 2 + kc - 1], sm_recv.at[k * 2 + kc - 1],
            (f ^ k, c ^ kc, t),
        )
        for k in range(groups)
        for kc in range(2)
        if k or kc
    ]
    for copy in small_copies:
        copy.start()

    def layer_out(b, carry):
        for j in range(per_block):
            finish(2, b * per_block + j)
        at = block_rows(b)
        out_ref[at, :] = (resid[at, :] + tot[2, at, :].astype(f32)).astype(bf16)
        return carry

    lax.fori_loop(0, rows // BLOCK, layer_out, 0)
    for n in range(3):
        reduce_finish(n)
    small_all[me] = small[...]
    for copy in small_copies:
        copy.wait_recv()
    total_small = small_all[0]
    for i in range(1, shards):
        total_small = total_small + small_all[i]
    to_own = (iota((width, BLOCK), 0) == iota((width, BLOCK), 1) + me * shard).astype(f32)
    gains_out_ref[...] = contract(total_small, to_own, 1, 0, highest)
    bias_out_ref[...] = total_small[:, 0:BLOCK]

    for copy in small_copies:
        copy.wait_send()
    for g in range(5):
        gather_drain(g)
    for copy in kv_copies:
        copy.wait_send()
    dkv_copy.wait_send()
    for a in range(4):
        drain(a)
    for n in range(3):
        reduce_drain(n)


def fused_layer(shards, x, cot, ids, gains, weights, table):
    rows, width = x.shape
    shard, head_width = weights[0].shape
    units = weights[4].shape[1]
    keys = ids.shape[1]
    heads = head_width // DH
    groups = shards // 2
    chunks = rows // CHUNK
    padded = head_width + (-head_width) % BLOCK
    if padded - head_width < heads * (rows // BLOCK):
        padded += BLOCK
    vmem, dma = pltpu.VMEM, pltpu.SemaphoreType.DMA
    out_shape = (
        jax.ShapeDtypeStruct((rows, width), bf16),
        jax.ShapeDtypeStruct((rows, width), f32),
        *[jax.ShapeDtypeStruct((shard, head_width), f32)] * 4,
        *[jax.ShapeDtypeStruct((shard, units), f32)] * 3,
        jax.ShapeDtypeStruct((8, BLOCK), f32),
        jax.ShapeDtypeStruct((8, BLOCK), f32),
    )
    in_vmem = pl.BlockSpec(memory_space=pltpu.VMEM)
    scratch = [
        vmem((shards, 4, shard, head_width), bf16),
        vmem((shards, 3, shard, units), bf16),
        vmem((shards, 8, BLOCK), f32),
        vmem((8, width), f32),
        vmem((heads, 5, BLOCK, BLOCK), f32),
        vmem((heads, keys, rows), f32),
        vmem((keys, QUERY_BLOCK), f32),
        vmem((heads, keys, rows), bf16),
        vmem((keys, QUERY_BLOCK), bf16),
        vmem((4, rows, width), bf16),
        vmem((4, rows, width), bf16),
        vmem((4, rows, width), bf16),
        vmem((rows, width), f32),
        vmem((rows, width), f32),
        vmem((rows, width), bf16),
        vmem((rows, width), bf16),
        vmem((rows, width), bf16),
        vmem((width, rows), bf16),
        vmem((rows, units), bf16),
        vmem((rows, units), bf16),
        vmem((rows, units), bf16),
        vmem((head_width, rows), bf16),
        vmem((keys, head_width), bf16),
        vmem((keys, head_width), bf16),
        vmem((head_width, keys), bf16),
        vmem((head_width, keys), bf16),
        vmem((head_width, rows), bf16),
        vmem((head_width, rows), bf16),
        vmem((head_width, rows), bf16),
        vmem((8, rows), f32),
        vmem((8, rows), f32),
        vmem((keys, padded), f32),
        vmem((keys, head_width), f32),
        vmem((heads, 3, BLOCK, BLOCK), f32),
        vmem((table.shape[0], BLOCK), f32),
        vmem((2, rows, head_width), bf16),
        vmem((2, rows, head_width), bf16),
        vmem((2, rows, head_width), bf16),
        vmem((groups, 2, 4, shard, head_width), bf16),
        vmem((groups, 2, 3, shard, units), bf16),
        vmem((groups, 4, shard, head_width), bf16),
        vmem((groups, 3, shard, units), bf16),
        vmem((groups, 4, shard, head_width), bf16),
        vmem((groups, 3, shard, units), bf16),
        vmem((groups - 1, 4, shard, head_width), bf16),
        vmem((groups - 1, 3, shard, units), bf16),
        vmem((8, width), f32),
        vmem((shards, 8, width), f32),
        dma((5, 2 * groups)),
        dma((5, 2 * groups)),
        dma((2,)),
        dma((2,)),
        dma((4, chunks)),
        dma((4, chunks)),
        dma((4, chunks)),
        dma((4, chunks)),
        dma((1,)),
        dma((1,)),
        dma((3,)),
        dma((3,)),
        dma((3, groups)),
        dma((3, groups)),
        dma((shards,)),
        dma((shards,)),
    ]
    return pl.pallas_call(
        functools.partial(layer_kernel, shards),
        out_shape=out_shape,
        in_specs=[in_vmem] * 11 + [pl.BlockSpec(memory_space=pltpu.SMEM)],
        out_specs=[in_vmem] * len(out_shape),
        scratch_shapes=scratch,
        name="layer",
        compiler_params=pltpu.CompilerParams(
            collective_id=0, has_side_effects=True, vmem_limit_bytes=63 << 20
        ),
    )(x, cot, ids, gains, *weights, table)


def on_device_fused(
    layer_input,
    doc_ids,
    query_weight,
    key_weight,
    value_weight,
    output_weight,
    gate_weight,
    up_weight,
    down_weight,
    first_gain,
    second_gain,
    position_bias,
    cotangent,
):
    shards = lax.axis_size("fsdp") * lax.axis_size("ctx")
    shard = first_gain.shape[0]
    heads = position_bias.shape[1]
    gains = jnp.pad(
        jnp.stack([first_gain, second_gain]).astype(f32), ((0, 6), (0, BLOCK - shard))
    )
    outs = fused_layer(
        shards,
        layer_input[0],
        cotangent[0],
        doc_ids,
        gains,
        (
            query_weight,
            key_weight,
            value_weight,
            output_weight,
            gate_weight,
            up_weight,
            down_weight,
        ),
        position_bias,
    )
    gains_out, bias_out = outs[9], outs[10]
    return (
        outs[0][None],
        outs[1][None],
        *outs[2:9],
        gains_out[0, :shard],
        gains_out[1, :shard],
        bias_out[2 : 2 + heads, : position_bias.shape[0]].T,
    )


def fits_kernel(mesh):
    return mesh.shape["ctx"] == 2 and mesh.shape["tp"] == 4 and mesh.shape["fsdp"] in (2, 4)


def solution(mesh):
    return jax.shard_map(
        on_device_fused if fits_kernel(mesh) else on_device,
        mesh=mesh,
        in_specs=(
            P("fsdp", "ctx", None),
            P("fsdp", None),
            P(("fsdp", "ctx"), "tp"),
            P(("fsdp", "ctx"), "tp"),
            P(("fsdp", "ctx"), "tp"),
            P(("fsdp", "ctx"), "tp"),
            P(("fsdp", "ctx"), "tp"),
            P(("fsdp", "ctx"), "tp"),
            P(("fsdp", "ctx"), "tp"),
            P(("fsdp", "ctx")),
            P(("fsdp", "ctx")),
            P(None, "tp"),
            P("fsdp", "ctx", None),
        ),
        out_specs=(
            P("fsdp", "ctx", None),
            P("fsdp", "ctx", None),
            P(("fsdp", "ctx"), "tp"),
            P(("fsdp", "ctx"), "tp"),
            P(("fsdp", "ctx"), "tp"),
            P(("fsdp", "ctx"), "tp"),
            P(("fsdp", "ctx"), "tp"),
            P(("fsdp", "ctx"), "tp"),
            P(("fsdp", "ctx"), "tp"),
            P(("fsdp", "ctx")),
            P(("fsdp", "ctx")),
            P(None, "tp"),
        ),
        check_vma=False,
    )
```

```python
import functools

import jax
import jax.numpy as jnp
from jax import lax
from jax.experimental import pallas as pl
from jax.experimental.pallas import tpu as pltpu
from jax.sharding import PartitionSpec as P

DH = 64


epsilon = 1e-06
masked_score = -1000000000.0
bucket_edges = (12, 16, 23, 32, 46, 64, 91)
highest = lax.Precision.HIGHEST


def bucket_of(relative):
    distance = jnp.abs(relative)
    beyond = jnp.zeros_like(distance) + 8
    for edge_value in bucket_edges:
        beyond = beyond + (distance >= edge_value).astype(jnp.int32)
    inside = jnp.where(distance < 8, distance, beyond)
    return jnp.where(relative > 0, 16, 0) + inside


def rms_norm(values, gain_vector):
    inverse = lax.rsqrt(jnp.mean(values * values, axis=-1, keepdims=True) + epsilon)
    return values * inverse * gain_vector


def gated_unit(gate_in, up_in):
    return jax.nn.gelu(gate_in, approximate=True) * up_in


def relative_bias(bias_table, query_rows, key_rows, offset):
    span_width = key_rows + query_rows
    relative = lax.iota(jnp.int32, span_width) - (query_rows - 1) - offset
    one_hot = (
        bucket_of(relative)[:, None] == lax.iota(jnp.int32, bias_table.shape[0])[None, :]
    ).astype(jnp.float32)
    per_shift = jnp.dot(one_hot, bias_table, precision=highest).T
    heads_here = bias_table.shape[1]
    toeplitz = jnp.broadcast_to(per_shift[:, None, :], (heads_here, query_rows, span_width))
    toeplitz = toeplitz.reshape(heads_here, query_rows * span_width)[
        :, : query_rows * (span_width - 1)
    ]
    toeplitz = toeplitz.reshape(heads_here, query_rows, span_width - 1)
    return (toeplitz[:, :, query_rows - 1 : query_rows - 1 + key_rows], one_hot)


def diagonal_sums(grad_scores, query_rows, key_rows):
    heads_here = grad_scores.shape[0]
    span_width = key_rows + query_rows
    placed = jnp.pad(grad_scores, ((0, 0), (0, 0), (query_rows - 1, 0)))
    placed = placed.reshape(heads_here, query_rows * (span_width - 1))
    placed = jnp.pad(placed, ((0, 0), (0, query_rows)))
    return jnp.sum(placed.reshape(heads_here, query_rows, span_width), axis=1)


def on_device(
    layer_input,
    doc_ids,
    query_weight,
    key_weight,
    value_weight,
    output_weight,
    gate_weight,
    up_weight,
    down_weight,
    first_gain,
    second_gain,
    position_bias,
    cotangent,
):
    query_rows = layer_input.shape[1]
    key_rows = query_rows * lax.axis_size("ctx")
    heads_here = position_bias.shape[1]
    head_width = heads_here * DH
    offset = lax.axis_index("ctx") * query_rows
    everything = (
        query_weight,
        key_weight,
        value_weight,
        output_weight,
        gate_weight,
        up_weight,
        down_weight,
        first_gain,
        second_gain,
    )
    (
        full_query,
        full_key,
        full_value,
        full_output,
        full_gate,
        full_up,
        full_down,
        gain_one,
        gain_two,
    ) = (
        lax.all_gather(everything[0], ("fsdp", "ctx"), axis=0, tiled=True),
        lax.all_gather(everything[1], ("fsdp", "ctx"), axis=0, tiled=True),
        lax.all_gather(everything[2], ("fsdp", "ctx"), axis=0, tiled=True),
        lax.all_gather(everything[3], ("fsdp", "ctx"), axis=0, tiled=True),
        lax.all_gather(everything[4], ("fsdp", "ctx"), axis=0, tiled=True),
        lax.all_gather(everything[5], ("fsdp", "ctx"), axis=0, tiled=True),
        lax.all_gather(everything[6], ("fsdp", "ctx"), axis=0, tiled=True),
        lax.all_gather(everything[7], ("fsdp", "ctx"), axis=0, tiled=True),
        lax.all_gather(everything[8], ("fsdp", "ctx"), axis=0, tiled=True),
    )
    inputs = layer_input.astype(jnp.float32)
    gain_first = gain_one.astype(jnp.float32)
    gain_second = gain_two.astype(jnp.float32)
    normed_one = rms_norm(inputs, gain_first).astype(jnp.bfloat16)
    queries = jnp.dot(normed_one, full_query, preferred_element_type=jnp.float32).astype(
        jnp.bfloat16
    )
    keys_local = jnp.dot(normed_one, full_key, preferred_element_type=jnp.float32).astype(
        jnp.bfloat16
    )
    values_local = jnp.dot(normed_one, full_value, preferred_element_type=jnp.float32).astype(
        jnp.bfloat16
    )
    keys_all, values_all = (
        lax.all_gather(keys_local, "ctx", axis=1, tiled=True),
        lax.all_gather(values_local, "ctx", axis=1, tiled=True),
    )
    bias_block, one_hot = relative_bias(position_bias, query_rows, key_rows, offset)

    def scores_of(query_heads, key_heads, id_row):
        raw_scores = jnp.einsum(
            "qhd,khd->hqk", query_heads, key_heads, preferred_element_type=jnp.float32
        )
        own_ids = lax.dynamic_slice_in_dim(id_row, offset, query_rows)
        same_doc = own_ids[:, None] == id_row[None, :]
        return jnp.where(same_doc[None], raw_scores + bias_block, masked_score)

    def forward_one(packed):
        query_seq, key_seq, value_seq, id_row = packed
        scores = scores_of(
            query_seq.reshape(query_rows, heads_here, DH),
            key_seq.reshape(key_rows, heads_here, DH),
            id_row,
        )
        row_max = jnp.max(scores, axis=-1, keepdims=True)
        exponentials = jnp.exp(scores - row_max)
        row_total = jnp.sum(exponentials, axis=-1, keepdims=True)
        probabilities = (exponentials / row_total).astype(jnp.bfloat16)
        attended = jnp.einsum(
            "hqk,khd->qhd",
            probabilities,
            value_seq.reshape(key_rows, heads_here, DH),
            preferred_element_type=jnp.float32,
        )
        log_row = row_max[..., 0] + jnp.log(row_total[..., 0])
        return (attended.reshape(query_rows, head_width).astype(jnp.bfloat16), log_row)

    attended, log_sums = lax.map(forward_one, (queries, keys_all, values_all, doc_ids))
    attention_terms = jnp.einsum(
        "sqe,de->sqd", attended, full_output, preferred_element_type=jnp.float32
    )
    residual = inputs + lax.psum(attention_terms.astype(jnp.bfloat16), "tp").astype(jnp.float32)
    normed_two = rms_norm(residual, gain_second).astype(jnp.bfloat16)
    gate_pre = jnp.dot(normed_two, full_gate, preferred_element_type=jnp.float32)
    up_pre = jnp.dot(normed_two, full_up, preferred_element_type=jnp.float32)
    activated = gated_unit(gate_pre, up_pre).astype(jnp.bfloat16)
    ffn_terms = jnp.einsum("sqf,df->sqd", activated, full_down, preferred_element_type=jnp.float32)
    output_rows = (
        residual + lax.psum(ffn_terms.astype(jnp.bfloat16), "tp").astype(jnp.float32)
    ).astype(jnp.bfloat16)
    grad_activated = jnp.einsum(
        "sqd,df->sqf", cotangent, full_down, preferred_element_type=jnp.float32
    )
    down_grad = jnp.einsum("sqd,sqf->df", cotangent, activated, preferred_element_type=jnp.float32)
    gated_value, gated_back = jax.vjp(gated_unit, gate_pre, up_pre)
    grad_gate, grad_up = gated_back(grad_activated)
    grad_gate = grad_gate.astype(jnp.bfloat16)
    grad_up = grad_up.astype(jnp.bfloat16)
    gate_grad = jnp.einsum("sqd,sqf->df", normed_two, grad_gate, preferred_element_type=jnp.float32)
    up_grad = jnp.einsum("sqd,sqf->df", normed_two, grad_up, preferred_element_type=jnp.float32)
    normed_two_terms = jnp.einsum(
        "sqf,df->sqd", grad_gate, full_gate, preferred_element_type=jnp.float32
    ) + jnp.einsum("sqf,df->sqd", grad_up, full_up, preferred_element_type=jnp.float32)
    grad_normed_two = lax.psum(normed_two_terms.astype(jnp.bfloat16), "tp").astype(jnp.float32)
    second_value, second_back = jax.vjp(rms_norm, residual, gain_second)
    grad_residual, second_gain_grad = second_back(grad_normed_two)
    grad_residual = grad_residual + cotangent.astype(jnp.float32)
    grad_low = grad_residual.astype(jnp.bfloat16)
    grad_attended = jnp.einsum(
        "sqd,de->sqe", grad_low, full_output, preferred_element_type=jnp.float32
    ).astype(jnp.bfloat16)
    output_grad = jnp.einsum("sqd,sqe->de", grad_low, attended, preferred_element_type=jnp.float32)

    def backward_one(running, packed):
        query_seq, key_seq, value_seq, id_row, grad_seq, log_row = packed
        query_heads = query_seq.reshape(query_rows, heads_here, DH)
        key_heads = key_seq.reshape(key_rows, heads_here, DH)
        value_heads = value_seq.reshape(key_rows, heads_here, DH)
        grad_heads = grad_seq.reshape(query_rows, heads_here, DH)
        scores = scores_of(query_heads, key_heads, id_row)
        probabilities = jnp.exp(scores - log_row[..., None])
        grad_probs = jnp.einsum(
            "qhd,khd->hqk", grad_heads, value_heads, preferred_element_type=jnp.float32
        )
        grad_values = jnp.einsum(
            "hqk,qhd->khd",
            probabilities.astype(jnp.bfloat16),
            grad_heads,
            preferred_element_type=jnp.float32,
        )
        grad_scores = probabilities * (
            grad_probs - jnp.sum(probabilities * grad_probs, axis=-1, keepdims=True)
        )
        low_scores = grad_scores.astype(jnp.bfloat16)
        grad_queries = jnp.einsum(
            "hqk,khd->qhd", low_scores, key_heads, preferred_element_type=jnp.float32
        )
        grad_keys = jnp.einsum(
            "hqk,qhd->khd", low_scores, query_heads, preferred_element_type=jnp.float32
        )
        running = running + diagonal_sums(grad_scores, query_rows, key_rows)
        return (
            running,
            (
                grad_queries.reshape(query_rows, head_width).astype(jnp.bfloat16),
                grad_keys.reshape(key_rows, head_width),
                grad_values.reshape(key_rows, head_width),
            ),
        )

    shift_grads, (grad_queries, key_parts, value_parts) = lax.scan(
        backward_one,
        jnp.zeros((heads_here, query_rows + key_rows), jnp.float32),
        (queries, keys_all, values_all, doc_ids, grad_attended, log_sums),
    )
    grad_keys, grad_values = (
        lax.psum_scatter(
            key_parts.astype(jnp.bfloat16), "ctx", scatter_dimension=1, tiled=True
        ).astype(jnp.float32),
        lax.psum_scatter(
            value_parts.astype(jnp.bfloat16), "ctx", scatter_dimension=1, tiled=True
        ).astype(jnp.float32),
    )
    grad_keys = grad_keys.astype(jnp.bfloat16)
    grad_values = grad_values.astype(jnp.bfloat16)
    normed_one_terms = (
        jnp.einsum("sqe,de->sqd", grad_queries, full_query, preferred_element_type=jnp.float32)
        + jnp.einsum("sqe,de->sqd", grad_keys, full_key, preferred_element_type=jnp.float32)
        + jnp.einsum("sqe,de->sqd", grad_values, full_value, preferred_element_type=jnp.float32)
    )
    grad_normed_one = lax.psum(normed_one_terms.astype(jnp.bfloat16), "tp").astype(jnp.float32)
    query_grad = jnp.einsum(
        "sqd,sqe->de", normed_one, grad_queries, preferred_element_type=jnp.float32
    )
    key_grad = jnp.einsum("sqd,sqe->de", normed_one, grad_keys, preferred_element_type=jnp.float32)
    value_grad = jnp.einsum(
        "sqd,sqe->de", normed_one, grad_values, preferred_element_type=jnp.float32
    )
    first_value, first_back = jax.vjp(rms_norm, inputs, gain_first)
    grad_inputs, first_gain_grad = first_back(grad_normed_one)
    input_rows = grad_residual + grad_inputs
    bias_gradient = lax.psum(jnp.dot(one_hot.T, shift_grads.T, precision=highest), ("fsdp", "ctx"))
    (
        query_total,
        key_total,
        value_total,
        output_total,
        gate_total,
        up_total,
        down_total,
        first_total,
        second_total,
    ) = (
        lax.psum_scatter(query_grad, ("fsdp", "ctx"), scatter_dimension=0, tiled=True),
        lax.psum_scatter(key_grad, ("fsdp", "ctx"), scatter_dimension=0, tiled=True),
        lax.psum_scatter(value_grad, ("fsdp", "ctx"), scatter_dimension=0, tiled=True),
        lax.psum_scatter(output_grad, ("fsdp", "ctx"), scatter_dimension=0, tiled=True),
        lax.psum_scatter(gate_grad, ("fsdp", "ctx"), scatter_dimension=0, tiled=True),
        lax.psum_scatter(up_grad, ("fsdp", "ctx"), scatter_dimension=0, tiled=True),
        lax.psum_scatter(down_grad, ("fsdp", "ctx"), scatter_dimension=0, tiled=True),
        lax.psum_scatter(first_gain_grad, ("fsdp", "ctx"), scatter_dimension=0, tiled=True),
        lax.psum_scatter(second_gain_grad, ("fsdp", "ctx"), scatter_dimension=0, tiled=True),
    )
    return (
        output_rows,
        input_rows,
        query_total,
        key_total,
        value_total,
        output_total,
        gate_total,
        up_total,
        down_total,
        first_total,
        second_total,
        bias_gradient,
    )


MESH = pl.DeviceIdType.MESH
bf16, f32 = jnp.bfloat16, jnp.float32
BLOCK = 128
QUERY_BLOCK = 256
CHUNK = 64
LAG = 2


def contract(left, right, left_dim, right_dim, precision=None):
    return lax.dot_general(
        left,
        right,
        (((left_dim,), (right_dim,)), ((), ())),
        preferred_element_type=f32,
        precision=precision,
    )


def iota(shape, dim):
    return lax.broadcasted_iota(jnp.int32, shape, dim)


def layer_kernel(
    shards,
    x_ref,
    cot_ref,
    ids_ref,
    gain_one_ref,
    gain_two_ref,
    wq_ref,
    wk_ref,
    wv_ref,
    wo_ref,
    wg_ref,
    wu_ref,
    wd_ref,
    table_ref,
    out_ref,
    gin_ref,
    gq_ref,
    gk_ref,
    gv_ref,
    go_ref,
    gg_ref,
    gu_ref,
    gd_ref,
    gain_one_out_ref,
    gain_two_out_ref,
    bias_out_ref,
    wa,
    wf,
    gains_all,
    gain_rows,
    tiles,
    masked_bias,
    score,
    expo,
    low_score,
    snd,
    part,
    tot,
    resid,
    grad_res,
    n1,
    n2,
    grl,
    n1t,
    act,
    ggate,
    gup,
    q_t,
    k_all,
    v_all,
    k_t,
    v_t,
    att_t,
    dos_t,
    dq_t,
    linv,
    delta,
    dk,
    dv,
    near,
    pick,
    dkv_send,
    dkv_recv,
    dkv,
    gsa,
    gsf,
    ra,
    rf,
    sa,
    sf,
    ra2,
    rf2,
    small,
    small_all,
    ag_send,
    ag_recv,
    kv_send,
    kv_recv,
    s1,
    r1,
    s2,
    r2,
    dkv_ssem,
    dkv_rsem,
    rs_send,
    rs_recv,
    rs2_send,
    rs2_recv,
    sm_send,
    sm_recv,
):
    groups = shards // 2
    f, c, t = lax.axis_index("fsdp"), lax.axis_index("ctx"), lax.axis_index("tp")
    me = f * 2 + c
    rows, width = x_ref.shape
    keys = k_all.shape[0]
    head_width = wq_ref.shape[1]
    heads = head_width // DH
    units = wg_ref.shape[1]
    shard = wq_ref.shape[0]
    chunks = rows // CHUNK
    partner = (f, 1 - c, t)
    outer = jnp.logical_or(t == 0, t == 3)
    inner = jnp.logical_or(t == 1, t == 2)
    near_end = jnp.where(t < 2, 1, 2)
    far_end = jnp.where(t < 2, 0, 3)
    middle = 3 - t

    def remote(source, target, send_sem, recv_sem, device):
        return pltpu.make_async_remote_copy(
            src_ref=source,
            dst_ref=target,
            send_sem=send_sem,
            recv_sem=recv_sem,
            device_id=device,
            device_id_type=MESH,
        )

    barrier = pltpu.get_barrier_semaphore()
    for k in range(groups):
        for kc in range(2):
            if k or kc:
                pl.semaphore_signal(
                    barrier, inc=1, device_id=(f ^ k, c ^ kc, t), device_id_type=MESH
                )

    @pl.when(outer)
    def _():
        pl.semaphore_signal(barrier, inc=1, device_id=(f, c, near_end), device_id_type=MESH)

    @pl.when(inner)
    def _():
        pl.semaphore_signal(barrier, inc=1, device_id=(f, c, far_end), device_id_type=MESH)
        pl.semaphore_signal(barrier, inc=1, device_id=(f, c, middle), device_id_type=MESH)

    wa[me, 0] = wq_ref[...]
    wa[me, 1] = wk_ref[...]
    wa[me, 2] = wv_ref[...]
    wa[me, 3] = wo_ref[...]
    wf[me, 0] = wg_ref[...]
    wf[me, 1] = wu_ref[...]
    wf[me, 2] = wd_ref[...]
    gains_all[me] = jnp.zeros((8, BLOCK), f32)
    gains_all[me, 0:1, 0:shard] = gain_one_ref[...].astype(f32)
    gains_all[me, 1:2, 0:shard] = gain_two_ref[...].astype(f32)

    @pl.when(outer)
    def _():
        pl.semaphore_wait(barrier, shards)

    @pl.when(inner)
    def _():
        pl.semaphore_wait(barrier, shards + 1)

    def piece(g, index):
        if g == 0:
            return wa.at[index, 0:3]
        if g == 1:
            return wa.at[index, 3:4]
        if g == 2:
            return wf.at[index, 0:2]
        if g == 3:
            return wf.at[index, 2:3]
        return gains_all.at[index]

    def gather_out(g, k):
        view = piece(g, me)
        return remote(view, view, ag_send.at[g, k - 1], ag_recv.at[g, k - 1], (f ^ k, c, t))

    def gather_over(g, k):
        view = piece(g, (f ^ k) * 2 + c)
        slot = groups - 1 + k
        return remote(view, view, ag_send.at[g, slot], ag_recv.at[g, slot], partner)

    def gather_start(g):
        for k in range(1, groups):
            gather_out(g, k).start()
        gather_over(g, 0).start()

    def gather_relay(g):
        for k in range(1, groups):
            gather_out(g, k).wait_recv()
            gather_over(g, k).start()

    def gather_finish(g):
        for k in range(groups):
            gather_over(g, k).wait_recv()

    def gather_drain(g):
        for k in range(1, groups):
            gather_out(g, k).wait_send()
        for k in range(groups):
            gather_over(g, k).wait_send()

    def span(j):
        return pl.ds(pl.multiple_of(j * CHUNK, CHUNK), CHUNK)

    def end_copy(a, j):
        return remote(
            snd.at[a, span(j)], part.at[a, span(j)], s1.at[a, j], r1.at[a, j], (f, c, near_end)
        )

    def mid_copy(a, j):
        return remote(
            snd.at[a, span(j)], tot.at[a, span(j)], s1.at[a, j], r2.at[a, j], (f, c, middle)
        )

    def total_copy(a, j):
        return remote(
            tot.at[a, span(j)], tot.at[a, span(j)], s2.at[a, j], r2.at[a, j], (f, c, far_end)
        )

    def put(a, j):
        @pl.when(outer)
        def _():
            end_copy(a, j).start()

    def relay_a(a, j):
        @pl.when(inner)
        def _():
            end_copy(a, j).wait_recv()
            snd[a, span(j)] = (
                snd[a, span(j)].astype(f32) + part[a, span(j)].astype(f32)
            ).astype(bf16)
            mid_copy(a, j).start()

    def relay_b(a, j):
        @pl.when(inner)
        def _():
            mid_copy(a, j).wait_recv()
            tot[a, span(j)] = (
                snd[a, span(j)].astype(f32) + tot[a, span(j)].astype(f32)
            ).astype(bf16)
            total_copy(a, j).start()

    def finish(a, j):
        @pl.when(outer)
        def _():
            total_copy(a, j).wait_recv()

    def service(step):
        if isinstance(step, int):
            behind, ahead = divmod(step - LAG, chunks), divmod(step, chunks)
        else:
            behind = (lax.div(step - LAG, chunks), lax.rem(step - LAG, chunks))
            ahead = (lax.div(step, chunks), lax.rem(step, chunks))
        if not isinstance(step, int) or LAG <= step:
            relay_b(*behind)
        if not isinstance(step, int) or step < 4 * chunks:
            relay_a(*ahead)

    def drain(a):
        def body(j, carry):
            @pl.when(outer)
            def _():
                end_copy(a, j).wait_send()

            @pl.when(inner)
            def _():
                mid_copy(a, j).wait_send()
                total_copy(a, j).wait_send()

            return carry

        lax.fori_loop(0, chunks, body, 0)

    gather_start(4)
    gather_start(0)

    half = table_ref.shape[1] // 2
    far = half - 1
    row_of, column_of = iota((BLOCK, BLOCK), 0), iota((BLOCK, BLOCK), 1)
    for h in range(heads):
        tiles[h, 0] = jnp.full((BLOCK, BLOCK), table_ref[h, far], f32)
        tiles[h, 4] = jnp.full((BLOCK, BLOCK), table_ref[h, half + far], f32)
    for d in (-1, 0, 1):
        bucket = bucket_of(d * BLOCK + row_of - column_of)
        members = range(half) if d < 0 else range(half, 2 * half) if d > 0 else range(2 * half)

        def per_head(h, carry, bucket=bucket, members=members, d=d):
            filled = jnp.zeros((BLOCK, BLOCK), f32)
            for b in members:
                filled = jnp.where(bucket == b, table_ref[h, b], filled)
            tiles[h, d + 2] = filled
            return carry

        lax.fori_loop(0, heads, per_head, 0)

    def bias_rows(kb, carry):
        key_rows = pl.ds(pl.multiple_of(kb * BLOCK, BLOCK), BLOCK)
        key_ids = jnp.broadcast_to(ids_ref[0:1, key_rows].astype(f32), (BLOCK, BLOCK)).T
        for qb in range(rows // BLOCK):
            start = pl.multiple_of(c * rows + qb * BLOCK, BLOCK)
            query_ids = ids_ref[0:1, pl.ds(start, BLOCK)].astype(f32)
            same = key_ids == query_ids
            d = jnp.clip(kb - c * (rows // BLOCK) - qb, -2, 2) + 2
            for h in range(heads):
                masked_bias[h, key_rows, qb * BLOCK : (qb + 1) * BLOCK] = jnp.where(
                    same, tiles[h, d], masked_score
                )
        return carry

    lax.fori_loop(0, keys // BLOCK, bias_rows, 0)
    near[...] = jnp.zeros_like(near)
    dk[...] = jnp.zeros_like(dk)
    dv[...] = jnp.zeros_like(dv)
    small[...] = jnp.zeros_like(small)

    gather_relay(4)
    gather_relay(0)
    for g in (1, 2, 3):
        gather_start(g)
    gather_finish(4)
    spread = jnp.zeros((8, width), f32)
    for i in range(shards):
        one_hot = (iota((BLOCK, width), 1) == iota((BLOCK, width), 0) + i * shard).astype(f32)
        spread = spread + contract(gains_all[i].astype(bf16), one_hot.astype(bf16), 1, 0)
    gain_rows[...] = spread

    def block_rows(b, size=BLOCK):
        return pl.ds(pl.multiple_of(b * size, size), size)

    def inverse_rms(values):
        return lax.rsqrt(jnp.mean(values * values, axis=-1, keepdims=True) + epsilon)

    def norm_one(b, carry):
        at = block_rows(b)
        xs = x_ref[at, :].astype(f32)
        n1[at, :] = (xs * inverse_rms(xs) * gain_rows[0:1, :]).astype(bf16)
        return carry

    lax.fori_loop(0, rows // BLOCK, norm_one, 0)
    gather_finish(0)

    def weight(buffer, a):
        return buffer[:, a].reshape(width, buffer.shape[-1])

    own_keys = pl.ds(pl.multiple_of(c * rows, rows), rows)
    normed = n1[...]
    k_all[own_keys, :] = contract(normed, weight(wa, 1), 1, 0).astype(bf16)
    v_all[own_keys, :] = contract(normed, weight(wa, 2), 1, 0).astype(bf16)
    kv_copies = [
        remote(ref.at[own_keys], ref.at[own_keys], kv_send.at[n], kv_recv.at[n], partner)
        for n, ref in enumerate((k_all, v_all))
    ]
    for copy in kv_copies:
        copy.start()
    q_t[...] = contract(normed, weight(wa, 0), 1, 0).astype(bf16).T
    n1t[...] = normed.T
    gather_relay(1)
    for copy in kv_copies:
        copy.wait_recv()
    k_t[...] = k_all[...].T
    v_t[...] = v_all[...].T
    gather_finish(1)

    head_of = iota((head_width, QUERY_BLOCK), 0)

    def head_only(values, h):
        inside = jnp.logical_and(head_of >= h * DH, head_of < (h + 1) * DH)
        return jnp.where(inside, values, jnp.zeros_like(values))

    def attend(qb, carry):
        at = block_rows(qb, QUERY_BLOCK)
        for h in range(heads):
            queries = head_only(q_t[:, at], h)
            top = jnp.full((8, QUERY_BLOCK), -jnp.inf, f32)
            for kb in range(keys // BLOCK):
                span_k = slice(kb * BLOCK, (kb + 1) * BLOCK)
                block = contract(k_all[span_k, :], queries, 1, 0) + masked_bias[h, span_k, at]
                score[span_k, :] = block
                top = jnp.maximum(top, jnp.max(block.reshape(BLOCK // 8, 8, QUERY_BLOCK), axis=0))
            top = jnp.max(top, axis=0, keepdims=True)
            total = jnp.zeros((8, QUERY_BLOCK), f32)
            for kb in range(keys // BLOCK):
                span_k = slice(kb * BLOCK, (kb + 1) * BLOCK)
                block = jnp.exp(score[span_k, :] - top)
                expo[h, span_k, at] = block.astype(bf16)
                total = total + jnp.sum(block.reshape(BLOCK // 8, 8, QUERY_BLOCK), axis=0)
            inverse = 1.0 / jnp.sum(total, axis=0, keepdims=True)
            linv[h : h + 1, at] = inverse
            mixed = contract(v_t[h * DH : (h + 1) * DH, :], expo[h, :, at], 1, 0)
            att_t[h * DH : (h + 1) * DH, at] = (mixed * inverse).astype(bf16)
        attended = att_t[:, at].T
        snd[0, at, :] = contract(attended, weight(wa, 3), 1, 1).astype(bf16)
        for j in range(QUERY_BLOCK // CHUNK):
            put(0, qb * (QUERY_BLOCK // CHUNK) + j)
        return carry

    lax.fori_loop(0, rows // QUERY_BLOCK, attend, 0)

    for g in (2, 3):
        gather_relay(g)
    for g in (2, 3):
        gather_finish(g)

    per_block = BLOCK // CHUNK
    blocks = rows // BLOCK
    scale = 0.7978845608028654
    for step in range(LAG):
        service(step)

    def feed_forward(b, carry):
        for j in range(per_block):
            service(b * per_block + LAG + j)
        for j in range(per_block):
            finish(0, b * per_block + j)
        at = block_rows(b)
        res = x_ref[at, :].astype(f32) + tot[0, at, :].astype(f32)
        resid[at, :] = res
        normed = (res * inverse_rms(res) * gain_rows[1:2, :]).astype(bf16)
        n2[at, :] = normed
        gate = contract(normed, weight(wf, 0), 1, 0)
        up = contract(normed, weight(wf, 1), 1, 0)
        down = weight(wf, 2)
        grad_act = contract(cot_ref[at, :], down, 1, 0)
        square = gate * gate
        curve = jnp.tanh(scale * (gate + 0.044715 * square * gate))
        left = 0.5 * (1.0 + curve)
        value = gate * left
        slope = left + 0.5 * gate * (1.0 - curve * curve) * scale * (1.0 + 0.134145 * square)
        low_act = (value * up).astype(bf16)
        low_gate = (grad_act * up * slope).astype(bf16)
        low_up = (grad_act * value).astype(bf16)
        act[at, :] = low_act
        ggate[at, :] = low_gate
        gup[at, :] = low_up
        snd[1, at, :] = (
            contract(low_gate, weight(wf, 0), 1, 1) + contract(low_up, weight(wf, 1), 1, 1)
        ).astype(bf16)
        for j in range(per_block):
            put(1, b * per_block + j)
        snd[2, at, :] = contract(low_act, down, 1, 1).astype(bf16)
        return carry

    lax.fori_loop(0, rows // BLOCK, feed_forward, 0)

    def put_all(a):
        def body(j, carry):
            put(a, j)
            return carry

        lax.fori_loop(0, chunks, body, 0)

    put_all(2)

    def sent(n, which):
        if n == 0:
            return gsf.at[:, which]
        return gsa.at[:, which, 3:4] if n == 1 else gsa.at[:, which, 0:3]

    def landed(n):
        return rf.at[...] if n == 0 else ra.at[:, 3:4] if n == 1 else ra.at[:, 0:3]

    def over_copy(n):
        return remote(sent(n, 1 - c), landed(n), rs_send.at[n], rs_recv.at[n], partner)

    def summed(n, index):
        return sf.at[index] if n == 0 else sa.at[index, 3:4] if n == 1 else sa.at[index, 0:3]

    def arrived(n, k):
        return rf2.at[k - 1] if n == 0 else ra2.at[k - 1, 3:4] if n == 1 else ra2.at[k - 1, 0:3]

    def out_copy(n, k):
        return remote(
            summed(n, f ^ k), arrived(n, k), rs2_send.at[n, k - 1], rs2_recv.at[n, k - 1],
            (f ^ k, c, t),
        )

    members_of = {0: (0, 1, 2), 1: (3,), 2: (0, 1, 2)}
    results = {
        0: (gg_ref, gu_ref, gd_ref),
        1: (go_ref,),
        2: (gq_ref, gk_ref, gv_ref),
    }

    def reduce_send(n):
        over_copy(n).wait_recv()
        own, got, total = (gsf, rf, sf) if n == 0 else (gsa, ra, sa)

        def body(k, carry):
            index = jnp.bitwise_xor(f, groups - 1 - k)
            for a in members_of[n]:
                total[index, a] = (
                    own[index, c, a].astype(f32) + got[index, a].astype(f32)
                ).astype(bf16)
            return carry

        lax.fori_loop(0, groups, body, 0)
        for k in range(1, groups):
            out_copy(n, k).start()

    def reduce_finish(n):
        total, got = (sf, rf2) if n == 0 else (sa, ra2)
        for k in range(1, groups):
            out_copy(n, k).wait_recv()
        for a, result in zip(members_of[n], results[n]):
            value = total[f, a].astype(f32)
            for k in range(1, groups):
                value = value + got[k - 1, a].astype(f32)
            result[...] = value

    def reduce_drain(n):
        over_copy(n).wait_send()
        for k in range(1, groups):
            out_copy(n, k).wait_send()

    both = 2 * shard

    def store_grad(buffer, i, a, value):
        buffer[i, :, a] = value.astype(bf16).reshape(2, shard, value.shape[-1])

    def feed_forward_weights(i):
        cut = slice(i * both, (i + 1) * both)
        n2_t = n2[:, cut].T
        store_grad(gsf, i, 0, contract(n2_t, ggate[...], 1, 0))
        store_grad(gsf, i, 1, contract(n2_t, gup[...], 1, 0))
        store_grad(gsf, i, 2, contract(cot_ref[:, cut].T, act[...], 1, 0))

    def residual_back(b):
        for j in range(per_block):
            finish(1, b * per_block + j)
        at = block_rows(b)
        grad_in = tot[1, at, :].astype(f32)
        res = resid[at, :]
        inverse = inverse_rms(res)
        u = res * inverse
        small[1:2, :] += jnp.sum(grad_in * u, axis=0, keepdims=True)
        g = grad_in * gain_rows[1:2, :]
        grad = cot_ref[at, :].astype(f32) + inverse * (
            g - u * jnp.mean(g * u, axis=-1, keepdims=True)
        )
        grad_res[at, :] = grad
        low_grad = grad.astype(bf16)
        grl[at, :] = low_grad
        grad_att = contract(low_grad, weight(wa, 3), 1, 0).astype(bf16)
        scaled = grad_att.T.astype(f32) * jnp.concatenate(
            [jnp.broadcast_to(linv[h : h + 1, at], (DH, BLOCK)) for h in range(heads)], axis=0
        )
        scaled = scaled.astype(bf16)
        dos_t[:, at] = scaled
        delta[0:heads, at] = jnp.sum(
            (scaled.astype(f32) * att_t[:, at].astype(f32)).reshape(heads, DH, BLOCK), axis=1
        )

    extra = dk.shape[1] - head_width
    query_blocks = rows // BLOCK

    def attend_back(qb, h):
        at = block_rows(qb, QUERY_BLOCK)
        if True:
            grads = head_only(dos_t[:, at], h)
            queries = head_only(q_t[:, at], h)
            flag = iota((extra, QUERY_BLOCK), 0)
            lane = iota((extra, QUERY_BLOCK), 1)
            flags = jnp.zeros((extra, QUERY_BLOCK), f32)
            for j in range(QUERY_BLOCK // BLOCK):
                hit = jnp.logical_and(
                    flag == h * query_blocks + qb * (QUERY_BLOCK // BLOCK) + j,
                    jnp.logical_and(lane >= j * BLOCK, lane < (j + 1) * BLOCK),
                )
                flags = jnp.where(hit, 1.0, flags)
            flagged = jnp.concatenate([queries, flags.astype(bf16)], axis=0)
            shift = delta[h : h + 1, at]
            for kb in range(keys // BLOCK):
                span_k = slice(kb * BLOCK, (kb + 1) * BLOCK)
                block = contract(v_all[span_k, :], grads, 1, 0)
                low_score[span_k, :] = (
                    expo[h, span_k, at].astype(f32) * (block - shift)
                ).astype(bf16)
            dv[...] += contract(expo[h, :, at], grads, 1, 1)
            dk[...] += contract(low_score[...], flagged, 1, 1)
            dq_t[h * DH : (h + 1) * DH, at] = contract(
                k_t[h * DH : (h + 1) * DH, :], low_score[...], 1, 0
            ).astype(bf16)
            for j in range(QUERY_BLOCK // BLOCK):
                home = c * query_blocks + qb * (QUERY_BLOCK // BLOCK) + j
                for d in (-1, 0, 1):
                    kb = home + d
                    valid = jnp.logical_and(kb >= 0, kb < keys // BLOCK)

                    @pl.when(valid)
                    def _():
                        where_k = jnp.clip(kb, 0, keys // BLOCK - 1)
                        near[h, d + 1] += low_score[
                            block_rows(where_k), j * BLOCK : (j + 1) * BLOCK
                        ].astype(f32)

    served = [blocks * per_block + LAG]

    def serve_to(end):
        while served[0] < end:
            service(served[0])
            served[0] += 1

    weight_parts = list(range(groups))
    ratio = QUERY_BLOCK // BLOCK
    for qb in range(rows // QUERY_BLOCK):
        for b in range(qb * ratio, (qb + 1) * ratio):
            serve_to(chunks + (b + 1) * per_block + LAG)
            residual_back(b)
        for h in range(heads):
            attend_back(qb, h)
            if weight_parts:
                feed_forward_weights(weight_parts.pop(0))
            if qb + 1 < rows // QUERY_BLOCK or h + 1 < heads:
                serve_to(served[0] + 1)
        if qb == 0:
            while weight_parts:
                feed_forward_weights(weight_parts.pop(0))
            over_copy(0).start()

    other_keys = pl.ds(pl.multiple_of((1 - c) * rows, rows), rows)
    dkv_send[0] = dk[other_keys, 0:head_width].astype(bf16)
    dkv_send[1] = dv[other_keys, :].astype(bf16)
    dkv_copy = remote(dkv_send.at[...], dkv_recv.at[...], dkv_ssem.at[0], dkv_rsem.at[0], partner)
    dkv_copy.start()
    reduce_send(0)
    dkv_copy.wait_recv()
    dkv[0] = (dk[own_keys, 0:head_width] + dkv_recv[0].astype(f32)).astype(bf16)
    dkv[1] = (dv[own_keys, :] + dkv_recv[1].astype(f32)).astype(bf16)

    def project_back(b):
        at = block_rows(b)
        total = contract(dq_t[:, at].T, weight(wa, 0), 1, 1)
        total = total + contract(dkv[0, at, :], weight(wa, 1), 1, 1)
        total = total + contract(dkv[1, at, :], weight(wa, 2), 1, 1)
        snd[3, at, :] = total.astype(bf16)
        for j in range(per_block):
            put(3, b * per_block + j)

    for b in range(blocks):
        project_back(b)
        serve_to(served[0] + 1)

    grl_t = grl[...].T
    for i in range(groups):
        cut = slice(i * both, (i + 1) * both)
        store_grad(gsa, i, 3, contract(grl_t[cut], att_t[...], 1, 1))
    over_copy(1).start()
    serve_to(3 * chunks + 1)

    def weights_back(i):
        cut = n1t[i * both : (i + 1) * both, :]
        store_grad(gsa, i, 0, contract(cut, dq_t[...], 1, 1))
        store_grad(gsa, i, 1, contract(cut, dkv[0], 1, 0))
        store_grad(gsa, i, 2, contract(cut, dkv[1], 1, 0))

    for i in range(groups):
        weights_back(i)
        if i % 2:
            serve_to(served[0] + 1)
    over_copy(2).start()
    reduce_send(1)
    serve_to(served[0] + 1)
    reduce_send(2)
    serve_to(served[0] + 1)

    def bucket_sums(h):
        for b in range(2 * half):
            summed_block = jnp.zeros((8, BLOCK), f32)
            for d in (-1, 0) if b < half else (0, 1):
                bucket = bucket_of(d * BLOCK + row_of - column_of)
                chosen = jnp.where(bucket == b, near[h, d + 1], 0.0)
                summed_block = summed_block + jnp.sum(
                    chosen.reshape(BLOCK // 8, 8, BLOCK), axis=0
                )
            pick[b : b + 1, :] = jnp.sum(summed_block, axis=0, keepdims=True)
        sums = contract(jnp.ones((8, BLOCK), f32), pick[...], 1, 1, highest)
        small[:, 0 : 2 * half] += jnp.where(iota((8, 2 * half), 0) == 2 + h, sums, 0.0)

    def far_sums():
        tail = dk.shape[1] - BLOCK
        first_lane = head_width - tail
        column_sums = dk[:, tail:]
        block_row = iota((keys, BLOCK), 0)
        lane = iota((keys, BLOCK), 1)
        left_sum = jnp.zeros((1, BLOCK), f32)
        right_sum = jnp.zeros((1, BLOCK), f32)
        for j in range(query_blocks):
            mine = jnp.zeros((keys, BLOCK), jnp.bool_)
            for h in range(heads):
                mine = jnp.logical_or(mine, lane == first_lane + h * query_blocks + j)
            home = c * query_blocks + j
            is_left = jnp.logical_and(mine, block_row < (home - 1) * BLOCK)
            is_right = jnp.logical_and(mine, block_row >= (home + 2) * BLOCK)
            left_sum += jnp.sum(jnp.where(is_left, column_sums, 0.0), axis=0, keepdims=True)
            right_sum += jnp.sum(jnp.where(is_right, column_sums, 0.0), axis=0, keepdims=True)
        from_lane, to_lane = iota((BLOCK, BLOCK), 0), iota((BLOCK, BLOCK), 1)
        for h in range(heads):
            start = first_lane + h * query_blocks
            inside = jnp.logical_and(from_lane >= start, from_lane < start + query_blocks)
            left_pick = jnp.logical_and(inside, to_lane == far).astype(f32)
            right_pick = jnp.logical_and(inside, to_lane == half + far).astype(f32)
            small[2 + h : 3 + h, 0:BLOCK] += (
                contract(jnp.broadcast_to(left_sum, (8, BLOCK)), left_pick, 1, 0, highest)
                + contract(jnp.broadcast_to(right_sum, (8, BLOCK)), right_pick, 1, 0, highest)
            )[0:1]

    def input_back(b):
        for j in range(per_block):
            finish(3, b * per_block + j)
        at = block_rows(b)
        grad_in = tot[3, at, :].astype(f32)
        xs = x_ref[at, :].astype(f32)
        inverse = inverse_rms(xs)
        u = xs * inverse
        small[0:1, :] += jnp.sum(grad_in * u, axis=0, keepdims=True)
        g = grad_in * gain_rows[0:1, :]
        gin_ref[at, :] = grad_res[at, :] + inverse * (
            g - u * jnp.mean(g * u, axis=-1, keepdims=True)
        )

    def layer_out(b):
        for j in range(per_block):
            finish(2, b * per_block + j)
        at = block_rows(b)
        out_ref[at, :] = (resid[at, :] + tot[2, at, :].astype(f32)).astype(bf16)

    fillers = [functools.partial(bucket_sums, h) for h in range(heads)] + [far_sums]
    fillers += [functools.partial(layer_out, b) for b in range(blocks)]
    fillers += [functools.partial(reduce_finish, n) for n in range(2)]
    for b in range(blocks):
        need = 3 * chunks + (b + 1) * per_block + LAG
        while served[0] < need:
            serve_to(served[0] + 1)
            if fillers and served[0] < need:
                fillers.pop(0)()
        input_back(b)
        if fillers and b + 1 < blocks:
            fillers.pop(0)()

    small_copies = [
        remote(
            small.at[...], small_all.at[me], sm_send.at[k * 2 + kc - 1], sm_recv.at[k * 2 + kc - 1],
            (f ^ k, c ^ kc, t),
        )
        for k in range(groups)
        for kc in range(2)
        if k or kc
    ]
    for copy in small_copies:
        copy.start()

    while fillers:
        fillers.pop(0)()
    reduce_finish(2)
    small_all[me] = small[...]
    for copy in small_copies:
        copy.wait_recv()
    total_small = small_all[0]
    for i in range(1, shards):
        total_small = total_small + small_all[i]
    to_own = (iota((width, BLOCK), 0) == iota((width, BLOCK), 1) + me * shard).astype(f32)
    own_gains = contract(total_small, to_own, 1, 0, highest)
    gain_one_out_ref[...] = own_gains[0:1, 0:shard]
    gain_two_out_ref[...] = own_gains[1:2, 0:shard]
    bias_out_ref[...] = total_small[2 : 2 + heads, 0 : 2 * half]

    for copy in small_copies:
        copy.wait_send()
    for g in range(5):
        gather_drain(g)
    for copy in kv_copies:
        copy.wait_send()
    dkv_copy.wait_send()
    for a in range(4):
        drain(a)
    for n in range(3):
        reduce_drain(n)


def fused_layer(shards, x, cot, ids, gain_one, gain_two, weights, table):
    rows, width = x.shape
    shard, head_width = weights[0].shape
    units = weights[4].shape[1]
    keys = ids.shape[1]
    heads = head_width // DH
    groups = shards // 2
    chunks = rows // CHUNK
    padded = head_width + (-head_width) % BLOCK
    if padded - head_width < heads * (rows // BLOCK):
        padded += BLOCK
    vmem, dma = pltpu.VMEM, pltpu.SemaphoreType.DMA
    out_shape = (
        jax.ShapeDtypeStruct((rows, width), bf16),
        jax.ShapeDtypeStruct((rows, width), f32),
        *[jax.ShapeDtypeStruct((shard, head_width), f32)] * 4,
        *[jax.ShapeDtypeStruct((shard, units), f32)] * 3,
        jax.ShapeDtypeStruct((1, shard), f32),
        jax.ShapeDtypeStruct((1, shard), f32),
        jax.ShapeDtypeStruct(table.shape, f32),
    )
    in_vmem = pl.BlockSpec(memory_space=pltpu.VMEM)
    scratch = [
        vmem((shards, 4, shard, head_width), bf16),
        vmem((shards, 3, shard, units), bf16),
        vmem((shards, 8, BLOCK), f32),
        vmem((8, width), f32),
        vmem((heads, 5, BLOCK, BLOCK), f32),
        vmem((heads, keys, rows), f32),
        vmem((keys, QUERY_BLOCK), f32),
        vmem((heads, keys, rows), bf16),
        vmem((keys, QUERY_BLOCK), bf16),
        vmem((4, rows, width), bf16),
        vmem((4, rows, width), bf16),
        vmem((4, rows, width), bf16),
        vmem((rows, width), f32),
        vmem((rows, width), f32),
        vmem((rows, width), bf16),
        vmem((rows, width), bf16),
        vmem((rows, width), bf16),
        vmem((width, rows), bf16),
        vmem((rows, units), bf16),
        vmem((rows, units), bf16),
        vmem((rows, units), bf16),
        vmem((head_width, rows), bf16),
        vmem((keys, head_width), bf16),
        vmem((keys, head_width), bf16),
        vmem((head_width, keys), bf16),
        vmem((head_width, keys), bf16),
        vmem((head_width, rows), bf16),
        vmem((head_width, rows), bf16),
        vmem((head_width, rows), bf16),
        vmem((8, rows), f32),
        vmem((8, rows), f32),
        vmem((keys, padded), f32),
        vmem((keys, head_width), f32),
        vmem((heads, 3, BLOCK, BLOCK), f32),
        vmem((table.shape[1], BLOCK), f32),
        vmem((2, rows, head_width), bf16),
        vmem((2, rows, head_width), bf16),
        vmem((2, rows, head_width), bf16),
        vmem((groups, 2, 4, shard, head_width), bf16),
        vmem((groups, 2, 3, shard, units), bf16),
        vmem((groups, 4, shard, head_width), bf16),
        vmem((groups, 3, shard, units), bf16),
        vmem((groups, 4, shard, head_width), bf16),
        vmem((groups, 3, shard, units), bf16),
        vmem((groups - 1, 4, shard, head_width), bf16),
        vmem((groups - 1, 3, shard, units), bf16),
        vmem((8, width), f32),
        vmem((shards, 8, width), f32),
        dma((5, 2 * groups)),
        dma((5, 2 * groups)),
        dma((2,)),
        dma((2,)),
        dma((4, chunks)),
        dma((4, chunks)),
        dma((4, chunks)),
        dma((4, chunks)),
        dma((1,)),
        dma((1,)),
        dma((3,)),
        dma((3,)),
        dma((3, groups)),
        dma((3, groups)),
        dma((shards,)),
        dma((shards,)),
    ]
    return pl.pallas_call(
        functools.partial(layer_kernel, shards),
        out_shape=out_shape,
        in_specs=[in_vmem] * 12 + [pl.BlockSpec(memory_space=pltpu.SMEM)],
        out_specs=[in_vmem] * len(out_shape),
        scratch_shapes=scratch,
        name="layer",
        compiler_params=pltpu.CompilerParams(
            collective_id=0, has_side_effects=True, vmem_limit_bytes=63 << 20
        ),
    )(x, cot, ids, gain_one, gain_two, *weights, table)


def publish_kernel(count, *refs):
    sources, targets = refs[:count], refs[count : 2 * count]
    held, in_sem, out_sem = refs[2 * count : 3 * count], refs[3 * count], refs[3 * count + 1]
    inward = [
        pltpu.make_async_copy(sources[i], held[i], in_sem.at[i]) for i in range(count)
    ]
    outward = [
        pltpu.make_async_copy(held[i], targets[i], out_sem.at[i]) for i in range(count)
    ]
    for copy in inward:
        copy.start()
    for arriving, leaving in zip(inward, outward):
        arriving.wait()
        leaving.start()
    for copy in outward:
        copy.wait()


def publish(values):
    count = len(values)
    anywhere = pl.BlockSpec(memory_space=pl.ANY)
    return pl.pallas_call(
        functools.partial(publish_kernel, count),
        out_shape=[jax.ShapeDtypeStruct(value.shape, value.dtype) for value in values],
        in_specs=[anywhere] * count,
        out_specs=[anywhere] * count,
        scratch_shapes=[pltpu.VMEM(value.shape, value.dtype) for value in values]
        + [pltpu.SemaphoreType.DMA((count,))] * 2,
        name="publish",
    )(*values)


def on_device_fused(
    layer_input,
    doc_ids,
    query_weight,
    key_weight,
    value_weight,
    output_weight,
    gate_weight,
    up_weight,
    down_weight,
    first_gain,
    second_gain,
    position_bias,
    cotangent,
):
    shards = lax.axis_size("fsdp") * lax.axis_size("ctx")
    outs = fused_layer(
        shards,
        layer_input[0],
        cotangent[0],
        doc_ids,
        first_gain[None],
        second_gain[None],
        (
            query_weight,
            key_weight,
            value_weight,
            output_weight,
            gate_weight,
            up_weight,
            down_weight,
        ),
        position_bias.T,
    )
    outs = publish(outs)
    return (
        outs[0][None],
        outs[1][None],
        *outs[2:9],
        outs[9][0],
        outs[10][0],
        outs[11].T,
    )


def fits_kernel(mesh):
    return mesh.shape["ctx"] == 2 and mesh.shape["tp"] == 4 and mesh.shape["fsdp"] in (2, 4)


def solution(mesh):
    return jax.shard_map(
        on_device_fused if fits_kernel(mesh) else on_device,
        mesh=mesh,
        in_specs=(
            P("fsdp", "ctx", None),
            P("fsdp", None),
            P(("fsdp", "ctx"), "tp"),
            P(("fsdp", "ctx"), "tp"),
            P(("fsdp", "ctx"), "tp"),
            P(("fsdp", "ctx"), "tp"),
            P(("fsdp", "ctx"), "tp"),
            P(("fsdp", "ctx"), "tp"),
            P(("fsdp", "ctx"), "tp"),
            P(("fsdp", "ctx")),
            P(("fsdp", "ctx")),
            P(None, "tp"),
            P("fsdp", "ctx", None),
        ),
        out_specs=(
            P("fsdp", "ctx", None),
            P("fsdp", "ctx", None),
            P(("fsdp", "ctx"), "tp"),
            P(("fsdp", "ctx"), "tp"),
            P(("fsdp", "ctx"), "tp"),
            P(("fsdp", "ctx"), "tp"),
            P(("fsdp", "ctx"), "tp"),
            P(("fsdp", "ctx"), "tp"),
            P(("fsdp", "ctx"), "tp"),
            P(("fsdp", "ctx")),
            P(("fsdp", "ctx")),
            P(None, "tp"),
        ),
        check_vma=False,
    )
```

```python
import functools

import jax
import jax.numpy as jnp
from jax import lax
from jax.experimental import pallas as pl
from jax.experimental.pallas import tpu as pltpu
from jax.sharding import PartitionSpec as P

DH = 64


epsilon = 1e-06
masked_score = -1000000000.0
bucket_edges = (12, 16, 23, 32, 46, 64, 91)
highest = lax.Precision.HIGHEST


def bucket_of(relative):
    distance = jnp.abs(relative)
    beyond = jnp.zeros_like(distance) + 8
    for edge_value in bucket_edges:
        beyond = beyond + (distance >= edge_value).astype(jnp.int32)
    inside = jnp.where(distance < 8, distance, beyond)
    return jnp.where(relative > 0, 16, 0) + inside


def rms_norm(values, gain_vector):
    inverse = lax.rsqrt(jnp.mean(values * values, axis=-1, keepdims=True) + epsilon)
    return values * inverse * gain_vector


def gated_unit(gate_in, up_in):
    return jax.nn.gelu(gate_in, approximate=True) * up_in


def relative_bias(bias_table, query_rows, key_rows, offset):
    span_width = key_rows + query_rows
    relative = lax.iota(jnp.int32, span_width) - (query_rows - 1) - offset
    one_hot = (
        bucket_of(relative)[:, None] == lax.iota(jnp.int32, bias_table.shape[0])[None, :]
    ).astype(jnp.float32)
    per_shift = jnp.dot(one_hot, bias_table, precision=highest).T
    heads_here = bias_table.shape[1]
    toeplitz = jnp.broadcast_to(per_shift[:, None, :], (heads_here, query_rows, span_width))
    toeplitz = toeplitz.reshape(heads_here, query_rows * span_width)[
        :, : query_rows * (span_width - 1)
    ]
    toeplitz = toeplitz.reshape(heads_here, query_rows, span_width - 1)
    return (toeplitz[:, :, query_rows - 1 : query_rows - 1 + key_rows], one_hot)


def diagonal_sums(grad_scores, query_rows, key_rows):
    heads_here = grad_scores.shape[0]
    span_width = key_rows + query_rows
    placed = jnp.pad(grad_scores, ((0, 0), (0, 0), (query_rows - 1, 0)))
    placed = placed.reshape(heads_here, query_rows * (span_width - 1))
    placed = jnp.pad(placed, ((0, 0), (0, query_rows)))
    return jnp.sum(placed.reshape(heads_here, query_rows, span_width), axis=1)


def on_device(
    layer_input,
    doc_ids,
    query_weight,
    key_weight,
    value_weight,
    output_weight,
    gate_weight,
    up_weight,
    down_weight,
    first_gain,
    second_gain,
    position_bias,
    cotangent,
):
    query_rows = layer_input.shape[1]
    key_rows = query_rows * lax.axis_size("ctx")
    heads_here = position_bias.shape[1]
    head_width = heads_here * DH
    offset = lax.axis_index("ctx") * query_rows
    everything = (
        query_weight,
        key_weight,
        value_weight,
        output_weight,
        gate_weight,
        up_weight,
        down_weight,
        first_gain,
        second_gain,
    )
    (
        full_query,
        full_key,
        full_value,
        full_output,
        full_gate,
        full_up,
        full_down,
        gain_one,
        gain_two,
    ) = (
        lax.all_gather(everything[0], ("fsdp", "ctx"), axis=0, tiled=True),
        lax.all_gather(everything[1], ("fsdp", "ctx"), axis=0, tiled=True),
        lax.all_gather(everything[2], ("fsdp", "ctx"), axis=0, tiled=True),
        lax.all_gather(everything[3], ("fsdp", "ctx"), axis=0, tiled=True),
        lax.all_gather(everything[4], ("fsdp", "ctx"), axis=0, tiled=True),
        lax.all_gather(everything[5], ("fsdp", "ctx"), axis=0, tiled=True),
        lax.all_gather(everything[6], ("fsdp", "ctx"), axis=0, tiled=True),
        lax.all_gather(everything[7], ("fsdp", "ctx"), axis=0, tiled=True),
        lax.all_gather(everything[8], ("fsdp", "ctx"), axis=0, tiled=True),
    )
    inputs = layer_input.astype(jnp.float32)
    gain_first = gain_one.astype(jnp.float32)
    gain_second = gain_two.astype(jnp.float32)
    normed_one = rms_norm(inputs, gain_first).astype(jnp.bfloat16)
    queries = jnp.dot(normed_one, full_query, preferred_element_type=jnp.float32).astype(
        jnp.bfloat16
    )
    keys_local = jnp.dot(normed_one, full_key, preferred_element_type=jnp.float32).astype(
        jnp.bfloat16
    )
    values_local = jnp.dot(normed_one, full_value, preferred_element_type=jnp.float32).astype(
        jnp.bfloat16
    )
    keys_all, values_all = (
        lax.all_gather(keys_local, "ctx", axis=1, tiled=True),
        lax.all_gather(values_local, "ctx", axis=1, tiled=True),
    )
    bias_block, one_hot = relative_bias(position_bias, query_rows, key_rows, offset)

    def scores_of(query_heads, key_heads, id_row):
        raw_scores = jnp.einsum(
            "qhd,khd->hqk", query_heads, key_heads, preferred_element_type=jnp.float32
        )
        own_ids = lax.dynamic_slice_in_dim(id_row, offset, query_rows)
        same_doc = own_ids[:, None] == id_row[None, :]
        return jnp.where(same_doc[None], raw_scores + bias_block, masked_score)

    def forward_one(packed):
        query_seq, key_seq, value_seq, id_row = packed
        scores = scores_of(
            query_seq.reshape(query_rows, heads_here, DH),
            key_seq.reshape(key_rows, heads_here, DH),
            id_row,
        )
        row_max = jnp.max(scores, axis=-1, keepdims=True)
        exponentials = jnp.exp(scores - row_max)
        row_total = jnp.sum(exponentials, axis=-1, keepdims=True)
        probabilities = (exponentials / row_total).astype(jnp.bfloat16)
        attended = jnp.einsum(
            "hqk,khd->qhd",
            probabilities,
            value_seq.reshape(key_rows, heads_here, DH),
            preferred_element_type=jnp.float32,
        )
        log_row = row_max[..., 0] + jnp.log(row_total[..., 0])
        return (attended.reshape(query_rows, head_width).astype(jnp.bfloat16), log_row)

    attended, log_sums = lax.map(forward_one, (queries, keys_all, values_all, doc_ids))
    attention_terms = jnp.einsum(
        "sqe,de->sqd", attended, full_output, preferred_element_type=jnp.float32
    )
    residual = inputs + lax.psum(attention_terms.astype(jnp.bfloat16), "tp").astype(jnp.float32)
    normed_two = rms_norm(residual, gain_second).astype(jnp.bfloat16)
    gate_pre = jnp.dot(normed_two, full_gate, preferred_element_type=jnp.float32)
    up_pre = jnp.dot(normed_two, full_up, preferred_element_type=jnp.float32)
    activated = gated_unit(gate_pre, up_pre).astype(jnp.bfloat16)
    ffn_terms = jnp.einsum("sqf,df->sqd", activated, full_down, preferred_element_type=jnp.float32)
    output_rows = (
        residual + lax.psum(ffn_terms.astype(jnp.bfloat16), "tp").astype(jnp.float32)
    ).astype(jnp.bfloat16)
    grad_activated = jnp.einsum(
        "sqd,df->sqf", cotangent, full_down, preferred_element_type=jnp.float32
    )
    down_grad = jnp.einsum("sqd,sqf->df", cotangent, activated, preferred_element_type=jnp.float32)
    gated_value, gated_back = jax.vjp(gated_unit, gate_pre, up_pre)
    grad_gate, grad_up = gated_back(grad_activated)
    grad_gate = grad_gate.astype(jnp.bfloat16)
    grad_up = grad_up.astype(jnp.bfloat16)
    gate_grad = jnp.einsum("sqd,sqf->df", normed_two, grad_gate, preferred_element_type=jnp.float32)
    up_grad = jnp.einsum("sqd,sqf->df", normed_two, grad_up, preferred_element_type=jnp.float32)
    normed_two_terms = jnp.einsum(
        "sqf,df->sqd", grad_gate, full_gate, preferred_element_type=jnp.float32
    ) + jnp.einsum("sqf,df->sqd", grad_up, full_up, preferred_element_type=jnp.float32)
    grad_normed_two = lax.psum(normed_two_terms.astype(jnp.bfloat16), "tp").astype(jnp.float32)
    second_value, second_back = jax.vjp(rms_norm, residual, gain_second)
    grad_residual, second_gain_grad = second_back(grad_normed_two)
    grad_residual = grad_residual + cotangent.astype(jnp.float32)
    grad_low = grad_residual.astype(jnp.bfloat16)
    grad_attended = jnp.einsum(
        "sqd,de->sqe", grad_low, full_output, preferred_element_type=jnp.float32
    ).astype(jnp.bfloat16)
    output_grad = jnp.einsum("sqd,sqe->de", grad_low, attended, preferred_element_type=jnp.float32)

    def backward_one(running, packed):
        query_seq, key_seq, value_seq, id_row, grad_seq, log_row = packed
        query_heads = query_seq.reshape(query_rows, heads_here, DH)
        key_heads = key_seq.reshape(key_rows, heads_here, DH)
        value_heads = value_seq.reshape(key_rows, heads_here, DH)
        grad_heads = grad_seq.reshape(query_rows, heads_here, DH)
        scores = scores_of(query_heads, key_heads, id_row)
        probabilities = jnp.exp(scores - log_row[..., None])
        grad_probs = jnp.einsum(
            "qhd,khd->hqk", grad_heads, value_heads, preferred_element_type=jnp.float32
        )
        grad_values = jnp.einsum(
            "hqk,qhd->khd",
            probabilities.astype(jnp.bfloat16),
            grad_heads,
            preferred_element_type=jnp.float32,
        )
        grad_scores = probabilities * (
            grad_probs - jnp.sum(probabilities * grad_probs, axis=-1, keepdims=True)
        )
        low_scores = grad_scores.astype(jnp.bfloat16)
        grad_queries = jnp.einsum(
            "hqk,khd->qhd", low_scores, key_heads, preferred_element_type=jnp.float32
        )
        grad_keys = jnp.einsum(
            "hqk,qhd->khd", low_scores, query_heads, preferred_element_type=jnp.float32
        )
        running = running + diagonal_sums(grad_scores, query_rows, key_rows)
        return (
            running,
            (
                grad_queries.reshape(query_rows, head_width).astype(jnp.bfloat16),
                grad_keys.reshape(key_rows, head_width),
                grad_values.reshape(key_rows, head_width),
            ),
        )

    shift_grads, (grad_queries, key_parts, value_parts) = lax.scan(
        backward_one,
        jnp.zeros((heads_here, query_rows + key_rows), jnp.float32),
        (queries, keys_all, values_all, doc_ids, grad_attended, log_sums),
    )
    grad_keys, grad_values = (
        lax.psum_scatter(
            key_parts.astype(jnp.bfloat16), "ctx", scatter_dimension=1, tiled=True
        ).astype(jnp.float32),
        lax.psum_scatter(
            value_parts.astype(jnp.bfloat16), "ctx", scatter_dimension=1, tiled=True
        ).astype(jnp.float32),
    )
    grad_keys = grad_keys.astype(jnp.bfloat16)
    grad_values = grad_values.astype(jnp.bfloat16)
    normed_one_terms = (
        jnp.einsum("sqe,de->sqd", grad_queries, full_query, preferred_element_type=jnp.float32)
        + jnp.einsum("sqe,de->sqd", grad_keys, full_key, preferred_element_type=jnp.float32)
        + jnp.einsum("sqe,de->sqd", grad_values, full_value, preferred_element_type=jnp.float32)
    )
    grad_normed_one = lax.psum(normed_one_terms.astype(jnp.bfloat16), "tp").astype(jnp.float32)
    query_grad = jnp.einsum(
        "sqd,sqe->de", normed_one, grad_queries, preferred_element_type=jnp.float32
    )
    key_grad = jnp.einsum("sqd,sqe->de", normed_one, grad_keys, preferred_element_type=jnp.float32)
    value_grad = jnp.einsum(
        "sqd,sqe->de", normed_one, grad_values, preferred_element_type=jnp.float32
    )
    first_value, first_back = jax.vjp(rms_norm, inputs, gain_first)
    grad_inputs, first_gain_grad = first_back(grad_normed_one)
    input_rows = grad_residual + grad_inputs
    bias_gradient = lax.psum(jnp.dot(one_hot.T, shift_grads.T, precision=highest), ("fsdp", "ctx"))
    (
        query_total,
        key_total,
        value_total,
        output_total,
        gate_total,
        up_total,
        down_total,
        first_total,
        second_total,
    ) = (
        lax.psum_scatter(query_grad, ("fsdp", "ctx"), scatter_dimension=0, tiled=True),
        lax.psum_scatter(key_grad, ("fsdp", "ctx"), scatter_dimension=0, tiled=True),
        lax.psum_scatter(value_grad, ("fsdp", "ctx"), scatter_dimension=0, tiled=True),
        lax.psum_scatter(output_grad, ("fsdp", "ctx"), scatter_dimension=0, tiled=True),
        lax.psum_scatter(gate_grad, ("fsdp", "ctx"), scatter_dimension=0, tiled=True),
        lax.psum_scatter(up_grad, ("fsdp", "ctx"), scatter_dimension=0, tiled=True),
        lax.psum_scatter(down_grad, ("fsdp", "ctx"), scatter_dimension=0, tiled=True),
        lax.psum_scatter(first_gain_grad, ("fsdp", "ctx"), scatter_dimension=0, tiled=True),
        lax.psum_scatter(second_gain_grad, ("fsdp", "ctx"), scatter_dimension=0, tiled=True),
    )
    return (
        output_rows,
        input_rows,
        query_total,
        key_total,
        value_total,
        output_total,
        gate_total,
        up_total,
        down_total,
        first_total,
        second_total,
        bias_gradient,
    )


MESH = pl.DeviceIdType.MESH
bf16, f32 = jnp.bfloat16, jnp.float32
BLOCK = 128
QUERY_BLOCK = 256
FORWARD_BLOCK = 256
CHUNK = 32
LAG = 4
RELAY_ROWS = 16
LATE_BLOCK = 1


def contract(left, right, left_dim, right_dim, precision=None):
    return lax.dot_general(
        left,
        right,
        (((left_dim,), (right_dim,)), ((), ())),
        preferred_element_type=f32,
        precision=precision,
    )


def iota(shape, dim):
    return lax.broadcasted_iota(jnp.int32, shape, dim)


def layer_kernel(
    shards,
    x_hbm,
    cot_hbm,
    ids_ref,
    gain_one_ref,
    gain_two_ref,
    wq_ref,
    wk_ref,
    wv_ref,
    wo_ref,
    wg_ref,
    wu_ref,
    wd_ref,
    table_ref,
    out_hbm,
    gin_hbm,
    gq_hbm,
    gk_hbm,
    gv_hbm,
    go_hbm,
    gg_hbm,
    gu_hbm,
    gd_hbm,
    gain_one_out_ref,
    gain_two_out_ref,
    bias_out_ref,
    x_ref,
    cot_ref,
    out_ref,
    gin_ref,
    ga_ref,
    gf_ref,
    staged,
    wkv,
    wqo,
    wo3,
    other_out,
    wo_all,
    wf,
    gains_all,
    gain_rows,
    tiles,
    masked_bias,
    score,
    expo,
    low_score,
    snd,
    part,
    tot,
    resid,
    grad_res,
    n1,
    n2,
    grl,
    n1t,
    turned,
    act,
    ggate,
    gup,
    q_t,
    k_all,
    v_all,
    k_t,
    v_t,
    att_all,
    dos_t,
    dq_t,
    linv,
    delta,
    dk,
    dv,
    near,
    pick,
    dkv_send,
    dkv_recv,
    dkv,
    gsa,
    gsf,
    ra,
    rf,
    sa,
    sf,
    ra2,
    rf2,
    small,
    small_all,
    gain_part,
    load_sem,
    store_sem,
    ag_send,
    ag_recv,
    zo_send,
    zo_recv,
    at_send,
    at_recv,
    kv_send,
    kv_recv,
    s1,
    r1,
    s2,
    r2,
    dkv_ssem,
    dkv_rsem,
    rs_send,
    rs_recv,
    rs2_send,
    rs2_recv,
    sm_send,
    sm_recv,
    gp_send,
    gp_recv,
):
    groups = shards // 2
    f, c, t = lax.axis_index("fsdp"), lax.axis_index("ctx"), lax.axis_index("tp")
    me = f * 2 + c
    rows, width = x_ref.shape
    keys = k_all.shape[0]
    head_width = wq_ref.shape[1]
    heads = head_width // DH
    units = wg_ref.shape[1]
    shard = wq_ref.shape[0]
    chunks = rows // CHUNK
    per_block = BLOCK // CHUNK
    partner = (f, 1 - c, t)
    outer = jnp.logical_or(t == 0, t == 3)
    inner = jnp.logical_or(t == 1, t == 2)
    near_end = jnp.where(t < 2, 1, 2)
    far_end = jnp.where(t < 2, 0, 3)
    middle = 3 - t

    def remote(source, target, send_sem, recv_sem, device):
        return pltpu.make_async_remote_copy(
            src_ref=source,
            dst_ref=target,
            send_sem=send_sem,
            recv_sem=recv_sem,
            device_id=device,
            device_id_type=MESH,
        )

    barrier = pltpu.get_barrier_semaphore()
    for k in range(groups):
        for kc in range(2):
            if k or kc:
                pl.semaphore_signal(
                    barrier, inc=1, device_id=(f ^ k, c ^ kc, t), device_id_type=MESH
                )

    for kt in range(1, 4):
        pl.semaphore_signal(
            barrier, inc=1, device_id=(f, c, t ^ kt), device_id_type=MESH
        )
    loads = [
        pltpu.make_async_copy(source, target, load_sem.at[n])
        for n, (source, target) in enumerate(
            (
                (wk_ref, staged.at[0]),
                (wv_ref, staged.at[1]),
                (wq_ref, staged.at[2]),
                (wo_ref, staged.at[3]),
                (x_hbm, x_ref),
                (wg_ref, wf.at[me, 0]),
                (wu_ref, wf.at[me, 1]),
                (wd_ref, wf.at[me, 2]),
                (cot_hbm, cot_ref),
            )
        )
    ]
    for copy in loads:
        copy.start()
    gains_all[me] = jnp.zeros((8, BLOCK), f32)
    gains_all[me, 0:1, 0:shard] = gain_one_ref[...].astype(f32)
    gains_all[me, 1:2, 0:shard] = gain_two_ref[...].astype(f32)
    for copy in loads[:4]:
        copy.wait()
    wkv[me, :, 0:head_width] = staged[0]
    wkv[me, :, head_width:] = staged[1]
    wqo[me, :, 0:head_width] = staged[2]
    wqo[me, :, head_width:] = staged[3]
    pl.semaphore_wait(barrier, shards - 1 + 3)

    def piece(g, index):
        if g < 2:
            return (wkv, wqo)[g].at[index]
        return wo3.at[index] if g == 5 else wf.at[index, g - 2]

    def half_piece(g, index, n):
        return piece(g, index).at[n * (shard // 2) : (n + 1) * (shard // 2)]

    def own_copy(g, k):
        view = piece(g, me)
        return remote(view, view, ag_send.at[g, k - 1], ag_recv.at[g, k - 1], (f ^ k, c, t))

    def pass_copy(g, k):
        view = half_piece(g, (f ^ k) * 2 + c, k - 1)
        return remote(view, view, ag_send.at[g, k + 1], ag_recv.at[g, k + 1], (f ^ (3 - k), c, t))

    def over_piece(g, k):
        view = piece(g, (f ^ k) * 2 + c)
        return remote(view, view, ag_send.at[g, 4 + k], ag_recv.at[g, 4 + k], partner)

    def gather_own(g):
        for k in (1, 2):
            own_copy(g, k).start()
        over_piece(g, 0).start()

    def gather_pass(g):
        for k in (1, 2):
            own_copy(g, k).wait_recv()
            pass_copy(g, k).start()
            over_piece(g, k).start()

    def gather_corner(g):
        for k in (1, 2):
            pass_copy(g, k).wait_recv()
        over_piece(g, 3).start()

    def gather_finish(g):
        for k in range(4):
            over_piece(g, k).wait_recv()

    def gather_drain(g):
        for k in (1, 2):
            own_copy(g, k).wait_send()
            pass_copy(g, k).wait_send()
        for k in range(4):
            over_piece(g, k).wait_send()

    def gain_copy(k):
        view = gains_all.at[me]
        return remote(view, view, ag_send.at[6, k], ag_recv.at[6, k], (f ^ k, c, t))

    def gain_over(k):
        view = gains_all.at[(f ^ k) * 2 + c]
        return remote(view, view, ag_send.at[6, 4 + k], ag_recv.at[6, 4 + k], partner)

    def span(j):
        if isinstance(j, int):
            return pl.ds(j * CHUNK, CHUNK)
        return pl.ds(pl.multiple_of(j * CHUNK, CHUNK), CHUNK)

    def end_copy(a, j):
        return remote(
            snd.at[a, span(j)], part.at[a, span(j)], s1.at[a, j], r1.at[a, j], (f, c, near_end)
        )

    def mid_copy(a, j):
        return remote(
            snd.at[a, span(j)], tot.at[a, span(j)], s1.at[a, j], r2.at[a, j], (f, c, middle)
        )

    def total_copy(a, j):
        return remote(
            tot.at[a, span(j)], tot.at[a, span(j)], s2.at[a, j], r2.at[a, j], (f, c, far_end)
        )

    def add_rows(target, a, j, left, right):
        def body(r, carry):
            at = pl.ds(pl.multiple_of(j * CHUNK + r * RELAY_ROWS, RELAY_ROWS), RELAY_ROWS)
            target[a, at] = (left[a, at].astype(f32) + right[a, at].astype(f32)).astype(bf16)
            return carry

        lax.fori_loop(0, CHUNK // RELAY_ROWS, body, 0)

    def service(step):
        def total_step():
            a, j = split(step - LAG)
            mid_copy(a, j).wait_recv()
            add_rows(tot, a, j, snd, tot)
            total_copy(a, j).start()

        def middle_step():
            a, j = split(step)
            end_copy(a, j).wait_recv()
            add_rows(snd, a, j, snd, part)
            mid_copy(a, j).start()

        def split(n):
            if isinstance(n, int):
                return divmod(n, chunks)
            return lax.div(n, chunks), lax.rem(n, chunks)

        if isinstance(step, int):
            if step >= LAG:
                pl.when(inner)(total_step)
            if step < 3 * chunks:
                pl.when(inner)(middle_step)
        else:
            pl.when(jnp.logical_and(inner, step >= LAG))(total_step)
            pl.when(jnp.logical_and(inner, step < 3 * chunks))(middle_step)

    def serve(start, count):
        for n in range(count):
            service(start + n)

    def put_block(a, b):
        @pl.when(outer)
        def _():
            for j in range(per_block):
                end_copy(a, b * per_block + j).start()

    def totals_of(a, b):
        @pl.when(outer)
        def _():
            for j in range(per_block):
                total_copy(a, b * per_block + j).wait_recv()

    def drain_all():
        def body(n, carry):
            a, j = lax.div(n, chunks), lax.rem(n, chunks)

            @pl.when(outer)
            def _():
                end_copy(a, j).wait_send()

            @pl.when(inner)
            def _():
                mid_copy(a, j).wait_send()
                total_copy(a, j).wait_send()

            return carry

        lax.fori_loop(0, 3 * chunks, body, 0)

    for k in range(1, 4):
        gain_copy(k).start()
    gain_over(0).start()
    gather_own(0)
    gather_own(1)
    out_copies = [
        remote(
            staged.at[3], other_out.at[k - 1], zo_send.at[k - 1], zo_recv.at[k - 1], (f, c, t ^ k)
        )
        for k in range(1, 4)
    ]
    for copy in out_copies:
        copy.start()

    half = table_ref.shape[1] // 2
    far = half - 1
    row_of, column_of = iota((BLOCK, BLOCK), 0), iota((BLOCK, BLOCK), 1)
    for h in range(heads):
        tiles[h, 0] = jnp.full((BLOCK, BLOCK), table_ref[h, far], f32)
        tiles[h, 4] = jnp.full((BLOCK, BLOCK), table_ref[h, half + far], f32)
    for d in (-1, 0, 1):
        bucket = bucket_of(d * BLOCK + row_of - column_of)
        members = range(half) if d < 0 else range(half, 2 * half) if d > 0 else range(2 * half)

        def per_head(h, carry, bucket=bucket, members=members, d=d):
            filled = jnp.zeros((BLOCK, BLOCK), f32)
            for b in members:
                filled = jnp.where(bucket == b, table_ref[h, b], filled)
            tiles[h, d + 2] = filled
            return carry

        lax.fori_loop(0, heads, per_head, 0)

    def bias_rows(kb, carry):
        key_rows = pl.ds(pl.multiple_of(kb * BLOCK, BLOCK), BLOCK)
        key_ids = jnp.broadcast_to(ids_ref[0:1, key_rows].astype(f32), (BLOCK, BLOCK)).T
        for qb in range(rows // BLOCK):
            start = pl.multiple_of(c * rows + qb * BLOCK, BLOCK)
            query_ids = ids_ref[0:1, pl.ds(start, BLOCK)].astype(f32)
            same = key_ids == query_ids
            d = jnp.clip(kb - c * (rows // BLOCK) - qb, -2, 2) + 2
            for h in range(heads):
                masked_bias[h, key_rows, qb * BLOCK : (qb + 1) * BLOCK] = jnp.where(
                    same, tiles[h, d], masked_score
                )
        return carry

    key_blocks = keys // BLOCK
    lax.fori_loop(0, key_blocks // 4, bias_rows, 0)
    for k in range(1, 4):
        gain_copy(k).wait_recv()
        gain_over(k).start()
    gather_pass(0)
    lax.fori_loop(key_blocks // 4, key_blocks // 2, bias_rows, 0)
    gather_pass(1)
    for copy in loads[4:]:
        copy.wait()
    gather_own(2)
    gather_own(3)
    for k in range(4):
        gain_over(k).wait_recv()
    spread = jnp.zeros((8, width), f32)
    for i in range(shards):
        one_hot = (iota((BLOCK, width), 1) == iota((BLOCK, width), 0) + i * shard).astype(f32)
        spread = spread + contract(gains_all[i].astype(bf16), one_hot.astype(bf16), 1, 0)
    gain_rows[...] = spread

    def block_rows(b, size=BLOCK):
        if isinstance(b, int):
            return pl.ds(b * size, size)
        return pl.ds(pl.multiple_of(b * size, size), size)

    def inverse_rms(values):
        return lax.rsqrt(jnp.mean(values * values, axis=-1, keepdims=True) + epsilon)

    def norm_one(b, carry):
        at = block_rows(b)
        xs = x_ref[at, :].astype(f32)
        n1[at, :] = (xs * inverse_rms(xs) * gain_rows[0:1, :]).astype(bf16)
        return carry

    lax.fori_loop(0, rows // BLOCK, norm_one, 0)

    def weight(buffer, a):
        return buffer[:, a].reshape(width, buffer.shape[-1])

    own_rows = pl.ds(pl.multiple_of(t * head_width, DH), head_width)
    own_keys = pl.ds(pl.multiple_of(c * rows, rows), rows)
    normed = n1[...]
    kv_copies = [
        remote(ref.at[own_keys], ref.at[own_keys], kv_send.at[n], kv_recv.at[n], partner)
        for n, ref in enumerate((k_all, v_all))
    ]
    gather_corner(0)
    lax.fori_loop(key_blocks // 2, key_blocks * 3 // 4, bias_rows, 0)
    gather_finish(0)
    mixed_kv = contract(normed, wkv[...].reshape(width, 2 * head_width), 1, 0).astype(bf16)
    k_all[own_keys, :] = mixed_kv[:, 0:head_width]
    kv_copies[0].start()
    v_all[own_keys, :] = mixed_kv[:, head_width:]
    kv_copies[1].start()
    gather_corner(1)
    lax.fori_loop(key_blocks * 3 // 4, key_blocks, bias_rows, 0)
    n1t[...] = normed.T
    gather_pass(2)
    for k in range(1, 4):
        out_copies[k - 1].wait_recv()
        wo3[me, :, (k - 1) * head_width : k * head_width] = other_out[k - 1]
    gather_own(5)
    gather_own(4)
    gather_finish(1)
    q_t[...] = contract(normed, wqo[:, :, 0:head_width].reshape(width, head_width), 1, 0).astype(bf16).T
    for copy in kv_copies:
        copy.wait_recv()
    v_t[...] = v_all[...].T

    def head_only(values, h):
        head_of = iota(values.shape, 0)
        inside = jnp.logical_and(head_of >= h * DH, head_of < (h + 1) * DH)
        return jnp.where(inside, values, jnp.zeros_like(values))

    def attended_copy(source, b, slot, target):
        view = att_all.at[
            pl.ds(pl.multiple_of(source * head_width, DH), head_width), block_rows(b)
        ]
        return remote(view, view, at_send.at[slot, b], at_recv.at[source, b], (f, c, target))

    def attended_start(b):
        @pl.when(outer)
        def _():
            attended_copy(t, b, 0, near_end).start()

        @pl.when(inner)
        def _():
            attended_copy(t, b, 0, far_end).start()
            attended_copy(t, b, 1, middle).start()

    def attended_relay(b, part):
        @pl.when(inner)
        def _():
            source = (far_end, middle, 3 - far_end)[part]
            attended_copy(source, b, 2 + part, middle if part == 0 else far_end).wait_recv()
            attended_copy(source, b, 2 + part, middle if part == 0 else far_end).start()

    def attended_wait(b):
        @pl.when(outer)
        def _():
            for source in (near_end, 3 - near_end, 3 - t):
                attended_copy(source, b, 0, near_end).wait_recv()

    def attended_drain(b, carry):
        attended_copy(t, b, 0, near_end).wait_send()

        @pl.when(inner)
        def _():
            for slot in range(1, 5):
                attended_copy(t, b, slot, middle).wait_send()

        return carry

    def attend(qb):
        at = block_rows(qb, FORWARD_BLOCK)

        def per_head(h, carry):
            queries = head_only(q_t[:, at], h)
            top = jnp.full((8, FORWARD_BLOCK), -jnp.inf, f32)
            for kb in range(keys // BLOCK):
                span_k = slice(kb * BLOCK, (kb + 1) * BLOCK)
                block = contract(k_all[span_k, :], queries, 1, 0) + masked_bias[h, span_k, at]
                score[span_k, 0:FORWARD_BLOCK] = block
                top = jnp.maximum(top, jnp.max(block.reshape(BLOCK // 8, 8, FORWARD_BLOCK), axis=0))
            top = jnp.max(top, axis=0, keepdims=True)
            total = jnp.zeros((8, FORWARD_BLOCK), f32)
            for kb in range(keys // BLOCK):
                span_k = slice(kb * BLOCK, (kb + 1) * BLOCK)
                block = jnp.exp(score[span_k, 0:FORWARD_BLOCK] - top)
                expo[h, span_k, at] = block.astype(bf16)
                total = total + jnp.sum(block.reshape(BLOCK // 8, 8, FORWARD_BLOCK), axis=0)
            inverse = 1.0 / jnp.sum(total, axis=0, keepdims=True)
            linv[h, :, at] = jnp.broadcast_to(inverse, (8, FORWARD_BLOCK))
            head_rows = pl.ds(pl.multiple_of(h * DH, DH), DH)
            own_head = pl.ds(pl.multiple_of(t * head_width + h * DH, DH), DH)
            mixed = contract(v_t[head_rows, :], expo[h, :, at], 1, 0)
            att_all[own_head, at] = (mixed * inverse).astype(bf16)
            return carry

        lax.fori_loop(0, heads, per_head, 0)
        for n in range(FORWARD_BLOCK // BLOCK):
            attended_start(qb * (FORWARD_BLOCK // BLOCK) + n)

    blocks = rows // BLOCK
    scale = 0.7978845608028654
    forward_blocks = rows // FORWARD_BLOCK

    def attend_loop(qb, carry):
        attend(qb)

        @pl.when(qb == 0)
        def _():
            gather_pass(3)

        return carry

    lax.fori_loop(0, forward_blocks, attend_loop, 0)
    per_forward = FORWARD_BLOCK // BLOCK
    for b in range(per_forward):
        attended_relay(b, 0)
        attended_relay(b, 1)
    gather_corner(2)
    gather_pass(5)
    gather_pass(4)
    for b in range(per_forward):
        attended_relay(b, 2)
    gather_corner(3)
    wo_all[t] = wqo[:, :, head_width:].reshape(width, head_width)
    for first in range(per_forward, blocks, per_forward):
        for b in range(first, first + per_forward):
            attended_relay(b, 0)
            attended_relay(b, 1)
        for b in range(first, first + per_forward):
            attended_relay(b, 2)
    near[...] = jnp.zeros_like(near)
    dk[...] = jnp.zeros_like(dk)
    dv[...] = jnp.zeros_like(dv)
    small[...] = jnp.zeros_like(small)
    k_t[...] = k_all[...].T
    gather_corner(5)
    gather_corner(4)
    gather_finish(5)
    for k in range(1, 4):
        wo_all[t ^ k] = wo3[:, :, (k - 1) * head_width : k * head_width].reshape(width, head_width)
    for g in (2, 3, 4):
        gather_finish(g)

    def feed_forward(b, carry):
        attended_wait(b)
        at = block_rows(b)
        res = x_ref[at, :].astype(f32)
        for source in range(4):
            attended = att_all[source * head_width : (source + 1) * head_width, at].T
            res = res + contract(attended, wo_all[source], 1, 1)
        resid[at, :] = res
        normed = (res * inverse_rms(res) * gain_rows[1:2, :]).astype(bf16)
        n2[at, :] = normed
        gate = contract(normed, weight(wf, 0), 1, 0)
        up = contract(normed, weight(wf, 1), 1, 0)
        down = weight(wf, 2)
        grad_act = contract(cot_ref[at, :], down, 1, 0)
        square = gate * gate
        curve = jnp.tanh(scale * (gate + 0.044715 * square * gate))
        left = 0.5 * (1.0 + curve)
        value = gate * left
        slope = left + 0.5 * gate * (1.0 - curve * curve) * scale * (1.0 + 0.134145 * square)
        low_act = (value * up).astype(bf16)
        low_gate = (grad_act * up * slope).astype(bf16)
        low_up = (grad_act * value).astype(bf16)
        act[at, :] = low_act
        ggate[at, :] = low_gate
        gup[at, :] = low_up
        snd[0, at, :] = (
            contract(low_gate, weight(wf, 0), 1, 1) + contract(low_up, weight(wf, 1), 1, 1)
        ).astype(bf16)
        put_block(0, b)
        snd[1, at, :] = contract(low_act, down, 1, 1).astype(bf16)

        @pl.when(b > 0)
        def _():
            serve((b - 1) * per_block, per_block)

        return carry

    lax.fori_loop(0, blocks, feed_forward, 0)

    def put_outputs(b, carry):
        put_block(1, b)
        return carry

    lax.fori_loop(0, blocks, put_outputs, 0)
    turned[0] = n2[...].T
    turned[1] = cot_ref[...].T

    def sent(n, which):
        if n == 0:
            return gsf.at[:, which]
        return gsa.at[:, which, 3:4] if n == 1 else gsa.at[:, which, 0:3]

    def landed(n):
        return rf.at[...] if n == 0 else ra.at[:, 3:4] if n == 1 else ra.at[:, 0:3]

    def over_copy(n):
        return remote(sent(n, 1 - c), landed(n), rs_send.at[n], rs_recv.at[n], partner)

    def summed(n, index):
        return sf.at[index] if n == 0 else sa.at[index, 3:4] if n == 1 else sa.at[index, 0:3]

    def arrived(n, k):
        return rf2.at[k - 1] if n == 0 else ra2.at[k - 1, 3:4] if n == 1 else ra2.at[k - 1, 0:3]

    def out_copy(n, k):
        return remote(
            summed(n, f ^ k), arrived(n, k), rs2_send.at[n, k - 1], rs2_recv.at[n, k - 1],
            (f ^ k, c, t),
        )

    members_of = {0: (0, 1, 2), 1: (3,), 2: (0, 1, 2)}
    outputs = {0: (gg_hbm, gu_hbm, gd_hbm), 1: (go_hbm,), 2: (gk_hbm, gv_hbm, gq_hbm)}

    def part_stores(n):
        results = gf_ref if n == 0 else ga_ref
        offset = (0, 3, 4)[n]
        return [
            pltpu.make_async_copy(results.at[a], target, store_sem.at[offset + i])
            for i, (a, target) in enumerate(zip(members_of[n], outputs[n]))
        ]

    def reduce_send(n):
        over_copy(n).wait_recv()
        own, got, total = (gsf, rf, sf) if n == 0 else (gsa, ra, sa)

        def body(k, carry):
            index = jnp.bitwise_xor(f, groups - 1 - k)
            for a in members_of[n]:
                total[index, a] = (
                    own[index, c, a].astype(f32) + got[index, a].astype(f32)
                ).astype(bf16)
            return carry

        lax.fori_loop(0, groups, body, 0)
        for k in range(1, groups):
            out_copy(n, k).start()

    def reduce_finish(n):
        total, got = (sf, rf2) if n == 0 else (sa, ra2)
        for k in range(1, groups):
            out_copy(n, k).wait_recv()
        results = gf_ref if n == 0 else ga_ref
        for a in members_of[n]:
            value = total[f, a].astype(f32)
            for k in range(1, groups):
                value = value + got[k - 1, a].astype(f32)
            results[a] = value
        for copy in part_stores(n):
            copy.start()

    def reduce_drain(n):
        over_copy(n).wait_send()
        for k in range(1, groups):
            out_copy(n, k).wait_send()

    both = 2 * shard

    def store_grad(buffer, i, a, value):
        buffer[i, :, a] = value.astype(bf16).reshape(2, shard, value.shape[-1])

    def pair_rows(i):
        return block_rows(i, both)

    def feed_forward_weights(i):
        at = pair_rows(i)
        store_grad(gsf, i, 0, contract(turned[0, at, :], ggate[...], 1, 0))
        store_grad(gsf, i, 1, contract(turned[0, at, :], gup[...], 1, 0))
        store_grad(gsf, i, 2, contract(turned[1, at, :], act[...], 1, 0))

    def residual_back(b):
        totals_of(0, b)
        at = block_rows(b)
        grad_in = tot[0, at, :].astype(f32)
        res = resid[at, :]
        inverse = inverse_rms(res)
        u = res * inverse
        small[1:2, :] += jnp.sum(grad_in * u, axis=0, keepdims=True)
        g = grad_in * gain_rows[1:2, :]
        grad = cot_ref[at, :].astype(f32) + inverse * (
            g - u * jnp.mean(g * u, axis=-1, keepdims=True)
        )
        grad_res[at, :] = grad
        low_grad = grad.astype(bf16)
        grl[at, :] = low_grad
        grad_att = contract(low_grad, wo_all[t], 1, 0).astype(bf16)
        scaled = grad_att.T.astype(f32) * jnp.concatenate(
            [jnp.broadcast_to(linv[h, 0:1, at], (DH, BLOCK)) for h in range(heads)], axis=0
        )
        scaled = scaled.astype(bf16)
        dos_t[:, at] = scaled
        products = scaled.astype(f32) * att_all[own_rows, at].astype(f32)
        for h in range(heads):
            delta[h, :, at] = jnp.broadcast_to(
                jnp.sum(products[h * DH : (h + 1) * DH], axis=0, keepdims=True), (8, BLOCK)
            )

    extra = dk.shape[1] - head_width
    query_blocks = rows // BLOCK

    def attend_back(start, size, h):
        at = slice(start, start + size)
        first = start // BLOCK
        head_rows = pl.ds(pl.multiple_of(h * DH, DH), DH)
        if True:
            grads = head_only(dos_t[:, at], h)
            queries = head_only(q_t[:, at], h)
            flag = iota((extra, size), 0)
            lane = iota((extra, size), 1)
            flags = jnp.zeros((extra, size), f32)
            for j in range(size // BLOCK):
                hit = jnp.logical_and(
                    flag == h * query_blocks + first + j,
                    jnp.logical_and(lane >= j * BLOCK, lane < (j + 1) * BLOCK),
                )
                flags = jnp.where(hit, 1.0, flags)
            flagged = jnp.concatenate([queries, flags.astype(bf16)], axis=0)
            shift = delta[h, 0:1, at]
            for kb in range(keys // BLOCK):
                span_k = slice(kb * BLOCK, (kb + 1) * BLOCK)
                block = contract(v_all[span_k, :], grads, 1, 0)
                low_score[span_k, 0:size] = (
                    expo[h, span_k, at].astype(f32) * (block - shift)
                ).astype(bf16)
            dv[...] += contract(expo[h, :, at], grads, 1, 1)
            dk[...] += contract(low_score[:, 0:size], flagged, 1, 1)
            dq_t[head_rows, at] = contract(
                k_t[head_rows, :], low_score[:, 0:size], 1, 0
            ).astype(bf16)
            for j in range(size // BLOCK):
                home = c * query_blocks + first + j
                for d in (-1, 0, 1):
                    kb = home + d
                    valid = jnp.logical_and(kb >= 0, kb < keys // BLOCK)

                    @pl.when(valid)
                    def _():
                        where_k = jnp.clip(kb, 0, keys // BLOCK - 1)
                        near[h, d + 1] += low_score[
                            block_rows(where_k), j * BLOCK : (j + 1) * BLOCK
                        ].astype(f32)

    pace = per_block // 2
    step = (blocks - 1) * per_block
    for qb in range(rows // QUERY_BLOCK):
        for b in range(qb * QUERY_BLOCK // BLOCK, (qb + 1) * QUERY_BLOCK // BLOCK):
            need = max((b + 1) * per_block + LAG, step)
            serve(step, need - step)
            step = need
            residual_back(b)

        def back_head(h, carry, qb=qb, step=step):
            attend_back(qb * QUERY_BLOCK, QUERY_BLOCK, h)
            if qb == 0:
                feed_forward_weights(h)
            serve(h * pace + step, pace)
            return carry

        lax.fori_loop(0, heads, back_head, 0)
        step += heads * pace
        if qb == 0:
            for i in range(heads, groups):
                feed_forward_weights(i)
            over_copy(0).start()

    other_keys = pl.ds(pl.multiple_of((1 - c) * rows, rows), rows)
    dkv_send[0] = dk[other_keys, 0:head_width].astype(bf16)
    dkv_send[1] = dv[other_keys, :].astype(bf16)
    dkv_copy = remote(dkv_send.at[...], dkv_recv.at[...], dkv_ssem.at[0], dkv_rsem.at[0], partner)
    dkv_copy.start()
    reduce_send(0)
    dkv_copy.wait_recv()
    dkv[:, 0:head_width] = (dk[own_keys, 0:head_width] + dkv_recv[0].astype(f32)).astype(bf16)
    dkv[:, head_width:] = (dv[own_keys, :] + dkv_recv[1].astype(f32)).astype(bf16)

    def project_back(b, carry):
        at = block_rows(b)
        total = contract(
            dq_t[:, at].T, wqo[:, :, 0:head_width].reshape(width, head_width), 1, 1
        )
        total = total + contract(dkv[at, :], wkv[...].reshape(width, 2 * head_width), 1, 1)
        snd[2, at, :] = total.astype(bf16)
        put_block(2, b)

        @pl.when(step + (b + 1) * pace <= 2 * chunks)
        def _():
            serve(step + b * pace, pace)

        return carry

    lax.fori_loop(0, blocks, project_back, 0)
    step += min(blocks, (2 * chunks - step) // pace) * pace

    def weights_back(i, carry):
        part_rows = n1t[pair_rows(i), :]
        mixed = contract(part_rows, dkv[...], 1, 0)
        store_grad(gsa, i, 0, mixed[:, 0:head_width])
        store_grad(gsa, i, 1, mixed[:, head_width:])
        store_grad(gsa, i, 2, contract(part_rows, dq_t[...], 1, 1))
        return carry

    lax.fori_loop(0, groups, weights_back, 0)
    over_copy(2).start()
    serve(step, 2 * chunks - step)
    step = 2 * chunks
    turned[0] = grl[...].T

    def output_weights(i, carry):
        store_grad(gsa, i, 3, contract(turned[0, pair_rows(i), :], att_all[own_rows, :], 1, 1))
        return carry

    lax.fori_loop(0, groups, output_weights, 0)
    over_copy(1).start()
    reduce_send(2)
    reduce_send(1)

    def bucket_sums(h, carry):
        for b in range(2 * half):
            summed_block = jnp.zeros((8, BLOCK), f32)
            for d in (-1, 0) if b < half else (0, 1):
                bucket = bucket_of(d * BLOCK + row_of - column_of)
                chosen = jnp.where(bucket == b, near[h, d + 1], 0.0)
                summed_block = summed_block + jnp.sum(
                    chosen.reshape(BLOCK // 8, 8, BLOCK), axis=0
                )
            pick[b : b + 1, :] = jnp.sum(summed_block, axis=0, keepdims=True)
        sums = contract(jnp.ones((8, BLOCK), f32), pick[...], 1, 1, highest)
        small[:, 0 : 2 * half] += jnp.where(iota((8, 2 * half), 0) == 2 + h, sums, 0.0)
        return carry

    def far_sums():
        tail = dk.shape[1] - BLOCK
        first_lane = head_width - tail
        column_sums = dk[:, tail:]
        block_row = iota((keys, BLOCK), 0)
        lane = iota((keys, BLOCK), 1)
        left_sum = jnp.zeros((1, BLOCK), f32)
        right_sum = jnp.zeros((1, BLOCK), f32)
        for j in range(query_blocks):
            mine = jnp.zeros((keys, BLOCK), jnp.bool_)
            for h in range(heads):
                mine = jnp.logical_or(mine, lane == first_lane + h * query_blocks + j)
            home = c * query_blocks + j
            is_left = jnp.logical_and(mine, block_row < (home - 1) * BLOCK)
            is_right = jnp.logical_and(mine, block_row >= (home + 2) * BLOCK)
            left_sum += jnp.sum(jnp.where(is_left, column_sums, 0.0), axis=0, keepdims=True)
            right_sum += jnp.sum(jnp.where(is_right, column_sums, 0.0), axis=0, keepdims=True)
        from_lane, to_lane = iota((BLOCK, BLOCK), 0), iota((BLOCK, BLOCK), 1)
        for h in range(heads):
            start = first_lane + h * query_blocks
            inside = jnp.logical_and(from_lane >= start, from_lane < start + query_blocks)
            left_pick = jnp.logical_and(inside, to_lane == far).astype(f32)
            right_pick = jnp.logical_and(inside, to_lane == half + far).astype(f32)
            small[2 + h : 3 + h, 0:BLOCK] += (
                contract(jnp.broadcast_to(left_sum, (8, BLOCK)), left_pick, 1, 0, highest)
                + contract(jnp.broadcast_to(right_sum, (8, BLOCK)), right_pick, 1, 0, highest)
            )[0:1]

    def block_store(n, source, target, b):
        at = block_rows(b)
        return pltpu.make_async_copy(source.at[at], target.at[at], store_sem.at[n])

    def input_back(b):
        totals_of(2, b)
        at = block_rows(b)
        grad_in = tot[2, at, :].astype(f32)
        xs = x_ref[at, :].astype(f32)
        inverse = inverse_rms(xs)
        u = xs * inverse
        g = grad_in * gain_rows[0:1, :]
        gin_ref[at, :] = grad_res[at, :] + inverse * (
            g - u * jnp.mean(g * u, axis=-1, keepdims=True)
        )
        block_store(7 + b, gin_ref, gin_hbm, b).start()

    def layer_out(b):
        totals_of(1, b)
        at = block_rows(b)
        out_ref[at, :] = (resid[at, :] + tot[1, at, :].astype(f32)).astype(bf16)
        block_store(7 + blocks + b, out_ref, out_hbm, b).start()

    small_copies = [
        remote(
            small.at[...], small_all.at[me], sm_send.at[k * 2 + kc - 1], sm_recv.at[k * 2 + kc - 1],
            (f ^ k, c ^ kc, t),
        )
        for k in range(groups)
        for kc in range(2)
        if k or kc
    ]

    def small_start():
        for copy in small_copies:
            copy.start()
        small_all[me] = small[...]

    def small_finish():
        for copy in small_copies:
            copy.wait_recv()
        total_small = small_all[0]
        for i in range(1, shards):
            total_small = total_small + small_all[i]
        to_own = (iota((width, BLOCK), 0) == iota((width, BLOCK), 1) + me * shard).astype(f32)
        own_gains = contract(total_small, to_own, 1, 0, highest)
        gain_two_out_ref[...] = own_gains[1:2, 0:shard]
        bias_out_ref[...] = total_small[2 : 2 + heads, 0 : 2 * half]

    gain_copies = [
        remote(
            gain_part.at[t], gain_part.at[t], gp_send.at[kt - 1], gp_recv.at[kt - 1], (f, c, t ^ kt)
        )
        for kt in range(1, 4)
    ]

    def gain_start():
        products = jnp.zeros((shard, head_width), f32)
        for a in members_of[2]:
            products = products + staged[a].astype(f32) * ga_ref[a]
        row_sums = contract(jnp.ones((8, head_width), f32), products, 1, 1, highest)
        gain_part[t, :, 0:shard] = row_sums / gain_one_ref[...].astype(f32)
        for copy in gain_copies:
            copy.start()

    def gain_finish():
        for copy in gain_copies:
            copy.wait_recv()
        total = gain_part[0, 0:1, 0:shard]
        for i in range(1, 4):
            total = total + gain_part[i, 0:1, 0:shard]
        gain_one_out_ref[...] = total

    lax.fori_loop(0, heads, bucket_sums, 0)
    far_sums()
    small_start()
    reduce_finish(0)
    serve(step, LAG)

    def last_rows(b, carry):
        serve(2 * chunks + b * per_block + LAG, per_block)

        @pl.when(b == LATE_BLOCK)
        def _():
            small_finish()
            reduce_finish(1)

        @pl.when(b == LATE_BLOCK + 1)
        def _():
            reduce_finish(2)
            gain_start()

        @pl.when(b == blocks - 1)
        def _():
            gain_finish()

        layer_out(b)
        input_back(b)
        return carry

    lax.fori_loop(0, blocks, last_rows, 0)

    for b in range(blocks):
        block_store(7 + b, gin_ref, gin_hbm, b).wait()
        block_store(7 + blocks + b, out_ref, out_hbm, b).wait()
    for n in range(3):
        for copy in part_stores(n):
            copy.wait()
    for copy in small_copies + gain_copies:
        copy.wait_send()
    for g in range(6):
        gather_drain(g)
    for copy in out_copies:
        copy.wait_send()
    lax.fori_loop(0, blocks, attended_drain, 0)
    for k in range(1, 4):
        gain_copy(k).wait_send()
    for k in range(4):
        gain_over(k).wait_send()
    for copy in kv_copies:
        copy.wait_send()
    dkv_copy.wait_send()
    drain_all()
    for n in range(3):
        reduce_drain(n)


def fused_layer(shards, x, cot, ids, gain_one, gain_two, weights, table):
    rows, width = x.shape
    shard, head_width = weights[0].shape
    units = weights[4].shape[1]
    keys = ids.shape[1]
    heads = head_width // DH
    groups = shards // 2
    chunks = rows // CHUNK
    padded = head_width + (-head_width) % BLOCK
    if padded - head_width < heads * (rows // BLOCK):
        padded += BLOCK
    vmem, dma = pltpu.VMEM, pltpu.SemaphoreType.DMA
    out_shape = (
        jax.ShapeDtypeStruct((rows, width), bf16),
        jax.ShapeDtypeStruct((rows, width), f32),
        *[jax.ShapeDtypeStruct((shard, head_width), f32)] * 4,
        *[jax.ShapeDtypeStruct((shard, units), f32)] * 3,
        jax.ShapeDtypeStruct((1, shard), f32),
        jax.ShapeDtypeStruct((1, shard), f32),
        jax.ShapeDtypeStruct(table.shape, f32),
    )
    in_vmem = pl.BlockSpec(memory_space=pltpu.VMEM)
    anywhere = pl.BlockSpec(memory_space=pl.ANY)
    scratch = [
        vmem((rows, width), bf16),
        vmem((rows, width), bf16),
        vmem((rows, width), bf16),
        vmem((rows, width), f32),
        vmem((4, shard, head_width), f32),
        vmem((3, shard, units), f32),
        vmem((4, shard, head_width), bf16),
        vmem((shards, shard, 2 * head_width), bf16),
        vmem((shards, shard, 2 * head_width), bf16),
        vmem((shards, shard, 3 * head_width), bf16),
        vmem((3, shard, head_width), bf16),
        vmem((4, width, head_width), bf16),
        vmem((shards, 3, shard, units), bf16),
        vmem((shards, 8, BLOCK), f32),
        vmem((8, width), f32),
        vmem((heads, 5, BLOCK, BLOCK), f32),
        vmem((heads, keys, rows), f32),
        vmem((keys, QUERY_BLOCK), f32),
        vmem((heads, keys, rows), bf16),
        vmem((keys, QUERY_BLOCK), bf16),
        vmem((3, rows, width), bf16),
        vmem((3, rows, width), bf16),
        vmem((3, rows, width), bf16),
        vmem((rows, width), f32),
        vmem((rows, width), f32),
        vmem((rows, width), bf16),
        vmem((rows, width), bf16),
        vmem((rows, width), bf16),
        vmem((width, rows), bf16),
        vmem((2, width, rows), bf16),
        vmem((rows, units), bf16),
        vmem((rows, units), bf16),
        vmem((rows, units), bf16),
        vmem((head_width, rows), bf16),
        vmem((keys, head_width), bf16),
        vmem((keys, head_width), bf16),
        vmem((head_width, keys), bf16),
        vmem((head_width, keys), bf16),
        vmem((4 * head_width, rows), bf16),
        vmem((head_width, rows), bf16),
        vmem((head_width, rows), bf16),
        vmem((heads, 8, rows), f32),
        vmem((heads, 8, rows), f32),
        vmem((keys, padded), f32),
        vmem((keys, head_width), f32),
        vmem((heads, 3, BLOCK, BLOCK), f32),
        vmem((table.shape[1], BLOCK), f32),
        vmem((2, rows, head_width), bf16),
        vmem((2, rows, head_width), bf16),
        vmem((rows, 2 * head_width), bf16),
        vmem((groups, 2, 4, shard, head_width), bf16),
        vmem((groups, 2, 3, shard, units), bf16),
        vmem((groups, 4, shard, head_width), bf16),
        vmem((groups, 3, shard, units), bf16),
        vmem((groups, 4, shard, head_width), bf16),
        vmem((groups, 3, shard, units), bf16),
        vmem((groups - 1, 4, shard, head_width), bf16),
        vmem((groups - 1, 3, shard, units), bf16),
        vmem((8, width), f32),
        vmem((shards, 8, width), f32),
        vmem((4, 8, BLOCK), f32),
        dma((9,)),
        dma((7 + 2 * (rows // BLOCK),)),
        dma((7, 8)),
        dma((7, 8)),
        dma((3,)),
        dma((3,)),
        dma((5, rows // BLOCK)),
        dma((4, rows // BLOCK)),
        dma((2,)),
        dma((2,)),
        dma((3, chunks)),
        dma((3, chunks)),
        dma((3, chunks)),
        dma((3, chunks)),
        dma((1,)),
        dma((1,)),
        dma((3,)),
        dma((3,)),
        dma((3, groups)),
        dma((3, groups)),
        dma((shards,)),
        dma((shards,)),
        dma((3,)),
        dma((3,)),
    ]
    return pl.pallas_call(
        functools.partial(layer_kernel, shards),
        out_shape=out_shape,
        in_specs=[anywhere] * 2
        + [in_vmem] * 3
        + [anywhere] * 7
        + [pl.BlockSpec(memory_space=pltpu.SMEM)],
        out_specs=[anywhere] * 9 + [in_vmem] * 3,
        scratch_shapes=scratch,
        name="layer",
        compiler_params=pltpu.CompilerParams(
            collective_id=0, has_side_effects=True, vmem_limit_bytes=63 << 20
        ),
    )(x, cot, ids, gain_one, gain_two, *weights, table)


def publish_kernel(count, *refs):
    sources, targets = refs[:count], refs[count : 2 * count]
    held, in_sem, out_sem = refs[2 * count : 3 * count], refs[3 * count], refs[3 * count + 1]
    inward = [
        pltpu.make_async_copy(sources[i], held[i], in_sem.at[i]) for i in range(count)
    ]
    outward = [
        pltpu.make_async_copy(held[i], targets[i], out_sem.at[i]) for i in range(count)
    ]
    for copy in inward:
        copy.start()
    for arriving, leaving in zip(inward, outward):
        arriving.wait()
        leaving.start()
    for copy in outward:
        copy.wait()


def publish(values):
    count = len(values)
    anywhere = pl.BlockSpec(memory_space=pl.ANY)
    return pl.pallas_call(
        functools.partial(publish_kernel, count),
        out_shape=[jax.ShapeDtypeStruct(value.shape, value.dtype) for value in values],
        in_specs=[anywhere] * count,
        out_specs=[anywhere] * count,
        scratch_shapes=[pltpu.VMEM(value.shape, value.dtype) for value in values]
        + [pltpu.SemaphoreType.DMA((count,))] * 2,
        name="publish",
    )(*values)


def on_device_fused(
    layer_input,
    doc_ids,
    query_weight,
    key_weight,
    value_weight,
    output_weight,
    gate_weight,
    up_weight,
    down_weight,
    first_gain,
    second_gain,
    position_bias,
    cotangent,
):
    shards = lax.axis_size("fsdp") * lax.axis_size("ctx")
    outs = fused_layer(
        shards,
        layer_input[0],
        cotangent[0],
        doc_ids,
        first_gain[None],
        second_gain[None],
        (
            query_weight,
            key_weight,
            value_weight,
            output_weight,
            gate_weight,
            up_weight,
            down_weight,
        ),
        position_bias.T,
    )
    outs = publish(outs)
    return (
        outs[0][None],
        outs[1][None],
        *outs[2:9],
        outs[9][0],
        outs[10][0],
        outs[11].T,
    )


def fits_kernel(mesh):
    return mesh.shape["ctx"] == 2 and mesh.shape["tp"] == 4 and mesh.shape["fsdp"] == 4


def solution(mesh):
    return jax.shard_map(
        on_device_fused if fits_kernel(mesh) else on_device,
        mesh=mesh,
        in_specs=(
            P("fsdp", "ctx", None),
            P("fsdp", None),
            P(("fsdp", "ctx"), "tp"),
            P(("fsdp", "ctx"), "tp"),
            P(("fsdp", "ctx"), "tp"),
            P(("fsdp", "ctx"), "tp"),
            P(("fsdp", "ctx"), "tp"),
            P(("fsdp", "ctx"), "tp"),
            P(("fsdp", "ctx"), "tp"),
            P(("fsdp", "ctx")),
            P(("fsdp", "ctx")),
            P(None, "tp"),
            P("fsdp", "ctx", None),
        ),
        out_specs=(
            P("fsdp", "ctx", None),
            P("fsdp", "ctx", None),
            P(("fsdp", "ctx"), "tp"),
            P(("fsdp", "ctx"), "tp"),
            P(("fsdp", "ctx"), "tp"),
            P(("fsdp", "ctx"), "tp"),
            P(("fsdp", "ctx"), "tp"),
            P(("fsdp", "ctx"), "tp"),
            P(("fsdp", "ctx"), "tp"),
            P(("fsdp", "ctx")),
            P(("fsdp", "ctx")),
            P(None, "tp"),
        ),
        check_vma=False,
    )
```

```python
import functools

import jax
import jax.numpy as jnp
from jax import lax
from jax.experimental import pallas as pl
from jax.experimental.pallas import tpu as pltpu
from jax.sharding import PartitionSpec as P

DH = 64


epsilon = 1e-06
masked_score = -1000000000.0
bucket_edges = (12, 16, 23, 32, 46, 64, 91)
highest = lax.Precision.HIGHEST


def bucket_of(relative):
    distance = jnp.abs(relative)
    beyond = jnp.zeros_like(distance) + 8
    for edge_value in bucket_edges:
        beyond = beyond + (distance >= edge_value).astype(jnp.int32)
    inside = jnp.where(distance < 8, distance, beyond)
    return jnp.where(relative > 0, 16, 0) + inside


def rms_norm(values, gain_vector):
    inverse = lax.rsqrt(jnp.mean(values * values, axis=-1, keepdims=True) + epsilon)
    return values * inverse * gain_vector


def gated_unit(gate_in, up_in):
    return jax.nn.gelu(gate_in, approximate=True) * up_in


def relative_bias(bias_table, query_rows, key_rows, offset):
    span_width = key_rows + query_rows
    relative = lax.iota(jnp.int32, span_width) - (query_rows - 1) - offset
    one_hot = (
        bucket_of(relative)[:, None] == lax.iota(jnp.int32, bias_table.shape[0])[None, :]
    ).astype(jnp.float32)
    per_shift = jnp.dot(one_hot, bias_table, precision=highest).T
    heads_here = bias_table.shape[1]
    toeplitz = jnp.broadcast_to(per_shift[:, None, :], (heads_here, query_rows, span_width))
    toeplitz = toeplitz.reshape(heads_here, query_rows * span_width)[
        :, : query_rows * (span_width - 1)
    ]
    toeplitz = toeplitz.reshape(heads_here, query_rows, span_width - 1)
    return (toeplitz[:, :, query_rows - 1 : query_rows - 1 + key_rows], one_hot)


def diagonal_sums(grad_scores, query_rows, key_rows):
    heads_here = grad_scores.shape[0]
    span_width = key_rows + query_rows
    placed = jnp.pad(grad_scores, ((0, 0), (0, 0), (query_rows - 1, 0)))
    placed = placed.reshape(heads_here, query_rows * (span_width - 1))
    placed = jnp.pad(placed, ((0, 0), (0, query_rows)))
    return jnp.sum(placed.reshape(heads_here, query_rows, span_width), axis=1)


def on_device(
    layer_input,
    doc_ids,
    query_weight,
    key_weight,
    value_weight,
    output_weight,
    gate_weight,
    up_weight,
    down_weight,
    first_gain,
    second_gain,
    position_bias,
    cotangent,
):
    query_rows = layer_input.shape[1]
    key_rows = query_rows * lax.axis_size("ctx")
    heads_here = position_bias.shape[1]
    head_width = heads_here * DH
    offset = lax.axis_index("ctx") * query_rows
    everything = (
        query_weight,
        key_weight,
        value_weight,
        output_weight,
        gate_weight,
        up_weight,
        down_weight,
        first_gain,
        second_gain,
    )
    (
        full_query,
        full_key,
        full_value,
        full_output,
        full_gate,
        full_up,
        full_down,
        gain_one,
        gain_two,
    ) = (
        lax.all_gather(everything[0], ("fsdp", "ctx"), axis=0, tiled=True),
        lax.all_gather(everything[1], ("fsdp", "ctx"), axis=0, tiled=True),
        lax.all_gather(everything[2], ("fsdp", "ctx"), axis=0, tiled=True),
        lax.all_gather(everything[3], ("fsdp", "ctx"), axis=0, tiled=True),
        lax.all_gather(everything[4], ("fsdp", "ctx"), axis=0, tiled=True),
        lax.all_gather(everything[5], ("fsdp", "ctx"), axis=0, tiled=True),
        lax.all_gather(everything[6], ("fsdp", "ctx"), axis=0, tiled=True),
        lax.all_gather(everything[7], ("fsdp", "ctx"), axis=0, tiled=True),
        lax.all_gather(everything[8], ("fsdp", "ctx"), axis=0, tiled=True),
    )
    inputs = layer_input.astype(jnp.float32)
    gain_first = gain_one.astype(jnp.float32)
    gain_second = gain_two.astype(jnp.float32)
    normed_one = rms_norm(inputs, gain_first).astype(jnp.bfloat16)
    queries = jnp.dot(normed_one, full_query, preferred_element_type=jnp.float32).astype(
        jnp.bfloat16
    )
    keys_local = jnp.dot(normed_one, full_key, preferred_element_type=jnp.float32).astype(
        jnp.bfloat16
    )
    values_local = jnp.dot(normed_one, full_value, preferred_element_type=jnp.float32).astype(
        jnp.bfloat16
    )
    keys_all, values_all = (
        lax.all_gather(keys_local, "ctx", axis=1, tiled=True),
        lax.all_gather(values_local, "ctx", axis=1, tiled=True),
    )
    bias_block, one_hot = relative_bias(position_bias, query_rows, key_rows, offset)

    def scores_of(query_heads, key_heads, id_row):
        raw_scores = jnp.einsum(
            "qhd,khd->hqk", query_heads, key_heads, preferred_element_type=jnp.float32
        )
        own_ids = lax.dynamic_slice_in_dim(id_row, offset, query_rows)
        same_doc = own_ids[:, None] == id_row[None, :]
        return jnp.where(same_doc[None], raw_scores + bias_block, masked_score)

    def forward_one(packed):
        query_seq, key_seq, value_seq, id_row = packed
        scores = scores_of(
            query_seq.reshape(query_rows, heads_here, DH),
            key_seq.reshape(key_rows, heads_here, DH),
            id_row,
        )
        row_max = jnp.max(scores, axis=-1, keepdims=True)
        exponentials = jnp.exp(scores - row_max)
        row_total = jnp.sum(exponentials, axis=-1, keepdims=True)
        probabilities = (exponentials / row_total).astype(jnp.bfloat16)
        attended = jnp.einsum(
            "hqk,khd->qhd",
            probabilities,
            value_seq.reshape(key_rows, heads_here, DH),
            preferred_element_type=jnp.float32,
        )
        log_row = row_max[..., 0] + jnp.log(row_total[..., 0])
        return (attended.reshape(query_rows, head_width).astype(jnp.bfloat16), log_row)

    attended, log_sums = lax.map(forward_one, (queries, keys_all, values_all, doc_ids))
    attention_terms = jnp.einsum(
        "sqe,de->sqd", attended, full_output, preferred_element_type=jnp.float32
    )
    residual = inputs + lax.psum(attention_terms.astype(jnp.bfloat16), "tp").astype(jnp.float32)
    normed_two = rms_norm(residual, gain_second).astype(jnp.bfloat16)
    gate_pre = jnp.dot(normed_two, full_gate, preferred_element_type=jnp.float32)
    up_pre = jnp.dot(normed_two, full_up, preferred_element_type=jnp.float32)
    activated = gated_unit(gate_pre, up_pre).astype(jnp.bfloat16)
    ffn_terms = jnp.einsum("sqf,df->sqd", activated, full_down, preferred_element_type=jnp.float32)
    output_rows = (
        residual + lax.psum(ffn_terms.astype(jnp.bfloat16), "tp").astype(jnp.float32)
    ).astype(jnp.bfloat16)
    grad_activated = jnp.einsum(
        "sqd,df->sqf", cotangent, full_down, preferred_element_type=jnp.float32
    )
    down_grad = jnp.einsum("sqd,sqf->df", cotangent, activated, preferred_element_type=jnp.float32)
    gated_value, gated_back = jax.vjp(gated_unit, gate_pre, up_pre)
    grad_gate, grad_up = gated_back(grad_activated)
    grad_gate = grad_gate.astype(jnp.bfloat16)
    grad_up = grad_up.astype(jnp.bfloat16)
    gate_grad = jnp.einsum("sqd,sqf->df", normed_two, grad_gate, preferred_element_type=jnp.float32)
    up_grad = jnp.einsum("sqd,sqf->df", normed_two, grad_up, preferred_element_type=jnp.float32)
    normed_two_terms = jnp.einsum(
        "sqf,df->sqd", grad_gate, full_gate, preferred_element_type=jnp.float32
    ) + jnp.einsum("sqf,df->sqd", grad_up, full_up, preferred_element_type=jnp.float32)
    grad_normed_two = lax.psum(normed_two_terms.astype(jnp.bfloat16), "tp").astype(jnp.float32)
    second_value, second_back = jax.vjp(rms_norm, residual, gain_second)
    grad_residual, second_gain_grad = second_back(grad_normed_two)
    grad_residual = grad_residual + cotangent.astype(jnp.float32)
    grad_low = grad_residual.astype(jnp.bfloat16)
    grad_attended = jnp.einsum(
        "sqd,de->sqe", grad_low, full_output, preferred_element_type=jnp.float32
    ).astype(jnp.bfloat16)
    output_grad = jnp.einsum("sqd,sqe->de", grad_low, attended, preferred_element_type=jnp.float32)

    def backward_one(running, packed):
        query_seq, key_seq, value_seq, id_row, grad_seq, log_row = packed
        query_heads = query_seq.reshape(query_rows, heads_here, DH)
        key_heads = key_seq.reshape(key_rows, heads_here, DH)
        value_heads = value_seq.reshape(key_rows, heads_here, DH)
        grad_heads = grad_seq.reshape(query_rows, heads_here, DH)
        scores = scores_of(query_heads, key_heads, id_row)
        probabilities = jnp.exp(scores - log_row[..., None])
        grad_probs = jnp.einsum(
            "qhd,khd->hqk", grad_heads, value_heads, preferred_element_type=jnp.float32
        )
        grad_values = jnp.einsum(
            "hqk,qhd->khd",
            probabilities.astype(jnp.bfloat16),
            grad_heads,
            preferred_element_type=jnp.float32,
        )
        grad_scores = probabilities * (
            grad_probs - jnp.sum(probabilities * grad_probs, axis=-1, keepdims=True)
        )
        low_scores = grad_scores.astype(jnp.bfloat16)
        grad_queries = jnp.einsum(
            "hqk,khd->qhd", low_scores, key_heads, preferred_element_type=jnp.float32
        )
        grad_keys = jnp.einsum(
            "hqk,qhd->khd", low_scores, query_heads, preferred_element_type=jnp.float32
        )
        running = running + diagonal_sums(grad_scores, query_rows, key_rows)
        return (
            running,
            (
                grad_queries.reshape(query_rows, head_width).astype(jnp.bfloat16),
                grad_keys.reshape(key_rows, head_width),
                grad_values.reshape(key_rows, head_width),
            ),
        )

    shift_grads, (grad_queries, key_parts, value_parts) = lax.scan(
        backward_one,
        jnp.zeros((heads_here, query_rows + key_rows), jnp.float32),
        (queries, keys_all, values_all, doc_ids, grad_attended, log_sums),
    )
    grad_keys, grad_values = (
        lax.psum_scatter(
            key_parts.astype(jnp.bfloat16), "ctx", scatter_dimension=1, tiled=True
        ).astype(jnp.float32),
        lax.psum_scatter(
            value_parts.astype(jnp.bfloat16), "ctx", scatter_dimension=1, tiled=True
        ).astype(jnp.float32),
    )
    grad_keys = grad_keys.astype(jnp.bfloat16)
    grad_values = grad_values.astype(jnp.bfloat16)
    normed_one_terms = (
        jnp.einsum("sqe,de->sqd", grad_queries, full_query, preferred_element_type=jnp.float32)
        + jnp.einsum("sqe,de->sqd", grad_keys, full_key, preferred_element_type=jnp.float32)
        + jnp.einsum("sqe,de->sqd", grad_values, full_value, preferred_element_type=jnp.float32)
    )
    grad_normed_one = lax.psum(normed_one_terms.astype(jnp.bfloat16), "tp").astype(jnp.float32)
    query_grad = jnp.einsum(
        "sqd,sqe->de", normed_one, grad_queries, preferred_element_type=jnp.float32
    )
    key_grad = jnp.einsum("sqd,sqe->de", normed_one, grad_keys, preferred_element_type=jnp.float32)
    value_grad = jnp.einsum(
        "sqd,sqe->de", normed_one, grad_values, preferred_element_type=jnp.float32
    )
    first_value, first_back = jax.vjp(rms_norm, inputs, gain_first)
    grad_inputs, first_gain_grad = first_back(grad_normed_one)
    input_rows = grad_residual + grad_inputs
    bias_gradient = lax.psum(jnp.dot(one_hot.T, shift_grads.T, precision=highest), ("fsdp", "ctx"))
    (
        query_total,
        key_total,
        value_total,
        output_total,
        gate_total,
        up_total,
        down_total,
        first_total,
        second_total,
    ) = (
        lax.psum_scatter(query_grad, ("fsdp", "ctx"), scatter_dimension=0, tiled=True),
        lax.psum_scatter(key_grad, ("fsdp", "ctx"), scatter_dimension=0, tiled=True),
        lax.psum_scatter(value_grad, ("fsdp", "ctx"), scatter_dimension=0, tiled=True),
        lax.psum_scatter(output_grad, ("fsdp", "ctx"), scatter_dimension=0, tiled=True),
        lax.psum_scatter(gate_grad, ("fsdp", "ctx"), scatter_dimension=0, tiled=True),
        lax.psum_scatter(up_grad, ("fsdp", "ctx"), scatter_dimension=0, tiled=True),
        lax.psum_scatter(down_grad, ("fsdp", "ctx"), scatter_dimension=0, tiled=True),
        lax.psum_scatter(first_gain_grad, ("fsdp", "ctx"), scatter_dimension=0, tiled=True),
        lax.psum_scatter(second_gain_grad, ("fsdp", "ctx"), scatter_dimension=0, tiled=True),
    )
    return (
        output_rows,
        input_rows,
        query_total,
        key_total,
        value_total,
        output_total,
        gate_total,
        up_total,
        down_total,
        first_total,
        second_total,
        bias_gradient,
    )


MESH = pl.DeviceIdType.MESH
bf16, f32 = jnp.bfloat16, jnp.float32
BLOCK = 128
QUERY_BLOCK = 256
FORWARD_BLOCK = 256
CHUNK = 32
LAG = 4
RELAY_ROWS = 32
EARLY = 4
PACES = (1, 1, 1)


def contract(left, right, left_dim, right_dim, precision=None):
    return lax.dot_general(
        left,
        right,
        (((left_dim,), (right_dim,)), ((), ())),
        preferred_element_type=f32,
        precision=precision,
    )


def iota(shape, dim):
    return lax.broadcasted_iota(jnp.int32, shape, dim)


def layer_kernel(
    shards,
    x_hbm,
    cot_hbm,
    ids_ref,
    gain_one_ref,
    gain_two_ref,
    wq_ref,
    wk_ref,
    wv_ref,
    wo_ref,
    wg_ref,
    wu_ref,
    wd_ref,
    table_ref,
    out_hbm,
    gin_hbm,
    gq_hbm,
    gk_hbm,
    gv_hbm,
    go_hbm,
    gg_hbm,
    gu_hbm,
    gd_hbm,
    gain_one_out_ref,
    gain_two_out_ref,
    bias_out_ref,
    x_ref,
    cot_ref,
    out_ref,
    gin_ref,
    ga_ref,
    gf_ref,
    staged,
    wkv,
    wqo,
    wo3,
    other_out,
    wo_all,
    wf,
    gains_all,
    gain_rows,
    tiles,
    masked_bias,
    score,
    expo,
    low_score,
    snd,
    part,
    tot,
    resid,
    grad_res,
    n1,
    n2,
    grl,
    n1t,
    turned,
    act,
    ggate,
    gup,
    q_t,
    k_all,
    v_all,
    k_t,
    v_t,
    att_all,
    dos_t,
    dq_t,
    linv,
    delta,
    dk,
    dv,
    near,
    pick,
    dkv_send,
    dkv_recv,
    dkv,
    gsa,
    gsf,
    ra,
    rf,
    sa,
    sf,
    ra2,
    rf2,
    small,
    small_all,
    gain_part,
    load_sem,
    store_sem,
    ag_send,
    ag_recv,
    zo_send,
    zo_recv,
    at_send,
    at_recv,
    kv_send,
    kv_recv,
    s1,
    r1,
    s2,
    r2,
    dkv_ssem,
    dkv_rsem,
    rs_send,
    rs_recv,
    rs2_send,
    rs2_recv,
    sm_send,
    sm_recv,
    gp_send,
    gp_recv,
):
    groups = shards // 2
    f, c, t = lax.axis_index("fsdp"), lax.axis_index("ctx"), lax.axis_index("tp")
    me = f * 2 + c
    rows, width = x_ref.shape
    keys = k_all.shape[0]
    head_width = wq_ref.shape[1]
    heads = head_width // DH
    units = wg_ref.shape[1]
    shard = wq_ref.shape[0]
    chunks = rows // CHUNK
    per_block = BLOCK // CHUNK
    partner = (f, 1 - c, t)
    outer = jnp.logical_or(t == 0, t == 3)
    inner = jnp.logical_or(t == 1, t == 2)
    near_end = jnp.where(t < 2, 1, 2)
    far_end = jnp.where(t < 2, 0, 3)
    middle = 3 - t

    def remote(source, target, send_sem, recv_sem, device):
        return pltpu.make_async_remote_copy(
            src_ref=source,
            dst_ref=target,
            send_sem=send_sem,
            recv_sem=recv_sem,
            device_id=device,
            device_id_type=MESH,
        )

    barrier = pltpu.get_barrier_semaphore()
    for k in range(groups):
        for kc in range(2):
            if k or kc:
                pl.semaphore_signal(
                    barrier, inc=1, device_id=(f ^ k, c ^ kc, t), device_id_type=MESH
                )

    for kt in range(1, 4):
        pl.semaphore_signal(
            barrier, inc=1, device_id=(f, c, t ^ kt), device_id_type=MESH
        )
    loads = [
        pltpu.make_async_copy(source, target, load_sem.at[n])
        for n, (source, target) in enumerate(
            (
                (wk_ref, staged.at[0]),
                (wv_ref, staged.at[1]),
                (wq_ref, staged.at[2]),
                (wo_ref, staged.at[3]),
                (x_hbm, x_ref),
                (wg_ref, wf.at[me, 0]),
                (wu_ref, wf.at[me, 1]),
                (wd_ref, wf.at[me, 2]),
                (cot_hbm, cot_ref),
            )
        )
    ]
    for copy in loads:
        copy.start()
    gains_all[me] = jnp.zeros((8, BLOCK), f32)
    gains_all[me, 0:1, 0:shard] = gain_one_ref[...].astype(f32)
    gains_all[me, 1:2, 0:shard] = gain_two_ref[...].astype(f32)
    for copy in loads[:4]:
        copy.wait()
    wkv[me, :, 0:head_width] = staged[0]
    wkv[me, :, head_width:] = staged[1]
    wqo[me, :, 0:head_width] = staged[2]
    wqo[me, :, head_width:] = staged[3]
    pl.semaphore_wait(barrier, shards - 1 + 3)

    def piece(g, index):
        if g < 2:
            return (wkv, wqo)[g].at[index]
        return wo3.at[index] if g == 5 else wf.at[index, g - 2]

    def half_piece(g, index, n):
        return piece(g, index).at[n * (shard // 2) : (n + 1) * (shard // 2)]

    def own_copy(g, k):
        view = piece(g, me)
        return remote(view, view, ag_send.at[g, k - 1], ag_recv.at[g, k - 1], (f ^ k, c, t))

    def pass_copy(g, k):
        view = half_piece(g, (f ^ k) * 2 + c, k - 1)
        return remote(view, view, ag_send.at[g, k + 1], ag_recv.at[g, k + 1], (f ^ (3 - k), c, t))

    def over_piece(g, k):
        view = piece(g, (f ^ k) * 2 + c)
        return remote(view, view, ag_send.at[g, 4 + k], ag_recv.at[g, 4 + k], partner)

    def gather_own(g):
        for k in (1, 2):
            own_copy(g, k).start()
        over_piece(g, 0).start()

    def gather_pass(g):
        for k in (1, 2):
            own_copy(g, k).wait_recv()
            pass_copy(g, k).start()
            over_piece(g, k).start()

    def gather_corner(g):
        for k in (1, 2):
            pass_copy(g, k).wait_recv()
        over_piece(g, 3).start()

    def gather_finish(g):
        for k in range(4):
            over_piece(g, k).wait_recv()

    def gather_drain(g):
        for k in (1, 2):
            own_copy(g, k).wait_send()
            pass_copy(g, k).wait_send()
        for k in range(4):
            over_piece(g, k).wait_send()

    def gain_copy(k):
        view = gains_all.at[me]
        return remote(view, view, ag_send.at[6, k], ag_recv.at[6, k], (f ^ k, c, t))

    def gain_over(k):
        view = gains_all.at[(f ^ k) * 2 + c]
        return remote(view, view, ag_send.at[6, 4 + k], ag_recv.at[6, 4 + k], partner)

    def span(j):
        if isinstance(j, int):
            return pl.ds(j * CHUNK, CHUNK)
        return pl.ds(pl.multiple_of(j * CHUNK, CHUNK), CHUNK)

    def end_copy(a, j):
        return remote(
            snd.at[a, span(j)], part.at[a, span(j)], s1.at[a, j], r1.at[a, j], (f, c, near_end)
        )

    def mid_copy(a, j):
        return remote(
            snd.at[a, span(j)], tot.at[a, span(j)], s1.at[a, j], r2.at[a, j], (f, c, middle)
        )

    def total_copy(a, j):
        return remote(
            tot.at[a, span(j)], tot.at[a, span(j)], s2.at[a, j], r2.at[a, j], (f, c, far_end)
        )

    def add_rows(target, a, j, left, right):
        def body(r, carry):
            at = pl.ds(pl.multiple_of(j * CHUNK + r * RELAY_ROWS, RELAY_ROWS), RELAY_ROWS)
            target[a, at] = (left[a, at].astype(f32) + right[a, at].astype(f32)).astype(bf16)
            return carry

        lax.fori_loop(0, CHUNK // RELAY_ROWS, body, 0)

    def flush(first, last):
        @pl.when(inner)
        def _():
            for n in range(first, last):
                a, j = divmod(n, chunks)
                mid_copy(a, j).wait_recv()
                add_rows(tot, a, j, snd, tot)
                total_copy(a, j).start()

    def service(step):
        def total_step():
            a, j = split(step - LAG)
            mid_copy(a, j).wait_recv()
            add_rows(tot, a, j, snd, tot)
            total_copy(a, j).start()

        def middle_step():
            a, j = split(step)
            end_copy(a, j).wait_recv()
            add_rows(snd, a, j, snd, part)
            mid_copy(a, j).start()

        def split(n):
            if isinstance(n, int):
                return divmod(n, chunks)
            return lax.div(n, chunks), lax.rem(n, chunks)

        if isinstance(step, int):
            if step >= LAG and not chunks <= step < chunks + LAG:
                pl.when(inner)(total_step)
            if step < 3 * chunks:
                pl.when(inner)(middle_step)
        else:
            flushed = jnp.logical_and(step >= chunks, step < chunks + LAG)
            due = jnp.logical_and(step >= LAG, jnp.logical_not(flushed))
            pl.when(jnp.logical_and(inner, due))(total_step)
            pl.when(jnp.logical_and(inner, step < 3 * chunks))(middle_step)

    def serve(start, count):
        for n in range(count):
            service(start + n)

    def put_block(a, b):
        @pl.when(outer)
        def _():
            for j in range(per_block):
                end_copy(a, b * per_block + j).start()

    def totals_of(a, b):
        @pl.when(outer)
        def _():
            for j in range(per_block):
                total_copy(a, b * per_block + j).wait_recv()

    def drain_all():
        def body(n, carry):
            a, j = lax.div(n, chunks), lax.rem(n, chunks)

            @pl.when(outer)
            def _():
                end_copy(a, j).wait_send()

            @pl.when(inner)
            def _():
                mid_copy(a, j).wait_send()
                total_copy(a, j).wait_send()

            return carry

        lax.fori_loop(0, 3 * chunks, body, 0)

    for k in range(1, 4):
        gain_copy(k).start()
    gain_over(0).start()
    gather_own(0)
    gather_own(1)
    out_copies = [
        remote(
            staged.at[3], other_out.at[k - 1], zo_send.at[k - 1], zo_recv.at[k - 1], (f, c, t ^ k)
        )
        for k in range(1, 4)
    ]
    for copy in out_copies:
        copy.start()

    half = table_ref.shape[1] // 2
    far = half - 1
    row_of, column_of = iota((BLOCK, BLOCK), 0), iota((BLOCK, BLOCK), 1)
    for h in range(heads):
        tiles[h, 0] = jnp.full((BLOCK, BLOCK), table_ref[h, far], f32)
        tiles[h, 4] = jnp.full((BLOCK, BLOCK), table_ref[h, half + far], f32)
    for d in (-1, 0, 1):
        bucket = bucket_of(d * BLOCK + row_of - column_of)
        members = range(half) if d < 0 else range(half, 2 * half) if d > 0 else range(2 * half)

        def per_head(h, carry, bucket=bucket, members=members, d=d):
            filled = jnp.zeros((BLOCK, BLOCK), f32)
            for b in members:
                filled = jnp.where(bucket == b, table_ref[h, b], filled)
            tiles[h, d + 2] = filled
            return carry

        lax.fori_loop(0, heads, per_head, 0)

    def bias_rows(kb, carry):
        key_rows = pl.ds(pl.multiple_of(kb * BLOCK, BLOCK), BLOCK)
        key_ids = jnp.broadcast_to(ids_ref[0:1, key_rows].astype(f32), (BLOCK, BLOCK)).T
        for qb in range(rows // BLOCK):
            start = pl.multiple_of(c * rows + qb * BLOCK, BLOCK)
            query_ids = ids_ref[0:1, pl.ds(start, BLOCK)].astype(f32)
            same = key_ids == query_ids
            d = jnp.clip(kb - c * (rows // BLOCK) - qb, -2, 2) + 2
            for h in range(heads):
                masked_bias[h, key_rows, qb * BLOCK : (qb + 1) * BLOCK] = jnp.where(
                    same, tiles[h, d], masked_score
                )
        return carry

    key_blocks = keys // BLOCK
    lax.fori_loop(0, key_blocks // 4, bias_rows, 0)
    for k in range(1, 4):
        gain_copy(k).wait_recv()
        gain_over(k).start()
    gather_pass(0)
    lax.fori_loop(key_blocks // 4, key_blocks // 2, bias_rows, 0)
    gather_pass(1)
    for copy in loads[4:]:
        copy.wait()
    gather_own(2)
    gather_own(3)
    for k in range(4):
        gain_over(k).wait_recv()
    spread = jnp.zeros((8, width), f32)
    for i in range(shards):
        one_hot = (iota((BLOCK, width), 1) == iota((BLOCK, width), 0) + i * shard).astype(f32)
        spread = spread + contract(gains_all[i].astype(bf16), one_hot.astype(bf16), 1, 0)
    gain_rows[...] = spread

    def block_rows(b, size=BLOCK):
        if isinstance(b, int):
            return pl.ds(b * size, size)
        return pl.ds(pl.multiple_of(b * size, size), size)

    def inverse_rms(values):
        return lax.rsqrt(jnp.mean(values * values, axis=-1, keepdims=True) + epsilon)

    def norm_one(b, carry):
        at = block_rows(b)
        xs = x_ref[at, :].astype(f32)
        n1[at, :] = (xs * inverse_rms(xs) * gain_rows[0:1, :]).astype(bf16)
        return carry

    lax.fori_loop(0, rows // BLOCK, norm_one, 0)

    def weight(buffer, a):
        return buffer[:, a].reshape(width, buffer.shape[-1])

    own_rows = pl.ds(pl.multiple_of(t * head_width, DH), head_width)
    own_keys = pl.ds(pl.multiple_of(c * rows, rows), rows)
    normed = n1[...]
    kv_copies = [
        remote(ref.at[own_keys], ref.at[own_keys], kv_send.at[n], kv_recv.at[n], partner)
        for n, ref in enumerate((k_all, v_all))
    ]
    gather_corner(0)
    lax.fori_loop(key_blocks // 2, key_blocks * 3 // 4, bias_rows, 0)
    gather_finish(0)
    mixed_kv = contract(normed, wkv[...].reshape(width, 2 * head_width), 1, 0).astype(bf16)
    k_all[own_keys, :] = mixed_kv[:, 0:head_width]
    kv_copies[0].start()
    v_all[own_keys, :] = mixed_kv[:, head_width:]
    kv_copies[1].start()
    gather_corner(1)
    lax.fori_loop(key_blocks * 3 // 4, key_blocks, bias_rows, 0)
    n1t[...] = normed.T
    gather_pass(2)
    for k in range(1, 4):
        out_copies[k - 1].wait_recv()
        wo3[me, :, (k - 1) * head_width : k * head_width] = other_out[k - 1]
    gather_own(5)
    gather_own(4)
    gather_finish(1)
    q_t[...] = contract(normed, wqo[:, :, 0:head_width].reshape(width, head_width), 1, 0).astype(bf16).T
    for copy in kv_copies:
        copy.wait_recv()
    v_t[...] = v_all[...].T

    def head_only(values, h):
        head_of = iota(values.shape, 0)
        inside = jnp.logical_and(head_of >= h * DH, head_of < (h + 1) * DH)
        return jnp.where(inside, values, jnp.zeros_like(values))

    def attended_copy(source, b, slot, target):
        view = att_all.at[
            pl.ds(pl.multiple_of(source * head_width, DH), head_width), block_rows(b)
        ]
        return remote(view, view, at_send.at[slot, b], at_recv.at[source, b], (f, c, target))

    def attended_start(b):
        @pl.when(outer)
        def _():
            attended_copy(t, b, 0, near_end).start()

        @pl.when(inner)
        def _():
            attended_copy(t, b, 0, far_end).start()
            attended_copy(t, b, 1, middle).start()

    def attended_relay(b, part):
        @pl.when(inner)
        def _():
            source = (far_end, middle, 3 - far_end)[part]
            attended_copy(source, b, 2 + part, middle if part == 0 else far_end).wait_recv()
            attended_copy(source, b, 2 + part, middle if part == 0 else far_end).start()

    def attended_wait(b):
        @pl.when(outer)
        def _():
            for source in (near_end, 3 - near_end, 3 - t):
                attended_copy(source, b, 0, near_end).wait_recv()

    def attended_drain(b, carry):
        attended_copy(t, b, 0, near_end).wait_send()

        @pl.when(inner)
        def _():
            for slot in range(1, 5):
                attended_copy(t, b, slot, middle).wait_send()

        return carry

    def attend(qb):
        at = block_rows(qb, FORWARD_BLOCK)

        def per_head(h, carry):
            queries = head_only(q_t[:, at], h)
            top = jnp.full((8, FORWARD_BLOCK), -jnp.inf, f32)
            for kb in range(keys // BLOCK):
                span_k = slice(kb * BLOCK, (kb + 1) * BLOCK)
                block = contract(k_all[span_k, :], queries, 1, 0) + masked_bias[h, span_k, at]
                score[span_k, 0:FORWARD_BLOCK] = block
                top = jnp.maximum(top, jnp.max(block.reshape(BLOCK // 8, 8, FORWARD_BLOCK), axis=0))
            top = jnp.max(top, axis=0, keepdims=True)
            total = jnp.zeros((8, FORWARD_BLOCK), f32)
            for kb in range(keys // BLOCK):
                span_k = slice(kb * BLOCK, (kb + 1) * BLOCK)
                block = jnp.exp(score[span_k, 0:FORWARD_BLOCK] - top)
                expo[h, span_k, at] = block.astype(bf16)
                total = total + jnp.sum(block.reshape(BLOCK // 8, 8, FORWARD_BLOCK), axis=0)
            inverse = 1.0 / jnp.sum(total, axis=0, keepdims=True)
            linv[h, :, at] = jnp.broadcast_to(inverse, (8, FORWARD_BLOCK))
            head_rows = pl.ds(pl.multiple_of(h * DH, DH), DH)
            own_head = pl.ds(pl.multiple_of(t * head_width + h * DH, DH), DH)
            mixed = contract(v_t[head_rows, :], expo[h, :, at], 1, 0)
            att_all[own_head, at] = (mixed * inverse).astype(bf16)
            return carry

        lax.fori_loop(0, heads, per_head, 0)
        for n in range(FORWARD_BLOCK // BLOCK):
            attended_start(qb * (FORWARD_BLOCK // BLOCK) + n)

    blocks = rows // BLOCK
    scale = 0.7978845608028654
    forward_blocks = rows // FORWARD_BLOCK

    def attend_loop(qb, carry):
        attend(qb)

        @pl.when(qb == 0)
        def _():
            gather_pass(3)

        return carry

    lax.fori_loop(0, forward_blocks, attend_loop, 0)
    per_forward = FORWARD_BLOCK // BLOCK
    early = range(per_forward)
    late = range(per_forward, blocks)

    def relays(group, part):
        for b in group:
            attended_relay(b, part)

    gather_corner(2)
    near[...] = jnp.zeros_like(near)
    wo_all[t] = wqo[:, :, head_width:].reshape(width, head_width)
    gather_pass(5)
    relays(early, 0)
    relays(early, 1)
    gather_pass(4)
    gather_corner(3)
    relays(late, 0)
    relays(late, 1)
    gather_corner(5)
    relays(early, 2)
    gather_corner(4)
    k_t[...] = k_all[...].T
    dk[...] = jnp.zeros_like(dk)
    dv[...] = jnp.zeros_like(dv)
    small[...] = jnp.zeros_like(small)
    gather_finish(5)
    for k in range(1, 4):
        wo_all[t ^ k] = wo3[:, :, (k - 1) * head_width : k * head_width].reshape(width, head_width)
    relays(late, 2)
    for g in (2, 3, 4):
        gather_finish(g)

    def feed_forward(b, carry):
        attended_wait(b)
        at = block_rows(b)
        res = x_ref[at, :].astype(f32)
        for source in range(4):
            attended = att_all[source * head_width : (source + 1) * head_width, at].T
            res = res + contract(attended, wo_all[source], 1, 1)
        resid[at, :] = res
        normed = (res * inverse_rms(res) * gain_rows[1:2, :]).astype(bf16)
        n2[at, :] = normed
        gate = contract(normed, weight(wf, 0), 1, 0)
        up = contract(normed, weight(wf, 1), 1, 0)
        down = weight(wf, 2)
        grad_act = contract(cot_ref[at, :], down, 1, 0)
        square = gate * gate
        curve = jnp.tanh(scale * (gate + 0.044715 * square * gate))
        left = 0.5 * (1.0 + curve)
        value = gate * left
        slope = left + 0.5 * gate * (1.0 - curve * curve) * scale * (1.0 + 0.134145 * square)
        low_act = (value * up).astype(bf16)
        low_gate = (grad_act * up * slope).astype(bf16)
        low_up = (grad_act * value).astype(bf16)
        act[at, :] = low_act
        ggate[at, :] = low_gate
        gup[at, :] = low_up
        snd[0, at, :] = (
            contract(low_gate, weight(wf, 0), 1, 1) + contract(low_up, weight(wf, 1), 1, 1)
        ).astype(bf16)
        put_block(0, b)
        snd[1, at, :] = contract(low_act, down, 1, 1).astype(bf16)

        @pl.when(b > 0)
        def _():
            serve((b - 1) * per_block, per_block)

        return carry

    lax.fori_loop(0, blocks, feed_forward, 0)

    def put_outputs(b, carry):
        put_block(1, b)
        return carry

    lax.fori_loop(0, blocks, put_outputs, 0)
    turned[0] = n2[...].T
    turned[1] = cot_ref[...].T

    def sent(n, which):
        if n == 0:
            return gsf.at[:, which]
        return gsa.at[:, which, 3:4] if n == 1 else gsa.at[:, which, 0:3]

    def landed(n):
        return rf.at[...] if n == 0 else ra.at[:, 3:4] if n == 1 else ra.at[:, 0:3]

    def over_copy(n):
        return remote(sent(n, 1 - c), landed(n), rs_send.at[n], rs_recv.at[n], partner)

    def summed(n, index):
        return sf.at[index] if n == 0 else sa.at[index, 3:4] if n == 1 else sa.at[index, 0:3]

    def arrived(n, k):
        return rf2.at[k - 1] if n == 0 else ra2.at[k - 1, 3:4] if n == 1 else ra2.at[k - 1, 0:3]

    def out_copy(n, k):
        return remote(
            summed(n, f ^ k), arrived(n, k), rs2_send.at[n, k - 1], rs2_recv.at[n, k - 1],
            (f ^ k, c, t),
        )

    members_of = {0: (0, 1, 2), 1: (3,), 2: (0, 1, 2)}
    outputs = {0: (gg_hbm, gu_hbm, gd_hbm), 1: (go_hbm,), 2: (gk_hbm, gv_hbm, gq_hbm)}

    def part_stores(n):
        results = gf_ref if n == 0 else ga_ref
        offset = (0, 3, 4)[n]
        return [
            pltpu.make_async_copy(results.at[a], target, store_sem.at[offset + i])
            for i, (a, target) in enumerate(zip(members_of[n], outputs[n]))
        ]

    def reduce_send(n):
        over_copy(n).wait_recv()
        own, got, total = (gsf, rf, sf) if n == 0 else (gsa, ra, sa)

        def body(k, carry):
            index = jnp.bitwise_xor(f, groups - 1 - k)
            for a in members_of[n]:
                total[index, a] = (
                    own[index, c, a].astype(f32) + got[index, a].astype(f32)
                ).astype(bf16)
            return carry

        lax.fori_loop(0, groups, body, 0)
        for k in range(1, groups):
            out_copy(n, k).start()

    def reduce_finish(n):
        total, got = (sf, rf2) if n == 0 else (sa, ra2)
        for k in range(1, groups):
            out_copy(n, k).wait_recv()
        results = gf_ref if n == 0 else ga_ref
        for a in members_of[n]:
            value = total[f, a].astype(f32)
            for k in range(1, groups):
                value = value + got[k - 1, a].astype(f32)
            results[a] = value
        for copy in part_stores(n):
            copy.start()

    def reduce_drain(n):
        over_copy(n).wait_send()
        for k in range(1, groups):
            out_copy(n, k).wait_send()

    both = 2 * shard

    def store_grad(buffer, i, a, value):
        buffer[i, :, a] = value.astype(bf16).reshape(2, shard, value.shape[-1])

    def pair_rows(i):
        return block_rows(i, both)

    def feed_forward_weights(i):
        at = pair_rows(i)
        store_grad(gsf, i, 0, contract(turned[0, at, :], ggate[...], 1, 0))
        store_grad(gsf, i, 1, contract(turned[0, at, :], gup[...], 1, 0))
        store_grad(gsf, i, 2, contract(turned[1, at, :], act[...], 1, 0))

    def residual_back(b):
        totals_of(0, b)
        at = block_rows(b)
        grad_in = tot[0, at, :].astype(f32)
        res = resid[at, :]
        inverse = inverse_rms(res)
        u = res * inverse
        small[1:2, :] += jnp.sum(grad_in * u, axis=0, keepdims=True)
        g = grad_in * gain_rows[1:2, :]
        grad = cot_ref[at, :].astype(f32) + inverse * (
            g - u * jnp.mean(g * u, axis=-1, keepdims=True)
        )
        grad_res[at, :] = grad
        low_grad = grad.astype(bf16)
        grl[at, :] = low_grad
        grad_att = contract(low_grad, wo_all[t], 1, 0).astype(bf16)
        scaled = grad_att.T.astype(f32) * jnp.concatenate(
            [jnp.broadcast_to(linv[h, 0:1, at], (DH, BLOCK)) for h in range(heads)], axis=0
        )
        scaled = scaled.astype(bf16)
        dos_t[:, at] = scaled
        products = scaled.astype(f32) * att_all[own_rows, at].astype(f32)
        for h in range(heads):
            delta[h, :, at] = jnp.broadcast_to(
                jnp.sum(products[h * DH : (h + 1) * DH], axis=0, keepdims=True), (8, BLOCK)
            )

    extra = dk.shape[1] - head_width
    query_blocks = rows // BLOCK

    def attend_back(start, size, h):
        at = slice(start, start + size)
        first = start // BLOCK
        head_rows = pl.ds(pl.multiple_of(h * DH, DH), DH)
        if True:
            grads = head_only(dos_t[:, at], h)
            queries = head_only(q_t[:, at], h)
            flag = iota((extra, size), 0)
            lane = iota((extra, size), 1)
            flags = jnp.zeros((extra, size), f32)
            for j in range(size // BLOCK):
                hit = jnp.logical_and(
                    flag == h * query_blocks + first + j,
                    jnp.logical_and(lane >= j * BLOCK, lane < (j + 1) * BLOCK),
                )
                flags = jnp.where(hit, 1.0, flags)
            flagged = jnp.concatenate([queries, flags.astype(bf16)], axis=0)
            shift = delta[h, 0:1, at]
            for kb in range(keys // BLOCK):
                span_k = slice(kb * BLOCK, (kb + 1) * BLOCK)
                block = contract(v_all[span_k, :], grads, 1, 0)
                low_score[span_k, 0:size] = (
                    expo[h, span_k, at].astype(f32) * (block - shift)
                ).astype(bf16)
            dv[...] += contract(expo[h, :, at], grads, 1, 1)
            dk[...] += contract(low_score[:, 0:size], flagged, 1, 1)
            dq_t[head_rows, at] = contract(
                k_t[head_rows, :], low_score[:, 0:size], 1, 0
            ).astype(bf16)
            for j in range(size // BLOCK):
                home = c * query_blocks + first + j
                for d in (-1, 0, 1):
                    kb = home + d
                    valid = jnp.logical_and(kb >= 0, kb < keys // BLOCK)

                    @pl.when(valid)
                    def _():
                        where_k = jnp.clip(kb, 0, keys // BLOCK - 1)
                        near[h, d + 1] += low_score[
                            block_rows(where_k), j * BLOCK : (j + 1) * BLOCK
                        ].astype(f32)

    pace = per_block // 2
    step = (blocks - 1) * per_block

    query_parts = [(start, QUERY_BLOCK) for start in range(0, rows - QUERY_BLOCK, QUERY_BLOCK)]
    query_parts += [(start, BLOCK) for start in range(rows - QUERY_BLOCK, rows, BLOCK)]
    for qb, (start, size) in enumerate(query_parts):
        for b in range(start // BLOCK, (start + size) // BLOCK):
            residual_back(b)
            if qb == 0:
                service(step)
                step += 1

        def back_head(h, carry, start=start, size=size, step=step, qb=qb):
            attend_back(start, size, h)
            serve(h * PACES[qb] + step, PACES[qb])
            return carry

        lax.fori_loop(0, heads, back_head, 0)
        step += heads * PACES[qb]
        if qb == 0:

            def early_weights(i, carry, step=step):
                feed_forward_weights(i)

                @pl.when(i < EARLY)
                def _():
                    service(i + step)

                return carry

            lax.fori_loop(0, groups, early_weights, 0)
            step += EARLY
            over_copy(0).start()
            flush(chunks - LAG, chunks)
        if qb == 1:
            reduce_send(0)

    other_keys = pl.ds(pl.multiple_of((1 - c) * rows, rows), rows)
    dkv_send[0] = dk[other_keys, 0:head_width].astype(bf16)
    dkv_send[1] = dv[other_keys, :].astype(bf16)
    dkv_copy = remote(dkv_send.at[...], dkv_recv.at[...], dkv_ssem.at[0], dkv_rsem.at[0], partner)
    dkv_copy.start()
    dkv_copy.wait_recv()
    dkv[:, 0:head_width] = (dk[own_keys, 0:head_width] + dkv_recv[0].astype(f32)).astype(bf16)
    dkv[:, head_width:] = (dv[own_keys, :] + dkv_recv[1].astype(f32)).astype(bf16)

    def project_back(b, carry):
        at = block_rows(b)
        total = contract(
            dq_t[:, at].T, wqo[:, :, 0:head_width].reshape(width, head_width), 1, 1
        )
        total = total + contract(dkv[at, :], wkv[...].reshape(width, 2 * head_width), 1, 1)
        snd[2, at, :] = total.astype(bf16)
        put_block(2, b)

        @pl.when(step + (b + 1) * pace <= 2 * chunks)
        def _():
            serve(step + b * pace, pace)

        return carry

    lax.fori_loop(0, blocks, project_back, 0)
    step += min(blocks, (2 * chunks - step) // pace) * pace

    def weights_back(i, carry):
        part_rows = n1t[pair_rows(i), :]
        mixed = contract(part_rows, dkv[...], 1, 0)
        store_grad(gsa, i, 0, mixed[:, 0:head_width])
        store_grad(gsa, i, 1, mixed[:, head_width:])
        store_grad(gsa, i, 2, contract(part_rows, dq_t[...], 1, 1))
        return carry

    lax.fori_loop(0, groups, weights_back, 0)
    over_copy(2).start()
    serve(step, 2 * chunks - step)
    step = 2 * chunks
    turned[0] = grl[...].T

    def output_weights(i, carry):
        store_grad(gsa, i, 3, contract(turned[0, pair_rows(i), :], att_all[own_rows, :], 1, 1))
        return carry

    lax.fori_loop(0, groups, output_weights, 0)
    over_copy(1).start()
    reduce_send(2)
    reduce_send(1)

    def bucket_sums(h, carry):
        for b in range(2 * half):
            summed_block = jnp.zeros((8, BLOCK), f32)
            for d in (-1, 0) if b < half else (0, 1):
                bucket = bucket_of(d * BLOCK + row_of - column_of)
                chosen = jnp.where(bucket == b, near[h, d + 1], 0.0)
                summed_block = summed_block + jnp.sum(
                    chosen.reshape(BLOCK // 8, 8, BLOCK), axis=0
                )
            pick[b : b + 1, :] = jnp.sum(summed_block, axis=0, keepdims=True)
        sums = contract(jnp.ones((8, BLOCK), f32), pick[...], 1, 1, highest)
        small[:, 0 : 2 * half] += jnp.where(iota((8, 2 * half), 0) == 2 + h, sums, 0.0)
        return carry

    def far_sums():
        tail = dk.shape[1] - BLOCK
        first_lane = head_width - tail
        column_sums = dk[:, tail:]
        block_row = iota((keys, BLOCK), 0)
        lane = iota((keys, BLOCK), 1)
        left_sum = jnp.zeros((1, BLOCK), f32)
        right_sum = jnp.zeros((1, BLOCK), f32)
        for j in range(query_blocks):
            mine = jnp.zeros((keys, BLOCK), jnp.bool_)
            for h in range(heads):
                mine = jnp.logical_or(mine, lane == first_lane + h * query_blocks + j)
            home = c * query_blocks + j
            is_left = jnp.logical_and(mine, block_row < (home - 1) * BLOCK)
            is_right = jnp.logical_and(mine, block_row >= (home + 2) * BLOCK)
            left_sum += jnp.sum(jnp.where(is_left, column_sums, 0.0), axis=0, keepdims=True)
            right_sum += jnp.sum(jnp.where(is_right, column_sums, 0.0), axis=0, keepdims=True)
        from_lane, to_lane = iota((BLOCK, BLOCK), 0), iota((BLOCK, BLOCK), 1)
        for h in range(heads):
            start = first_lane + h * query_blocks
            inside = jnp.logical_and(from_lane >= start, from_lane < start + query_blocks)
            left_pick = jnp.logical_and(inside, to_lane == far).astype(f32)
            right_pick = jnp.logical_and(inside, to_lane == half + far).astype(f32)
            small[2 + h : 3 + h, 0:BLOCK] += (
                contract(jnp.broadcast_to(left_sum, (8, BLOCK)), left_pick, 1, 0, highest)
                + contract(jnp.broadcast_to(right_sum, (8, BLOCK)), right_pick, 1, 0, highest)
            )[0:1]

    def block_store(n, source, target, b):
        at = block_rows(b)
        return pltpu.make_async_copy(source.at[at], target.at[at], store_sem.at[n])

    def input_back(b):
        totals_of(2, b)
        at = block_rows(b)
        grad_in = tot[2, at, :].astype(f32)
        xs = x_ref[at, :].astype(f32)
        inverse = inverse_rms(xs)
        u = xs * inverse
        g = grad_in * gain_rows[0:1, :]
        gin_ref[at, :] = grad_res[at, :] + inverse * (
            g - u * jnp.mean(g * u, axis=-1, keepdims=True)
        )
        block_store(7 + b, gin_ref, gin_hbm, b).start()

    def layer_out(b):
        totals_of(1, b)
        at = block_rows(b)
        out_ref[at, :] = (resid[at, :] + tot[1, at, :].astype(f32)).astype(bf16)
        block_store(7 + blocks + b, out_ref, out_hbm, b).start()

    small_copies = [
        remote(
            small.at[...], small_all.at[me], sm_send.at[k * 2 + kc - 1], sm_recv.at[k * 2 + kc - 1],
            (f ^ k, c ^ kc, t),
        )
        for k in range(groups)
        for kc in range(2)
        if k or kc
    ]

    def small_start():
        for copy in small_copies:
            copy.start()
        small_all[me] = small[...]

    def small_finish():
        for copy in small_copies:
            copy.wait_recv()
        total_small = small_all[0]
        for i in range(1, shards):
            total_small = total_small + small_all[i]
        to_own = (iota((width, BLOCK), 0) == iota((width, BLOCK), 1) + me * shard).astype(f32)
        own_gains = contract(total_small, to_own, 1, 0, highest)
        gain_two_out_ref[...] = own_gains[1:2, 0:shard]
        bias_out_ref[...] = total_small[2 : 2 + heads, 0 : 2 * half]

    gain_copies = [
        remote(
            gain_part.at[t], gain_part.at[t], gp_send.at[kt - 1], gp_recv.at[kt - 1], (f, c, t ^ kt)
        )
        for kt in range(1, 4)
    ]

    def gain_start():
        products = jnp.zeros((shard, head_width), f32)
        for a in members_of[2]:
            products = products + staged[a].astype(f32) * ga_ref[a]
        row_sums = contract(jnp.ones((8, head_width), f32), products, 1, 1, highest)
        gain_part[t, :, 0:shard] = row_sums / gain_one_ref[...].astype(f32)
        for copy in gain_copies:
            copy.start()

    def gain_finish():
        for copy in gain_copies:
            copy.wait_recv()
        total = gain_part[0, 0:1, 0:shard]
        for i in range(1, 4):
            total = total + gain_part[i, 0:1, 0:shard]
        gain_one_out_ref[...] = total

    @pl.when(outer)
    def _():
        lax.fori_loop(0, heads, bucket_sums, 0)
        far_sums()

    def at_step(n, value, run):
        pl.when(n == value)(run)

    def last_steps(n, carry):
        service(2 * chunks + n)

        @pl.when(jnp.logical_and(inner, jnp.logical_and(lax.rem(n, 2) == 0, n < 2 * heads)))
        def _():
            bucket_sums(lax.div(n, 2), 0)

        pl.when(jnp.logical_and(inner, n == 2 * heads))(far_sums)
        at_step(n, 2 * heads + 1, small_start)
        at_step(n, 2 * heads + 2, functools.partial(reduce_finish, 0))

        @pl.when(jnp.logical_and(n > 2 * heads + 2, n <= 2 * heads + 2 + blocks))
        def _():
            layer_out(n - 2 * heads - 3)

        def gains():
            reduce_finish(2)
            gain_start()

        at_step(n, 2 * heads + 3 + blocks, gains)
        at_step(n, 2 * heads + 4 + blocks, small_finish)
        at_step(n, 2 * heads + 5 + blocks, functools.partial(reduce_finish, 1))
        at_step(n, chunks + LAG - 2, gain_finish)

        due = n - (per_block - 1) - LAG

        @pl.when(jnp.logical_and(due >= 0, lax.rem(due, per_block) == 0))
        def _():
            input_back(lax.div(due, per_block))

        return carry

    lax.fori_loop(0, chunks + LAG, last_steps, 0)
    for b in range(blocks):
        block_store(7 + b, gin_ref, gin_hbm, b).wait()
        block_store(7 + blocks + b, out_ref, out_hbm, b).wait()
    for n in range(3):
        for copy in part_stores(n):
            copy.wait()
    for copy in small_copies + gain_copies:
        copy.wait_send()
    for g in range(6):
        gather_drain(g)
    for copy in out_copies:
        copy.wait_send()
    lax.fori_loop(0, blocks, attended_drain, 0)
    for k in range(1, 4):
        gain_copy(k).wait_send()
    for k in range(4):
        gain_over(k).wait_send()
    for copy in kv_copies:
        copy.wait_send()
    dkv_copy.wait_send()
    drain_all()
    for n in range(3):
        reduce_drain(n)


def fused_layer(shards, x, cot, ids, gain_one, gain_two, weights, table):
    rows, width = x.shape
    shard, head_width = weights[0].shape
    units = weights[4].shape[1]
    keys = ids.shape[1]
    heads = head_width // DH
    groups = shards // 2
    chunks = rows // CHUNK
    padded = head_width + (-head_width) % BLOCK
    if padded - head_width < heads * (rows // BLOCK):
        padded += BLOCK
    vmem, dma = pltpu.VMEM, pltpu.SemaphoreType.DMA
    out_shape = (
        jax.ShapeDtypeStruct((rows, width), bf16),
        jax.ShapeDtypeStruct((rows, width), f32),
        *[jax.ShapeDtypeStruct((shard, head_width), f32)] * 4,
        *[jax.ShapeDtypeStruct((shard, units), f32)] * 3,
        jax.ShapeDtypeStruct((1, shard), f32),
        jax.ShapeDtypeStruct((1, shard), f32),
        jax.ShapeDtypeStruct(table.shape, f32),
    )
    in_vmem = pl.BlockSpec(memory_space=pltpu.VMEM)
    anywhere = pl.BlockSpec(memory_space=pl.ANY)
    scratch = [
        vmem((rows, width), bf16),
        vmem((rows, width), bf16),
        vmem((rows, width), bf16),
        vmem((rows, width), f32),
        vmem((4, shard, head_width), f32),
        vmem((3, shard, units), f32),
        vmem((4, shard, head_width), bf16),
        vmem((shards, shard, 2 * head_width), bf16),
        vmem((shards, shard, 2 * head_width), bf16),
        vmem((shards, shard, 3 * head_width), bf16),
        vmem((3, shard, head_width), bf16),
        vmem((4, width, head_width), bf16),
        vmem((shards, 3, shard, units), bf16),
        vmem((shards, 8, BLOCK), f32),
        vmem((8, width), f32),
        vmem((heads, 5, BLOCK, BLOCK), f32),
        vmem((heads, keys, rows), f32),
        vmem((keys, QUERY_BLOCK), f32),
        vmem((heads, keys, rows), bf16),
        vmem((keys, QUERY_BLOCK), bf16),
        vmem((3, rows, width), bf16),
        vmem((3, rows, width), bf16),
        vmem((3, rows, width), bf16),
        vmem((rows, width), f32),
        vmem((rows, width), f32),
        vmem((rows, width), bf16),
        vmem((rows, width), bf16),
        vmem((rows, width), bf16),
        vmem((width, rows), bf16),
        vmem((2, width, rows), bf16),
        vmem((rows, units), bf16),
        vmem((rows, units), bf16),
        vmem((rows, units), bf16),
        vmem((head_width, rows), bf16),
        vmem((keys, head_width), bf16),
        vmem((keys, head_width), bf16),
        vmem((head_width, keys), bf16),
        vmem((head_width, keys), bf16),
        vmem((4 * head_width, rows), bf16),
        vmem((head_width, rows), bf16),
        vmem((head_width, rows), bf16),
        vmem((heads, 8, rows), f32),
        vmem((heads, 8, rows), f32),
        vmem((keys, padded), f32),
        vmem((keys, head_width), f32),
        vmem((heads, 3, BLOCK, BLOCK), f32),
        vmem((table.shape[1], BLOCK), f32),
        vmem((2, rows, head_width), bf16),
        vmem((2, rows, head_width), bf16),
        vmem((rows, 2 * head_width), bf16),
        vmem((groups, 2, 4, shard, head_width), bf16),
        vmem((groups, 2, 3, shard, units), bf16),
        vmem((groups, 4, shard, head_width), bf16),
        vmem((groups, 3, shard, units), bf16),
        vmem((groups, 4, shard, head_width), bf16),
        vmem((groups, 3, shard, units), bf16),
        vmem((groups - 1, 4, shard, head_width), bf16),
        vmem((groups - 1, 3, shard, units), bf16),
        vmem((8, width), f32),
        vmem((shards, 8, width), f32),
        vmem((4, 8, BLOCK), f32),
        dma((9,)),
        dma((7 + 2 * (rows // BLOCK),)),
        dma((7, 8)),
        dma((7, 8)),
        dma((3,)),
        dma((3,)),
        dma((5, rows // BLOCK)),
        dma((4, rows // BLOCK)),
        dma((2,)),
        dma((2,)),
        dma((3, chunks)),
        dma((3, chunks)),
        dma((3, chunks)),
        dma((3, chunks)),
        dma((1,)),
        dma((1,)),
        dma((3,)),
        dma((3,)),
        dma((3, groups)),
        dma((3, groups)),
        dma((shards,)),
        dma((shards,)),
        dma((3,)),
        dma((3,)),
    ]
    return pl.pallas_call(
        functools.partial(layer_kernel, shards),
        out_shape=out_shape,
        in_specs=[anywhere] * 2
        + [in_vmem] * 3
        + [anywhere] * 7
        + [pl.BlockSpec(memory_space=pltpu.SMEM)],
        out_specs=[anywhere] * 9 + [in_vmem] * 3,
        scratch_shapes=scratch,
        name="layer",
        compiler_params=pltpu.CompilerParams(
            collective_id=0, has_side_effects=True, vmem_limit_bytes=63 << 20
        ),
    )(x, cot, ids, gain_one, gain_two, *weights, table)


def publish_kernel(count, *refs):
    sources, targets = refs[:count], refs[count : 2 * count]
    held, in_sem, out_sem = refs[2 * count : 3 * count], refs[3 * count], refs[3 * count + 1]
    inward = [
        pltpu.make_async_copy(sources[i], held[i], in_sem.at[i]) for i in range(count)
    ]
    outward = [
        pltpu.make_async_copy(held[i], targets[i], out_sem.at[i]) for i in range(count)
    ]
    for copy in inward:
        copy.start()
    for arriving, leaving in zip(inward, outward):
        arriving.wait()
        leaving.start()
    for copy in outward:
        copy.wait()


def publish(values):
    count = len(values)
    anywhere = pl.BlockSpec(memory_space=pl.ANY)
    return pl.pallas_call(
        functools.partial(publish_kernel, count),
        out_shape=[jax.ShapeDtypeStruct(value.shape, value.dtype) for value in values],
        in_specs=[anywhere] * count,
        out_specs=[anywhere] * count,
        scratch_shapes=[pltpu.VMEM(value.shape, value.dtype) for value in values]
        + [pltpu.SemaphoreType.DMA((count,))] * 2,
        name="publish",
    )(*values)


def on_device_fused(
    layer_input,
    doc_ids,
    query_weight,
    key_weight,
    value_weight,
    output_weight,
    gate_weight,
    up_weight,
    down_weight,
    first_gain,
    second_gain,
    position_bias,
    cotangent,
):
    shards = lax.axis_size("fsdp") * lax.axis_size("ctx")
    outs = fused_layer(
        shards,
        layer_input[0],
        cotangent[0],
        doc_ids,
        first_gain[None],
        second_gain[None],
        (
            query_weight,
            key_weight,
            value_weight,
            output_weight,
            gate_weight,
            up_weight,
            down_weight,
        ),
        position_bias.T,
    )
    outs = publish(outs)
    return (
        outs[0][None],
        outs[1][None],
        *outs[2:9],
        outs[9][0],
        outs[10][0],
        outs[11].T,
    )


def fits_kernel(mesh):
    return mesh.shape["ctx"] == 2 and mesh.shape["tp"] == 4 and mesh.shape["fsdp"] == 4


def solution(mesh):
    return jax.shard_map(
        on_device_fused if fits_kernel(mesh) else on_device,
        mesh=mesh,
        in_specs=(
            P("fsdp", "ctx", None),
            P("fsdp", None),
            P(("fsdp", "ctx"), "tp"),
            P(("fsdp", "ctx"), "tp"),
            P(("fsdp", "ctx"), "tp"),
            P(("fsdp", "ctx"), "tp"),
            P(("fsdp", "ctx"), "tp"),
            P(("fsdp", "ctx"), "tp"),
            P(("fsdp", "ctx"), "tp"),
            P(("fsdp", "ctx")),
            P(("fsdp", "ctx")),
            P(None, "tp"),
            P("fsdp", "ctx", None),
        ),
        out_specs=(
            P("fsdp", "ctx", None),
            P("fsdp", "ctx", None),
            P(("fsdp", "ctx"), "tp"),
            P(("fsdp", "ctx"), "tp"),
            P(("fsdp", "ctx"), "tp"),
            P(("fsdp", "ctx"), "tp"),
            P(("fsdp", "ctx"), "tp"),
            P(("fsdp", "ctx"), "tp"),
            P(("fsdp", "ctx"), "tp"),
            P(("fsdp", "ctx")),
            P(("fsdp", "ctx")),
            P(None, "tp"),
        ),
        check_vma=False,
    )
```

```python
import functools

import jax
import jax.numpy as jnp
from jax import lax
from jax.experimental import pallas as pl
from jax.experimental.pallas import tpu as pltpu
from jax.sharding import PartitionSpec as P

DH = 64


epsilon = 1e-06
masked_score = -1000000000.0
bucket_edges = (12, 16, 23, 32, 46, 64, 91)
highest = lax.Precision.HIGHEST


def bucket_of(relative):
    distance = jnp.abs(relative)
    beyond = jnp.zeros_like(distance) + 8
    for edge_value in bucket_edges:
        beyond = beyond + (distance >= edge_value).astype(jnp.int32)
    inside = jnp.where(distance < 8, distance, beyond)
    return jnp.where(relative > 0, 16, 0) + inside


def rms_norm(values, gain_vector):
    inverse = lax.rsqrt(jnp.mean(values * values, axis=-1, keepdims=True) + epsilon)
    return values * inverse * gain_vector


def gated_unit(gate_in, up_in):
    return jax.nn.gelu(gate_in, approximate=True) * up_in


def relative_bias(bias_table, query_rows, key_rows, offset):
    span_width = key_rows + query_rows
    relative = lax.iota(jnp.int32, span_width) - (query_rows - 1) - offset
    one_hot = (
        bucket_of(relative)[:, None] == lax.iota(jnp.int32, bias_table.shape[0])[None, :]
    ).astype(jnp.float32)
    per_shift = jnp.dot(one_hot, bias_table, precision=highest).T
    heads_here = bias_table.shape[1]
    toeplitz = jnp.broadcast_to(per_shift[:, None, :], (heads_here, query_rows, span_width))
    toeplitz = toeplitz.reshape(heads_here, query_rows * span_width)[
        :, : query_rows * (span_width - 1)
    ]
    toeplitz = toeplitz.reshape(heads_here, query_rows, span_width - 1)
    return (toeplitz[:, :, query_rows - 1 : query_rows - 1 + key_rows], one_hot)


def diagonal_sums(grad_scores, query_rows, key_rows):
    heads_here = grad_scores.shape[0]
    span_width = key_rows + query_rows
    placed = jnp.pad(grad_scores, ((0, 0), (0, 0), (query_rows - 1, 0)))
    placed = placed.reshape(heads_here, query_rows * (span_width - 1))
    placed = jnp.pad(placed, ((0, 0), (0, query_rows)))
    return jnp.sum(placed.reshape(heads_here, query_rows, span_width), axis=1)


def on_device(
    layer_input,
    doc_ids,
    query_weight,
    key_weight,
    value_weight,
    output_weight,
    gate_weight,
    up_weight,
    down_weight,
    first_gain,
    second_gain,
    position_bias,
    cotangent,
):
    query_rows = layer_input.shape[1]
    key_rows = query_rows * lax.axis_size("ctx")
    heads_here = position_bias.shape[1]
    head_width = heads_here * DH
    offset = lax.axis_index("ctx") * query_rows
    everything = (
        query_weight,
        key_weight,
        value_weight,
        output_weight,
        gate_weight,
        up_weight,
        down_weight,
        first_gain,
        second_gain,
    )
    (
        full_query,
        full_key,
        full_value,
        full_output,
        full_gate,
        full_up,
        full_down,
        gain_one,
        gain_two,
    ) = (
        lax.all_gather(everything[0], ("fsdp", "ctx"), axis=0, tiled=True),
        lax.all_gather(everything[1], ("fsdp", "ctx"), axis=0, tiled=True),
        lax.all_gather(everything[2], ("fsdp", "ctx"), axis=0, tiled=True),
        lax.all_gather(everything[3], ("fsdp", "ctx"), axis=0, tiled=True),
        lax.all_gather(everything[4], ("fsdp", "ctx"), axis=0, tiled=True),
        lax.all_gather(everything[5], ("fsdp", "ctx"), axis=0, tiled=True),
        lax.all_gather(everything[6], ("fsdp", "ctx"), axis=0, tiled=True),
        lax.all_gather(everything[7], ("fsdp", "ctx"), axis=0, tiled=True),
        lax.all_gather(everything[8], ("fsdp", "ctx"), axis=0, tiled=True),
    )
    inputs = layer_input.astype(jnp.float32)
    gain_first = gain_one.astype(jnp.float32)
    gain_second = gain_two.astype(jnp.float32)
    normed_one = rms_norm(inputs, gain_first).astype(jnp.bfloat16)
    queries = jnp.dot(normed_one, full_query, preferred_element_type=jnp.float32).astype(
        jnp.bfloat16
    )
    keys_local = jnp.dot(normed_one, full_key, preferred_element_type=jnp.float32).astype(
        jnp.bfloat16
    )
    values_local = jnp.dot(normed_one, full_value, preferred_element_type=jnp.float32).astype(
        jnp.bfloat16
    )
    keys_all, values_all = (
        lax.all_gather(keys_local, "ctx", axis=1, tiled=True),
        lax.all_gather(values_local, "ctx", axis=1, tiled=True),
    )
    bias_block, one_hot = relative_bias(position_bias, query_rows, key_rows, offset)

    def scores_of(query_heads, key_heads, id_row):
        raw_scores = jnp.einsum(
            "qhd,khd->hqk", query_heads, key_heads, preferred_element_type=jnp.float32
        )
        own_ids = lax.dynamic_slice_in_dim(id_row, offset, query_rows)
        same_doc = own_ids[:, None] == id_row[None, :]
        return jnp.where(same_doc[None], raw_scores + bias_block, masked_score)

    def forward_one(packed):
        query_seq, key_seq, value_seq, id_row = packed
        scores = scores_of(
            query_seq.reshape(query_rows, heads_here, DH),
            key_seq.reshape(key_rows, heads_here, DH),
            id_row,
        )
        row_max = jnp.max(scores, axis=-1, keepdims=True)
        exponentials = jnp.exp(scores - row_max)
        row_total = jnp.sum(exponentials, axis=-1, keepdims=True)
        probabilities = (exponentials / row_total).astype(jnp.bfloat16)
        attended = jnp.einsum(
            "hqk,khd->qhd",
            probabilities,
            value_seq.reshape(key_rows, heads_here, DH),
            preferred_element_type=jnp.float32,
        )
        log_row = row_max[..., 0] + jnp.log(row_total[..., 0])
        return (attended.reshape(query_rows, head_width).astype(jnp.bfloat16), log_row)

    attended, log_sums = lax.map(forward_one, (queries, keys_all, values_all, doc_ids))
    attention_terms = jnp.einsum(
        "sqe,de->sqd", attended, full_output, preferred_element_type=jnp.float32
    )
    residual = inputs + lax.psum(attention_terms.astype(jnp.bfloat16), "tp").astype(jnp.float32)
    normed_two = rms_norm(residual, gain_second).astype(jnp.bfloat16)
    gate_pre = jnp.dot(normed_two, full_gate, preferred_element_type=jnp.float32)
    up_pre = jnp.dot(normed_two, full_up, preferred_element_type=jnp.float32)
    activated = gated_unit(gate_pre, up_pre).astype(jnp.bfloat16)
    ffn_terms = jnp.einsum("sqf,df->sqd", activated, full_down, preferred_element_type=jnp.float32)
    output_rows = (
        residual + lax.psum(ffn_terms.astype(jnp.bfloat16), "tp").astype(jnp.float32)
    ).astype(jnp.bfloat16)
    grad_activated = jnp.einsum(
        "sqd,df->sqf", cotangent, full_down, preferred_element_type=jnp.float32
    )
    down_grad = jnp.einsum("sqd,sqf->df", cotangent, activated, preferred_element_type=jnp.float32)
    gated_value, gated_back = jax.vjp(gated_unit, gate_pre, up_pre)
    grad_gate, grad_up = gated_back(grad_activated)
    grad_gate = grad_gate.astype(jnp.bfloat16)
    grad_up = grad_up.astype(jnp.bfloat16)
    gate_grad = jnp.einsum("sqd,sqf->df", normed_two, grad_gate, preferred_element_type=jnp.float32)
    up_grad = jnp.einsum("sqd,sqf->df", normed_two, grad_up, preferred_element_type=jnp.float32)
    normed_two_terms = jnp.einsum(
        "sqf,df->sqd", grad_gate, full_gate, preferred_element_type=jnp.float32
    ) + jnp.einsum("sqf,df->sqd", grad_up, full_up, preferred_element_type=jnp.float32)
    grad_normed_two = lax.psum(normed_two_terms.astype(jnp.bfloat16), "tp").astype(jnp.float32)
    second_value, second_back = jax.vjp(rms_norm, residual, gain_second)
    grad_residual, second_gain_grad = second_back(grad_normed_two)
    grad_residual = grad_residual + cotangent.astype(jnp.float32)
    grad_low = grad_residual.astype(jnp.bfloat16)
    grad_attended = jnp.einsum(
        "sqd,de->sqe", grad_low, full_output, preferred_element_type=jnp.float32
    ).astype(jnp.bfloat16)
    output_grad = jnp.einsum("sqd,sqe->de", grad_low, attended, preferred_element_type=jnp.float32)

    def backward_one(running, packed):
        query_seq, key_seq, value_seq, id_row, grad_seq, log_row = packed
        query_heads = query_seq.reshape(query_rows, heads_here, DH)
        key_heads = key_seq.reshape(key_rows, heads_here, DH)
        value_heads = value_seq.reshape(key_rows, heads_here, DH)
        grad_heads = grad_seq.reshape(query_rows, heads_here, DH)
        scores = scores_of(query_heads, key_heads, id_row)
        probabilities = jnp.exp(scores - log_row[..., None])
        grad_probs = jnp.einsum(
            "qhd,khd->hqk", grad_heads, value_heads, preferred_element_type=jnp.float32
        )
        grad_values = jnp.einsum(
            "hqk,qhd->khd",
            probabilities.astype(jnp.bfloat16),
            grad_heads,
            preferred_element_type=jnp.float32,
        )
        grad_scores = probabilities * (
            grad_probs - jnp.sum(probabilities * grad_probs, axis=-1, keepdims=True)
        )
        low_scores = grad_scores.astype(jnp.bfloat16)
        grad_queries = jnp.einsum(
            "hqk,khd->qhd", low_scores, key_heads, preferred_element_type=jnp.float32
        )
        grad_keys = jnp.einsum(
            "hqk,qhd->khd", low_scores, query_heads, preferred_element_type=jnp.float32
        )
        running = running + diagonal_sums(grad_scores, query_rows, key_rows)
        return (
            running,
            (
                grad_queries.reshape(query_rows, head_width).astype(jnp.bfloat16),
                grad_keys.reshape(key_rows, head_width),
                grad_values.reshape(key_rows, head_width),
            ),
        )

    shift_grads, (grad_queries, key_parts, value_parts) = lax.scan(
        backward_one,
        jnp.zeros((heads_here, query_rows + key_rows), jnp.float32),
        (queries, keys_all, values_all, doc_ids, grad_attended, log_sums),
    )
    grad_keys, grad_values = (
        lax.psum_scatter(
            key_parts.astype(jnp.bfloat16), "ctx", scatter_dimension=1, tiled=True
        ).astype(jnp.float32),
        lax.psum_scatter(
            value_parts.astype(jnp.bfloat16), "ctx", scatter_dimension=1, tiled=True
        ).astype(jnp.float32),
    )
    grad_keys = grad_keys.astype(jnp.bfloat16)
    grad_values = grad_values.astype(jnp.bfloat16)
    normed_one_terms = (
        jnp.einsum("sqe,de->sqd", grad_queries, full_query, preferred_element_type=jnp.float32)
        + jnp.einsum("sqe,de->sqd", grad_keys, full_key, preferred_element_type=jnp.float32)
        + jnp.einsum("sqe,de->sqd", grad_values, full_value, preferred_element_type=jnp.float32)
    )
    grad_normed_one = lax.psum(normed_one_terms.astype(jnp.bfloat16), "tp").astype(jnp.float32)
    query_grad = jnp.einsum(
        "sqd,sqe->de", normed_one, grad_queries, preferred_element_type=jnp.float32
    )
    key_grad = jnp.einsum("sqd,sqe->de", normed_one, grad_keys, preferred_element_type=jnp.float32)
    value_grad = jnp.einsum(
        "sqd,sqe->de", normed_one, grad_values, preferred_element_type=jnp.float32
    )
    first_value, first_back = jax.vjp(rms_norm, inputs, gain_first)
    grad_inputs, first_gain_grad = first_back(grad_normed_one)
    input_rows = grad_residual + grad_inputs
    bias_gradient = lax.psum(jnp.dot(one_hot.T, shift_grads.T, precision=highest), ("fsdp", "ctx"))
    (
        query_total,
        key_total,
        value_total,
        output_total,
        gate_total,
        up_total,
        down_total,
        first_total,
        second_total,
    ) = (
        lax.psum_scatter(query_grad, ("fsdp", "ctx"), scatter_dimension=0, tiled=True),
        lax.psum_scatter(key_grad, ("fsdp", "ctx"), scatter_dimension=0, tiled=True),
        lax.psum_scatter(value_grad, ("fsdp", "ctx"), scatter_dimension=0, tiled=True),
        lax.psum_scatter(output_grad, ("fsdp", "ctx"), scatter_dimension=0, tiled=True),
        lax.psum_scatter(gate_grad, ("fsdp", "ctx"), scatter_dimension=0, tiled=True),
        lax.psum_scatter(up_grad, ("fsdp", "ctx"), scatter_dimension=0, tiled=True),
        lax.psum_scatter(down_grad, ("fsdp", "ctx"), scatter_dimension=0, tiled=True),
        lax.psum_scatter(first_gain_grad, ("fsdp", "ctx"), scatter_dimension=0, tiled=True),
        lax.psum_scatter(second_gain_grad, ("fsdp", "ctx"), scatter_dimension=0, tiled=True),
    )
    return (
        output_rows,
        input_rows,
        query_total,
        key_total,
        value_total,
        output_total,
        gate_total,
        up_total,
        down_total,
        first_total,
        second_total,
        bias_gradient,
    )


MESH = pl.DeviceIdType.MESH
bf16, f32 = jnp.bfloat16, jnp.float32
BLOCK = 128
QUERY_BLOCK = 256
FORWARD_BLOCK = 256
CHUNK = 32
LAG = 4
RELAY_ROWS = 32
EARLY = 4
PACES = (1, 1, 1)


def contract(left, right, left_dim, right_dim, precision=None):
    return lax.dot_general(
        left,
        right,
        (((left_dim,), (right_dim,)), ((), ())),
        preferred_element_type=f32,
        precision=precision,
    )


def iota(shape, dim):
    return lax.broadcasted_iota(jnp.int32, shape, dim)


def layer_kernel(
    shards,
    x_hbm,
    cot_hbm,
    ids_ref,
    gain_one_ref,
    gain_two_ref,
    wq_ref,
    wk_ref,
    wv_ref,
    wo_ref,
    wg_ref,
    wu_ref,
    wd_ref,
    table_ref,
    out_hbm,
    gin_hbm,
    gq_hbm,
    gk_hbm,
    gv_hbm,
    go_hbm,
    gg_hbm,
    gu_hbm,
    gd_hbm,
    gain_one_out_ref,
    gain_two_out_ref,
    bias_out_ref,
    x_ref,
    cot_ref,
    out_ref,
    gin_ref,
    ga_ref,
    gf_ref,
    staged,
    wkv,
    wqo,
    wo3,
    other_out,
    wo_all,
    wf,
    gains_all,
    gain_rows,
    tiles,
    masked_bias,
    score,
    expo,
    low_score,
    snd,
    part,
    tot,
    resid,
    grad_res,
    n1,
    n2,
    grl,
    n1t,
    turned,
    act,
    ggate,
    gup,
    q_t,
    k_all,
    v_all,
    k_t,
    v_t,
    att_all,
    dos_t,
    dq_t,
    linv,
    delta,
    dk,
    dv,
    near,
    pick,
    dkv_send,
    dkv_recv,
    dkv,
    gsa,
    gsf,
    ra,
    rf,
    sa,
    sf,
    ra2,
    rf2,
    small,
    small_all,
    gain_part,
    load_sem,
    store_sem,
    ag_send,
    ag_recv,
    zo_send,
    zo_recv,
    at_send,
    at_recv,
    kv_send,
    kv_recv,
    s1,
    r1,
    s2,
    r2,
    dkv_ssem,
    dkv_rsem,
    rs_send,
    rs_recv,
    rs2_send,
    rs2_recv,
    sm_send,
    sm_recv,
    gp_send,
    gp_recv,
):
    groups = shards // 2
    f, c, t = lax.axis_index("fsdp"), lax.axis_index("ctx"), lax.axis_index("tp")
    me = f * 2 + c
    rows, width = x_ref.shape
    keys = k_all.shape[0]
    head_width = wq_ref.shape[1]
    heads = head_width // DH
    units = wg_ref.shape[1]
    shard = wq_ref.shape[0]
    chunks = rows // CHUNK
    per_block = BLOCK // CHUNK
    partner = (f, 1 - c, t)
    outer = jnp.logical_or(t == 0, t == 3)
    inner = jnp.logical_or(t == 1, t == 2)
    near_end = jnp.where(t < 2, 1, 2)
    far_end = jnp.where(t < 2, 0, 3)
    middle = 3 - t

    def remote(source, target, send_sem, recv_sem, device):
        return pltpu.make_async_remote_copy(
            src_ref=source,
            dst_ref=target,
            send_sem=send_sem,
            recv_sem=recv_sem,
            device_id=device,
            device_id_type=MESH,
        )

    barrier = pltpu.get_barrier_semaphore()
    for k in range(groups):
        for kc in range(2):
            if k or kc:
                pl.semaphore_signal(
                    barrier, inc=1, device_id=(f ^ k, c ^ kc, t), device_id_type=MESH
                )

    for kt in range(1, 4):
        pl.semaphore_signal(
            barrier, inc=1, device_id=(f, c, t ^ kt), device_id_type=MESH
        )
    loads = [
        pltpu.make_async_copy(source, target, load_sem.at[n])
        for n, (source, target) in enumerate(
            (
                (wk_ref, staged.at[0]),
                (wv_ref, staged.at[1]),
                (wq_ref, staged.at[2]),
                (wo_ref, staged.at[3]),
                (x_hbm, x_ref),
                (wg_ref, wf.at[me, 0]),
                (wu_ref, wf.at[me, 1]),
                (wd_ref, wf.at[me, 2]),
                (cot_hbm, cot_ref),
            )
        )
    ]
    for copy in loads:
        copy.start()
    gains_all[me] = jnp.zeros((8, BLOCK), f32)
    gains_all[me, 0:1, 0:shard] = gain_one_ref[...].astype(f32)
    gains_all[me, 1:2, 0:shard] = gain_two_ref[...].astype(f32)
    for copy in loads[:4]:
        copy.wait()
    wkv[me, :, 0:head_width] = staged[0]
    wkv[me, :, head_width:] = staged[1]
    wqo[me, :, 0:head_width] = staged[2]
    wqo[me, :, head_width:] = staged[3]
    pl.semaphore_wait(barrier, shards - 1 + 3)

    def piece(g, index):
        if g < 2:
            return (wkv, wqo)[g].at[index]
        return wo3.at[index] if g == 5 else wf.at[index, g - 2]

    def half_piece(g, index, n):
        return piece(g, index).at[n * (shard // 2) : (n + 1) * (shard // 2)]

    def own_copy(g, k):
        view = piece(g, me)
        return remote(view, view, ag_send.at[g, k - 1], ag_recv.at[g, k - 1], (f ^ k, c, t))

    def pass_copy(g, k):
        view = half_piece(g, (f ^ k) * 2 + c, k - 1)
        return remote(view, view, ag_send.at[g, k + 1], ag_recv.at[g, k + 1], (f ^ (3 - k), c, t))

    def over_piece(g, k):
        view = piece(g, (f ^ k) * 2 + c)
        return remote(view, view, ag_send.at[g, 4 + k], ag_recv.at[g, 4 + k], partner)

    def gather_own(g):
        for k in (1, 2):
            own_copy(g, k).start()
        over_piece(g, 0).start()

    def gather_pass(g):
        for k in (1, 2):
            own_copy(g, k).wait_recv()
            pass_copy(g, k).start()
            over_piece(g, k).start()

    def gather_corner(g):
        for k in (1, 2):
            pass_copy(g, k).wait_recv()
        over_piece(g, 3).start()

    def gather_finish(g):
        for k in range(4):
            over_piece(g, k).wait_recv()

    def gather_drain(g):
        for k in (1, 2):
            own_copy(g, k).wait_send()
            pass_copy(g, k).wait_send()
        for k in range(4):
            over_piece(g, k).wait_send()

    def gain_copy(k):
        view = gains_all.at[me]
        return remote(view, view, ag_send.at[6, k], ag_recv.at[6, k], (f ^ k, c, t))

    def gain_over(k):
        view = gains_all.at[(f ^ k) * 2 + c]
        return remote(view, view, ag_send.at[6, 4 + k], ag_recv.at[6, 4 + k], partner)

    def span(j):
        if isinstance(j, int):
            return pl.ds(j * CHUNK, CHUNK)
        return pl.ds(pl.multiple_of(j * CHUNK, CHUNK), CHUNK)

    def end_copy(a, j):
        return remote(
            snd.at[a, span(j)], part.at[a, span(j)], s1.at[a, j], r1.at[a, j], (f, c, near_end)
        )

    def mid_copy(a, j):
        return remote(
            snd.at[a, span(j)], tot.at[a, span(j)], s1.at[a, j], r2.at[a, j], (f, c, middle)
        )

    def total_copy(a, j):
        return remote(
            tot.at[a, span(j)], tot.at[a, span(j)], s2.at[a, j], r2.at[a, j], (f, c, far_end)
        )

    def add_rows(target, a, j, left, right):
        def body(r, carry):
            at = pl.ds(pl.multiple_of(j * CHUNK + r * RELAY_ROWS, RELAY_ROWS), RELAY_ROWS)
            target[a, at] = (left[a, at].astype(f32) + right[a, at].astype(f32)).astype(bf16)
            return carry

        lax.fori_loop(0, CHUNK // RELAY_ROWS, body, 0)

    def flush(first, last):
        @pl.when(inner)
        def _():
            for n in range(first, last):
                a, j = divmod(n, chunks)
                mid_copy(a, j).wait_recv()
                add_rows(tot, a, j, snd, tot)
                total_copy(a, j).start()

    def service(step):
        def total_step():
            a, j = split(step - LAG)
            mid_copy(a, j).wait_recv()
            add_rows(tot, a, j, snd, tot)
            total_copy(a, j).start()

        def middle_step():
            a, j = split(step)
            end_copy(a, j).wait_recv()
            add_rows(snd, a, j, snd, part)
            mid_copy(a, j).start()

        def split(n):
            if isinstance(n, int):
                return divmod(n, chunks)
            return lax.div(n, chunks), lax.rem(n, chunks)

        if isinstance(step, int):
            if step >= LAG and not chunks <= step < chunks + LAG:
                pl.when(inner)(total_step)
            if step < 3 * chunks:
                pl.when(inner)(middle_step)
        else:
            flushed = jnp.logical_and(step >= chunks, step < chunks + LAG)
            due = jnp.logical_and(step >= LAG, jnp.logical_not(flushed))
            pl.when(jnp.logical_and(inner, due))(total_step)
            pl.when(jnp.logical_and(inner, step < 3 * chunks))(middle_step)

    def serve(start, count):
        for n in range(count):
            service(start + n)

    def put_block(a, b):
        @pl.when(outer)
        def _():
            for j in range(per_block):
                end_copy(a, b * per_block + j).start()

    def totals_of(a, b):
        @pl.when(outer)
        def _():
            for j in range(per_block):
                total_copy(a, b * per_block + j).wait_recv()

    def drain_all():
        def body(n, carry):
            a, j = lax.div(n, chunks), lax.rem(n, chunks)

            @pl.when(outer)
            def _():
                end_copy(a, j).wait_send()

            @pl.when(inner)
            def _():
                mid_copy(a, j).wait_send()
                total_copy(a, j).wait_send()

            return carry

        lax.fori_loop(0, 3 * chunks, body, 0)

    for k in range(1, 4):
        gain_copy(k).start()
    gain_over(0).start()
    gather_own(0)
    gather_own(1)
    out_copies = [
        remote(
            staged.at[3], other_out.at[k - 1], zo_send.at[k - 1], zo_recv.at[k - 1], (f, c, t ^ k)
        )
        for k in range(1, 4)
    ]
    for copy in out_copies:
        copy.start()

    half = table_ref.shape[1] // 2
    far = half - 1
    row_of, column_of = iota((BLOCK, BLOCK), 0), iota((BLOCK, BLOCK), 1)
    for h in range(heads):
        tiles[h, 0] = jnp.full((BLOCK, BLOCK), table_ref[h, far], f32)
        tiles[h, 4] = jnp.full((BLOCK, BLOCK), table_ref[h, half + far], f32)
    for d in (-1, 0, 1):
        bucket = bucket_of(d * BLOCK + row_of - column_of)
        members = range(half) if d < 0 else range(half, 2 * half) if d > 0 else range(2 * half)

        def per_head(h, carry, bucket=bucket, members=members, d=d):
            filled = jnp.zeros((BLOCK, BLOCK), f32)
            for b in members:
                filled = jnp.where(bucket == b, table_ref[h, b], filled)
            tiles[h, d + 2] = filled
            return carry

        lax.fori_loop(0, heads, per_head, 0)

    def bias_rows(kb, carry):
        key_rows = pl.ds(pl.multiple_of(kb * BLOCK, BLOCK), BLOCK)
        key_ids = jnp.broadcast_to(ids_ref[0:1, key_rows].astype(f32), (BLOCK, BLOCK)).T
        for qb in range(rows // BLOCK):
            start = pl.multiple_of(c * rows + qb * BLOCK, BLOCK)
            query_ids = ids_ref[0:1, pl.ds(start, BLOCK)].astype(f32)
            same = key_ids == query_ids
            d = jnp.clip(kb - c * (rows // BLOCK) - qb, -2, 2) + 2
            for h in range(heads):
                masked_bias[h, key_rows, qb * BLOCK : (qb + 1) * BLOCK] = jnp.where(
                    same, tiles[h, d], masked_score
                )
        return carry

    key_blocks = keys // BLOCK
    lax.fori_loop(0, key_blocks // 4, bias_rows, 0)
    for k in range(1, 4):
        gain_copy(k).wait_recv()
        gain_over(k).start()
    gather_pass(0)
    lax.fori_loop(key_blocks // 4, key_blocks // 2, bias_rows, 0)
    gather_pass(1)
    for copy in loads[4:]:
        copy.wait()
    gather_own(2)
    gather_own(3)
    for k in range(4):
        gain_over(k).wait_recv()
    spread = jnp.zeros((8, width), f32)
    for i in range(shards):
        one_hot = (iota((BLOCK, width), 1) == iota((BLOCK, width), 0) + i * shard).astype(f32)
        spread = spread + contract(gains_all[i].astype(bf16), one_hot.astype(bf16), 1, 0)
    gain_rows[...] = spread

    def block_rows(b, size=BLOCK):
        if isinstance(b, int):
            return pl.ds(b * size, size)
        return pl.ds(pl.multiple_of(b * size, size), size)

    def inverse_rms(values):
        return lax.rsqrt(jnp.mean(values * values, axis=-1, keepdims=True) + epsilon)

    def norm_one(b, carry):
        at = block_rows(b)
        xs = x_ref[at, :].astype(f32)
        n1[at, :] = (xs * inverse_rms(xs) * gain_rows[0:1, :]).astype(bf16)
        return carry

    lax.fori_loop(0, rows // BLOCK, norm_one, 0)

    def weight(buffer, a):
        return buffer[:, a].reshape(width, buffer.shape[-1])

    own_rows = pl.ds(pl.multiple_of(t * head_width, DH), head_width)
    own_keys = pl.ds(pl.multiple_of(c * rows, rows), rows)
    normed = n1[...]
    kv_copies = [
        remote(ref.at[own_keys], ref.at[own_keys], kv_send.at[n], kv_recv.at[n], partner)
        for n, ref in enumerate((k_all, v_all))
    ]
    gather_corner(0)
    lax.fori_loop(key_blocks // 2, key_blocks * 3 // 4, bias_rows, 0)
    gather_finish(0)
    mixed_kv = contract(normed, wkv[...].reshape(width, 2 * head_width), 1, 0).astype(bf16)
    k_all[own_keys, :] = mixed_kv[:, 0:head_width]
    kv_copies[0].start()
    v_all[own_keys, :] = mixed_kv[:, head_width:]
    kv_copies[1].start()
    gather_corner(1)
    lax.fori_loop(key_blocks * 3 // 4, key_blocks, bias_rows, 0)
    gather_pass(2)
    for k in range(1, 4):
        out_copies[k - 1].wait_recv()
        wo3[me, :, (k - 1) * head_width : k * head_width] = other_out[k - 1]
    gather_own(5)
    gather_own(4)
    gather_finish(1)
    q_t[...] = contract(normed, wqo[:, :, 0:head_width].reshape(width, head_width), 1, 0).astype(bf16).T
    for copy in kv_copies:
        copy.wait_recv()
    v_t[...] = v_all[...].T

    def head_only(values, h):
        head_of = iota(values.shape, 0)
        inside = jnp.logical_and(head_of >= h * DH, head_of < (h + 1) * DH)
        return jnp.where(inside, values, jnp.zeros_like(values))

    def attended_copy(source, b, slot, target):
        view = att_all.at[
            pl.ds(pl.multiple_of(source * head_width, DH), head_width), block_rows(b)
        ]
        return remote(view, view, at_send.at[slot, b], at_recv.at[source, b], (f, c, target))

    def attended_start(b):
        @pl.when(outer)
        def _():
            attended_copy(t, b, 0, near_end).start()

        @pl.when(inner)
        def _():
            attended_copy(t, b, 0, far_end).start()
            attended_copy(t, b, 1, middle).start()

    def attended_relay(b, part):
        @pl.when(inner)
        def _():
            source = (far_end, middle, 3 - far_end)[part]
            attended_copy(source, b, 2 + part, middle if part == 0 else far_end).wait_recv()
            attended_copy(source, b, 2 + part, middle if part == 0 else far_end).start()

    def attended_wait(b):
        @pl.when(outer)
        def _():
            for source in (near_end, 3 - near_end, 3 - t):
                attended_copy(source, b, 0, near_end).wait_recv()

    def attended_drain(b, carry):
        attended_copy(t, b, 0, near_end).wait_send()

        @pl.when(inner)
        def _():
            for slot in range(1, 5):
                attended_copy(t, b, slot, middle).wait_send()

        return carry

    def attend(qb):
        at = block_rows(qb, FORWARD_BLOCK)

        def per_head(h, carry):
            queries = head_only(q_t[:, at], h)
            top = jnp.full((8, FORWARD_BLOCK), -jnp.inf, f32)
            for kb in range(keys // BLOCK):
                span_k = slice(kb * BLOCK, (kb + 1) * BLOCK)
                block = contract(k_all[span_k, :], queries, 1, 0) + masked_bias[h, span_k, at]
                score[span_k, 0:FORWARD_BLOCK] = block
                top = jnp.maximum(top, jnp.max(block.reshape(BLOCK // 8, 8, FORWARD_BLOCK), axis=0))
            top = jnp.max(top, axis=0, keepdims=True)
            total = jnp.zeros((8, FORWARD_BLOCK), f32)
            for kb in range(keys // BLOCK):
                span_k = slice(kb * BLOCK, (kb + 1) * BLOCK)
                block = jnp.exp(score[span_k, 0:FORWARD_BLOCK] - top)
                expo[h, span_k, at] = block.astype(bf16)
                total = total + jnp.sum(block.reshape(BLOCK // 8, 8, FORWARD_BLOCK), axis=0)
            inverse = 1.0 / jnp.sum(total, axis=0, keepdims=True)
            linv[h, :, at] = jnp.broadcast_to(inverse, (8, FORWARD_BLOCK))
            head_rows = pl.ds(pl.multiple_of(h * DH, DH), DH)
            own_head = pl.ds(pl.multiple_of(t * head_width + h * DH, DH), DH)
            mixed = contract(v_t[head_rows, :], expo[h, :, at], 1, 0)
            att_all[own_head, at] = (mixed * inverse).astype(bf16)
            return carry

        lax.fori_loop(0, heads, per_head, 0)
        for n in range(FORWARD_BLOCK // BLOCK):
            attended_start(qb * (FORWARD_BLOCK // BLOCK) + n)

    blocks = rows // BLOCK
    scale = 0.7978845608028654
    forward_blocks = rows // FORWARD_BLOCK

    def attend_loop(qb, carry):
        attend(qb)

        @pl.when(qb == 0)
        def _():
            gather_pass(3)

        return carry

    lax.fori_loop(0, forward_blocks, attend_loop, 0)
    per_forward = FORWARD_BLOCK // BLOCK
    early = range(per_forward)
    late = range(per_forward, blocks)

    def relays(group, part):
        for b in group:
            attended_relay(b, part)

    gather_corner(2)
    near[...] = jnp.zeros_like(near)
    wo_all[t] = wqo[:, :, head_width:].reshape(width, head_width)
    gather_pass(5)
    relays(early, 0)
    relays(early, 1)
    gather_pass(4)
    gather_corner(3)
    relays(late, 0)
    relays(late, 1)
    gather_corner(5)
    relays(early, 2)
    gather_corner(4)
    k_t[...] = k_all[...].T
    n1t[...] = n1[...].T
    dk[...] = jnp.zeros_like(dk)
    dv[...] = jnp.zeros_like(dv)
    small[...] = jnp.zeros_like(small)
    gather_finish(5)
    for k in range(1, 4):
        wo_all[t ^ k] = wo3[:, :, (k - 1) * head_width : k * head_width].reshape(width, head_width)
    relays(late, 2)
    for g in (2, 3, 4):
        gather_finish(g)

    def feed_forward(b, carry):
        attended_wait(b)
        at = block_rows(b)
        res = x_ref[at, :].astype(f32)
        for source in range(4):
            attended = att_all[source * head_width : (source + 1) * head_width, at].T
            res = res + contract(attended, wo_all[source], 1, 1)
        resid[at, :] = res
        normed = (res * inverse_rms(res) * gain_rows[1:2, :]).astype(bf16)
        n2[at, :] = normed
        gate = contract(normed, weight(wf, 0), 1, 0)
        up = contract(normed, weight(wf, 1), 1, 0)
        down = weight(wf, 2)
        grad_act = contract(cot_ref[at, :], down, 1, 0)

        @pl.when(b > 1)
        def _():
            serve((b - 2) * per_block + per_block // 2, per_block // 2)

        square = gate * gate
        curve = jnp.tanh(scale * (gate + 0.044715 * square * gate))
        left = 0.5 * (1.0 + curve)
        value = gate * left
        slope = left + 0.5 * gate * (1.0 - curve * curve) * scale * (1.0 + 0.134145 * square)
        low_act = (value * up).astype(bf16)
        low_gate = (grad_act * up * slope).astype(bf16)
        low_up = (grad_act * value).astype(bf16)
        act[at, :] = low_act
        ggate[at, :] = low_gate
        gup[at, :] = low_up
        snd[0, at, :] = (
            contract(low_gate, weight(wf, 0), 1, 1) + contract(low_up, weight(wf, 1), 1, 1)
        ).astype(bf16)
        put_block(0, b)
        snd[1, at, :] = contract(low_act, down, 1, 1).astype(bf16)

        @pl.when(b > 0)
        def _():
            serve((b - 1) * per_block, per_block // 2)

        return carry

    lax.fori_loop(0, blocks, feed_forward, 0)
    serve((blocks - 2) * per_block + per_block // 2, per_block // 2)

    def put_outputs(b, carry):
        put_block(1, b)
        return carry

    lax.fori_loop(0, blocks, put_outputs, 0)
    turned[0] = n2[...].T
    turned[1] = cot_ref[...].T

    def sent(n, which):
        if n == 0:
            return gsf.at[:, which]
        return gsa.at[:, which, 3:4] if n == 1 else gsa.at[:, which, 0:3]

    def landed(n):
        return rf.at[...] if n == 0 else ra.at[:, 3:4] if n == 1 else ra.at[:, 0:3]

    def over_copy(n):
        return remote(sent(n, 1 - c), landed(n), rs_send.at[n], rs_recv.at[n], partner)

    def summed(n, index):
        return sf.at[index] if n == 0 else sa.at[index, 3:4] if n == 1 else sa.at[index, 0:3]

    def arrived(n, k):
        return rf2.at[k - 1] if n == 0 else ra2.at[k - 1, 3:4] if n == 1 else ra2.at[k - 1, 0:3]

    def out_copy(n, k):
        return remote(
            summed(n, f ^ k), arrived(n, k), rs2_send.at[n, k - 1], rs2_recv.at[n, k - 1],
            (f ^ k, c, t),
        )

    members_of = {0: (0, 1, 2), 1: (3,), 2: (0, 1, 2)}
    outputs = {0: (gg_hbm, gu_hbm, gd_hbm), 1: (go_hbm,), 2: (gk_hbm, gv_hbm, gq_hbm)}

    def part_stores(n):
        results = gf_ref if n == 0 else ga_ref
        offset = (0, 3, 4)[n]
        return [
            pltpu.make_async_copy(results.at[a], target, store_sem.at[offset + i])
            for i, (a, target) in enumerate(zip(members_of[n], outputs[n]))
        ]

    def reduce_send(n):
        over_copy(n).wait_recv()
        own, got, total = (gsf, rf, sf) if n == 0 else (gsa, ra, sa)

        def body(k, carry):
            index = jnp.bitwise_xor(f, groups - 1 - k)
            for a in members_of[n]:
                total[index, a] = (
                    own[index, c, a].astype(f32) + got[index, a].astype(f32)
                ).astype(bf16)
            return carry

        lax.fori_loop(0, groups, body, 0)
        for k in range(1, groups):
            out_copy(n, k).start()

    def reduce_finish(n):
        total, got = (sf, rf2) if n == 0 else (sa, ra2)
        for k in range(1, groups):
            out_copy(n, k).wait_recv()
        results = gf_ref if n == 0 else ga_ref
        for a in members_of[n]:
            value = total[f, a].astype(f32)
            for k in range(1, groups):
                value = value + got[k - 1, a].astype(f32)
            results[a] = value
        for copy in part_stores(n):
            copy.start()

    def reduce_drain(n):
        over_copy(n).wait_send()
        for k in range(1, groups):
            out_copy(n, k).wait_send()

    both = 2 * shard

    def store_grad(buffer, i, a, value):
        buffer[i, :, a] = value.astype(bf16).reshape(2, shard, value.shape[-1])

    def pair_rows(i):
        return block_rows(i, both)

    def feed_forward_weights(i):
        at = pair_rows(i)
        store_grad(gsf, i, 0, contract(turned[0, at, :], ggate[...], 1, 0))
        store_grad(gsf, i, 1, contract(turned[0, at, :], gup[...], 1, 0))
        store_grad(gsf, i, 2, contract(turned[1, at, :], act[...], 1, 0))

    def residual_back(b):
        totals_of(0, b)
        at = block_rows(b)
        grad_in = tot[0, at, :].astype(f32)
        res = resid[at, :]
        inverse = inverse_rms(res)
        u = res * inverse
        small[1:2, :] += jnp.sum(grad_in * u, axis=0, keepdims=True)
        g = grad_in * gain_rows[1:2, :]
        grad = cot_ref[at, :].astype(f32) + inverse * (
            g - u * jnp.mean(g * u, axis=-1, keepdims=True)
        )
        grad_res[at, :] = grad
        low_grad = grad.astype(bf16)
        grl[at, :] = low_grad
        grad_att = contract(low_grad, wo_all[t], 1, 0).astype(bf16)
        scaled = grad_att.T.astype(f32) * jnp.concatenate(
            [jnp.broadcast_to(linv[h, 0:1, at], (DH, BLOCK)) for h in range(heads)], axis=0
        )
        scaled = scaled.astype(bf16)
        dos_t[:, at] = scaled
        products = scaled.astype(f32) * att_all[own_rows, at].astype(f32)
        for h in range(heads):
            delta[h, :, at] = jnp.broadcast_to(
                jnp.sum(products[h * DH : (h + 1) * DH], axis=0, keepdims=True), (8, BLOCK)
            )

    extra = dk.shape[1] - head_width
    query_blocks = rows // BLOCK

    def attend_back(start, size, h):
        at = slice(start, start + size)
        first = start // BLOCK
        head_rows = pl.ds(pl.multiple_of(h * DH, DH), DH)
        if True:
            grads = head_only(dos_t[:, at], h)
            queries = head_only(q_t[:, at], h)
            flag = iota((extra, size), 0)
            lane = iota((extra, size), 1)
            flags = jnp.zeros((extra, size), f32)
            for j in range(size // BLOCK):
                hit = jnp.logical_and(
                    flag == h * query_blocks + first + j,
                    jnp.logical_and(lane >= j * BLOCK, lane < (j + 1) * BLOCK),
                )
                flags = jnp.where(hit, 1.0, flags)
            flagged = jnp.concatenate([queries, flags.astype(bf16)], axis=0)
            shift = delta[h, 0:1, at]
            for kb in range(keys // BLOCK):
                span_k = slice(kb * BLOCK, (kb + 1) * BLOCK)
                block = contract(v_all[span_k, :], grads, 1, 0)
                low_score[span_k, 0:size] = (
                    expo[h, span_k, at].astype(f32) * (block - shift)
                ).astype(bf16)
            dv[...] += contract(expo[h, :, at], grads, 1, 1)
            dk[...] += contract(low_score[:, 0:size], flagged, 1, 1)
            dq_t[head_rows, at] = contract(
                k_t[head_rows, :], low_score[:, 0:size], 1, 0
            ).astype(bf16)
            for j in range(size // BLOCK):
                home = c * query_blocks + first + j
                for d in (-1, 0, 1):
                    kb = home + d
                    valid = jnp.logical_and(kb >= 0, kb < keys // BLOCK)

                    @pl.when(valid)
                    def _():
                        where_k = jnp.clip(kb, 0, keys // BLOCK - 1)
                        near[h, d + 1] += low_score[
                            block_rows(where_k), j * BLOCK : (j + 1) * BLOCK
                        ].astype(f32)

    pace = per_block // 2
    step = (blocks - 1) * per_block

    query_parts = [(start, QUERY_BLOCK) for start in range(0, rows - QUERY_BLOCK, QUERY_BLOCK)]
    query_parts += [(start, BLOCK) for start in range(rows - QUERY_BLOCK, rows, BLOCK)]
    for qb, (start, size) in enumerate(query_parts):
        for b in range(start // BLOCK, (start + size) // BLOCK):
            residual_back(b)
            if qb == 0:
                service(step)
                step += 1

        def back_head(h, carry, start=start, size=size, step=step, qb=qb):
            attend_back(start, size, h)
            serve(h * PACES[qb] + step, PACES[qb])
            return carry

        lax.fori_loop(0, heads, back_head, 0)
        step += heads * PACES[qb]
        if qb == 0:

            def early_weights(i, carry, step=step):
                feed_forward_weights(i)

                @pl.when(i < EARLY)
                def _():
                    service(i + step)

                return carry

            lax.fori_loop(0, groups, early_weights, 0)
            step += EARLY
            over_copy(0).start()
            flush(chunks - LAG, chunks)
        if qb == 1:
            reduce_send(0)

    other_keys = pl.ds(pl.multiple_of((1 - c) * rows, rows), rows)
    dkv_send[0] = dk[other_keys, 0:head_width].astype(bf16)
    dkv_send[1] = dv[other_keys, :].astype(bf16)
    dkv_copy = remote(dkv_send.at[...], dkv_recv.at[...], dkv_ssem.at[0], dkv_rsem.at[0], partner)
    dkv_copy.start()
    dkv_copy.wait_recv()
    dkv[:, 0:head_width] = (dk[own_keys, 0:head_width] + dkv_recv[0].astype(f32)).astype(bf16)
    dkv[:, head_width:] = (dv[own_keys, :] + dkv_recv[1].astype(f32)).astype(bf16)

    def project_back(b, carry):
        at = block_rows(b)
        total = contract(
            dq_t[:, at].T, wqo[:, :, 0:head_width].reshape(width, head_width), 1, 1
        )
        total = total + contract(dkv[at, :], wkv[...].reshape(width, 2 * head_width), 1, 1)
        snd[2, at, :] = total.astype(bf16)
        put_block(2, b)

        @pl.when(step + (b + 1) * pace <= 2 * chunks)
        def _():
            serve(step + b * pace, pace)

        return carry

    lax.fori_loop(0, blocks, project_back, 0)
    step += min(blocks, (2 * chunks - step) // pace) * pace

    def weights_back(i, carry):
        part_rows = n1t[pair_rows(i), :]
        mixed = contract(part_rows, dkv[...], 1, 0)
        store_grad(gsa, i, 0, mixed[:, 0:head_width])
        store_grad(gsa, i, 1, mixed[:, head_width:])
        store_grad(gsa, i, 2, contract(part_rows, dq_t[...], 1, 1))
        return carry

    serve(step, 2 * chunks - step)
    step = 2 * chunks

    def output_weights(i, carry):
        store_grad(gsa, i, 3, contract(turned[0, pair_rows(i), :], att_all[own_rows, :], 1, 1))
        return carry


    def bucket_sums(h, carry):
        for b in range(2 * half):
            summed_block = jnp.zeros((8, BLOCK), f32)
            for d in (-1, 0) if b < half else (0, 1):
                bucket = bucket_of(d * BLOCK + row_of - column_of)
                chosen = jnp.where(bucket == b, near[h, d + 1], 0.0)
                summed_block = summed_block + jnp.sum(
                    chosen.reshape(BLOCK // 8, 8, BLOCK), axis=0
                )
            pick[b : b + 1, :] = jnp.sum(summed_block, axis=0, keepdims=True)
        sums = contract(jnp.ones((8, BLOCK), f32), pick[...], 1, 1, highest)
        small[:, 0 : 2 * half] += jnp.where(iota((8, 2 * half), 0) == 2 + h, sums, 0.0)
        return carry

    def far_sums():
        tail = dk.shape[1] - BLOCK
        first_lane = head_width - tail
        column_sums = dk[:, tail:]
        block_row = iota((keys, BLOCK), 0)
        lane = iota((keys, BLOCK), 1)
        left_sum = jnp.zeros((1, BLOCK), f32)
        right_sum = jnp.zeros((1, BLOCK), f32)
        for j in range(query_blocks):
            mine = jnp.zeros((keys, BLOCK), jnp.bool_)
            for h in range(heads):
                mine = jnp.logical_or(mine, lane == first_lane + h * query_blocks + j)
            home = c * query_blocks + j
            is_left = jnp.logical_and(mine, block_row < (home - 1) * BLOCK)
            is_right = jnp.logical_and(mine, block_row >= (home + 2) * BLOCK)
            left_sum += jnp.sum(jnp.where(is_left, column_sums, 0.0), axis=0, keepdims=True)
            right_sum += jnp.sum(jnp.where(is_right, column_sums, 0.0), axis=0, keepdims=True)
        from_lane, to_lane = iota((BLOCK, BLOCK), 0), iota((BLOCK, BLOCK), 1)
        for h in range(heads):
            start = first_lane + h * query_blocks
            inside = jnp.logical_and(from_lane >= start, from_lane < start + query_blocks)
            left_pick = jnp.logical_and(inside, to_lane == far).astype(f32)
            right_pick = jnp.logical_and(inside, to_lane == half + far).astype(f32)
            small[2 + h : 3 + h, 0:BLOCK] += (
                contract(jnp.broadcast_to(left_sum, (8, BLOCK)), left_pick, 1, 0, highest)
                + contract(jnp.broadcast_to(right_sum, (8, BLOCK)), right_pick, 1, 0, highest)
            )[0:1]

    def block_store(n, source, target, b):
        at = block_rows(b)
        return pltpu.make_async_copy(source.at[at], target.at[at], store_sem.at[n])

    def input_back(b):
        totals_of(2, b)
        at = block_rows(b)
        grad_in = tot[2, at, :].astype(f32)
        xs = x_ref[at, :].astype(f32)
        inverse = inverse_rms(xs)
        u = xs * inverse
        g = grad_in * gain_rows[0:1, :]
        gin_ref[at, :] = grad_res[at, :] + inverse * (
            g - u * jnp.mean(g * u, axis=-1, keepdims=True)
        )
        block_store(7 + b, gin_ref, gin_hbm, b).start()

    def layer_out(b):
        totals_of(1, b)
        at = block_rows(b)
        out_ref[at, :] = (resid[at, :] + tot[1, at, :].astype(f32)).astype(bf16)
        block_store(7 + blocks + b, out_ref, out_hbm, b).start()

    small_copies = [
        remote(
            small.at[...], small_all.at[me], sm_send.at[k * 2 + kc - 1], sm_recv.at[k * 2 + kc - 1],
            (f ^ k, c ^ kc, t),
        )
        for k in range(groups)
        for kc in range(2)
        if k or kc
    ]

    def small_start():
        for copy in small_copies:
            copy.start()
        small_all[me] = small[...]

    def small_finish():
        for copy in small_copies:
            copy.wait_recv()
        total_small = small_all[0]
        for i in range(1, shards):
            total_small = total_small + small_all[i]
        to_own = (iota((width, BLOCK), 0) == iota((width, BLOCK), 1) + me * shard).astype(f32)
        own_gains = contract(total_small, to_own, 1, 0, highest)
        gain_two_out_ref[...] = own_gains[1:2, 0:shard]
        bias_out_ref[...] = total_small[2 : 2 + heads, 0 : 2 * half]

    gain_copies = [
        remote(
            gain_part.at[t], gain_part.at[t], gp_send.at[kt - 1], gp_recv.at[kt - 1], (f, c, t ^ kt)
        )
        for kt in range(1, 4)
    ]

    def gain_start():
        products = jnp.zeros((shard, head_width), f32)
        for a in members_of[2]:
            products = products + staged[a].astype(f32) * ga_ref[a]
        row_sums = contract(jnp.ones((8, head_width), f32), products, 1, 1, highest)
        gain_part[t, :, 0:shard] = row_sums / gain_one_ref[...].astype(f32)
        for copy in gain_copies:
            copy.start()

    def gain_finish():
        for copy in gain_copies:
            copy.wait_recv()
        total = gain_part[0, 0:1, 0:shard]
        for i in range(1, 4):
            total = total + gain_part[i, 0:1, 0:shard]
        gain_one_out_ref[...] = total

    @pl.when(outer)
    def _():
        lax.fori_loop(0, heads, bucket_sums, 0)
        far_sums()

    def at_step(n, value, run):
        pl.when(n == value)(run)

    def last_steps(n, carry):
        service(2 * chunks + n)

        @pl.when(n < groups)
        def _():
            weights_back(n, 0)

        def turn():
            over_copy(2).start()
            turned[0] = grl[...].T

        at_step(n, groups - 1, turn)

        @pl.when(jnp.logical_and(n >= groups, n < 2 * groups))
        def _():
            output_weights(n - groups, 0)

        at_step(n, groups + 1, functools.partial(reduce_send, 2))
        at_step(n, 2 * groups - 1, over_copy(1).start)
        at_step(n, 2 * groups + 1, functools.partial(reduce_send, 1))
        after = n - 2 * groups

        @pl.when(
            jnp.logical_and(
                jnp.logical_and(inner, lax.rem(n, 2) == 0),
                jnp.logical_and(after >= 0, after < 2 * heads),
            )
        )
        def _():
            bucket_sums(lax.div(after, 2), 0)

        def sums_out():
            pl.when(inner)(far_sums)
            small_start()

        at_step(n, 2 * groups + 2 * heads - 1, sums_out)
        for due_step, b in zip((6, 9, 13, 14), range(blocks)):

            @pl.when(n == due_step)
            def _(b=b):
                layer_out(b)

        at_step(n, chunks - 2, functools.partial(reduce_finish, 0))

        def gains():
            reduce_finish(2)
            gain_start()

        at_step(n, chunks, gains)
        at_step(n, chunks + 1, small_finish)
        at_step(n, chunks + 2, functools.partial(reduce_finish, 1))
        at_step(n, chunks + 3, gain_finish)

        due = n - (per_block - 1) - LAG

        @pl.when(jnp.logical_and(due >= 0, lax.rem(due, per_block) == 0))
        def _():
            input_back(lax.div(due, per_block))

        return carry

    lax.fori_loop(0, chunks + LAG, last_steps, 0)
    for b in range(blocks):
        block_store(7 + b, gin_ref, gin_hbm, b).wait()
        block_store(7 + blocks + b, out_ref, out_hbm, b).wait()
    for n in range(3):
        for copy in part_stores(n):
            copy.wait()
    for copy in small_copies + gain_copies:
        copy.wait_send()
    for g in range(6):
        gather_drain(g)
    for copy in out_copies:
        copy.wait_send()
    lax.fori_loop(0, blocks, attended_drain, 0)
    for k in range(1, 4):
        gain_copy(k).wait_send()
    for k in range(4):
        gain_over(k).wait_send()
    for copy in kv_copies:
        copy.wait_send()
    dkv_copy.wait_send()
    drain_all()
    for n in range(3):
        reduce_drain(n)


def fused_layer(shards, x, cot, ids, gain_one, gain_two, weights, table):
    rows, width = x.shape
    shard, head_width = weights[0].shape
    units = weights[4].shape[1]
    keys = ids.shape[1]
    heads = head_width // DH
    groups = shards // 2
    chunks = rows // CHUNK
    padded = head_width + (-head_width) % BLOCK
    if padded - head_width < heads * (rows // BLOCK):
        padded += BLOCK
    vmem, dma = pltpu.VMEM, pltpu.SemaphoreType.DMA
    out_shape = (
        jax.ShapeDtypeStruct((rows, width), bf16),
        jax.ShapeDtypeStruct((rows, width), f32),
        *[jax.ShapeDtypeStruct((shard, head_width), f32)] * 4,
        *[jax.ShapeDtypeStruct((shard, units), f32)] * 3,
        jax.ShapeDtypeStruct((1, shard), f32),
        jax.ShapeDtypeStruct((1, shard), f32),
        jax.ShapeDtypeStruct(table.shape, f32),
    )
    in_vmem = pl.BlockSpec(memory_space=pltpu.VMEM)
    anywhere = pl.BlockSpec(memory_space=pl.ANY)
    scratch = [
        vmem((rows, width), bf16),
        vmem((rows, width), bf16),
        vmem((rows, width), bf16),
        vmem((rows, width), f32),
        vmem((4, shard, head_width), f32),
        vmem((3, shard, units), f32),
        vmem((4, shard, head_width), bf16),
        vmem((shards, shard, 2 * head_width), bf16),
        vmem((shards, shard, 2 * head_width), bf16),
        vmem((shards, shard, 3 * head_width), bf16),
        vmem((3, shard, head_width), bf16),
        vmem((4, width, head_width), bf16),
        vmem((shards, 3, shard, units), bf16),
        vmem((shards, 8, BLOCK), f32),
        vmem((8, width), f32),
        vmem((heads, 5, BLOCK, BLOCK), f32),
        vmem((heads, keys, rows), f32),
        vmem((keys, QUERY_BLOCK), f32),
        vmem((heads, keys, rows), bf16),
        vmem((keys, QUERY_BLOCK), bf16),
        vmem((3, rows, width), bf16),
        vmem((3, rows, width), bf16),
        vmem((3, rows, width), bf16),
        vmem((rows, width), f32),
        vmem((rows, width), f32),
        vmem((rows, width), bf16),
        vmem((rows, width), bf16),
        vmem((rows, width), bf16),
        vmem((width, rows), bf16),
        vmem((2, width, rows), bf16),
        vmem((rows, units), bf16),
        vmem((rows, units), bf16),
        vmem((rows, units), bf16),
        vmem((head_width, rows), bf16),
        vmem((keys, head_width), bf16),
        vmem((keys, head_width), bf16),
        vmem((head_width, keys), bf16),
        vmem((head_width, keys), bf16),
        vmem((4 * head_width, rows), bf16),
        vmem((head_width, rows), bf16),
        vmem((head_width, rows), bf16),
        vmem((heads, 8, rows), f32),
        vmem((heads, 8, rows), f32),
        vmem((keys, padded), f32),
        vmem((keys, head_width), f32),
        vmem((heads, 3, BLOCK, BLOCK), f32),
        vmem((table.shape[1], BLOCK), f32),
        vmem((2, rows, head_width), bf16),
        vmem((2, rows, head_width), bf16),
        vmem((rows, 2 * head_width), bf16),
        vmem((groups, 2, 4, shard, head_width), bf16),
        vmem((groups, 2, 3, shard, units), bf16),
        vmem((groups, 4, shard, head_width), bf16),
        vmem((groups, 3, shard, units), bf16),
        vmem((groups, 4, shard, head_width), bf16),
        vmem((groups, 3, shard, units), bf16),
        vmem((groups - 1, 4, shard, head_width), bf16),
        vmem((groups - 1, 3, shard, units), bf16),
        vmem((8, width), f32),
        vmem((shards, 8, width), f32),
        vmem((4, 8, BLOCK), f32),
        dma((9,)),
        dma((7 + 2 * (rows // BLOCK),)),
        dma((7, 8)),
        dma((7, 8)),
        dma((3,)),
        dma((3,)),
        dma((5, rows // BLOCK)),
        dma((4, rows // BLOCK)),
        dma((2,)),
        dma((2,)),
        dma((3, chunks)),
        dma((3, chunks)),
        dma((3, chunks)),
        dma((3, chunks)),
        dma((1,)),
        dma((1,)),
        dma((3,)),
        dma((3,)),
        dma((3, groups)),
        dma((3, groups)),
        dma((shards,)),
        dma((shards,)),
        dma((3,)),
        dma((3,)),
    ]
    return pl.pallas_call(
        functools.partial(layer_kernel, shards),
        out_shape=out_shape,
        in_specs=[anywhere] * 2
        + [in_vmem] * 3
        + [anywhere] * 7
        + [pl.BlockSpec(memory_space=pltpu.SMEM)],
        out_specs=[anywhere] * 9 + [in_vmem] * 3,
        scratch_shapes=scratch,
        name="layer",
        compiler_params=pltpu.CompilerParams(
            collective_id=0, has_side_effects=True, vmem_limit_bytes=63 << 20
        ),
    )(x, cot, ids, gain_one, gain_two, *weights, table)


def publish_kernel(count, *refs):
    sources, targets = refs[:count], refs[count : 2 * count]
    held, in_sem, out_sem = refs[2 * count : 3 * count], refs[3 * count], refs[3 * count + 1]
    inward = [
        pltpu.make_async_copy(sources[i], held[i], in_sem.at[i]) for i in range(count)
    ]
    outward = [
        pltpu.make_async_copy(held[i], targets[i], out_sem.at[i]) for i in range(count)
    ]
    for copy in inward:
        copy.start()
    for arriving, leaving in zip(inward, outward):
        arriving.wait()
        leaving.start()
    for copy in outward:
        copy.wait()


def publish(values):
    count = len(values)
    anywhere = pl.BlockSpec(memory_space=pl.ANY)
    return pl.pallas_call(
        functools.partial(publish_kernel, count),
        out_shape=[jax.ShapeDtypeStruct(value.shape, value.dtype) for value in values],
        in_specs=[anywhere] * count,
        out_specs=[anywhere] * count,
        scratch_shapes=[pltpu.VMEM(value.shape, value.dtype) for value in values]
        + [pltpu.SemaphoreType.DMA((count,))] * 2,
        name="publish",
    )(*values)


def on_device_fused(
    layer_input,
    doc_ids,
    query_weight,
    key_weight,
    value_weight,
    output_weight,
    gate_weight,
    up_weight,
    down_weight,
    first_gain,
    second_gain,
    position_bias,
    cotangent,
):
    shards = lax.axis_size("fsdp") * lax.axis_size("ctx")
    outs = fused_layer(
        shards,
        layer_input[0],
        cotangent[0],
        doc_ids,
        first_gain[None],
        second_gain[None],
        (
            query_weight,
            key_weight,
            value_weight,
            output_weight,
            gate_weight,
            up_weight,
            down_weight,
        ),
        position_bias.T,
    )
    outs = publish(outs)
    return (
        outs[0][None],
        outs[1][None],
        *outs[2:9],
        outs[9][0],
        outs[10][0],
        outs[11].T,
    )


def fits_kernel(mesh):
    return mesh.shape["ctx"] == 2 and mesh.shape["tp"] == 4 and mesh.shape["fsdp"] == 4


def solution(mesh):
    return jax.shard_map(
        on_device_fused if fits_kernel(mesh) else on_device,
        mesh=mesh,
        in_specs=(
            P("fsdp", "ctx", None),
            P("fsdp", None),
            P(("fsdp", "ctx"), "tp"),
            P(("fsdp", "ctx"), "tp"),
            P(("fsdp", "ctx"), "tp"),
            P(("fsdp", "ctx"), "tp"),
            P(("fsdp", "ctx"), "tp"),
            P(("fsdp", "ctx"), "tp"),
            P(("fsdp", "ctx"), "tp"),
            P(("fsdp", "ctx")),
            P(("fsdp", "ctx")),
            P(None, "tp"),
            P("fsdp", "ctx", None),
        ),
        out_specs=(
            P("fsdp", "ctx", None),
            P("fsdp", "ctx", None),
            P(("fsdp", "ctx"), "tp"),
            P(("fsdp", "ctx"), "tp"),
            P(("fsdp", "ctx"), "tp"),
            P(("fsdp", "ctx"), "tp"),
            P(("fsdp", "ctx"), "tp"),
            P(("fsdp", "ctx"), "tp"),
            P(("fsdp", "ctx"), "tp"),
            P(("fsdp", "ctx")),
            P(("fsdp", "ctx")),
            P(None, "tp"),
        ),
        check_vma=False,
    )
```

```python
import functools

import jax
import jax.numpy as jnp
from jax import lax
from jax.experimental import pallas as pl
from jax.experimental.pallas import tpu as pltpu
from jax.sharding import PartitionSpec as P

DH = 64


epsilon = 1e-06
masked_score = -1000000000.0
bucket_edges = (12, 16, 23, 32, 46, 64, 91)
highest = lax.Precision.HIGHEST


def bucket_of(relative):
    distance = jnp.abs(relative)
    beyond = jnp.zeros_like(distance) + 8
    for edge_value in bucket_edges:
        beyond = beyond + (distance >= edge_value).astype(jnp.int32)
    inside = jnp.where(distance < 8, distance, beyond)
    return jnp.where(relative > 0, 16, 0) + inside


def rms_norm(values, gain_vector):
    inverse = lax.rsqrt(jnp.mean(values * values, axis=-1, keepdims=True) + epsilon)
    return values * inverse * gain_vector


def gated_unit(gate_in, up_in):
    return jax.nn.gelu(gate_in, approximate=True) * up_in


def relative_bias(bias_table, query_rows, key_rows, offset):
    span_width = key_rows + query_rows
    relative = lax.iota(jnp.int32, span_width) - (query_rows - 1) - offset
    one_hot = (
        bucket_of(relative)[:, None] == lax.iota(jnp.int32, bias_table.shape[0])[None, :]
    ).astype(jnp.float32)
    per_shift = jnp.dot(one_hot, bias_table, precision=highest).T
    heads_here = bias_table.shape[1]
    toeplitz = jnp.broadcast_to(per_shift[:, None, :], (heads_here, query_rows, span_width))
    toeplitz = toeplitz.reshape(heads_here, query_rows * span_width)[
        :, : query_rows * (span_width - 1)
    ]
    toeplitz = toeplitz.reshape(heads_here, query_rows, span_width - 1)
    return (toeplitz[:, :, query_rows - 1 : query_rows - 1 + key_rows], one_hot)


def diagonal_sums(grad_scores, query_rows, key_rows):
    heads_here = grad_scores.shape[0]
    span_width = key_rows + query_rows
    placed = jnp.pad(grad_scores, ((0, 0), (0, 0), (query_rows - 1, 0)))
    placed = placed.reshape(heads_here, query_rows * (span_width - 1))
    placed = jnp.pad(placed, ((0, 0), (0, query_rows)))
    return jnp.sum(placed.reshape(heads_here, query_rows, span_width), axis=1)


def on_device(
    layer_input,
    doc_ids,
    query_weight,
    key_weight,
    value_weight,
    output_weight,
    gate_weight,
    up_weight,
    down_weight,
    first_gain,
    second_gain,
    position_bias,
    cotangent,
):
    query_rows = layer_input.shape[1]
    key_rows = query_rows * lax.axis_size("ctx")
    heads_here = position_bias.shape[1]
    head_width = heads_here * DH
    offset = lax.axis_index("ctx") * query_rows
    everything = (
        query_weight,
        key_weight,
        value_weight,
        output_weight,
        gate_weight,
        up_weight,
        down_weight,
        first_gain,
        second_gain,
    )
    (
        full_query,
        full_key,
        full_value,
        full_output,
        full_gate,
        full_up,
        full_down,
        gain_one,
        gain_two,
    ) = (
        lax.all_gather(everything[0], ("fsdp", "ctx"), axis=0, tiled=True),
        lax.all_gather(everything[1], ("fsdp", "ctx"), axis=0, tiled=True),
        lax.all_gather(everything[2], ("fsdp", "ctx"), axis=0, tiled=True),
        lax.all_gather(everything[3], ("fsdp", "ctx"), axis=0, tiled=True),
        lax.all_gather(everything[4], ("fsdp", "ctx"), axis=0, tiled=True),
        lax.all_gather(everything[5], ("fsdp", "ctx"), axis=0, tiled=True),
        lax.all_gather(everything[6], ("fsdp", "ctx"), axis=0, tiled=True),
        lax.all_gather(everything[7], ("fsdp", "ctx"), axis=0, tiled=True),
        lax.all_gather(everything[8], ("fsdp", "ctx"), axis=0, tiled=True),
    )
    inputs = layer_input.astype(jnp.float32)
    gain_first = gain_one.astype(jnp.float32)
    gain_second = gain_two.astype(jnp.float32)
    normed_one = rms_norm(inputs, gain_first).astype(jnp.bfloat16)
    queries = jnp.dot(normed_one, full_query, preferred_element_type=jnp.float32).astype(
        jnp.bfloat16
    )
    keys_local = jnp.dot(normed_one, full_key, preferred_element_type=jnp.float32).astype(
        jnp.bfloat16
    )
    values_local = jnp.dot(normed_one, full_value, preferred_element_type=jnp.float32).astype(
        jnp.bfloat16
    )
    keys_all, values_all = (
        lax.all_gather(keys_local, "ctx", axis=1, tiled=True),
        lax.all_gather(values_local, "ctx", axis=1, tiled=True),
    )
    bias_block, one_hot = relative_bias(position_bias, query_rows, key_rows, offset)

    def scores_of(query_heads, key_heads, id_row):
        raw_scores = jnp.einsum(
            "qhd,khd->hqk", query_heads, key_heads, preferred_element_type=jnp.float32
        )
        own_ids = lax.dynamic_slice_in_dim(id_row, offset, query_rows)
        same_doc = own_ids[:, None] == id_row[None, :]
        return jnp.where(same_doc[None], raw_scores + bias_block, masked_score)

    def forward_one(packed):
        query_seq, key_seq, value_seq, id_row = packed
        scores = scores_of(
            query_seq.reshape(query_rows, heads_here, DH),
            key_seq.reshape(key_rows, heads_here, DH),
            id_row,
        )
        row_max = jnp.max(scores, axis=-1, keepdims=True)
        exponentials = jnp.exp(scores - row_max)
        row_total = jnp.sum(exponentials, axis=-1, keepdims=True)
        probabilities = (exponentials / row_total).astype(jnp.bfloat16)
        attended = jnp.einsum(
            "hqk,khd->qhd",
            probabilities,
            value_seq.reshape(key_rows, heads_here, DH),
            preferred_element_type=jnp.float32,
        )
        log_row = row_max[..., 0] + jnp.log(row_total[..., 0])
        return (attended.reshape(query_rows, head_width).astype(jnp.bfloat16), log_row)

    attended, log_sums = lax.map(forward_one, (queries, keys_all, values_all, doc_ids))
    attention_terms = jnp.einsum(
        "sqe,de->sqd", attended, full_output, preferred_element_type=jnp.float32
    )
    residual = inputs + lax.psum(attention_terms.astype(jnp.bfloat16), "tp").astype(jnp.float32)
    normed_two = rms_norm(residual, gain_second).astype(jnp.bfloat16)
    gate_pre = jnp.dot(normed_two, full_gate, preferred_element_type=jnp.float32)
    up_pre = jnp.dot(normed_two, full_up, preferred_element_type=jnp.float32)
    activated = gated_unit(gate_pre, up_pre).astype(jnp.bfloat16)
    ffn_terms = jnp.einsum("sqf,df->sqd", activated, full_down, preferred_element_type=jnp.float32)
    output_rows = (
        residual + lax.psum(ffn_terms.astype(jnp.bfloat16), "tp").astype(jnp.float32)
    ).astype(jnp.bfloat16)
    grad_activated = jnp.einsum(
        "sqd,df->sqf", cotangent, full_down, preferred_element_type=jnp.float32
    )
    down_grad = jnp.einsum("sqd,sqf->df", cotangent, activated, preferred_element_type=jnp.float32)
    gated_value, gated_back = jax.vjp(gated_unit, gate_pre, up_pre)
    grad_gate, grad_up = gated_back(grad_activated)
    grad_gate = grad_gate.astype(jnp.bfloat16)
    grad_up = grad_up.astype(jnp.bfloat16)
    gate_grad = jnp.einsum("sqd,sqf->df", normed_two, grad_gate, preferred_element_type=jnp.float32)
    up_grad = jnp.einsum("sqd,sqf->df", normed_two, grad_up, preferred_element_type=jnp.float32)
    normed_two_terms = jnp.einsum(
        "sqf,df->sqd", grad_gate, full_gate, preferred_element_type=jnp.float32
    ) + jnp.einsum("sqf,df->sqd", grad_up, full_up, preferred_element_type=jnp.float32)
    grad_normed_two = lax.psum(normed_two_terms.astype(jnp.bfloat16), "tp").astype(jnp.float32)
    second_value, second_back = jax.vjp(rms_norm, residual, gain_second)
    grad_residual, second_gain_grad = second_back(grad_normed_two)
    grad_residual = grad_residual + cotangent.astype(jnp.float32)
    grad_low = grad_residual.astype(jnp.bfloat16)
    grad_attended = jnp.einsum(
        "sqd,de->sqe", grad_low, full_output, preferred_element_type=jnp.float32
    ).astype(jnp.bfloat16)
    output_grad = jnp.einsum("sqd,sqe->de", grad_low, attended, preferred_element_type=jnp.float32)

    def backward_one(running, packed):
        query_seq, key_seq, value_seq, id_row, grad_seq, log_row = packed
        query_heads = query_seq.reshape(query_rows, heads_here, DH)
        key_heads = key_seq.reshape(key_rows, heads_here, DH)
        value_heads = value_seq.reshape(key_rows, heads_here, DH)
        grad_heads = grad_seq.reshape(query_rows, heads_here, DH)
        scores = scores_of(query_heads, key_heads, id_row)
        probabilities = jnp.exp(scores - log_row[..., None])
        grad_probs = jnp.einsum(
            "qhd,khd->hqk", grad_heads, value_heads, preferred_element_type=jnp.float32
        )
        grad_values = jnp.einsum(
            "hqk,qhd->khd",
            probabilities.astype(jnp.bfloat16),
            grad_heads,
            preferred_element_type=jnp.float32,
        )
        grad_scores = probabilities * (
            grad_probs - jnp.sum(probabilities * grad_probs, axis=-1, keepdims=True)
        )
        low_scores = grad_scores.astype(jnp.bfloat16)
        grad_queries = jnp.einsum(
            "hqk,khd->qhd", low_scores, key_heads, preferred_element_type=jnp.float32
        )
        grad_keys = jnp.einsum(
            "hqk,qhd->khd", low_scores, query_heads, preferred_element_type=jnp.float32
        )
        running = running + diagonal_sums(grad_scores, query_rows, key_rows)
        return (
            running,
            (
                grad_queries.reshape(query_rows, head_width).astype(jnp.bfloat16),
                grad_keys.reshape(key_rows, head_width),
                grad_values.reshape(key_rows, head_width),
            ),
        )

    shift_grads, (grad_queries, key_parts, value_parts) = lax.scan(
        backward_one,
        jnp.zeros((heads_here, query_rows + key_rows), jnp.float32),
        (queries, keys_all, values_all, doc_ids, grad_attended, log_sums),
    )
    grad_keys, grad_values = (
        lax.psum_scatter(
            key_parts.astype(jnp.bfloat16), "ctx", scatter_dimension=1, tiled=True
        ).astype(jnp.float32),
        lax.psum_scatter(
            value_parts.astype(jnp.bfloat16), "ctx", scatter_dimension=1, tiled=True
        ).astype(jnp.float32),
    )
    grad_keys = grad_keys.astype(jnp.bfloat16)
    grad_values = grad_values.astype(jnp.bfloat16)
    normed_one_terms = (
        jnp.einsum("sqe,de->sqd", grad_queries, full_query, preferred_element_type=jnp.float32)
        + jnp.einsum("sqe,de->sqd", grad_keys, full_key, preferred_element_type=jnp.float32)
        + jnp.einsum("sqe,de->sqd", grad_values, full_value, preferred_element_type=jnp.float32)
    )
    grad_normed_one = lax.psum(normed_one_terms.astype(jnp.bfloat16), "tp").astype(jnp.float32)
    query_grad = jnp.einsum(
        "sqd,sqe->de", normed_one, grad_queries, preferred_element_type=jnp.float32
    )
    key_grad = jnp.einsum("sqd,sqe->de", normed_one, grad_keys, preferred_element_type=jnp.float32)
    value_grad = jnp.einsum(
        "sqd,sqe->de", normed_one, grad_values, preferred_element_type=jnp.float32
    )
    first_value, first_back = jax.vjp(rms_norm, inputs, gain_first)
    grad_inputs, first_gain_grad = first_back(grad_normed_one)
    input_rows = grad_residual + grad_inputs
    bias_gradient = lax.psum(jnp.dot(one_hot.T, shift_grads.T, precision=highest), ("fsdp", "ctx"))
    (
        query_total,
        key_total,
        value_total,
        output_total,
        gate_total,
        up_total,
        down_total,
        first_total,
        second_total,
    ) = (
        lax.psum_scatter(query_grad, ("fsdp", "ctx"), scatter_dimension=0, tiled=True),
        lax.psum_scatter(key_grad, ("fsdp", "ctx"), scatter_dimension=0, tiled=True),
        lax.psum_scatter(value_grad, ("fsdp", "ctx"), scatter_dimension=0, tiled=True),
        lax.psum_scatter(output_grad, ("fsdp", "ctx"), scatter_dimension=0, tiled=True),
        lax.psum_scatter(gate_grad, ("fsdp", "ctx"), scatter_dimension=0, tiled=True),
        lax.psum_scatter(up_grad, ("fsdp", "ctx"), scatter_dimension=0, tiled=True),
        lax.psum_scatter(down_grad, ("fsdp", "ctx"), scatter_dimension=0, tiled=True),
        lax.psum_scatter(first_gain_grad, ("fsdp", "ctx"), scatter_dimension=0, tiled=True),
        lax.psum_scatter(second_gain_grad, ("fsdp", "ctx"), scatter_dimension=0, tiled=True),
    )
    return (
        output_rows,
        input_rows,
        query_total,
        key_total,
        value_total,
        output_total,
        gate_total,
        up_total,
        down_total,
        first_total,
        second_total,
        bias_gradient,
    )


MESH = pl.DeviceIdType.MESH
bf16, f32 = jnp.bfloat16, jnp.float32
BLOCK = 128
QUERY_BLOCK = 256
FORWARD_BLOCK = 256
CHUNK = 32
LAG = 4
RELAY_ROWS = 32
EARLY = 4
PACES = (1, 2, 1)


def contract(left, right, left_dim, right_dim, precision=None):
    return lax.dot_general(
        left,
        right,
        (((left_dim,), (right_dim,)), ((), ())),
        preferred_element_type=f32,
        precision=precision,
    )


def iota(shape, dim):
    return lax.broadcasted_iota(jnp.int32, shape, dim)


def layer_kernel(
    shards,
    x_hbm,
    cot_hbm,
    ids_ref,
    gain_one_ref,
    gain_two_ref,
    wq_ref,
    wk_ref,
    wv_ref,
    wo_ref,
    wg_ref,
    wu_ref,
    wd_ref,
    table_ref,
    out_hbm,
    gin_hbm,
    gq_hbm,
    gk_hbm,
    gv_hbm,
    go_hbm,
    gg_hbm,
    gu_hbm,
    gd_hbm,
    gain_one_out_ref,
    gain_two_out_ref,
    bias_out_ref,
    x_ref,
    cot_ref,
    out_ref,
    gin_ref,
    ga_ref,
    gf_ref,
    staged,
    wkv,
    wqo,
    wo3,
    other_out,
    wo_all,
    wf,
    gains_all,
    gain_rows,
    tiles,
    masked_bias,
    score,
    expo,
    low_score,
    snd,
    part,
    tot,
    resid,
    grad_res,
    n1,
    n2,
    grl,
    n1t,
    turned,
    act,
    ggate,
    gup,
    q_t,
    k_all,
    v_all,
    k_t,
    v_t,
    att_all,
    dos_t,
    dq_t,
    linv,
    delta,
    dk,
    dv,
    near,
    pick,
    dkv_send,
    dkv_recv,
    dkv,
    gsa,
    gsf,
    ra,
    rf,
    sa,
    sf,
    ra2,
    rf2,
    small,
    small_all,
    gain_part,
    load_sem,
    store_sem,
    ag_send,
    ag_recv,
    zo_send,
    zo_recv,
    at_send,
    at_recv,
    kv_send,
    kv_recv,
    s1,
    r1,
    s2,
    r2,
    dkv_ssem,
    dkv_rsem,
    rs_send,
    rs_recv,
    rs2_send,
    rs2_recv,
    sm_send,
    sm_recv,
    gp_send,
    gp_recv,
):
    groups = shards // 2
    f, c, t = lax.axis_index("fsdp"), lax.axis_index("ctx"), lax.axis_index("tp")
    me = f * 2 + c
    rows, width = x_ref.shape
    keys = k_all.shape[0]
    head_width = wq_ref.shape[1]
    heads = head_width // DH
    units = wg_ref.shape[1]
    shard = wq_ref.shape[0]
    chunks = rows // CHUNK
    per_block = BLOCK // CHUNK
    partner = (f, 1 - c, t)
    outer = jnp.logical_or(t == 0, t == 3)
    inner = jnp.logical_or(t == 1, t == 2)
    near_end = jnp.where(t < 2, 1, 2)
    far_end = jnp.where(t < 2, 0, 3)
    middle = 3 - t

    def remote(source, target, send_sem, recv_sem, device):
        return pltpu.make_async_remote_copy(
            src_ref=source,
            dst_ref=target,
            send_sem=send_sem,
            recv_sem=recv_sem,
            device_id=device,
            device_id_type=MESH,
        )

    barrier = pltpu.get_barrier_semaphore()
    for k in range(groups):
        for kc in range(2):
            if k or kc:
                pl.semaphore_signal(
                    barrier, inc=1, device_id=(f ^ k, c ^ kc, t), device_id_type=MESH
                )

    for kt in range(1, 4):
        pl.semaphore_signal(
            barrier, inc=1, device_id=(f, c, t ^ kt), device_id_type=MESH
        )
    loads = [
        pltpu.make_async_copy(source, target, load_sem.at[n])
        for n, (source, target) in enumerate(
            (
                (wk_ref, staged.at[0]),
                (wv_ref, staged.at[1]),
                (wq_ref, staged.at[2]),
                (wo_ref, staged.at[3]),
                (x_hbm, x_ref),
                (wg_ref, wf.at[me, 0]),
                (wu_ref, wf.at[me, 1]),
                (wd_ref, wf.at[me, 2]),
                (cot_hbm, cot_ref),
            )
        )
    ]
    for copy in loads:
        copy.start()
    gains_all[me] = jnp.zeros((8, BLOCK), f32)
    gains_all[me, 0:1, 0:shard] = gain_one_ref[...].astype(f32)
    gains_all[me, 1:2, 0:shard] = gain_two_ref[...].astype(f32)
    for copy in loads[:4]:
        copy.wait()
    wkv[me, :, 0:head_width] = staged[0]
    wkv[me, :, head_width:] = staged[1]
    wqo[me, :, 0:head_width] = staged[2]
    wqo[me, :, head_width:] = staged[3]
    pl.semaphore_wait(barrier, shards - 1 + 3)

    def piece(g, index):
        if g < 2:
            return (wkv, wqo)[g].at[index]
        return wo3.at[index] if g == 5 else wf.at[index, g - 2]

    def half_piece(g, index, n):
        return piece(g, index).at[n * (shard // 2) : (n + 1) * (shard // 2)]

    def own_copy(g, k):
        view = piece(g, me)
        return remote(view, view, ag_send.at[g, k - 1], ag_recv.at[g, k - 1], (f ^ k, c, t))

    def pass_copy(g, k):
        view = half_piece(g, (f ^ k) * 2 + c, k - 1)
        return remote(view, view, ag_send.at[g, k + 1], ag_recv.at[g, k + 1], (f ^ (3 - k), c, t))

    def over_piece(g, k):
        view = piece(g, (f ^ k) * 2 + c)
        return remote(view, view, ag_send.at[g, 4 + k], ag_recv.at[g, 4 + k], partner)

    def gather_own(g):
        for k in (1, 2):
            own_copy(g, k).start()
        over_piece(g, 0).start()

    def gather_pass(g):
        for k in (1, 2):
            own_copy(g, k).wait_recv()
            pass_copy(g, k).start()
            over_piece(g, k).start()

    def gather_corner(g):
        for k in (1, 2):
            pass_copy(g, k).wait_recv()
        over_piece(g, 3).start()

    def gather_finish(g):
        for k in range(4):
            over_piece(g, k).wait_recv()

    def gather_drain(g):
        for k in (1, 2):
            own_copy(g, k).wait_send()
            pass_copy(g, k).wait_send()
        for k in range(4):
            over_piece(g, k).wait_send()

    def gain_copy(k):
        view = gains_all.at[me]
        return remote(view, view, ag_send.at[6, k], ag_recv.at[6, k], (f ^ k, c, t))

    def gain_over(k):
        view = gains_all.at[(f ^ k) * 2 + c]
        return remote(view, view, ag_send.at[6, 4 + k], ag_recv.at[6, 4 + k], partner)

    def span(j):
        if isinstance(j, int):
            return pl.ds(j * CHUNK, CHUNK)
        return pl.ds(pl.multiple_of(j * CHUNK, CHUNK), CHUNK)

    def end_copy(a, j):
        return remote(
            snd.at[a, span(j)], part.at[a, span(j)], s1.at[a, j], r1.at[a, j], (f, c, near_end)
        )

    def mid_copy(a, j):
        return remote(
            snd.at[a, span(j)], tot.at[a, span(j)], s1.at[a, j], r2.at[a, j], (f, c, middle)
        )

    def total_copy(a, j):
        return remote(
            tot.at[a, span(j)], tot.at[a, span(j)], s2.at[a, j], r2.at[a, j], (f, c, far_end)
        )

    def add_rows(target, a, j, left, right):
        def body(r, carry):
            at = pl.ds(pl.multiple_of(j * CHUNK + r * RELAY_ROWS, RELAY_ROWS), RELAY_ROWS)
            target[a, at] = (left[a, at].astype(f32) + right[a, at].astype(f32)).astype(bf16)
            return carry

        lax.fori_loop(0, CHUNK // RELAY_ROWS, body, 0)

    def flush(first, last):
        @pl.when(inner)
        def _():
            for n in range(first, last):
                a, j = divmod(n, chunks)
                mid_copy(a, j).wait_recv()
                add_rows(tot, a, j, snd, tot)
                total_copy(a, j).start()

    def service(step):
        def total_step():
            a, j = split(step - LAG)
            mid_copy(a, j).wait_recv()
            add_rows(tot, a, j, snd, tot)
            total_copy(a, j).start()

        def middle_step():
            a, j = split(step)
            end_copy(a, j).wait_recv()
            add_rows(snd, a, j, snd, part)
            mid_copy(a, j).start()

        def split(n):
            if isinstance(n, int):
                return divmod(n, chunks)
            return lax.div(n, chunks), lax.rem(n, chunks)

        if isinstance(step, int):
            if step >= LAG and not chunks <= step < chunks + LAG:
                pl.when(inner)(total_step)
            if step < 3 * chunks:
                pl.when(inner)(middle_step)
        else:
            flushed = jnp.logical_and(step >= chunks, step < chunks + LAG)
            due = jnp.logical_and(step >= LAG, jnp.logical_not(flushed))
            pl.when(jnp.logical_and(inner, due))(total_step)
            pl.when(jnp.logical_and(inner, step < 3 * chunks))(middle_step)

    def serve(start, count):
        for n in range(count):
            service(start + n)

    def put_block(a, b):
        @pl.when(outer)
        def _():
            for j in range(per_block):
                end_copy(a, b * per_block + j).start()

    def totals_of(a, b):
        @pl.when(outer)
        def _():
            for j in range(per_block):
                total_copy(a, b * per_block + j).wait_recv()

    def drain_all():
        def body(n, carry):
            a, j = lax.div(n, chunks), lax.rem(n, chunks)

            @pl.when(outer)
            def _():
                end_copy(a, j).wait_send()

            @pl.when(inner)
            def _():
                mid_copy(a, j).wait_send()
                total_copy(a, j).wait_send()

            return carry

        lax.fori_loop(0, 3 * chunks, body, 0)

    for k in range(1, 4):
        gain_copy(k).start()
    gain_over(0).start()
    gather_own(0)
    gather_own(1)
    out_copies = [
        remote(
            staged.at[3], other_out.at[k - 1], zo_send.at[k - 1], zo_recv.at[k - 1], (f, c, t ^ k)
        )
        for k in range(1, 4)
    ]
    for copy in out_copies:
        copy.start()

    half = table_ref.shape[1] // 2
    far = half - 1
    row_of, column_of = iota((BLOCK, BLOCK), 0), iota((BLOCK, BLOCK), 1)
    for h in range(heads):
        tiles[h, 0] = jnp.full((BLOCK, BLOCK), table_ref[h, far], f32)
        tiles[h, 4] = jnp.full((BLOCK, BLOCK), table_ref[h, half + far], f32)
    for d in (-1, 0, 1):
        bucket = bucket_of(d * BLOCK + row_of - column_of)
        members = range(half) if d < 0 else range(half, 2 * half) if d > 0 else range(2 * half)

        def per_head(h, carry, bucket=bucket, members=members, d=d):
            filled = jnp.zeros((BLOCK, BLOCK), f32)
            for b in members:
                filled = jnp.where(bucket == b, table_ref[h, b], filled)
            tiles[h, d + 2] = filled
            return carry

        lax.fori_loop(0, heads, per_head, 0)

    def bias_rows(kb, carry):
        key_rows = pl.ds(pl.multiple_of(kb * BLOCK, BLOCK), BLOCK)
        key_ids = jnp.broadcast_to(ids_ref[0:1, key_rows].astype(f32), (BLOCK, BLOCK)).T
        for qb in range(rows // BLOCK):
            start = pl.multiple_of(c * rows + qb * BLOCK, BLOCK)
            query_ids = ids_ref[0:1, pl.ds(start, BLOCK)].astype(f32)
            same = key_ids == query_ids
            d = jnp.clip(kb - c * (rows // BLOCK) - qb, -2, 2) + 2
            for h in range(heads):
                masked_bias[h, key_rows, qb * BLOCK : (qb + 1) * BLOCK] = jnp.where(
                    same, tiles[h, d], masked_score
                )
        return carry

    key_blocks = keys // BLOCK
    lax.fori_loop(0, key_blocks // 4, bias_rows, 0)
    for k in range(1, 4):
        gain_copy(k).wait_recv()
        gain_over(k).start()
    gather_pass(0)
    lax.fori_loop(key_blocks // 4, key_blocks // 2, bias_rows, 0)
    gather_pass(1)
    for copy in loads[4:]:
        copy.wait()
    gather_own(2)
    gather_own(3)
    for k in range(4):
        gain_over(k).wait_recv()
    spread = jnp.zeros((8, width), f32)
    for i in range(shards):
        one_hot = (iota((BLOCK, width), 1) == iota((BLOCK, width), 0) + i * shard).astype(f32)
        spread = spread + contract(gains_all[i].astype(bf16), one_hot.astype(bf16), 1, 0)
    gain_rows[...] = spread

    def block_rows(b, size=BLOCK):
        if isinstance(b, int):
            return pl.ds(b * size, size)
        return pl.ds(pl.multiple_of(b * size, size), size)

    def inverse_rms(values):
        return lax.rsqrt(jnp.mean(values * values, axis=-1, keepdims=True) + epsilon)

    def norm_one(b, carry):
        at = block_rows(b)
        xs = x_ref[at, :].astype(f32)
        n1[at, :] = (xs * inverse_rms(xs) * gain_rows[0:1, :]).astype(bf16)
        return carry

    lax.fori_loop(0, rows // BLOCK, norm_one, 0)

    def weight(buffer, a):
        return buffer[:, a].reshape(width, buffer.shape[-1])

    own_rows = pl.ds(pl.multiple_of(t * head_width, DH), head_width)
    own_keys = pl.ds(pl.multiple_of(c * rows, rows), rows)
    normed = n1[...]
    kv_copies = [
        remote(ref.at[own_keys], ref.at[own_keys], kv_send.at[n], kv_recv.at[n], partner)
        for n, ref in enumerate((k_all, v_all))
    ]
    gather_corner(0)
    lax.fori_loop(key_blocks // 2, key_blocks * 3 // 4, bias_rows, 0)
    gather_finish(0)
    mixed_kv = contract(normed, wkv[...].reshape(width, 2 * head_width), 1, 0).astype(bf16)
    k_all[own_keys, :] = mixed_kv[:, 0:head_width]
    kv_copies[0].start()
    v_all[own_keys, :] = mixed_kv[:, head_width:]
    kv_copies[1].start()
    gather_corner(1)
    lax.fori_loop(key_blocks * 3 // 4, key_blocks, bias_rows, 0)
    gather_pass(2)
    for k in range(1, 4):
        out_copies[k - 1].wait_recv()
        wo3[me, :, (k - 1) * head_width : k * head_width] = other_out[k - 1]
    gather_own(5)
    gather_own(4)
    gather_finish(1)
    q_t[...] = contract(normed, wqo[:, :, 0:head_width].reshape(width, head_width), 1, 0).astype(bf16).T
    for copy in kv_copies:
        copy.wait_recv()
    v_t[...] = v_all[...].T

    def head_only(values, h):
        head_of = iota(values.shape, 0)
        inside = jnp.logical_and(head_of >= h * DH, head_of < (h + 1) * DH)
        return jnp.where(inside, values, jnp.zeros_like(values))

    def attended_copy(source, b, slot, target):
        view = att_all.at[
            pl.ds(pl.multiple_of(source * head_width, DH), head_width), block_rows(b)
        ]
        return remote(view, view, at_send.at[slot, b], at_recv.at[source, b], (f, c, target))

    def attended_start(b):
        @pl.when(outer)
        def _():
            attended_copy(t, b, 0, near_end).start()

        @pl.when(inner)
        def _():
            attended_copy(t, b, 0, far_end).start()
            attended_copy(t, b, 1, middle).start()

    def attended_relay(b, part):
        @pl.when(inner)
        def _():
            source = (far_end, middle, 3 - far_end)[part]
            attended_copy(source, b, 2 + part, middle if part == 0 else far_end).wait_recv()
            attended_copy(source, b, 2 + part, middle if part == 0 else far_end).start()

    def attended_wait(b):
        @pl.when(outer)
        def _():
            for source in (near_end, 3 - near_end, 3 - t):
                attended_copy(source, b, 0, near_end).wait_recv()

    def attended_drain(b, carry):
        attended_copy(t, b, 0, near_end).wait_send()

        @pl.when(inner)
        def _():
            for slot in range(1, 5):
                attended_copy(t, b, slot, middle).wait_send()

        return carry

    def attend(qb):
        at = block_rows(qb, FORWARD_BLOCK)

        def per_head(h, carry):
            queries = head_only(q_t[:, at], h)
            top = jnp.full((8, FORWARD_BLOCK), -jnp.inf, f32)
            for kb in range(keys // BLOCK):
                span_k = slice(kb * BLOCK, (kb + 1) * BLOCK)
                block = contract(k_all[span_k, :], queries, 1, 0) + masked_bias[h, span_k, at]
                score[span_k, 0:FORWARD_BLOCK] = block
                top = jnp.maximum(top, jnp.max(block.reshape(BLOCK // 8, 8, FORWARD_BLOCK), axis=0))
            top = jnp.max(top, axis=0, keepdims=True)
            total = jnp.zeros((8, FORWARD_BLOCK), f32)
            for kb in range(keys // BLOCK):
                span_k = slice(kb * BLOCK, (kb + 1) * BLOCK)
                block = jnp.exp(score[span_k, 0:FORWARD_BLOCK] - top)
                expo[h, span_k, at] = block.astype(bf16)
                total = total + jnp.sum(block.reshape(BLOCK // 8, 8, FORWARD_BLOCK), axis=0)
            inverse = 1.0 / jnp.sum(total, axis=0, keepdims=True)
            linv[h, :, at] = jnp.broadcast_to(inverse, (8, FORWARD_BLOCK))
            head_rows = pl.ds(pl.multiple_of(h * DH, DH), DH)
            own_head = pl.ds(pl.multiple_of(t * head_width + h * DH, DH), DH)
            mixed = contract(v_t[head_rows, :], expo[h, :, at], 1, 0)
            att_all[own_head, at] = (mixed * inverse).astype(bf16)
            return carry

        lax.fori_loop(0, heads, per_head, 0)
        for n in range(FORWARD_BLOCK // BLOCK):
            attended_start(qb * (FORWARD_BLOCK // BLOCK) + n)

    blocks = rows // BLOCK
    scale = 0.7978845608028654
    forward_blocks = rows // FORWARD_BLOCK

    def attend_loop(qb, carry):
        attend(qb)

        @pl.when(qb == 0)
        def _():
            gather_pass(3)

        return carry

    lax.fori_loop(0, forward_blocks, attend_loop, 0)
    per_forward = FORWARD_BLOCK // BLOCK
    early = range(per_forward)
    late = range(per_forward, blocks)

    def relays(group, part):
        for b in group:
            attended_relay(b, part)

    gather_corner(2)
    near[...] = jnp.zeros_like(near)
    wo_all[t] = wqo[:, :, head_width:].reshape(width, head_width)
    gather_pass(5)
    relays(early, 0)
    relays(early, 1)
    gather_pass(4)
    gather_corner(3)
    relays(late, 0)
    relays(late, 1)
    gather_corner(5)
    relays(early, 2)
    gather_corner(4)
    k_t[...] = k_all[...].T
    n1t[...] = n1[...].T
    dk[...] = jnp.zeros_like(dk)
    dv[...] = jnp.zeros_like(dv)
    small[...] = jnp.zeros_like(small)
    gather_finish(5)
    for k in range(1, 4):
        wo_all[t ^ k] = wo3[:, :, (k - 1) * head_width : k * head_width].reshape(width, head_width)
    relays(late, 2)
    for g in (2, 3, 4):
        gather_finish(g)

    def feed_forward(b, carry):
        attended_wait(b)
        at = block_rows(b)
        res = x_ref[at, :].astype(f32)
        for source in range(4):
            attended = att_all[source * head_width : (source + 1) * head_width, at].T
            res = res + contract(attended, wo_all[source], 1, 1)
        resid[at, :] = res
        normed = (res * inverse_rms(res) * gain_rows[1:2, :]).astype(bf16)
        n2[at, :] = normed
        gate = contract(normed, weight(wf, 0), 1, 0)
        up = contract(normed, weight(wf, 1), 1, 0)
        down = weight(wf, 2)
        grad_act = contract(cot_ref[at, :], down, 1, 0)

        @pl.when(b > 1)
        def _():
            serve((b - 2) * per_block + per_block // 2, per_block // 2)

        square = gate * gate
        curve = jnp.tanh(scale * (gate + 0.044715 * square * gate))
        left = 0.5 * (1.0 + curve)
        value = gate * left
        slope = left + 0.5 * gate * (1.0 - curve * curve) * scale * (1.0 + 0.134145 * square)
        low_act = (value * up).astype(bf16)
        low_gate = (grad_act * up * slope).astype(bf16)
        low_up = (grad_act * value).astype(bf16)
        act[at, :] = low_act
        ggate[at, :] = low_gate
        gup[at, :] = low_up
        snd[0, at, :] = (
            contract(low_gate, weight(wf, 0), 1, 1) + contract(low_up, weight(wf, 1), 1, 1)
        ).astype(bf16)
        put_block(0, b)
        snd[1, at, :] = contract(low_act, down, 1, 1).astype(bf16)

        @pl.when(b > 0)
        def _():
            serve((b - 1) * per_block, per_block // 2)

        return carry

    lax.fori_loop(0, blocks, feed_forward, 0)
    serve((blocks - 2) * per_block + per_block // 2, per_block // 2)

    def put_outputs(b, carry):
        put_block(1, b)
        return carry

    lax.fori_loop(0, blocks, put_outputs, 0)
    turned[0] = n2[...].T
    turned[1] = cot_ref[...].T

    def sent(n, which):
        if n == 0:
            return gsf.at[:, which]
        return gsa.at[:, which, 3:4] if n == 1 else gsa.at[:, which, 0:3]

    def landed(n):
        return rf.at[...] if n == 0 else ra.at[:, 3:4] if n == 1 else ra.at[:, 0:3]

    def over_copy(n):
        return remote(sent(n, 1 - c), landed(n), rs_send.at[n], rs_recv.at[n], partner)

    def summed(n, index):
        return sf.at[index] if n == 0 else sa.at[index, 3:4] if n == 1 else sa.at[index, 0:3]

    def arrived(n, k):
        return rf2.at[k - 1] if n == 0 else ra2.at[k - 1, 3:4] if n == 1 else ra2.at[k - 1, 0:3]

    def out_copy(n, k):
        return remote(
            summed(n, f ^ k), arrived(n, k), rs2_send.at[n, k - 1], rs2_recv.at[n, k - 1],
            (f ^ k, c, t),
        )

    members_of = {0: (0, 1, 2), 1: (3,), 2: (0, 1, 2)}
    outputs = {0: (gg_hbm, gu_hbm, gd_hbm), 1: (go_hbm,), 2: (gk_hbm, gv_hbm, gq_hbm)}

    def part_stores(n):
        results = gf_ref if n == 0 else ga_ref
        offset = (0, 3, 4)[n]
        return [
            pltpu.make_async_copy(results.at[a], target, store_sem.at[offset + i])
            for i, (a, target) in enumerate(zip(members_of[n], outputs[n]))
        ]

    def reduce_send(n):
        over_copy(n).wait_recv()
        own, got, total = (gsf, rf, sf) if n == 0 else (gsa, ra, sa)

        def body(k, carry):
            index = jnp.bitwise_xor(f, groups - 1 - k)
            for a in members_of[n]:
                total[index, a] = (
                    own[index, c, a].astype(f32) + got[index, a].astype(f32)
                ).astype(bf16)
            return carry

        lax.fori_loop(0, groups, body, 0)
        for k in range(1, groups):
            out_copy(n, k).start()

    def reduce_finish(n):
        total, got = (sf, rf2) if n == 0 else (sa, ra2)
        for k in range(1, groups):
            out_copy(n, k).wait_recv()
        results = gf_ref if n == 0 else ga_ref
        for a in members_of[n]:
            value = total[f, a].astype(f32)
            for k in range(1, groups):
                value = value + got[k - 1, a].astype(f32)
            results[a] = value
        for copy in part_stores(n):
            copy.start()

    def reduce_drain(n):
        over_copy(n).wait_send()
        for k in range(1, groups):
            out_copy(n, k).wait_send()

    both = 2 * shard

    def store_grad(buffer, i, a, value):
        buffer[i, :, a] = value.astype(bf16).reshape(2, shard, value.shape[-1])

    def pair_rows(i):
        return block_rows(i, both)

    def feed_forward_weights(i):
        at = pair_rows(i)
        store_grad(gsf, i, 0, contract(turned[0, at, :], ggate[...], 1, 0))
        store_grad(gsf, i, 1, contract(turned[0, at, :], gup[...], 1, 0))
        store_grad(gsf, i, 2, contract(turned[1, at, :], act[...], 1, 0))

    def residual_back(b):
        totals_of(0, b)
        at = block_rows(b)
        grad_in = tot[0, at, :].astype(f32)
        res = resid[at, :]
        inverse = inverse_rms(res)
        u = res * inverse
        small[1:2, :] += jnp.sum(grad_in * u, axis=0, keepdims=True)
        g = grad_in * gain_rows[1:2, :]
        grad = cot_ref[at, :].astype(f32) + inverse * (
            g - u * jnp.mean(g * u, axis=-1, keepdims=True)
        )
        grad_res[at, :] = grad
        low_grad = grad.astype(bf16)
        grl[at, :] = low_grad
        grad_att = contract(low_grad, wo_all[t], 1, 0).astype(bf16)
        scaled = grad_att.T.astype(f32) * jnp.concatenate(
            [jnp.broadcast_to(linv[h, 0:1, at], (DH, BLOCK)) for h in range(heads)], axis=0
        )
        scaled = scaled.astype(bf16)
        dos_t[:, at] = scaled
        products = scaled.astype(f32) * att_all[own_rows, at].astype(f32)
        for h in range(heads):
            delta[h, :, at] = jnp.broadcast_to(
                jnp.sum(products[h * DH : (h + 1) * DH], axis=0, keepdims=True), (8, BLOCK)
            )

    extra = dk.shape[1] - head_width
    query_blocks = rows // BLOCK

    def attend_back(start, size, h):
        at = slice(start, start + size)
        first = start // BLOCK
        head_rows = pl.ds(pl.multiple_of(h * DH, DH), DH)
        if True:
            grads = head_only(dos_t[:, at], h)
            queries = head_only(q_t[:, at], h)
            flag = iota((extra, size), 0)
            lane = iota((extra, size), 1)
            flags = jnp.zeros((extra, size), f32)
            for j in range(size // BLOCK):
                hit = jnp.logical_and(
                    flag == h * query_blocks + first + j,
                    jnp.logical_and(lane >= j * BLOCK, lane < (j + 1) * BLOCK),
                )
                flags = jnp.where(hit, 1.0, flags)
            flagged = jnp.concatenate([queries, flags.astype(bf16)], axis=0)
            shift = delta[h, 0:1, at]
            for kb in range(keys // BLOCK):
                span_k = slice(kb * BLOCK, (kb + 1) * BLOCK)
                block = contract(v_all[span_k, :], grads, 1, 0)
                low_score[span_k, 0:size] = (
                    expo[h, span_k, at].astype(f32) * (block - shift)
                ).astype(bf16)
            dv[...] += contract(expo[h, :, at], grads, 1, 1)
            dk[...] += contract(low_score[:, 0:size], flagged, 1, 1)
            dq_t[head_rows, at] = contract(
                k_t[head_rows, :], low_score[:, 0:size], 1, 0
            ).astype(bf16)
            for j in range(size // BLOCK):
                home = c * query_blocks + first + j
                for d in (-1, 0, 1):
                    kb = home + d
                    valid = jnp.logical_and(kb >= 0, kb < keys // BLOCK)

                    @pl.when(valid)
                    def _():
                        where_k = jnp.clip(kb, 0, keys // BLOCK - 1)
                        near[h, d + 1] += low_score[
                            block_rows(where_k), j * BLOCK : (j + 1) * BLOCK
                        ].astype(f32)

    pace = per_block // 2
    step = (blocks - 1) * per_block

    query_parts = [(start, QUERY_BLOCK) for start in range(0, rows - QUERY_BLOCK, QUERY_BLOCK)]
    query_parts += [(start, BLOCK) for start in range(rows - QUERY_BLOCK, rows, BLOCK)]
    for qb, (start, size) in enumerate(query_parts):
        for b in range(start // BLOCK, (start + size) // BLOCK):
            residual_back(b)
            if qb == 0:
                service(step)
                step += 1

        def back_head(h, carry, start=start, size=size, step=step, qb=qb):
            attend_back(start, size, h)
            serve(h * PACES[qb] + step, PACES[qb])
            return carry

        lax.fori_loop(0, heads, back_head, 0)
        step += heads * PACES[qb]
        if qb == 0:

            def early_weights(i, carry, step=step):
                feed_forward_weights(i)

                @pl.when(i < EARLY)
                def _():
                    service(i + step)

                return carry

            lax.fori_loop(0, groups, early_weights, 0)
            step += EARLY
            over_copy(0).start()
            flush(chunks - LAG, chunks)
        if qb == 1:
            reduce_send(0)

    other_keys = pl.ds(pl.multiple_of((1 - c) * rows, rows), rows)
    dkv_send[0] = dk[other_keys, 0:head_width].astype(bf16)
    dkv_send[1] = dv[other_keys, :].astype(bf16)
    dkv_copy = remote(dkv_send.at[...], dkv_recv.at[...], dkv_ssem.at[0], dkv_rsem.at[0], partner)
    dkv_copy.start()
    dkv_copy.wait_recv()
    dkv[:, 0:head_width] = (dk[own_keys, 0:head_width] + dkv_recv[0].astype(f32)).astype(bf16)
    dkv[:, head_width:] = (dv[own_keys, :] + dkv_recv[1].astype(f32)).astype(bf16)

    def project_back(b, carry):
        at = block_rows(b)
        total = contract(
            dq_t[:, at].T, wqo[:, :, 0:head_width].reshape(width, head_width), 1, 1
        )
        total = total + contract(dkv[at, :], wkv[...].reshape(width, 2 * head_width), 1, 1)
        snd[2, at, :] = total.astype(bf16)
        put_block(2, b)

        @pl.when(step + (b + 1) * pace <= 2 * chunks)
        def _():
            serve(step + b * pace, pace)

        return carry

    lax.fori_loop(0, blocks, project_back, 0)
    step += min(blocks, (2 * chunks - step) // pace) * pace

    def weights_back(i, carry):
        part_rows = n1t[pair_rows(i), :]
        mixed = contract(part_rows, dkv[...], 1, 0)
        store_grad(gsa, i, 0, mixed[:, 0:head_width])
        store_grad(gsa, i, 1, mixed[:, head_width:])
        store_grad(gsa, i, 2, contract(part_rows, dq_t[...], 1, 1))
        return carry

    serve(step, 2 * chunks - step)
    step = 2 * chunks

    def output_weights(i, carry):
        store_grad(gsa, i, 3, contract(turned[0, pair_rows(i), :], att_all[own_rows, :], 1, 1))
        return carry


    def bucket_sums(h, carry):
        for b in range(2 * half):
            summed_block = jnp.zeros((8, BLOCK), f32)
            for d in (-1, 0) if b < half else (0, 1):
                bucket = bucket_of(d * BLOCK + row_of - column_of)
                chosen = jnp.where(bucket == b, near[h, d + 1], 0.0)
                summed_block = summed_block + jnp.sum(
                    chosen.reshape(BLOCK // 8, 8, BLOCK), axis=0
                )
            pick[b : b + 1, :] = jnp.sum(summed_block, axis=0, keepdims=True)
        sums = contract(jnp.ones((8, BLOCK), f32), pick[...], 1, 1, highest)
        small[:, 0 : 2 * half] += jnp.where(iota((8, 2 * half), 0) == 2 + h, sums, 0.0)
        return carry

    def far_sums():
        tail = dk.shape[1] - BLOCK
        first_lane = head_width - tail
        column_sums = dk[:, tail:]
        block_row = iota((keys, BLOCK), 0)
        lane = iota((keys, BLOCK), 1)
        left_sum = jnp.zeros((1, BLOCK), f32)
        right_sum = jnp.zeros((1, BLOCK), f32)
        for j in range(query_blocks):
            mine = jnp.zeros((keys, BLOCK), jnp.bool_)
            for h in range(heads):
                mine = jnp.logical_or(mine, lane == first_lane + h * query_blocks + j)
            home = c * query_blocks + j
            is_left = jnp.logical_and(mine, block_row < (home - 1) * BLOCK)
            is_right = jnp.logical_and(mine, block_row >= (home + 2) * BLOCK)
            left_sum += jnp.sum(jnp.where(is_left, column_sums, 0.0), axis=0, keepdims=True)
            right_sum += jnp.sum(jnp.where(is_right, column_sums, 0.0), axis=0, keepdims=True)
        from_lane, to_lane = iota((BLOCK, BLOCK), 0), iota((BLOCK, BLOCK), 1)
        for h in range(heads):
            start = first_lane + h * query_blocks
            inside = jnp.logical_and(from_lane >= start, from_lane < start + query_blocks)
            left_pick = jnp.logical_and(inside, to_lane == far).astype(f32)
            right_pick = jnp.logical_and(inside, to_lane == half + far).astype(f32)
            small[2 + h : 3 + h, 0:BLOCK] += (
                contract(jnp.broadcast_to(left_sum, (8, BLOCK)), left_pick, 1, 0, highest)
                + contract(jnp.broadcast_to(right_sum, (8, BLOCK)), right_pick, 1, 0, highest)
            )[0:1]

    def block_store(n, source, target, b):
        at = block_rows(b)
        return pltpu.make_async_copy(source.at[at], target.at[at], store_sem.at[n])

    def input_back(b):
        totals_of(2, b)
        at = block_rows(b)
        grad_in = tot[2, at, :].astype(f32)
        xs = x_ref[at, :].astype(f32)
        inverse = inverse_rms(xs)
        u = xs * inverse
        g = grad_in * gain_rows[0:1, :]
        gin_ref[at, :] = grad_res[at, :] + inverse * (
            g - u * jnp.mean(g * u, axis=-1, keepdims=True)
        )
        block_store(7 + b, gin_ref, gin_hbm, b).start()

    def layer_out(b):
        totals_of(1, b)
        at = block_rows(b)
        out_ref[at, :] = (resid[at, :] + tot[1, at, :].astype(f32)).astype(bf16)
        block_store(7 + blocks + b, out_ref, out_hbm, b).start()

    small_copies = [
        remote(
            small.at[...], small_all.at[me], sm_send.at[k * 2 + kc - 1], sm_recv.at[k * 2 + kc - 1],
            (f ^ k, c ^ kc, t),
        )
        for k in range(groups)
        for kc in range(2)
        if k or kc
    ]

    def small_start():
        for copy in small_copies:
            copy.start()
        small_all[me] = small[...]

    def small_finish():
        for copy in small_copies:
            copy.wait_recv()
        total_small = small_all[0]
        for i in range(1, shards):
            total_small = total_small + small_all[i]
        to_own = (iota((width, BLOCK), 0) == iota((width, BLOCK), 1) + me * shard).astype(f32)
        own_gains = contract(total_small, to_own, 1, 0, highest)
        gain_two_out_ref[...] = own_gains[1:2, 0:shard]
        bias_out_ref[...] = total_small[2 : 2 + heads, 0 : 2 * half]

    gain_copies = [
        remote(
            gain_part.at[t], gain_part.at[t], gp_send.at[kt - 1], gp_recv.at[kt - 1], (f, c, t ^ kt)
        )
        for kt in range(1, 4)
    ]

    def gain_start():
        products = jnp.zeros((shard, head_width), f32)
        for a in members_of[2]:
            products = products + staged[a].astype(f32) * ga_ref[a]
        row_sums = contract(jnp.ones((8, head_width), f32), products, 1, 1, highest)
        gain_part[t, :, 0:shard] = row_sums / gain_one_ref[...].astype(f32)
        for copy in gain_copies:
            copy.start()

    def gain_finish():
        for copy in gain_copies:
            copy.wait_recv()
        total = gain_part[0, 0:1, 0:shard]
        for i in range(1, 4):
            total = total + gain_part[i, 0:1, 0:shard]
        gain_one_out_ref[...] = total

    @pl.when(outer)
    def _():
        lax.fori_loop(0, heads, bucket_sums, 0)
        far_sums()

    def at_step(n, value, run):
        pl.when(n == value)(run)

    def last_steps(n, carry):
        service(2 * chunks + n)

        @pl.when(n < groups)
        def _():
            weights_back(n, 0)

        def turn():
            over_copy(2).start()
            turned[0] = grl[...].T

        at_step(n, groups - 1, turn)

        @pl.when(jnp.logical_and(n >= groups, n < 2 * groups))
        def _():
            output_weights(n - groups, 0)

        at_step(n, groups + 1, functools.partial(reduce_send, 2))
        at_step(n, 2 * groups - 1, over_copy(1).start)
        at_step(n, 2 * groups + 1, functools.partial(reduce_send, 1))
        after = n - 2 * groups

        @pl.when(
            jnp.logical_and(
                jnp.logical_and(inner, lax.rem(n, 2) == 0),
                jnp.logical_and(after >= 0, after < 2 * heads),
            )
        )
        def _():
            bucket_sums(lax.div(after, 2), 0)

        def sums_out():
            pl.when(inner)(far_sums)
            small_start()

        at_step(n, 2 * groups + 2 * heads - 1, sums_out)
        for due_step, b in zip((6, 9, 13, 14), range(blocks)):

            @pl.when(n == due_step)
            def _(b=b):
                layer_out(b)

        at_step(n, chunks - 2, functools.partial(reduce_finish, 0))

        def gains():
            reduce_finish(2)
            gain_start()

        at_step(n, chunks, gains)
        at_step(n, chunks + 1, small_finish)
        at_step(n, chunks + 2, functools.partial(reduce_finish, 1))

        due = n - (per_block - 1) - LAG

        @pl.when(jnp.logical_and(due >= 0, lax.rem(due, per_block) == 0))
        def _():
            input_back(lax.div(due, per_block))

        return carry

    lax.fori_loop(0, chunks + LAG, last_steps, 0)
    gain_finish()
    for b in range(blocks):
        block_store(7 + b, gin_ref, gin_hbm, b).wait()
        block_store(7 + blocks + b, out_ref, out_hbm, b).wait()
    for n in range(3):
        for copy in part_stores(n):
            copy.wait()
    for copy in small_copies + gain_copies:
        copy.wait_send()
    for g in range(6):
        gather_drain(g)
    for copy in out_copies:
        copy.wait_send()
    lax.fori_loop(0, blocks, attended_drain, 0)
    for k in range(1, 4):
        gain_copy(k).wait_send()
    for k in range(4):
        gain_over(k).wait_send()
    for copy in kv_copies:
        copy.wait_send()
    dkv_copy.wait_send()
    drain_all()
    for n in range(3):
        reduce_drain(n)


def fused_layer(shards, x, cot, ids, gain_one, gain_two, weights, table):
    rows, width = x.shape
    shard, head_width = weights[0].shape
    units = weights[4].shape[1]
    keys = ids.shape[1]
    heads = head_width // DH
    groups = shards // 2
    chunks = rows // CHUNK
    padded = head_width + (-head_width) % BLOCK
    if padded - head_width < heads * (rows // BLOCK):
        padded += BLOCK
    vmem, dma = pltpu.VMEM, pltpu.SemaphoreType.DMA
    out_shape = (
        jax.ShapeDtypeStruct((rows, width), bf16),
        jax.ShapeDtypeStruct((rows, width), f32),
        *[jax.ShapeDtypeStruct((shard, head_width), f32)] * 4,
        *[jax.ShapeDtypeStruct((shard, units), f32)] * 3,
        jax.ShapeDtypeStruct((1, shard), f32),
        jax.ShapeDtypeStruct((1, shard), f32),
        jax.ShapeDtypeStruct(table.shape, f32),
    )
    in_vmem = pl.BlockSpec(memory_space=pltpu.VMEM)
    anywhere = pl.BlockSpec(memory_space=pl.ANY)
    scratch = [
        vmem((rows, width), bf16),
        vmem((rows, width), bf16),
        vmem((rows, width), bf16),
        vmem((rows, width), f32),
        vmem((4, shard, head_width), f32),
        vmem((3, shard, units), f32),
        vmem((4, shard, head_width), bf16),
        vmem((shards, shard, 2 * head_width), bf16),
        vmem((shards, shard, 2 * head_width), bf16),
        vmem((shards, shard, 3 * head_width), bf16),
        vmem((3, shard, head_width), bf16),
        vmem((4, width, head_width), bf16),
        vmem((shards, 3, shard, units), bf16),
        vmem((shards, 8, BLOCK), f32),
        vmem((8, width), f32),
        vmem((heads, 5, BLOCK, BLOCK), f32),
        vmem((heads, keys, rows), f32),
        vmem((keys, QUERY_BLOCK), f32),
        vmem((heads, keys, rows), bf16),
        vmem((keys, QUERY_BLOCK), bf16),
        vmem((3, rows, width), bf16),
        vmem((3, rows, width), bf16),
        vmem((3, rows, width), bf16),
        vmem((rows, width), f32),
        vmem((rows, width), f32),
        vmem((rows, width), bf16),
        vmem((rows, width), bf16),
        vmem((rows, width), bf16),
        vmem((width, rows), bf16),
        vmem((2, width, rows), bf16),
        vmem((rows, units), bf16),
        vmem((rows, units), bf16),
        vmem((rows, units), bf16),
        vmem((head_width, rows), bf16),
        vmem((keys, head_width), bf16),
        vmem((keys, head_width), bf16),
        vmem((head_width, keys), bf16),
        vmem((head_width, keys), bf16),
        vmem((4 * head_width, rows), bf16),
        vmem((head_width, rows), bf16),
        vmem((head_width, rows), bf16),
        vmem((heads, 8, rows), f32),
        vmem((heads, 8, rows), f32),
        vmem((keys, padded), f32),
        vmem((keys, head_width), f32),
        vmem((heads, 3, BLOCK, BLOCK), f32),
        vmem((table.shape[1], BLOCK), f32),
        vmem((2, rows, head_width), bf16),
        vmem((2, rows, head_width), bf16),
        vmem((rows, 2 * head_width), bf16),
        vmem((groups, 2, 4, shard, head_width), bf16),
        vmem((groups, 2, 3, shard, units), bf16),
        vmem((groups, 4, shard, head_width), bf16),
        vmem((groups, 3, shard, units), bf16),
        vmem((groups, 4, shard, head_width), bf16),
        vmem((groups, 3, shard, units), bf16),
        vmem((groups - 1, 4, shard, head_width), bf16),
        vmem((groups - 1, 3, shard, units), bf16),
        vmem((8, width), f32),
        vmem((shards, 8, width), f32),
        vmem((4, 8, BLOCK), f32),
        dma((9,)),
        dma((7 + 2 * (rows // BLOCK),)),
        dma((7, 8)),
        dma((7, 8)),
        dma((3,)),
        dma((3,)),
        dma((5, rows // BLOCK)),
        dma((4, rows // BLOCK)),
        dma((2,)),
        dma((2,)),
        dma((3, chunks)),
        dma((3, chunks)),
        dma((3, chunks)),
        dma((3, chunks)),
        dma((1,)),
        dma((1,)),
        dma((3,)),
        dma((3,)),
        dma((3, groups)),
        dma((3, groups)),
        dma((shards,)),
        dma((shards,)),
        dma((3,)),
        dma((3,)),
    ]
    return pl.pallas_call(
        functools.partial(layer_kernel, shards),
        out_shape=out_shape,
        in_specs=[anywhere] * 2
        + [in_vmem] * 3
        + [anywhere] * 7
        + [pl.BlockSpec(memory_space=pltpu.SMEM)],
        out_specs=[anywhere] * 9 + [in_vmem] * 3,
        scratch_shapes=scratch,
        name="layer",
        compiler_params=pltpu.CompilerParams(
            collective_id=0, has_side_effects=True, vmem_limit_bytes=63 << 20
        ),
    )(x, cot, ids, gain_one, gain_two, *weights, table)


def publish_kernel(count, *refs):
    sources, targets = refs[:count], refs[count : 2 * count]
    held, in_sem, out_sem = refs[2 * count : 3 * count], refs[3 * count], refs[3 * count + 1]
    inward = [
        pltpu.make_async_copy(sources[i], held[i], in_sem.at[i]) for i in range(count)
    ]
    outward = [
        pltpu.make_async_copy(held[i], targets[i], out_sem.at[i]) for i in range(count)
    ]
    for copy in inward:
        copy.start()
    for arriving, leaving in zip(inward, outward):
        arriving.wait()
        leaving.start()
    for copy in outward:
        copy.wait()


def publish(values):
    count = len(values)
    anywhere = pl.BlockSpec(memory_space=pl.ANY)
    return pl.pallas_call(
        functools.partial(publish_kernel, count),
        out_shape=[jax.ShapeDtypeStruct(value.shape, value.dtype) for value in values],
        in_specs=[anywhere] * count,
        out_specs=[anywhere] * count,
        scratch_shapes=[pltpu.VMEM(value.shape, value.dtype) for value in values]
        + [pltpu.SemaphoreType.DMA((count,))] * 2,
        name="publish",
    )(*values)


def on_device_fused(
    layer_input,
    doc_ids,
    query_weight,
    key_weight,
    value_weight,
    output_weight,
    gate_weight,
    up_weight,
    down_weight,
    first_gain,
    second_gain,
    position_bias,
    cotangent,
):
    shards = lax.axis_size("fsdp") * lax.axis_size("ctx")
    outs = fused_layer(
        shards,
        layer_input[0],
        cotangent[0],
        doc_ids,
        first_gain[None],
        second_gain[None],
        (
            query_weight,
            key_weight,
            value_weight,
            output_weight,
            gate_weight,
            up_weight,
            down_weight,
        ),
        position_bias.T,
    )
    outs = publish(outs)
    return (
        outs[0][None],
        outs[1][None],
        *outs[2:9],
        outs[9][0],
        outs[10][0],
        outs[11].T,
    )


def fits_kernel(mesh):
    return mesh.shape["ctx"] == 2 and mesh.shape["tp"] == 4 and mesh.shape["fsdp"] == 4


def solution(mesh):
    return jax.shard_map(
        on_device_fused if fits_kernel(mesh) else on_device,
        mesh=mesh,
        in_specs=(
            P("fsdp", "ctx", None),
            P("fsdp", None),
            P(("fsdp", "ctx"), "tp"),
            P(("fsdp", "ctx"), "tp"),
            P(("fsdp", "ctx"), "tp"),
            P(("fsdp", "ctx"), "tp"),
            P(("fsdp", "ctx"), "tp"),
            P(("fsdp", "ctx"), "tp"),
            P(("fsdp", "ctx"), "tp"),
            P(("fsdp", "ctx")),
            P(("fsdp", "ctx")),
            P(None, "tp"),
            P("fsdp", "ctx", None),
        ),
        out_specs=(
            P("fsdp", "ctx", None),
            P("fsdp", "ctx", None),
            P(("fsdp", "ctx"), "tp"),
            P(("fsdp", "ctx"), "tp"),
            P(("fsdp", "ctx"), "tp"),
            P(("fsdp", "ctx"), "tp"),
            P(("fsdp", "ctx"), "tp"),
            P(("fsdp", "ctx"), "tp"),
            P(("fsdp", "ctx"), "tp"),
            P(("fsdp", "ctx")),
            P(("fsdp", "ctx")),
            P(None, "tp"),
        ),
        check_vma=False,
    )
```

```python
import functools

import jax
import jax.numpy as jnp
from jax import lax
from jax.experimental import pallas as pl
from jax.experimental.pallas import tpu as pltpu
from jax.sharding import PartitionSpec as P

DH = 64


epsilon = 1e-06
masked_score = -1000000000.0
bucket_edges = (12, 16, 23, 32, 46, 64, 91)
highest = lax.Precision.HIGHEST


def bucket_of(relative):
    distance = jnp.abs(relative)
    beyond = jnp.zeros_like(distance) + 8
    for edge_value in bucket_edges:
        beyond = beyond + (distance >= edge_value).astype(jnp.int32)
    inside = jnp.where(distance < 8, distance, beyond)
    return jnp.where(relative > 0, 16, 0) + inside


def rms_norm(values, gain_vector):
    inverse = lax.rsqrt(jnp.mean(values * values, axis=-1, keepdims=True) + epsilon)
    return values * inverse * gain_vector


def gated_unit(gate_in, up_in):
    return jax.nn.gelu(gate_in, approximate=True) * up_in


def relative_bias(bias_table, query_rows, key_rows, offset):
    span_width = key_rows + query_rows
    relative = lax.iota(jnp.int32, span_width) - (query_rows - 1) - offset
    one_hot = (
        bucket_of(relative)[:, None] == lax.iota(jnp.int32, bias_table.shape[0])[None, :]
    ).astype(jnp.float32)
    per_shift = jnp.dot(one_hot, bias_table, precision=highest).T
    heads_here = bias_table.shape[1]
    toeplitz = jnp.broadcast_to(per_shift[:, None, :], (heads_here, query_rows, span_width))
    toeplitz = toeplitz.reshape(heads_here, query_rows * span_width)[
        :, : query_rows * (span_width - 1)
    ]
    toeplitz = toeplitz.reshape(heads_here, query_rows, span_width - 1)
    return (toeplitz[:, :, query_rows - 1 : query_rows - 1 + key_rows], one_hot)


def diagonal_sums(grad_scores, query_rows, key_rows):
    heads_here = grad_scores.shape[0]
    span_width = key_rows + query_rows
    placed = jnp.pad(grad_scores, ((0, 0), (0, 0), (query_rows - 1, 0)))
    placed = placed.reshape(heads_here, query_rows * (span_width - 1))
    placed = jnp.pad(placed, ((0, 0), (0, query_rows)))
    return jnp.sum(placed.reshape(heads_here, query_rows, span_width), axis=1)


def on_device(
    layer_input,
    doc_ids,
    query_weight,
    key_weight,
    value_weight,
    output_weight,
    gate_weight,
    up_weight,
    down_weight,
    first_gain,
    second_gain,
    position_bias,
    cotangent,
):
    query_rows = layer_input.shape[1]
    key_rows = query_rows * lax.axis_size("ctx")
    heads_here = position_bias.shape[1]
    head_width = heads_here * DH
    offset = lax.axis_index("ctx") * query_rows
    everything = (
        query_weight,
        key_weight,
        value_weight,
        output_weight,
        gate_weight,
        up_weight,
        down_weight,
        first_gain,
        second_gain,
    )
    (
        full_query,
        full_key,
        full_value,
        full_output,
        full_gate,
        full_up,
        full_down,
        gain_one,
        gain_two,
    ) = (
        lax.all_gather(everything[0], ("fsdp", "ctx"), axis=0, tiled=True),
        lax.all_gather(everything[1], ("fsdp", "ctx"), axis=0, tiled=True),
        lax.all_gather(everything[2], ("fsdp", "ctx"), axis=0, tiled=True),
        lax.all_gather(everything[3], ("fsdp", "ctx"), axis=0, tiled=True),
        lax.all_gather(everything[4], ("fsdp", "ctx"), axis=0, tiled=True),
        lax.all_gather(everything[5], ("fsdp", "ctx"), axis=0, tiled=True),
        lax.all_gather(everything[6], ("fsdp", "ctx"), axis=0, tiled=True),
        lax.all_gather(everything[7], ("fsdp", "ctx"), axis=0, tiled=True),
        lax.all_gather(everything[8], ("fsdp", "ctx"), axis=0, tiled=True),
    )
    inputs = layer_input.astype(jnp.float32)
    gain_first = gain_one.astype(jnp.float32)
    gain_second = gain_two.astype(jnp.float32)
    normed_one = rms_norm(inputs, gain_first).astype(jnp.bfloat16)
    queries = jnp.dot(normed_one, full_query, preferred_element_type=jnp.float32).astype(
        jnp.bfloat16
    )
    keys_local = jnp.dot(normed_one, full_key, preferred_element_type=jnp.float32).astype(
        jnp.bfloat16
    )
    values_local = jnp.dot(normed_one, full_value, preferred_element_type=jnp.float32).astype(
        jnp.bfloat16
    )
    keys_all, values_all = (
        lax.all_gather(keys_local, "ctx", axis=1, tiled=True),
        lax.all_gather(values_local, "ctx", axis=1, tiled=True),
    )
    bias_block, one_hot = relative_bias(position_bias, query_rows, key_rows, offset)

    def scores_of(query_heads, key_heads, id_row):
        raw_scores = jnp.einsum(
            "qhd,khd->hqk", query_heads, key_heads, preferred_element_type=jnp.float32
        )
        own_ids = lax.dynamic_slice_in_dim(id_row, offset, query_rows)
        same_doc = own_ids[:, None] == id_row[None, :]
        return jnp.where(same_doc[None], raw_scores + bias_block, masked_score)

    def forward_one(packed):
        query_seq, key_seq, value_seq, id_row = packed
        scores = scores_of(
            query_seq.reshape(query_rows, heads_here, DH),
            key_seq.reshape(key_rows, heads_here, DH),
            id_row,
        )
        row_max = jnp.max(scores, axis=-1, keepdims=True)
        exponentials = jnp.exp(scores - row_max)
        row_total = jnp.sum(exponentials, axis=-1, keepdims=True)
        probabilities = (exponentials / row_total).astype(jnp.bfloat16)
        attended = jnp.einsum(
            "hqk,khd->qhd",
            probabilities,
            value_seq.reshape(key_rows, heads_here, DH),
            preferred_element_type=jnp.float32,
        )
        log_row = row_max[..., 0] + jnp.log(row_total[..., 0])
        return (attended.reshape(query_rows, head_width).astype(jnp.bfloat16), log_row)

    attended, log_sums = lax.map(forward_one, (queries, keys_all, values_all, doc_ids))
    attention_terms = jnp.einsum(
        "sqe,de->sqd", attended, full_output, preferred_element_type=jnp.float32
    )
    residual = inputs + lax.psum(attention_terms.astype(jnp.bfloat16), "tp").astype(jnp.float32)
    normed_two = rms_norm(residual, gain_second).astype(jnp.bfloat16)
    gate_pre = jnp.dot(normed_two, full_gate, preferred_element_type=jnp.float32)
    up_pre = jnp.dot(normed_two, full_up, preferred_element_type=jnp.float32)
    activated = gated_unit(gate_pre, up_pre).astype(jnp.bfloat16)
    ffn_terms = jnp.einsum("sqf,df->sqd", activated, full_down, preferred_element_type=jnp.float32)
    output_rows = (
        residual + lax.psum(ffn_terms.astype(jnp.bfloat16), "tp").astype(jnp.float32)
    ).astype(jnp.bfloat16)
    grad_activated = jnp.einsum(
        "sqd,df->sqf", cotangent, full_down, preferred_element_type=jnp.float32
    )
    down_grad = jnp.einsum("sqd,sqf->df", cotangent, activated, preferred_element_type=jnp.float32)
    gated_value, gated_back = jax.vjp(gated_unit, gate_pre, up_pre)
    grad_gate, grad_up = gated_back(grad_activated)
    grad_gate = grad_gate.astype(jnp.bfloat16)
    grad_up = grad_up.astype(jnp.bfloat16)
    gate_grad = jnp.einsum("sqd,sqf->df", normed_two, grad_gate, preferred_element_type=jnp.float32)
    up_grad = jnp.einsum("sqd,sqf->df", normed_two, grad_up, preferred_element_type=jnp.float32)
    normed_two_terms = jnp.einsum(
        "sqf,df->sqd", grad_gate, full_gate, preferred_element_type=jnp.float32
    ) + jnp.einsum("sqf,df->sqd", grad_up, full_up, preferred_element_type=jnp.float32)
    grad_normed_two = lax.psum(normed_two_terms.astype(jnp.bfloat16), "tp").astype(jnp.float32)
    second_value, second_back = jax.vjp(rms_norm, residual, gain_second)
    grad_residual, second_gain_grad = second_back(grad_normed_two)
    grad_residual = grad_residual + cotangent.astype(jnp.float32)
    grad_low = grad_residual.astype(jnp.bfloat16)
    grad_attended = jnp.einsum(
        "sqd,de->sqe", grad_low, full_output, preferred_element_type=jnp.float32
    ).astype(jnp.bfloat16)
    output_grad = jnp.einsum("sqd,sqe->de", grad_low, attended, preferred_element_type=jnp.float32)

    def backward_one(running, packed):
        query_seq, key_seq, value_seq, id_row, grad_seq, log_row = packed
        query_heads = query_seq.reshape(query_rows, heads_here, DH)
        key_heads = key_seq.reshape(key_rows, heads_here, DH)
        value_heads = value_seq.reshape(key_rows, heads_here, DH)
        grad_heads = grad_seq.reshape(query_rows, heads_here, DH)
        scores = scores_of(query_heads, key_heads, id_row)
        probabilities = jnp.exp(scores - log_row[..., None])
        grad_probs = jnp.einsum(
            "qhd,khd->hqk", grad_heads, value_heads, preferred_element_type=jnp.float32
        )
        grad_values = jnp.einsum(
            "hqk,qhd->khd",
            probabilities.astype(jnp.bfloat16),
            grad_heads,
            preferred_element_type=jnp.float32,
        )
        grad_scores = probabilities * (
            grad_probs - jnp.sum(probabilities * grad_probs, axis=-1, keepdims=True)
        )
        low_scores = grad_scores.astype(jnp.bfloat16)
        grad_queries = jnp.einsum(
            "hqk,khd->qhd", low_scores, key_heads, preferred_element_type=jnp.float32
        )
        grad_keys = jnp.einsum(
            "hqk,qhd->khd", low_scores, query_heads, preferred_element_type=jnp.float32
        )
        running = running + diagonal_sums(grad_scores, query_rows, key_rows)
        return (
            running,
            (
                grad_queries.reshape(query_rows, head_width).astype(jnp.bfloat16),
                grad_keys.reshape(key_rows, head_width),
                grad_values.reshape(key_rows, head_width),
            ),
        )

    shift_grads, (grad_queries, key_parts, value_parts) = lax.scan(
        backward_one,
        jnp.zeros((heads_here, query_rows + key_rows), jnp.float32),
        (queries, keys_all, values_all, doc_ids, grad_attended, log_sums),
    )
    grad_keys, grad_values = (
        lax.psum_scatter(
            key_parts.astype(jnp.bfloat16), "ctx", scatter_dimension=1, tiled=True
        ).astype(jnp.float32),
        lax.psum_scatter(
            value_parts.astype(jnp.bfloat16), "ctx", scatter_dimension=1, tiled=True
        ).astype(jnp.float32),
    )
    grad_keys = grad_keys.astype(jnp.bfloat16)
    grad_values = grad_values.astype(jnp.bfloat16)
    normed_one_terms = (
        jnp.einsum("sqe,de->sqd", grad_queries, full_query, preferred_element_type=jnp.float32)
        + jnp.einsum("sqe,de->sqd", grad_keys, full_key, preferred_element_type=jnp.float32)
        + jnp.einsum("sqe,de->sqd", grad_values, full_value, preferred_element_type=jnp.float32)
    )
    grad_normed_one = lax.psum(normed_one_terms.astype(jnp.bfloat16), "tp").astype(jnp.float32)
    query_grad = jnp.einsum(
        "sqd,sqe->de", normed_one, grad_queries, preferred_element_type=jnp.float32
    )
    key_grad = jnp.einsum("sqd,sqe->de", normed_one, grad_keys, preferred_element_type=jnp.float32)
    value_grad = jnp.einsum(
        "sqd,sqe->de", normed_one, grad_values, preferred_element_type=jnp.float32
    )
    first_value, first_back = jax.vjp(rms_norm, inputs, gain_first)
    grad_inputs, first_gain_grad = first_back(grad_normed_one)
    input_rows = grad_residual + grad_inputs
    bias_gradient = lax.psum(jnp.dot(one_hot.T, shift_grads.T, precision=highest), ("fsdp", "ctx"))
    (
        query_total,
        key_total,
        value_total,
        output_total,
        gate_total,
        up_total,
        down_total,
        first_total,
        second_total,
    ) = (
        lax.psum_scatter(query_grad, ("fsdp", "ctx"), scatter_dimension=0, tiled=True),
        lax.psum_scatter(key_grad, ("fsdp", "ctx"), scatter_dimension=0, tiled=True),
        lax.psum_scatter(value_grad, ("fsdp", "ctx"), scatter_dimension=0, tiled=True),
        lax.psum_scatter(output_grad, ("fsdp", "ctx"), scatter_dimension=0, tiled=True),
        lax.psum_scatter(gate_grad, ("fsdp", "ctx"), scatter_dimension=0, tiled=True),
        lax.psum_scatter(up_grad, ("fsdp", "ctx"), scatter_dimension=0, tiled=True),
        lax.psum_scatter(down_grad, ("fsdp", "ctx"), scatter_dimension=0, tiled=True),
        lax.psum_scatter(first_gain_grad, ("fsdp", "ctx"), scatter_dimension=0, tiled=True),
        lax.psum_scatter(second_gain_grad, ("fsdp", "ctx"), scatter_dimension=0, tiled=True),
    )
    return (
        output_rows,
        input_rows,
        query_total,
        key_total,
        value_total,
        output_total,
        gate_total,
        up_total,
        down_total,
        first_total,
        second_total,
        bias_gradient,
    )


MESH = pl.DeviceIdType.MESH
bf16, f32 = jnp.bfloat16, jnp.float32
BLOCK = 128
QUERY_BLOCK = 256
FORWARD_BLOCK = 256
CHUNK = 32
LAG = 4
RELAY_ROWS = 32
EARLY = 4
PACES = (1, 2, 1)


def contract(left, right, left_dim, right_dim, precision=None):
    return lax.dot_general(
        left,
        right,
        (((left_dim,), (right_dim,)), ((), ())),
        preferred_element_type=f32,
        precision=precision,
    )


def iota(shape, dim):
    return lax.broadcasted_iota(jnp.int32, shape, dim)


def layer_kernel(
    shards,
    x_hbm,
    cot_hbm,
    ids_ref,
    gain_one_ref,
    gain_two_ref,
    wq_ref,
    wk_ref,
    wv_ref,
    wo_ref,
    wg_ref,
    wu_ref,
    wd_ref,
    table_ref,
    out_hbm,
    gin_hbm,
    gq_hbm,
    gk_hbm,
    gv_hbm,
    go_hbm,
    gg_hbm,
    gu_hbm,
    gd_hbm,
    gain_one_out_ref,
    gain_two_out_ref,
    bias_out_ref,
    x_ref,
    cot_ref,
    out_ref,
    gin_ref,
    ga_ref,
    gf_ref,
    staged,
    wkv,
    wqo,
    wo3,
    other_out,
    wo_all,
    wf,
    gains_all,
    gain_rows,
    tiles,
    masked_bias,
    score,
    expo,
    low_score,
    snd,
    part,
    tot,
    resid,
    grad_res,
    n1,
    n2,
    grl,
    n1t,
    turned,
    act,
    ggate,
    gup,
    q_t,
    k_all,
    v_all,
    k_t,
    v_t,
    att_all,
    dos_t,
    dq_t,
    linv,
    delta,
    dk,
    dv,
    near,
    pick,
    dkv_send,
    dkv_recv,
    dkv,
    gsa,
    gsf,
    ra,
    rf,
    sa,
    sf,
    ra2,
    rf2,
    small,
    small_all,
    gain_part,
    load_sem,
    store_sem,
    ag_send,
    ag_recv,
    zo_send,
    zo_recv,
    at_send,
    at_recv,
    kv_send,
    kv_recv,
    s1,
    r1,
    s2,
    r2,
    dkv_ssem,
    dkv_rsem,
    rs_send,
    rs_recv,
    rs2_send,
    rs2_recv,
    sm_send,
    sm_recv,
    gp_send,
    gp_recv,
):
    groups = shards // 2
    f, c, t = lax.axis_index("fsdp"), lax.axis_index("ctx"), lax.axis_index("tp")
    me = f * 2 + c
    rows, width = x_ref.shape
    keys = k_all.shape[0]
    head_width = wq_ref.shape[1]
    heads = head_width // DH
    units = wg_ref.shape[1]
    shard = wq_ref.shape[0]
    chunks = rows // CHUNK
    per_block = BLOCK // CHUNK
    partner = (f, 1 - c, t)
    outer = jnp.logical_or(t == 0, t == 3)
    inner = jnp.logical_or(t == 1, t == 2)
    near_end = jnp.where(t < 2, 1, 2)
    far_end = jnp.where(t < 2, 0, 3)
    middle = 3 - t

    def remote(source, target, send_sem, recv_sem, device):
        return pltpu.make_async_remote_copy(
            src_ref=source,
            dst_ref=target,
            send_sem=send_sem,
            recv_sem=recv_sem,
            device_id=device,
            device_id_type=MESH,
        )

    barrier = pltpu.get_barrier_semaphore()
    for k in range(groups):
        for kc in range(2):
            if k or kc:
                pl.semaphore_signal(
                    barrier, inc=1, device_id=(f ^ k, c ^ kc, t), device_id_type=MESH
                )

    for kt in range(1, 4):
        pl.semaphore_signal(
            barrier, inc=1, device_id=(f, c, t ^ kt), device_id_type=MESH
        )
    loads = [
        pltpu.make_async_copy(source, target, load_sem.at[n])
        for n, (source, target) in enumerate(
            (
                (wk_ref, staged.at[0]),
                (wv_ref, staged.at[1]),
                (wq_ref, staged.at[2]),
                (wo_ref, staged.at[3]),
                (x_hbm, x_ref),
                (wg_ref, wf.at[me, 0]),
                (wu_ref, wf.at[me, 1]),
                (wd_ref, wf.at[me, 2]),
                (cot_hbm, cot_ref),
            )
        )
    ]
    for copy in loads:
        copy.start()
    gains_all[me] = jnp.zeros((8, BLOCK), f32)
    gains_all[me, 0:1, 0:shard] = gain_one_ref[...].astype(f32)
    gains_all[me, 1:2, 0:shard] = gain_two_ref[...].astype(f32)
    for copy in loads[:4]:
        copy.wait()
    wkv[me, :, 0:head_width] = staged[0]
    wkv[me, :, head_width:] = staged[1]
    wqo[me, :, 0:head_width] = staged[2]
    wqo[me, :, head_width:] = staged[3]
    pl.semaphore_wait(barrier, shards - 1 + 3)

    def piece(g, index):
        if g < 2:
            return (wkv, wqo)[g].at[index]
        return wo3.at[index] if g == 5 else wf.at[index, g - 2]

    def half_piece(g, index, n):
        return piece(g, index).at[n * (shard // 2) : (n + 1) * (shard // 2)]

    def own_copy(g, k):
        view = piece(g, me)
        return remote(view, view, ag_send.at[g, k - 1], ag_recv.at[g, k - 1], (f ^ k, c, t))

    def pass_copy(g, k):
        view = half_piece(g, (f ^ k) * 2 + c, k - 1)
        return remote(view, view, ag_send.at[g, k + 1], ag_recv.at[g, k + 1], (f ^ (3 - k), c, t))

    def over_piece(g, k):
        view = piece(g, (f ^ k) * 2 + c)
        return remote(view, view, ag_send.at[g, 4 + k], ag_recv.at[g, 4 + k], partner)

    def gather_own(g):
        for k in (1, 2):
            own_copy(g, k).start()
        over_piece(g, 0).start()

    def gather_pass(g):
        for k in (1, 2):
            own_copy(g, k).wait_recv()
            pass_copy(g, k).start()
            over_piece(g, k).start()

    def gather_corner(g):
        for k in (1, 2):
            pass_copy(g, k).wait_recv()
        over_piece(g, 3).start()

    def gather_finish(g):
        for k in range(4):
            over_piece(g, k).wait_recv()

    def gather_drain(g):
        for k in (1, 2):
            own_copy(g, k).wait_send()
            pass_copy(g, k).wait_send()
        for k in range(4):
            over_piece(g, k).wait_send()

    def gain_copy(k):
        view = gains_all.at[me]
        return remote(view, view, ag_send.at[6, k], ag_recv.at[6, k], (f ^ k, c, t))

    def gain_over(k):
        view = gains_all.at[(f ^ k) * 2 + c]
        return remote(view, view, ag_send.at[6, 4 + k], ag_recv.at[6, 4 + k], partner)

    def span(j):
        if isinstance(j, int):
            return pl.ds(j * CHUNK, CHUNK)
        return pl.ds(pl.multiple_of(j * CHUNK, CHUNK), CHUNK)

    def end_copy(a, j):
        return remote(
            snd.at[a, span(j)], part.at[a, span(j)], s1.at[a, j], r1.at[a, j], (f, c, near_end)
        )

    def mid_copy(a, j):
        return remote(
            snd.at[a, span(j)], tot.at[a, span(j)], s1.at[a, j], r2.at[a, j], (f, c, middle)
        )

    def total_copy(a, j):
        return remote(
            tot.at[a, span(j)], tot.at[a, span(j)], s2.at[a, j], r2.at[a, j], (f, c, far_end)
        )

    def add_rows(target, a, j, left, right):
        def body(r, carry):
            at = pl.ds(pl.multiple_of(j * CHUNK + r * RELAY_ROWS, RELAY_ROWS), RELAY_ROWS)
            target[a, at] = (left[a, at].astype(f32) + right[a, at].astype(f32)).astype(bf16)
            return carry

        lax.fori_loop(0, CHUNK // RELAY_ROWS, body, 0)

    def flush(first, last):
        @pl.when(inner)
        def _():
            for n in range(first, last):
                a, j = divmod(n, chunks)
                mid_copy(a, j).wait_recv()
                add_rows(tot, a, j, snd, tot)
                total_copy(a, j).start()

    def service(step):
        def total_step():
            a, j = split(step - LAG)
            mid_copy(a, j).wait_recv()
            add_rows(tot, a, j, snd, tot)
            total_copy(a, j).start()

        def middle_step():
            a, j = split(step)
            end_copy(a, j).wait_recv()
            add_rows(snd, a, j, snd, part)
            mid_copy(a, j).start()

        def split(n):
            if isinstance(n, int):
                return divmod(n, chunks)
            return lax.div(n, chunks), lax.rem(n, chunks)

        if isinstance(step, int):
            if step >= LAG and not chunks <= step < chunks + LAG:
                pl.when(inner)(total_step)
            if step < 3 * chunks:
                pl.when(inner)(middle_step)
        else:
            flushed = jnp.logical_and(step >= chunks, step < chunks + LAG)
            due = jnp.logical_and(step >= LAG, jnp.logical_not(flushed))
            pl.when(jnp.logical_and(inner, due))(total_step)
            pl.when(jnp.logical_and(inner, step < 3 * chunks))(middle_step)

    def serve(start, count):
        for n in range(count):
            service(start + n)

    def put_block(a, b):
        @pl.when(outer)
        def _():
            for j in range(per_block):
                end_copy(a, b * per_block + j).start()

    def totals_of(a, b):
        @pl.when(outer)
        def _():
            for j in range(per_block):
                total_copy(a, b * per_block + j).wait_recv()

    def drain_all():
        def body(n, carry):
            a, j = lax.div(n, chunks), lax.rem(n, chunks)

            @pl.when(outer)
            def _():
                end_copy(a, j).wait_send()

            @pl.when(inner)
            def _():
                mid_copy(a, j).wait_send()
                total_copy(a, j).wait_send()

            return carry

        lax.fori_loop(0, 3 * chunks, body, 0)

    for k in range(1, 4):
        gain_copy(k).start()
    gain_over(0).start()
    gather_own(0)
    gather_own(1)
    out_copies = [
        remote(
            staged.at[3], other_out.at[k - 1], zo_send.at[k - 1], zo_recv.at[k - 1], (f, c, t ^ k)
        )
        for k in range(1, 4)
    ]
    for copy in out_copies:
        copy.start()

    half = table_ref.shape[1] // 2
    far = half - 1
    row_of, column_of = iota((BLOCK, BLOCK), 0), iota((BLOCK, BLOCK), 1)
    for h in range(heads):
        tiles[h, 0] = jnp.full((BLOCK, BLOCK), table_ref[h, far], f32)
        tiles[h, 4] = jnp.full((BLOCK, BLOCK), table_ref[h, half + far], f32)
    for d in (-1, 0, 1):
        bucket = bucket_of(d * BLOCK + row_of - column_of)
        members = range(half) if d < 0 else range(half, 2 * half) if d > 0 else range(2 * half)

        def per_head(h, carry, bucket=bucket, members=members, d=d):
            filled = jnp.zeros((BLOCK, BLOCK), f32)
            for b in members:
                filled = jnp.where(bucket == b, table_ref[h, b], filled)
            tiles[h, d + 2] = filled
            return carry

        lax.fori_loop(0, heads, per_head, 0)

    def bias_rows(kb, carry):
        key_rows = pl.ds(pl.multiple_of(kb * BLOCK, BLOCK), BLOCK)
        key_ids = jnp.broadcast_to(ids_ref[0:1, key_rows].astype(f32), (BLOCK, BLOCK)).T
        for qb in range(rows // BLOCK):
            start = pl.multiple_of(c * rows + qb * BLOCK, BLOCK)
            query_ids = ids_ref[0:1, pl.ds(start, BLOCK)].astype(f32)
            same = key_ids == query_ids
            d = jnp.clip(kb - c * (rows // BLOCK) - qb, -2, 2) + 2
            for h in range(heads):
                masked_bias[h, key_rows, qb * BLOCK : (qb + 1) * BLOCK] = jnp.where(
                    same, tiles[h, d], masked_score
                )
        return carry

    key_blocks = keys // BLOCK
    lax.fori_loop(0, key_blocks // 4, bias_rows, 0)
    for k in range(1, 4):
        gain_copy(k).wait_recv()
        gain_over(k).start()
    gather_pass(0)
    lax.fori_loop(key_blocks // 4, key_blocks // 2, bias_rows, 0)
    gather_pass(1)
    for copy in loads[4:]:
        copy.wait()
    gather_own(2)
    gather_own(3)
    for k in range(4):
        gain_over(k).wait_recv()
    spread = jnp.zeros((8, width), f32)
    for i in range(shards):
        one_hot = (iota((BLOCK, width), 1) == iota((BLOCK, width), 0) + i * shard).astype(f32)
        spread = spread + contract(gains_all[i].astype(bf16), one_hot.astype(bf16), 1, 0)
    gain_rows[...] = spread

    def block_rows(b, size=BLOCK):
        if isinstance(b, int):
            return pl.ds(b * size, size)
        return pl.ds(pl.multiple_of(b * size, size), size)

    def inverse_rms(values):
        return lax.rsqrt(jnp.mean(values * values, axis=-1, keepdims=True) + epsilon)

    def norm_one(b, carry):
        at = block_rows(b)
        xs = x_ref[at, :].astype(f32)
        n1[at, :] = (xs * inverse_rms(xs) * gain_rows[0:1, :]).astype(bf16)
        return carry

    lax.fori_loop(0, rows // BLOCK, norm_one, 0)

    def weight(buffer, a):
        return buffer[:, a].reshape(width, buffer.shape[-1])

    own_rows = pl.ds(pl.multiple_of(t * head_width, DH), head_width)
    own_keys = pl.ds(pl.multiple_of(c * rows, rows), rows)
    normed = n1[...]
    kv_copies = [
        remote(ref.at[own_keys], ref.at[own_keys], kv_send.at[n], kv_recv.at[n], partner)
        for n, ref in enumerate((k_all, v_all))
    ]
    gather_corner(0)
    lax.fori_loop(key_blocks // 2, key_blocks * 3 // 4, bias_rows, 0)
    gather_finish(0)
    mixed_kv = contract(normed, wkv[...].reshape(width, 2 * head_width), 1, 0).astype(bf16)
    k_all[own_keys, :] = mixed_kv[:, 0:head_width]
    kv_copies[0].start()
    v_all[own_keys, :] = mixed_kv[:, head_width:]
    kv_copies[1].start()
    gather_corner(1)
    lax.fori_loop(key_blocks * 3 // 4, key_blocks, bias_rows, 0)
    gather_pass(2)
    for k in range(1, 4):
        out_copies[k - 1].wait_recv()
        wo3[me, :, (k - 1) * head_width : k * head_width] = other_out[k - 1]
    gather_own(5)
    gather_own(4)
    gather_finish(1)
    q_t[...] = contract(normed, wqo[:, :, 0:head_width].reshape(width, head_width), 1, 0).astype(bf16).T
    for copy in kv_copies:
        copy.wait_recv()
    v_t[...] = v_all[...].T

    def head_only(values, h):
        head_of = iota(values.shape, 0)
        inside = jnp.logical_and(head_of >= h * DH, head_of < (h + 1) * DH)
        return jnp.where(inside, values, jnp.zeros_like(values))

    def attended_copy(source, b, slot, target):
        view = att_all.at[
            pl.ds(pl.multiple_of(source * head_width, DH), head_width), block_rows(b)
        ]
        return remote(view, view, at_send.at[slot, b], at_recv.at[source, b], (f, c, target))

    def attended_start(b):
        @pl.when(outer)
        def _():
            attended_copy(t, b, 0, near_end).start()

        @pl.when(inner)
        def _():
            attended_copy(t, b, 0, far_end).start()
            attended_copy(t, b, 1, middle).start()

    def attended_relay(b, part):
        @pl.when(inner)
        def _():
            source = (far_end, middle, 3 - far_end)[part]
            attended_copy(source, b, 2 + part, middle if part == 0 else far_end).wait_recv()
            attended_copy(source, b, 2 + part, middle if part == 0 else far_end).start()

    def attended_wait(b):
        @pl.when(outer)
        def _():
            for source in (near_end, 3 - near_end, 3 - t):
                attended_copy(source, b, 0, near_end).wait_recv()

    def attended_drain(b, carry):
        attended_copy(t, b, 0, near_end).wait_send()

        @pl.when(inner)
        def _():
            for slot in range(1, 5):
                attended_copy(t, b, slot, middle).wait_send()

        return carry

    def attend(qb):
        at = block_rows(qb, FORWARD_BLOCK)

        def per_head(h, carry):
            queries = head_only(q_t[:, at], h)
            top = jnp.full((8, FORWARD_BLOCK), -jnp.inf, f32)
            for kb in range(keys // BLOCK):
                span_k = slice(kb * BLOCK, (kb + 1) * BLOCK)
                block = contract(k_all[span_k, :], queries, 1, 0) + masked_bias[h, span_k, at]
                score[span_k, 0:FORWARD_BLOCK] = block
                top = jnp.maximum(top, jnp.max(block.reshape(BLOCK // 8, 8, FORWARD_BLOCK), axis=0))
            top = jnp.max(top, axis=0, keepdims=True)
            total = jnp.zeros((8, FORWARD_BLOCK), f32)
            for kb in range(keys // BLOCK):
                span_k = slice(kb * BLOCK, (kb + 1) * BLOCK)
                block = jnp.exp(score[span_k, 0:FORWARD_BLOCK] - top)
                expo[h, span_k, at] = block.astype(bf16)
                total = total + jnp.sum(block.reshape(BLOCK // 8, 8, FORWARD_BLOCK), axis=0)
            inverse = 1.0 / jnp.sum(total, axis=0, keepdims=True)
            linv[h, :, at] = jnp.broadcast_to(inverse, (8, FORWARD_BLOCK))
            head_rows = pl.ds(pl.multiple_of(h * DH, DH), DH)
            own_head = pl.ds(pl.multiple_of(t * head_width + h * DH, DH), DH)
            mixed = contract(v_t[head_rows, :], expo[h, :, at], 1, 0)
            att_all[own_head, at] = (mixed * inverse).astype(bf16)
            return carry

        lax.fori_loop(0, heads, per_head, 0)
        for n in range(FORWARD_BLOCK // BLOCK):
            attended_start(qb * (FORWARD_BLOCK // BLOCK) + n)

    blocks = rows // BLOCK
    scale = 0.7978845608028654
    forward_blocks = rows // FORWARD_BLOCK

    def attend_loop(qb, carry):
        attend(qb)

        @pl.when(qb == 0)
        def _():
            gather_pass(3)

        return carry

    lax.fori_loop(0, forward_blocks, attend_loop, 0)
    per_forward = FORWARD_BLOCK // BLOCK
    early = range(per_forward)
    late = range(per_forward, blocks)

    def relays(group, part):
        for b in group:
            attended_relay(b, part)

    gather_corner(2)
    near[...] = jnp.zeros_like(near)
    wo_all[t] = wqo[:, :, head_width:].reshape(width, head_width)
    gather_pass(5)
    relays(early, 0)
    relays(early, 1)
    gather_pass(4)
    gather_corner(3)
    relays(late, 0)
    relays(late, 1)
    gather_corner(5)
    relays(early, 2)
    gather_corner(4)
    k_t[...] = k_all[...].T
    n1t[...] = n1[...].T
    dk[...] = jnp.zeros_like(dk)
    dv[...] = jnp.zeros_like(dv)
    small[...] = jnp.zeros_like(small)
    gather_finish(5)
    for k in range(1, 4):
        wo_all[t ^ k] = wo3[:, :, (k - 1) * head_width : k * head_width].reshape(width, head_width)
    relays(late, 2)
    for g in (2, 3, 4):
        gather_finish(g)

    def feed_forward(b, carry):
        attended_wait(b)
        at = block_rows(b)
        res = x_ref[at, :].astype(f32)
        for source in range(4):
            attended = att_all[source * head_width : (source + 1) * head_width, at].T
            res = res + contract(attended, wo_all[source], 1, 1)
        resid[at, :] = res
        normed = (res * inverse_rms(res) * gain_rows[1:2, :]).astype(bf16)
        n2[at, :] = normed
        gate = contract(normed, weight(wf, 0), 1, 0)
        up = contract(normed, weight(wf, 1), 1, 0)
        down = weight(wf, 2)
        grad_act = contract(cot_ref[at, :], down, 1, 0)

        @pl.when(b > 1)
        def _():
            serve((b - 2) * per_block + per_block // 2, per_block // 2)

        square = gate * gate
        curve = jnp.tanh(scale * (gate + 0.044715 * square * gate))
        left = 0.5 * (1.0 + curve)
        value = gate * left
        slope = left + 0.5 * gate * (1.0 - curve * curve) * scale * (1.0 + 0.134145 * square)
        low_act = (value * up).astype(bf16)
        low_gate = (grad_act * up * slope).astype(bf16)
        low_up = (grad_act * value).astype(bf16)
        act[at, :] = low_act
        ggate[at, :] = low_gate
        gup[at, :] = low_up
        snd[0, at, :] = (
            contract(low_gate, weight(wf, 0), 1, 1) + contract(low_up, weight(wf, 1), 1, 1)
        ).astype(bf16)
        put_block(0, b)
        snd[1, at, :] = contract(low_act, down, 1, 1).astype(bf16)

        @pl.when(b > 0)
        def _():
            serve((b - 1) * per_block, per_block // 2)

        return carry

    lax.fori_loop(0, blocks, feed_forward, 0)
    serve((blocks - 2) * per_block + per_block // 2, per_block // 2)

    def put_outputs(b, carry):
        put_block(1, b)
        return carry

    lax.fori_loop(0, blocks, put_outputs, 0)
    turned[0] = n2[...].T
    turned[1] = cot_ref[...].T

    def sent(n, which):
        if n == 0:
            return gsf.at[:, which]
        return gsa.at[:, which, 3:4] if n == 1 else gsa.at[:, which, 0:3]

    def landed(n):
        return rf.at[...] if n == 0 else ra.at[:, 3:4] if n == 1 else ra.at[:, 0:3]

    def over_copy(n):
        return remote(sent(n, 1 - c), landed(n), rs_send.at[n], rs_recv.at[n], partner)

    def summed(n, index):
        return sf.at[index] if n == 0 else sa.at[index, 3:4] if n == 1 else sa.at[index, 0:3]

    def arrived(n, k):
        return rf2.at[k - 1] if n == 0 else ra2.at[k - 1, 3:4] if n == 1 else ra2.at[k - 1, 0:3]

    def out_copy(n, k):
        return remote(
            summed(n, f ^ k), arrived(n, k), rs2_send.at[n, k - 1], rs2_recv.at[n, k - 1],
            (f ^ k, c, t),
        )

    members_of = {0: (0, 1, 2), 1: (3,), 2: (0, 1, 2)}
    outputs = {0: (gg_hbm, gu_hbm, gd_hbm), 1: (go_hbm,), 2: (gk_hbm, gv_hbm, gq_hbm)}

    def part_stores(n):
        results = gf_ref if n == 0 else ga_ref
        offset = (0, 3, 4)[n]
        return [
            pltpu.make_async_copy(results.at[a], target, store_sem.at[offset + i])
            for i, (a, target) in enumerate(zip(members_of[n], outputs[n]))
        ]

    def reduce_send(n):
        over_copy(n).wait_recv()
        own, got, total = (gsf, rf, sf) if n == 0 else (gsa, ra, sa)

        def body(k, carry):
            index = jnp.bitwise_xor(f, groups - 1 - k)
            for a in members_of[n]:
                total[index, a] = (
                    own[index, c, a].astype(f32) + got[index, a].astype(f32)
                ).astype(bf16)
            return carry

        lax.fori_loop(0, groups, body, 0)
        for k in range(1, groups):
            out_copy(n, k).start()

    def reduce_finish(n):
        total, got = (sf, rf2) if n == 0 else (sa, ra2)
        for k in range(1, groups):
            out_copy(n, k).wait_recv()
        results = gf_ref if n == 0 else ga_ref
        for a in members_of[n]:
            value = total[f, a].astype(f32)
            for k in range(1, groups):
                value = value + got[k - 1, a].astype(f32)
            results[a] = value
        for copy in part_stores(n):
            copy.start()

    def reduce_drain(n):
        over_copy(n).wait_send()
        for k in range(1, groups):
            out_copy(n, k).wait_send()

    both = 2 * shard

    def store_grad(buffer, i, a, value):
        buffer[i, :, a] = value.astype(bf16).reshape(2, shard, value.shape[-1])

    def pair_rows(i):
        return block_rows(i, both)

    def feed_forward_weights(i):
        at = pair_rows(i)
        store_grad(gsf, i, 0, contract(turned[0, at, :], ggate[...], 1, 0))
        store_grad(gsf, i, 1, contract(turned[0, at, :], gup[...], 1, 0))
        store_grad(gsf, i, 2, contract(turned[1, at, :], act[...], 1, 0))

    def residual_back(b):
        totals_of(0, b)
        at = block_rows(b)
        grad_in = tot[0, at, :].astype(f32)
        res = resid[at, :]
        inverse = inverse_rms(res)
        u = res * inverse
        small[1:2, :] += jnp.sum(grad_in * u, axis=0, keepdims=True)
        g = grad_in * gain_rows[1:2, :]
        grad = cot_ref[at, :].astype(f32) + inverse * (
            g - u * jnp.mean(g * u, axis=-1, keepdims=True)
        )
        grad_res[at, :] = grad
        low_grad = grad.astype(bf16)
        grl[at, :] = low_grad
        grad_att = contract(low_grad, wo_all[t], 1, 0).astype(bf16)
        scaled = grad_att.T.astype(f32) * jnp.concatenate(
            [jnp.broadcast_to(linv[h, 0:1, at], (DH, BLOCK)) for h in range(heads)], axis=0
        )
        scaled = scaled.astype(bf16)
        dos_t[:, at] = scaled
        products = scaled.astype(f32) * att_all[own_rows, at].astype(f32)
        for h in range(heads):
            delta[h, :, at] = jnp.broadcast_to(
                jnp.sum(products[h * DH : (h + 1) * DH], axis=0, keepdims=True), (8, BLOCK)
            )

    extra = dk.shape[1] - head_width
    query_blocks = rows // BLOCK

    def attend_back(start, size, h):
        at = slice(start, start + size)
        first = start // BLOCK
        head_rows = pl.ds(pl.multiple_of(h * DH, DH), DH)
        if True:
            grads = head_only(dos_t[:, at], h)
            queries = head_only(q_t[:, at], h)
            flag = iota((extra, size), 0)
            lane = iota((extra, size), 1)
            flags = jnp.zeros((extra, size), f32)
            for j in range(size // BLOCK):
                hit = jnp.logical_and(
                    flag == h * query_blocks + first + j,
                    jnp.logical_and(lane >= j * BLOCK, lane < (j + 1) * BLOCK),
                )
                flags = jnp.where(hit, 1.0, flags)
            flagged = jnp.concatenate([queries, flags.astype(bf16)], axis=0)
            shift = delta[h, 0:1, at]
            for kb in range(keys // BLOCK):
                span_k = slice(kb * BLOCK, (kb + 1) * BLOCK)
                block = contract(v_all[span_k, :], grads, 1, 0)
                low_score[span_k, 0:size] = (
                    expo[h, span_k, at].astype(f32) * (block - shift)
                ).astype(bf16)
            dv[...] += contract(expo[h, :, at], grads, 1, 1)
            dk[...] += contract(low_score[:, 0:size], flagged, 1, 1)
            dq_t[head_rows, at] = contract(
                k_t[head_rows, :], low_score[:, 0:size], 1, 0
            ).astype(bf16)
            for j in range(size // BLOCK):
                home = c * query_blocks + first + j
                for d in (-1, 0, 1):
                    kb = home + d
                    valid = jnp.logical_and(kb >= 0, kb < keys // BLOCK)

                    @pl.when(valid)
                    def _():
                        where_k = jnp.clip(kb, 0, keys // BLOCK - 1)
                        near[h, d + 1] += low_score[
                            block_rows(where_k), j * BLOCK : (j + 1) * BLOCK
                        ].astype(f32)

    pace = per_block // 2
    step = (blocks - 1) * per_block

    query_parts = [(start, QUERY_BLOCK) for start in range(0, rows - QUERY_BLOCK, QUERY_BLOCK)]
    query_parts += [(start, BLOCK) for start in range(rows - QUERY_BLOCK, rows, BLOCK)]
    for qb, (start, size) in enumerate(query_parts):
        for b in range(start // BLOCK, (start + size) // BLOCK):
            residual_back(b)
            if qb == 0:
                service(step)
                step += 1

        def back_head(h, carry, start=start, size=size, step=step, qb=qb):
            attend_back(start, size, h)
            serve(h * PACES[qb] + step, PACES[qb])
            return carry

        lax.fori_loop(0, heads, back_head, 0)
        step += heads * PACES[qb]
        if qb == 0:

            def early_weights(i, carry, step=step):
                feed_forward_weights(i)

                @pl.when(i < EARLY)
                def _():
                    service(i + step)

                return carry

            lax.fori_loop(0, groups, early_weights, 0)
            step += EARLY
            over_copy(0).start()
            flush(chunks - LAG, chunks)
        if qb == 1:
            reduce_send(0)

    other_keys = pl.ds(pl.multiple_of((1 - c) * rows, rows), rows)
    dkv_send[0] = dk[other_keys, 0:head_width].astype(bf16)
    dkv_send[1] = dv[other_keys, :].astype(bf16)
    dkv_copy = remote(dkv_send.at[...], dkv_recv.at[...], dkv_ssem.at[0], dkv_rsem.at[0], partner)
    dkv_copy.start()
    dkv_copy.wait_recv()
    dkv[:, 0:head_width] = (dk[own_keys, 0:head_width] + dkv_recv[0].astype(f32)).astype(bf16)
    dkv[:, head_width:] = (dv[own_keys, :] + dkv_recv[1].astype(f32)).astype(bf16)

    def project_back(b, carry):
        at = block_rows(b)
        total = contract(
            dq_t[:, at].T, wqo[:, :, 0:head_width].reshape(width, head_width), 1, 1
        )
        total = total + contract(dkv[at, :], wkv[...].reshape(width, 2 * head_width), 1, 1)
        snd[2, at, :] = total.astype(bf16)
        put_block(2, b)

        @pl.when(step + (b + 1) * pace <= 2 * chunks)
        def _():
            serve(step + b * pace, pace)

        return carry

    lax.fori_loop(0, blocks, project_back, 0)
    step += min(blocks, (2 * chunks - step) // pace) * pace

    def weights_back(i, carry):
        part_rows = n1t[pair_rows(i), :]
        mixed = contract(part_rows, dkv[...], 1, 0)
        store_grad(gsa, i, 0, mixed[:, 0:head_width])
        store_grad(gsa, i, 1, mixed[:, head_width:])
        store_grad(gsa, i, 2, contract(part_rows, dq_t[...], 1, 1))
        return carry

    serve(step, 2 * chunks - step)
    step = 2 * chunks

    def output_weights(i, carry):
        store_grad(gsa, i, 3, contract(turned[0, pair_rows(i), :], att_all[own_rows, :], 1, 1))
        return carry


    def bucket_sums(h, carry):
        for b in range(2 * half):
            summed_block = jnp.zeros((8, BLOCK), f32)
            for d in (-1, 0) if b < half else (0, 1):
                bucket = bucket_of(d * BLOCK + row_of - column_of)
                chosen = jnp.where(bucket == b, near[h, d + 1], 0.0)
                summed_block = summed_block + jnp.sum(
                    chosen.reshape(BLOCK // 8, 8, BLOCK), axis=0
                )
            pick[b : b + 1, :] = jnp.sum(summed_block, axis=0, keepdims=True)
        sums = contract(jnp.ones((8, BLOCK), f32), pick[...], 1, 1, highest)
        small[:, 0 : 2 * half] += jnp.where(iota((8, 2 * half), 0) == 2 + h, sums, 0.0)
        return carry

    def far_sums():
        tail = dk.shape[1] - BLOCK
        first_lane = head_width - tail
        column_sums = dk[:, tail:]
        block_row = iota((keys, BLOCK), 0)
        lane = iota((keys, BLOCK), 1)
        left_sum = jnp.zeros((1, BLOCK), f32)
        right_sum = jnp.zeros((1, BLOCK), f32)
        for j in range(query_blocks):
            mine = jnp.zeros((keys, BLOCK), jnp.bool_)
            for h in range(heads):
                mine = jnp.logical_or(mine, lane == first_lane + h * query_blocks + j)
            home = c * query_blocks + j
            is_left = jnp.logical_and(mine, block_row < (home - 1) * BLOCK)
            is_right = jnp.logical_and(mine, block_row >= (home + 2) * BLOCK)
            left_sum += jnp.sum(jnp.where(is_left, column_sums, 0.0), axis=0, keepdims=True)
            right_sum += jnp.sum(jnp.where(is_right, column_sums, 0.0), axis=0, keepdims=True)
        from_lane, to_lane = iota((BLOCK, BLOCK), 0), iota((BLOCK, BLOCK), 1)
        for h in range(heads):
            start = first_lane + h * query_blocks
            inside = jnp.logical_and(from_lane >= start, from_lane < start + query_blocks)
            left_pick = jnp.logical_and(inside, to_lane == far).astype(f32)
            right_pick = jnp.logical_and(inside, to_lane == half + far).astype(f32)
            small[2 + h : 3 + h, 0:BLOCK] += (
                contract(jnp.broadcast_to(left_sum, (8, BLOCK)), left_pick, 1, 0, highest)
                + contract(jnp.broadcast_to(right_sum, (8, BLOCK)), right_pick, 1, 0, highest)
            )[0:1]

    def block_store(n, source, target, b):
        at = block_rows(b)
        return pltpu.make_async_copy(source.at[at], target.at[at], store_sem.at[n])

    def input_back(b):
        totals_of(2, b)
        at = block_rows(b)
        grad_in = tot[2, at, :].astype(f32)
        xs = x_ref[at, :].astype(f32)
        inverse = inverse_rms(xs)
        u = xs * inverse
        g = grad_in * gain_rows[0:1, :]
        gin_ref[at, :] = grad_res[at, :] + inverse * (
            g - u * jnp.mean(g * u, axis=-1, keepdims=True)
        )
        block_store(7 + b, gin_ref, gin_hbm, b).start()

    def layer_out(b):
        totals_of(1, b)
        at = block_rows(b)
        out_ref[at, :] = (resid[at, :] + tot[1, at, :].astype(f32)).astype(bf16)
        block_store(7 + blocks + b, out_ref, out_hbm, b).start()

    small_copies = [
        remote(
            small.at[...], small_all.at[me], sm_send.at[k * 2 + kc - 1], sm_recv.at[k * 2 + kc - 1],
            (f ^ k, c ^ kc, t),
        )
        for k in range(groups)
        for kc in range(2)
        if k or kc
    ]

    def small_start():
        for copy in small_copies:
            copy.start()
        small_all[me] = small[...]

    def small_finish():
        for copy in small_copies:
            copy.wait_recv()
        total_small = small_all[0]
        for i in range(1, shards):
            total_small = total_small + small_all[i]
        to_own = (iota((width, BLOCK), 0) == iota((width, BLOCK), 1) + me * shard).astype(f32)
        own_gains = contract(total_small, to_own, 1, 0, highest)
        gain_two_out_ref[...] = own_gains[1:2, 0:shard]
        bias_out_ref[...] = total_small[2 : 2 + heads, 0 : 2 * half]

    gain_copies = [
        remote(
            gain_part.at[t], gain_part.at[t], gp_send.at[kt - 1], gp_recv.at[kt - 1], (f, c, t ^ kt)
        )
        for kt in range(1, 4)
    ]

    def gain_start():
        products = jnp.zeros((shard, head_width), f32)
        for a in members_of[2]:
            products = products + staged[a].astype(f32) * ga_ref[a]
        row_sums = contract(jnp.ones((8, head_width), f32), products, 1, 1, highest)
        gain_part[t, :, 0:shard] = row_sums / gain_one_ref[...].astype(f32)
        for copy in gain_copies:
            copy.start()

    def gain_finish():
        for copy in gain_copies:
            copy.wait_recv()
        total = gain_part[0, 0:1, 0:shard]
        for i in range(1, 4):
            total = total + gain_part[i, 0:1, 0:shard]
        gain_one_out_ref[...] = total

    @pl.when(outer)
    def _():
        lax.fori_loop(0, heads, bucket_sums, 0)
        far_sums()

    def at_step(n, value, run):
        pl.when(n == value)(run)

    def last_steps(n, carry):
        service(2 * chunks + n)

        @pl.when(n < groups)
        def _():
            weights_back(n, 0)

        def turn():
            over_copy(2).start()
            turned[0] = grl[...].T

        at_step(n, groups - 1, turn)

        @pl.when(jnp.logical_and(n >= groups, n < 2 * groups))
        def _():
            output_weights(n - groups, 0)

        at_step(n, groups + 1, functools.partial(reduce_send, 2))
        at_step(n, 2 * groups - 1, over_copy(1).start)
        at_step(n, 2 * groups + 1, functools.partial(reduce_send, 1))
        after = n - 2 * groups

        @pl.when(
            jnp.logical_and(
                jnp.logical_and(inner, lax.rem(n, 2) == 0),
                jnp.logical_and(after >= 0, after < 2 * heads),
            )
        )
        def _():
            bucket_sums(lax.div(after, 2), 0)

        def sums_out():
            pl.when(inner)(far_sums)
            small_start()

        at_step(n, 2 * groups + 2 * heads - 1, sums_out)
        for due_step, b in zip((6, 9, 13, 14), range(blocks)):

            @pl.when(n == due_step)
            def _(b=b):
                layer_out(b)

        at_step(n, chunks - 2, functools.partial(reduce_finish, 0))

        def gains():
            reduce_finish(2)
            gain_start()

        at_step(n, chunks - 1, gains)
        at_step(n, chunks + 1, small_finish)
        at_step(n, chunks + 2, functools.partial(reduce_finish, 1))

        due = n - (per_block - 1) - LAG

        @pl.when(jnp.logical_and(due >= 0, lax.rem(due, per_block) == 0))
        def _():
            input_back(lax.div(due, per_block))

        return carry

    lax.fori_loop(0, chunks + LAG, last_steps, 0)
    gain_finish()
    for b in range(blocks):
        block_store(7 + b, gin_ref, gin_hbm, b).wait()
        block_store(7 + blocks + b, out_ref, out_hbm, b).wait()
    for n in range(3):
        for copy in part_stores(n):
            copy.wait()
    for copy in small_copies + gain_copies:
        copy.wait_send()
    for g in range(6):
        gather_drain(g)
    for copy in out_copies:
        copy.wait_send()
    lax.fori_loop(0, blocks, attended_drain, 0)
    for k in range(1, 4):
        gain_copy(k).wait_send()
    for k in range(4):
        gain_over(k).wait_send()
    for copy in kv_copies:
        copy.wait_send()
    dkv_copy.wait_send()
    drain_all()
    for n in range(3):
        reduce_drain(n)


def fused_layer(shards, x, cot, ids, gain_one, gain_two, weights, table):
    rows, width = x.shape
    shard, head_width = weights[0].shape
    units = weights[4].shape[1]
    keys = ids.shape[1]
    heads = head_width // DH
    groups = shards // 2
    chunks = rows // CHUNK
    padded = head_width + (-head_width) % BLOCK
    if padded - head_width < heads * (rows // BLOCK):
        padded += BLOCK
    vmem, dma = pltpu.VMEM, pltpu.SemaphoreType.DMA
    out_shape = (
        jax.ShapeDtypeStruct((rows, width), bf16),
        jax.ShapeDtypeStruct((rows, width), f32),
        *[jax.ShapeDtypeStruct((shard, head_width), f32)] * 4,
        *[jax.ShapeDtypeStruct((shard, units), f32)] * 3,
        jax.ShapeDtypeStruct((1, shard), f32),
        jax.ShapeDtypeStruct((1, shard), f32),
        jax.ShapeDtypeStruct(table.shape, f32),
    )
    in_vmem = pl.BlockSpec(memory_space=pltpu.VMEM)
    anywhere = pl.BlockSpec(memory_space=pl.ANY)
    scratch = [
        vmem((rows, width), bf16),
        vmem((rows, width), bf16),
        vmem((rows, width), bf16),
        vmem((rows, width), f32),
        vmem((4, shard, head_width), f32),
        vmem((3, shard, units), f32),
        vmem((4, shard, head_width), bf16),
        vmem((shards, shard, 2 * head_width), bf16),
        vmem((shards, shard, 2 * head_width), bf16),
        vmem((shards, shard, 3 * head_width), bf16),
        vmem((3, shard, head_width), bf16),
        vmem((4, width, head_width), bf16),
        vmem((shards, 3, shard, units), bf16),
        vmem((shards, 8, BLOCK), f32),
        vmem((8, width), f32),
        vmem((heads, 5, BLOCK, BLOCK), f32),
        vmem((heads, keys, rows), f32),
        vmem((keys, QUERY_BLOCK), f32),
        vmem((heads, keys, rows), bf16),
        vmem((keys, QUERY_BLOCK), bf16),
        vmem((3, rows, width), bf16),
        vmem((3, rows, width), bf16),
        vmem((3, rows, width), bf16),
        vmem((rows, width), f32),
        vmem((rows, width), f32),
        vmem((rows, width), bf16),
        vmem((rows, width), bf16),
        vmem((rows, width), bf16),
        vmem((width, rows), bf16),
        vmem((2, width, rows), bf16),
        vmem((rows, units), bf16),
        vmem((rows, units), bf16),
        vmem((rows, units), bf16),
        vmem((head_width, rows), bf16),
        vmem((keys, head_width), bf16),
        vmem((keys, head_width), bf16),
        vmem((head_width, keys), bf16),
        vmem((head_width, keys), bf16),
        vmem((4 * head_width, rows), bf16),
        vmem((head_width, rows), bf16),
        vmem((head_width, rows), bf16),
        vmem((heads, 8, rows), f32),
        vmem((heads, 8, rows), f32),
        vmem((keys, padded), f32),
        vmem((keys, head_width), f32),
        vmem((heads, 3, BLOCK, BLOCK), f32),
        vmem((table.shape[1], BLOCK), f32),
        vmem((2, rows, head_width), bf16),
        vmem((2, rows, head_width), bf16),
        vmem((rows, 2 * head_width), bf16),
        vmem((groups, 2, 4, shard, head_width), bf16),
        vmem((groups, 2, 3, shard, units), bf16),
        vmem((groups, 4, shard, head_width), bf16),
        vmem((groups, 3, shard, units), bf16),
        vmem((groups, 4, shard, head_width), bf16),
        vmem((groups, 3, shard, units), bf16),
        vmem((groups - 1, 4, shard, head_width), bf16),
        vmem((groups - 1, 3, shard, units), bf16),
        vmem((8, width), f32),
        vmem((shards, 8, width), f32),
        vmem((4, 8, BLOCK), f32),
        dma((9,)),
        dma((7 + 2 * (rows // BLOCK),)),
        dma((7, 8)),
        dma((7, 8)),
        dma((3,)),
        dma((3,)),
        dma((5, rows // BLOCK)),
        dma((4, rows // BLOCK)),
        dma((2,)),
        dma((2,)),
        dma((3, chunks)),
        dma((3, chunks)),
        dma((3, chunks)),
        dma((3, chunks)),
        dma((1,)),
        dma((1,)),
        dma((3,)),
        dma((3,)),
        dma((3, groups)),
        dma((3, groups)),
        dma((shards,)),
        dma((shards,)),
        dma((3,)),
        dma((3,)),
    ]
    return pl.pallas_call(
        functools.partial(layer_kernel, shards),
        out_shape=out_shape,
        in_specs=[anywhere] * 2
        + [in_vmem] * 3
        + [anywhere] * 7
        + [pl.BlockSpec(memory_space=pltpu.SMEM)],
        out_specs=[anywhere] * 9 + [in_vmem] * 3,
        scratch_shapes=scratch,
        name="layer",
        compiler_params=pltpu.CompilerParams(
            collective_id=0, has_side_effects=True, vmem_limit_bytes=63 << 20
        ),
    )(x, cot, ids, gain_one, gain_two, *weights, table)


def publish_kernel(count, *refs):
    sources, targets = refs[:count], refs[count : 2 * count]
    held, in_sem, out_sem = refs[2 * count : 3 * count], refs[3 * count], refs[3 * count + 1]
    inward = [
        pltpu.make_async_copy(sources[i], held[i], in_sem.at[i]) for i in range(count)
    ]
    outward = [
        pltpu.make_async_copy(held[i], targets[i], out_sem.at[i]) for i in range(count)
    ]
    for copy in inward:
        copy.start()
    for arriving, leaving in zip(inward, outward):
        arriving.wait()
        leaving.start()
    for copy in outward:
        copy.wait()


def publish(values):
    count = len(values)
    anywhere = pl.BlockSpec(memory_space=pl.ANY)
    return pl.pallas_call(
        functools.partial(publish_kernel, count),
        out_shape=[jax.ShapeDtypeStruct(value.shape, value.dtype) for value in values],
        in_specs=[anywhere] * count,
        out_specs=[anywhere] * count,
        scratch_shapes=[pltpu.VMEM(value.shape, value.dtype) for value in values]
        + [pltpu.SemaphoreType.DMA((count,))] * 2,
        name="publish",
    )(*values)


def on_device_fused(
    layer_input,
    doc_ids,
    query_weight,
    key_weight,
    value_weight,
    output_weight,
    gate_weight,
    up_weight,
    down_weight,
    first_gain,
    second_gain,
    position_bias,
    cotangent,
):
    shards = lax.axis_size("fsdp") * lax.axis_size("ctx")
    outs = fused_layer(
        shards,
        layer_input[0],
        cotangent[0],
        doc_ids,
        first_gain[None],
        second_gain[None],
        (
            query_weight,
            key_weight,
            value_weight,
            output_weight,
            gate_weight,
            up_weight,
            down_weight,
        ),
        position_bias.T,
    )
    outs = publish(outs)
    return (
        outs[0][None],
        outs[1][None],
        *outs[2:9],
        outs[9][0],
        outs[10][0],
        outs[11].T,
    )


def fits_kernel(mesh):
    return mesh.shape["ctx"] == 2 and mesh.shape["tp"] == 4 and mesh.shape["fsdp"] == 4


def solution(mesh):
    return jax.shard_map(
        on_device_fused if fits_kernel(mesh) else on_device,
        mesh=mesh,
        in_specs=(
            P("fsdp", "ctx", None),
            P("fsdp", None),
            P(("fsdp", "ctx"), "tp"),
            P(("fsdp", "ctx"), "tp"),
            P(("fsdp", "ctx"), "tp"),
            P(("fsdp", "ctx"), "tp"),
            P(("fsdp", "ctx"), "tp"),
            P(("fsdp", "ctx"), "tp"),
            P(("fsdp", "ctx"), "tp"),
            P(("fsdp", "ctx")),
            P(("fsdp", "ctx")),
            P(None, "tp"),
            P("fsdp", "ctx", None),
        ),
        out_specs=(
            P("fsdp", "ctx", None),
            P("fsdp", "ctx", None),
            P(("fsdp", "ctx"), "tp"),
            P(("fsdp", "ctx"), "tp"),
            P(("fsdp", "ctx"), "tp"),
            P(("fsdp", "ctx"), "tp"),
            P(("fsdp", "ctx"), "tp"),
            P(("fsdp", "ctx"), "tp"),
            P(("fsdp", "ctx"), "tp"),
            P(("fsdp", "ctx")),
            P(("fsdp", "ctx")),
            P(None, "tp"),
        ),
        check_vma=False,
    )
```
